32 devices in a mesh: ep: 16 (over z, x, core), tp: 2 (over y).
Axes of the slice: x: 2, y: 2, z: 4, core: 2. Of those that a mesh axis runs over, the one named last changes fastest.
Arguments:
- tokens: bfloat16 [32768, 1024], P('ep'), may hold values from -6 to 6
- out_grad: bfloat16 [32768, 1024], P(('ep', 'tp')), may hold values from -12 to 12
- lengths: int32 [16], P('ep'), may hold values from 256 to 2048, as said below
- expert_ids: int32 [32768], P('ep'), may hold values from 0 to 15, as said below
- w_query: bfloat16 [1024, 1024], P(None, 'tp'), may hold values from -0.1875 to 0.1875
- w_key: bfloat16 [1024, 1024], P(None, 'tp'), may hold values from -0.1875 to 0.1875
- w_value: bfloat16 [1024, 1024], P(None, 'tp'), may hold values from -0.1875 to 0.1875
- w_output: bfloat16 [1024, 1024], P(None, 'tp'), may hold values from -1.5 to 1.5
- w_hidden: bfloat16 [1024, 4096], P(None, 'tp'), may hold values from -0.1875 to 0.1875
- w_return: bfloat16 [1024, 4096], P(None, 'tp'), may hold values from -0.09375 to 0.09375
- router: bfloat16 [1024, 16], replicated, may hold values from -0.125 to 0.125
- mix_weight: bfloat16 [1024, 2], replicated, may hold values from -0.125 to 0.125
- gain_attn: bfloat16 [1024], replicated, may hold values from 0.5 to 1.5
- bias_attn: bfloat16 [1024], replicated, may hold values from -1.25 to 1.25
- gain_ffn: bfloat16 [1024], replicated, may hold values from 0.5 to 1.5
- bias_ffn: bfloat16 [1024], replicated, may hold values from -1.25 to 1.25
- expert_in: bfloat16 [16, 1024, 4096], P('ep', None, 'tp'), may hold values from -0.1875 to 0.1875
- expert_out: bfloat16 [16, 1024, 4096], P('ep', None, 'tp'), may hold values from -0.09375 to 0.09375
Outputs:
- block_out: bfloat16 [32768, 1024], P(('ep', 'tp'))
- token_grad: float32 [32768, 1024], P(('ep', 'tp'))
- grad_query: float32 [1024, 1024], P('ep', 'tp')
- grad_key: float32 [1024, 1024], P('ep', 'tp')
- grad_value: float32 [1024, 1024], P('ep', 'tp')
- grad_output: float32 [1024, 1024], P('ep', 'tp')
- grad_hidden: float32 [1024, 4096], P('ep', 'tp')
- grad_return: float32 [1024, 4096], P('ep', 'tp')
- grad_router: float32 [1024, 16], replicated
- grad_mix: float32 [1024, 2], replicated
- grad_gain_attn: float32 [1024], replicated
- grad_bias_attn: float32 [1024], replicated
- grad_gain_ffn: float32 [1024], replicated
- grad_bias_ffn: float32 [1024], replicated
- grad_expert_in: float32 [16, 1024, 4096], P('ep', None, 'tp')
- grad_expert_out: float32 [16, 1024, 4096], P('ep', None, 'tp')
The draws below stay inside these ranges and needn't reach their ends.
Inputs may be any that keep to these rules, and one draw needn't show every extreme that they name: `lengths`: entry i belongs to the sequence at rows i * 2048 to i * 2048 + 2047; positions at and past its length are padding. `expert_ids`: among the live rows of one index of ep (its 2048 rows) no expert is named more than 128 times; values on padding rows are never used.
All inputs are finite; a program needn't handle non-finite values.
Results may differ from the reference program's by a relative error of at most 0.018.
Values may be sent and summed in bfloat16 or wider, within the bound.
A program may use at most 320 MiB of HBM per device.

```python
import jax
import jax.numpy as jnp
from jax import lax

D = 1024
HEADS = 16
HEAD_DIM = 64
FF = 4096
SEQ = 2048
MIN_LEN = 256
SEQS_DEV = 1
TOK_DEV = 2048
SEQS = 16
TOKENS = 32768
EXPERTS = 16
CAP = 128
N_EP = 16


def draw_length_table(key):
    base_key = jax.random.fold_in(key, 11)
    drawn_lengths = jax.random.randint(jax.random.fold_in(base_key, 1), (SEQS,), MIN_LEN, SEQ + 1)
    longest = jax.random.randint(jax.random.fold_in(base_key, 2), (), 0, SEQS)
    shortest = (longest + 1 + jax.random.randint(jax.random.fold_in(base_key, 3), (), 0, SEQS - 1)) % SEQS
    places = jnp.arange(SEQS)
    drawn_lengths = jnp.where(places == longest, SEQ, drawn_lengths)
    return jnp.where(places == shortest, MIN_LEN, drawn_lengths).astype(jnp.int32)


def draw_lengths(key, part):
    return draw_length_table(key)


def draw_expert_ids(key, part):
    length_table = draw_length_table(key)
    route_key = jax.random.fold_in(key, 23)
    hot_expert = jax.random.randint(jax.random.fold_in(route_key, 0), (), 0, EXPERTS)
    owners = SEQS // SEQS_DEV
    ticket_base = jnp.arange((EXPERTS - 1) * CAP) // CAP
    others = ticket_base + (ticket_base >= hot_expert).astype(ticket_base.dtype)
    positions = jnp.arange(TOK_DEV)
    spread = 2 ** 30 // TOK_DEV

    def one_device(device):
        device_key = jax.random.fold_in(route_key, device + 1)
        shuffled = jax.random.permutation(jax.random.fold_in(device_key, 0), others)
        tickets = jnp.concatenate([jnp.full((CAP,), hot_expert, jnp.int32), shuffled.astype(jnp.int32)])
        local_lengths = lax.dynamic_slice_in_dim(length_table, device * SEQS_DEV, SEQS_DEV)
        seq_index = positions // SEQ
        row_limit = jnp.sum(jnp.where(seq_index[:, None] == jnp.arange(SEQS_DEV)[None, :], local_lengths[None, :], 0), axis=1)
        live_rows = positions % SEQ < row_limit
        drawn_scores = jax.random.randint(jax.random.fold_in(device_key, 1), (TOK_DEV,), 0, spread)
        scores = jnp.where(live_rows, drawn_scores * TOK_DEV + positions, 2 ** 30 + positions)
        row_ranks = jnp.argsort(jnp.argsort(scores))
        filler = jax.random.randint(jax.random.fold_in(device_key, 2), (TOK_DEV,), 0, EXPERTS)
        return jnp.where(live_rows, tickets[row_ranks], filler.astype(jnp.int32))
    return jax.vmap(one_device)(jnp.arange(owners)).reshape(TOKENS).astype(jnp.int32)


def strengthened(array, own_key, source, target, blocks, factor):
    owner, partner = [(jnp.arange(array.shape[position]) // (array.shape[position] // blocks)).reshape([-1 if axis == position else 1 for axis in range(array.ndim)]) for position in (source, target)]
    chosen = jax.random.permutation(own_key, blocks)[partner]
    strong = (owner == chosen) | (owner == (partner + blocks // 2) % blocks)
    return jnp.where(strong, factor * array, array)


def steps_of(key, dims, pieces, least, top_value):
    loudness = 1.0
    for dim, shards_of in pieces:
        heights = jax.random.uniform(jax.random.fold_in(jax.random.fold_in(key, 6), dim), (shards_of,), jnp.float32, least / len(pieces), top_value / len(pieces))
        loudness = loudness * jnp.repeat(jnp.exp(heights), dims[dim] // shards_of).reshape((-1,) + (1,) * (len(dims) - 1 - dim))
    return loudness


def normal_values(own_key, shape, width, most, cuts=(), kind=jnp.bfloat16):
    loudness = steps_of(own_key, shape, cuts, -0.22, 0.18) if cuts else 1.0
    array = jax.random.normal(own_key, shape, jnp.float32) * width * loudness
    return jnp.minimum(jnp.maximum(array, -most), most).astype(kind)


def heavy_noise(rng, dims, scale, reach, pieces, heavy, held_as=jnp.bfloat16):
    array = scale * jax.random.normal(rng, dims, jnp.float32)
    if pieces:
        array = array * steps_of(rng, dims, pieces, -0.22, 0.18)
    return jnp.clip(strengthened(array, jax.random.fold_in(rng, 3), *heavy), -reach, reach).astype(held_as)


def setup_inputs(seed: int = 0) -> dict:
    splits = jax.random.split(jax.random.key(seed), 19)
    tokens = normal_values(splits[0], (TOKENS, D), 1.0, 6.0, ((0, 16),))
    out_grad = heavy_noise(splits[1], (TOKENS, D), 1.0, 12.0, ((0, 32),), (0, 1, 32, 2.75))
    lengths = draw_lengths(jax.random.fold_in(splits[18], 71), 0)
    expert_ids = draw_expert_ids(jax.random.fold_in(splits[18], 71), 0)
    w_query = normal_values(splits[4], (D, D), D ** -0.5, 0.1875, ((1, 2),))
    w_key = normal_values(splits[5], (D, D), D ** -0.5, 0.1875, ((1, 2),))
    w_value = normal_values(splits[6], (D, D), D ** -0.5, 0.1875, ((1, 2),))
    w_output = normal_values(splits[7], (D, D), (D // 64) ** -0.5, 1.5, ((1, 2),))
    w_hidden = normal_values(splits[8], (D, FF), D ** -0.5, 0.1875, ((1, 2),))
    w_return = normal_values(splits[9], (D, FF), FF ** -0.5, 0.09375, ((1, 2),))
    router = normal_values(splits[10], (D, EXPERTS), (2 * D) ** -0.5, 0.125)
    mix_weight = normal_values(splits[11], (D, 2), (2 * D) ** -0.5, 0.125)
    gain_attn = jnp.clip(1.0 + 0.1 * jax.random.normal(splits[12], (D,), jnp.float32), 0.5, 1.5).astype(jnp.bfloat16)
    bias_attn = normal_values(splits[13], (D,), 0.2, 1.25)
    gain_ffn = jnp.clip(1.0 + 0.1 * jax.random.normal(splits[14], (D,), jnp.float32), 0.5, 1.5).astype(jnp.bfloat16)
    bias_ffn = normal_values(splits[15], (D,), 0.2, 1.25)
    expert_in = normal_values(splits[16], (EXPERTS, D, FF), D ** -0.5, 0.1875, ((0, 16), (2, 2)))
    expert_out = normal_values(splits[17], (EXPERTS, D, FF), FF ** -0.5, 0.09375, ((0, 16), (2, 2)))
    return {"tokens": tokens, "out_grad": out_grad, "lengths": lengths, "expert_ids": expert_ids, "w_query": w_query, "w_key": w_key, "w_value": w_value, "w_output": w_output, "w_hidden": w_hidden, "w_return": w_return, "router": router, "mix_weight": mix_weight, "gain_attn": gain_attn, "bias_attn": bias_attn, "gain_ffn": gain_ffn, "bias_ffn": bias_ffn, "expert_in": expert_in, "expert_out": expert_out}


EPS = 1e-05
NEG = -1e+30
HIGH = lax.Precision.HIGHEST

@jax.custom_vjp
def low(v):
    return lax.optimization_barrier(v.astype(jnp.bfloat16)).astype(jnp.float32)

@jax.custom_vjp
def low_back(v):
    return v

def low_keep(v):
    return (low(v), None)

def low_pass(kept, grad):
    return (grad,)

def back_keep(v):
    return (v, None)

def back_low(kept, grad):
    return (low(grad),)
low.defvjp(low_keep, low_pass)
low_back.defvjp(back_keep, back_low)

def layer_norm(values, gain, bias):
    middle = lax.optimization_barrier(jnp.mean(values, axis=-1, keepdims=True))
    centred = values - middle
    spread = lax.optimization_barrier(jnp.mean(centred * centred, axis=-1, keepdims=True))
    return centred * lax.rsqrt(spread + EPS) * gain + bias

def gelu_tanh(values):
    return jax.nn.gelu(values, approximate=True)

def product(left, right):
    return jnp.dot(left, right, precision=HIGH, preferred_element_type=jnp.float32)

def attend(queries, key_all, values):
    block_rows = min(512, SEQ)
    score_scale = HEAD_DIM ** (-0.5)
    count_blocks = SEQ // block_rows
    blocks = queries.reshape(count_blocks, block_rows, HEADS, HEAD_DIM)
    firsts = (jnp.arange(count_blocks) * block_rows).astype(jnp.int32)
    key_pos = jnp.arange(SEQ).astype(jnp.int32)

    def one_block(inputs):
        query_block, first_row = inputs
        scores = jnp.einsum('qhd,khd->hqk', query_block, key_all, precision=HIGH) * score_scale
        scores = low_back(scores)
        query_pos = first_row + jnp.arange(block_rows).astype(jnp.int32)
        allowed = key_pos[None, :] <= query_pos[:, None]
        scores = jnp.where(allowed[None], scores, NEG)
        weights = low(jax.nn.softmax(scores, axis=-1))
        return jnp.einsum('hqk,khd->qhd', weights, values, precision=HIGH)
    return lax.map(jax.checkpoint(one_block), (blocks, firsts)).reshape(SEQ, HEADS, HEAD_DIM)

def block_forward(weights, tokens, ids, lengths):
    w_query, w_key, w_value, w_output, w_hidden, w_return, router, mix_weight, gain_attn, bias_attn, gain_ffn, bias_ffn, expert_in, expert_out = weights
    positions = jnp.arange(TOK_DEV).astype(jnp.int32)
    seq_index = positions // SEQ
    row_limit = lax.optimization_barrier(jnp.sum(jnp.where(seq_index[:, None] == jnp.arange(SEQS_DEV).astype(jnp.int32)[None, :], lengths[None, :], 0), axis=1))
    live = (positions % SEQ < row_limit).astype(jnp.float32)[:, None]
    attn_in = low(layer_norm(tokens, gain_attn, bias_attn))
    head_shape = (SEQS_DEV, SEQ, HEADS, HEAD_DIM)
    queries = low(low_back(product(attn_in, w_query))).reshape(head_shape)
    key_all = low(low_back(product(attn_in, w_key))).reshape(head_shape)
    values = low(low_back(product(attn_in, w_value))).reshape(head_shape)
    attended = jax.vmap(attend)(queries, key_all, values).reshape(TOK_DEV, D)
    attended = low(low_back(attended))
    resid = tokens + low_back(product(attended, w_output.T))
    ffn_in = low(layer_norm(resid, gain_ffn, bias_ffn))
    logits = low_back(product(ffn_in, router))
    mix_logits = low_back(product(ffn_in, mix_weight))
    one_hot = (ids[:, None] == jnp.arange(EXPERTS).astype(jnp.int32)[None, :]).astype(jnp.float32)
    gate = lax.optimization_barrier(jnp.sum(jax.nn.softmax(logits, axis=-1) * one_hot, axis=1, keepdims=True))
    mix = jax.nn.softmax(mix_logits, axis=-1)
    hidden = low(gelu_tanh(low_back(product(ffn_in, w_hidden))))
    dense = low_back(product(hidden, w_return.T))
    routed = one_hot * live
    slots = lax.optimization_barrier(jnp.sum((jnp.cumsum(routed, axis=0) - routed) * one_hot, axis=1)).astype(jnp.int32)
    target = jnp.where(live[:, 0] > 0, ids * CAP + slots, EXPERTS * CAP).astype(jnp.int32)
    safe_target = jnp.minimum(target, EXPERTS * CAP - 1).astype(jnp.int32)
    packed = jnp.zeros((EXPERTS * CAP, D), jnp.float32).at[target].set(ffn_in, mode='drop').reshape(EXPERTS, CAP, D)
    expert_pre = low_back(jnp.einsum('ecd,edf->ecf', packed, expert_in, precision=HIGH))
    expert_act = low(gelu_tanh(expert_pre))
    expert_res = low_back(jnp.einsum('ecf,edf->ecd', expert_act, expert_out, precision=HIGH))
    moe = expert_res.reshape(EXPERTS * CAP, D)[safe_target] * live
    return live * (resid + mix[:, 0:1] * dense + mix[:, 1:2] * gate * moe)

def reference(tokens, out_grad, lengths, expert_ids, w_query, w_key, w_value, w_output, w_hidden, w_return, router, mix_weight, gain_attn, bias_attn, gain_ffn, bias_ffn, expert_in, expert_out):
    weights = tuple((item.astype(jnp.float32) for item in (w_query, w_key, w_value, w_output, w_hidden, w_return, router, mix_weight, gain_attn, bias_attn, gain_ffn, bias_ffn, expert_in, expert_out)))
    token_blocks = tokens.astype(jnp.float32).reshape(N_EP, TOK_DEV, D)
    id_blocks = expert_ids.astype(jnp.int32).reshape(N_EP, TOK_DEV)
    length_blocks = lengths.astype(jnp.int32).reshape(N_EP, SEQS_DEV)
    checked = jax.checkpoint(block_forward)

    def forward(weights, token_blocks):

        def step(running, inputs):
            block_tokens, block_ids, block_lengths = inputs
            return (running, checked(weights, block_tokens, block_ids, block_lengths))
        return lax.scan(step, jnp.zeros((), jnp.float32), (token_blocks, id_blocks, length_blocks))[1]
    outputs, pull = jax.vjp(forward, weights, token_blocks)
    weight_grads, token_grads = pull(out_grad.astype(jnp.float32).reshape(N_EP, TOK_DEV, D))
    grad_query, grad_key, grad_value, grad_output, grad_hidden, grad_return, grad_router, grad_mix, grad_gain_attn, grad_bias_attn, grad_gain_ffn, grad_bias_ffn, grad_expert_in, grad_expert_out = weight_grads
    return (outputs.reshape(TOKENS, D).astype(jnp.bfloat16), token_grads.reshape(TOKENS, D), grad_query, grad_key, grad_value, grad_output, grad_hidden, grad_return, grad_router, grad_mix, grad_gain_attn, grad_bias_attn, grad_gain_ffn, grad_bias_ffn, grad_expert_in, grad_expert_out)
```

```python
import functools
from functools import partial

import jax
import jax.numpy as jnp
from jax import lax
from jax.experimental import pallas as pl
from jax.experimental.pallas import tpu as pltpu
from jax.sharding import PartitionSpec as P

HEAD_DIM = 64
PAIR = 2 * HEAD_DIM


EPS = 1e-05
NEG = -1e30
F32 = jnp.float32
BF16 = jnp.bfloat16
NT = (((1,), (1,)), ((), ()))


def layer_norm(values, gain, bias):
    middle = jnp.mean(values, axis=-1, keepdims=True)
    centred = values - middle
    spread = jnp.mean(centred * centred, axis=-1, keepdims=True)
    return centred * lax.rsqrt(spread + EPS) * gain + bias


def gelu_tanh(values):
    return jax.nn.gelu(values, approximate=True)


def matmul(left, right):
    return jnp.dot(left, right, preferred_element_type=jnp.float32)


def matmul_nt(left, right):
    return lax.dot_general(left, right, NT, preferred_element_type=jnp.float32)


def matmul_tn(left, right):
    return lax.dot_general(
        left, right, (((0,), (0,)), ((), ())), preferred_element_type=jnp.float32
    )


def gate_and_mix(logits, mix_logits, one_hot):
    chances = jax.nn.softmax(logits, axis=-1)
    return (jnp.sum(chances * one_hot, axis=-1), jax.nn.softmax(mix_logits, axis=-1))


def attention_forward_kernel(q_ref, k_ref, v_ref, o_ref, lse_ref, vt_ref, *, bq, bk, scale):
    qi = pl.program_id(2)

    @pl.when(qi == 0)
    def _():
        vt_ref[...] = v_ref[...].T

    lane = lax.broadcasted_iota(jnp.int32, (bq, PAIR), 1)
    q = q_ref[...] * jnp.asarray(scale, BF16)
    zero = jnp.zeros_like(q)
    halves = [jnp.where(lane < HEAD_DIM, q, zero), jnp.where(lane < HEAD_DIM, zero, q)]

    def step(j, carry, masked):
        off = pl.multiple_of(j * bk, bk)
        k = k_ref[pl.ds(off, bk), :]
        vt = vt_ref[:, pl.ds(off, bk)]
        scores = [lax.dot_general(k, half, NT, preferred_element_type=F32) for half in halves]
        if masked:
            key_pos = off + lax.broadcasted_iota(jnp.int32, (bk, bq), 0)
            query_pos = qi * bq + lax.broadcasted_iota(jnp.int32, (bk, bq), 1)
            allowed = key_pos <= query_pos
            scores = [jnp.where(allowed, s, NEG) for s in scores]
        new = []
        for h in range(2):
            m, l, acc = carry[h]
            m_new = jnp.maximum(m, jnp.max(scores[h], axis=0, keepdims=True))
            alpha = jnp.exp(m - m_new)
            p = jnp.exp(scores[h] - m_new)
            l = l * alpha + jnp.sum(p, axis=0, keepdims=True)
            part = jnp.dot(
                vt[h * HEAD_DIM : (h + 1) * HEAD_DIM], p.astype(BF16), preferred_element_type=F32
            )
            new.append((m_new, l, acc * alpha + part))
        return tuple(new)

    init = tuple(
        (jnp.full((1, bq), NEG, F32), jnp.zeros((1, bq), F32), jnp.zeros((HEAD_DIM, bq), F32))
        for _ in range(2)
    )
    full = qi * (bq // bk)
    carry = lax.fori_loop(0, full, lambda j, c: step(j, c, False), init)
    for d in range(bq // bk):
        carry = step(full + d, carry, True)
    outs = []
    for h in range(2):
        m, l, acc = carry[h]
        outs.append(acc / l)
        lse_ref[0, h : h + 1, :] = m + jnp.log(l)
    o_ref[...] = jnp.concatenate(outs, axis=0).T.astype(BF16)


def attention_forward(proj, seqs, heads, bq=512, bk=512):
    rows = proj.shape[0]
    length = rows // seqs
    pairs = heads // 2
    nq = length // bq
    flops = 2 * rows * length * heads * HEAD_DIM
    return pl.pallas_call(
        partial(attention_forward_kernel, bq=bq, bk=bk, scale=HEAD_DIM**-0.5),
        grid=(seqs, pairs, nq),
        in_specs=[
            pl.BlockSpec((bq, PAIR), lambda s, p, i: (s * nq + i, p)),
            pl.BlockSpec((length, PAIR), lambda s, p, i: (s, pairs + p)),
            pl.BlockSpec((length, PAIR), lambda s, p, i: (s, 2 * pairs + p)),
        ],
        out_specs=[
            pl.BlockSpec((bq, PAIR), lambda s, p, i: (s * nq + i, p)),
            pl.BlockSpec((1, 2, bq), lambda s, p, i: (p, 0, s * nq + i)),
        ],
        out_shape=[
            jax.ShapeDtypeStruct((rows, heads * HEAD_DIM), BF16),
            jax.ShapeDtypeStruct((pairs, 2, rows), F32),
        ],
        scratch_shapes=[pltpu.VMEM((PAIR, length), BF16)],
        cost_estimate=pl.CostEstimate(
            flops=flops * 4, bytes_accessed=8 * rows * heads * HEAD_DIM, transcendentals=0
        ),
        name="attention_forward",
    )(proj, proj, proj)


def attention_backward_kernel(
    q_ref,
    k_ref,
    v_ref,
    o_ref,
    do_ref,
    lse_ref,
    dq_ref,
    dk_ref,
    dv_ref,
    dqt_ref,
    qs_ref,
    dos_ref,
    kt_ref,
    dl_ref,
    *,
    bq,
    bk,
    scale,
    length,
):
    lane = lax.broadcasted_iota(jnp.int32, (length, PAIR), 1)
    first = lane < HEAD_DIM
    q = q_ref[...] * jnp.asarray(scale, BF16)
    do = do_ref[...]
    zero = jnp.zeros_like(q)
    qs_ref[0] = jnp.where(first, q, zero)
    qs_ref[1] = jnp.where(first, zero, q)
    dos_ref[0] = jnp.where(first, do, zero)
    dos_ref[1] = jnp.where(first, zero, do)
    kt_ref[...] = (k_ref[...] * jnp.asarray(scale, BF16)).T
    prod = (do.astype(F32) * o_ref[...].astype(F32)).T
    dl_ref[0:1, :] = jnp.sum(prod[:HEAD_DIM], axis=0, keepdims=True)
    dl_ref[1:2, :] = jnp.sum(prod[HEAD_DIM:], axis=0, keepdims=True)
    dqt_ref[...] = jnp.zeros_like(dqt_ref)
    nq = length // bq
    nk = length // bk

    def key_block(j, _):
        koff = pl.multiple_of(j * bk, bk)
        k = k_ref[pl.ds(koff, bk), :]
        v = v_ref[pl.ds(koff, bk), :]
        kt = kt_ref[:, pl.ds(koff, bk)]

        def step(i, carry, masked):
            dk, dv = carry
            qoff = pl.multiple_of(i * bq, bq)
            if masked:
                key_pos = koff + lax.broadcasted_iota(jnp.int32, (bk, bq), 0)
                query_pos = qoff + lax.broadcasted_iota(jnp.int32, (bk, bq), 1)
                allowed = key_pos <= query_pos
            qh = [qs_ref[h, pl.ds(qoff, bq), :] for h in range(2)]
            dh = [dos_ref[h, pl.ds(qoff, bq), :] for h in range(2)]
            scores = [lax.dot_general(k, x, NT, preferred_element_type=F32) for x in qh]
            pulls = [lax.dot_general(v, x, NT, preferred_element_type=F32) for x in dh]
            dqs = []
            for h in range(2):
                p = jnp.exp(scores[h] - lse_ref[0, h : h + 1, pl.ds(qoff, bq)])
                if masked:
                    p = jnp.where(allowed, p, 0.0)
                ds = (p * (pulls[h] - dl_ref[h : h + 1, pl.ds(qoff, bq)])).astype(BF16)
                dv = dv + jnp.dot(p.astype(BF16), dh[h], preferred_element_type=F32)
                dk = dk + jnp.dot(ds, qh[h], preferred_element_type=F32)
                dqs.append(
                    jnp.dot(
                        kt[h * HEAD_DIM : (h + 1) * HEAD_DIM], ds, preferred_element_type=F32
                    )
                )
            dqt_ref[:, pl.ds(qoff, bq)] += jnp.concatenate(dqs, axis=0)
            return dk, dv

        carry = (jnp.zeros((bk, PAIR), F32), jnp.zeros((bk, PAIR), F32))
        i0 = j * (bk // bq)
        for d in range(bk // bq):
            carry = step(i0 + d, carry, True)
        dk, dv = lax.fori_loop(i0 + bk // bq, nq, lambda i, c: step(i, c, False), carry)
        dk_ref[pl.ds(koff, bk), :] = dk.astype(BF16)
        dv_ref[pl.ds(koff, bk), :] = dv.astype(BF16)
        return 0

    lax.fori_loop(0, nk, key_block, 0)
    dq_ref[...] = dqt_ref[...].T.astype(BF16)


def attention_backward(proj, out, out_grad, lse, seqs, heads, bq=512, bk=512):
    rows = proj.shape[0]
    length = rows // seqs
    pairs = heads // 2

    def block(off):
        return pl.BlockSpec((length, PAIR), lambda s, p: (s, off + p))

    grad = jax.ShapeDtypeStruct((rows, heads * HEAD_DIM), BF16)
    flops = 5 * rows * length * heads * HEAD_DIM
    return pl.pallas_call(
        partial(attention_backward_kernel, bq=bq, bk=bk, scale=HEAD_DIM**-0.5, length=length),
        grid=(seqs, pairs),
        in_specs=[
            block(0),
            block(pairs),
            block(2 * pairs),
            block(0),
            block(0),
            pl.BlockSpec((1, 2, length), lambda s, p: (p, 0, s)),
        ],
        out_specs=[block(0)] * 3,
        out_shape=[grad] * 3,
        scratch_shapes=[
            pltpu.VMEM((PAIR, length), F32),
            pltpu.VMEM((2, length, PAIR), BF16),
            pltpu.VMEM((2, length, PAIR), BF16),
            pltpu.VMEM((PAIR, length), BF16),
            pltpu.VMEM((2, length), F32),
        ],
        cost_estimate=pl.CostEstimate(
            flops=flops * 4, bytes_accessed=16 * rows * heads * HEAD_DIM, transcendentals=0
        ),
        compiler_params=pltpu.CompilerParams(vmem_limit_bytes=40 * 1024 * 1024),
        name="attention_backward",
    )(proj, proj, proj, out, out_grad, lse)


def on_device(
    tp,
    tokens,
    out_grad,
    lengths,
    expert_ids,
    w_query,
    w_key,
    w_value,
    w_output,
    w_hidden,
    w_return,
    router,
    mix_weight,
    gain_attn,
    bias_attn,
    gain_ffn,
    bias_ffn,
    expert_in,
    expert_out,
):
    shard_rows = out_grad.shape[0]
    all_rows = tokens.shape[0]
    model_width = tokens.shape[1]
    expert_count = router.shape[1]
    capacity = all_rows // expert_count
    seq_count = lengths.shape[0]
    seq_len = all_rows // seq_count
    local_width = w_query.shape[1]
    local_heads = local_width // HEAD_DIM
    tp_index = lax.axis_index("tp")
    first_row = tp_index * shard_rows
    swap = [(0, 1), (1, 0)]

    def shard_of(values):
        return lax.dynamic_slice_in_dim(values, first_row, shard_rows, 0)

    def gather_rows(values):
        if tp != 2:
            return lax.all_gather(values, "tp", axis=0, tiled=True)
        other = lax.ppermute(values, "tp", swap)
        low = jnp.where(tp_index == 0, values, other)
        high = jnp.where(tp_index == 0, other, values)
        return jnp.concatenate([low, high], axis=0)

    def scatter_rows(partial_sums):
        if tp != 2:
            return lax.psum_scatter(
                partial_sums.astype(BF16), "tp", scatter_dimension=0, tiled=True
            ).astype(F32)
        theirs = lax.dynamic_slice_in_dim(partial_sums, shard_rows - first_row, shard_rows, 0)
        return shard_of(partial_sums) + lax.ppermute(theirs.astype(BF16), "tp", swap).astype(F32)

    def exchange(values):
        return lax.all_to_all(values, "ep", split_axis=0, concat_axis=0, tiled=True)

    positions = jnp.arange(all_rows)
    seq_index = positions // seq_len
    row_limit = jnp.sum(
        jnp.where(seq_index[:, None] == jnp.arange(seq_count)[None, :], lengths[None, :], 0), axis=1
    )
    live_all = (positions % seq_len < row_limit).astype(jnp.float32)[:, None]
    live = shard_of(live_all)
    one_hot = (expert_ids[:, None] == jnp.arange(expert_count)[None, :]).astype(jnp.float32)
    routed = one_hot * live_all
    slots = jnp.sum((jnp.cumsum(routed, axis=0) - routed) * one_hot, axis=1).astype(jnp.int32)
    slot_count = expert_count * capacity
    target = jnp.where(live_all[:, 0] > 0, expert_ids * capacity + slots, slot_count)
    mine = (live_all[:, 0] > 0) & (slots >= 0) & (slots < capacity)
    take_index = jnp.where(mine, expert_ids * capacity + slots, 0)
    mine_col = mine.astype(jnp.float32)[:, None]

    def pack(rows):
        packed = jnp.zeros((slot_count, model_width), BF16).at[target].set(rows, mode="drop")
        return packed.reshape(expert_count, capacity, model_width)

    grad_all = gather_rows(out_grad)
    grad_rows = exchange(pack(grad_all)).reshape(slot_count, model_width)

    attn_gain = gain_attn.astype(jnp.float32)
    attn_bias = bias_attn.astype(jnp.float32)
    ffn_gain = gain_ffn.astype(jnp.float32)
    ffn_bias = bias_ffn.astype(jnp.float32)
    tokens_wide = tokens.astype(jnp.float32)
    attn_in = layer_norm(tokens_wide, attn_gain, attn_bias).astype(BF16)
    qkv_weight = jnp.concatenate([w_query, w_key, w_value], axis=1)
    projected = matmul(attn_in, qkv_weight).astype(BF16)
    attn_out, log_sums = attention_forward(projected, seq_count, local_heads)
    if tp == 2:
        w_other = lax.ppermute(w_output, "tp", swap)
        heads_other = lax.ppermute(attn_out, "tp", swap)
        attn_sum = matmul_nt(attn_out, w_output) + matmul_nt(heads_other, w_other)
    else:
        w_all = lax.all_gather(w_output, "tp", axis=1, tiled=True)
        attn_sum = matmul_nt(lax.all_gather(attn_out, "tp", axis=1, tiled=True), w_all)
    resid = tokens_wide + attn_sum
    ffn_in = layer_norm(resid, ffn_gain, ffn_bias).astype(BF16)
    sent_rows = exchange(pack(ffn_in)).reshape(slot_count, model_width)

    logits = matmul(ffn_in, router)
    mix_logits = matmul(ffn_in, mix_weight)
    gate_all, mix_all = gate_and_mix(logits, mix_logits, one_hot)

    live_grad_all = live_all * grad_all.astype(jnp.float32)
    dense_grad = (live_grad_all * mix_all[:, 0:1]).astype(BF16)
    hidden_pre = matmul(ffn_in, w_hidden)
    hidden_low, gelu_pull = jax.vjp(gelu_tanh, hidden_pre)
    hidden_low = hidden_low.astype(BF16)
    dense_part = matmul_nt(hidden_low, w_return)
    hidden_grad = matmul(dense_grad, w_return)
    grad_return = matmul_tn(dense_grad, hidden_low)
    pre_grad = gelu_pull(hidden_grad)[0].astype(BF16)
    grad_hidden = matmul_tn(ffn_in, pre_grad)
    input_part = matmul_nt(pre_grad, w_hidden)
    first_dot = jnp.sum(live_grad_all * dense_part, axis=1)

    my_expert = lax.axis_index("ep")
    here = (jnp.arange(expert_count) == my_expert).astype(F32)[None, :]
    gate_here, mix_here = gate_and_mix(
        matmul(sent_rows, router), matmul(sent_rows, mix_weight), here
    )
    moe_grad = (grad_rows.astype(F32) * mix_here[:, 1:2] * gate_here[:, None]).astype(BF16)
    w_in = expert_in[0]
    w_out = expert_out[0]
    expert_pre = matmul(sent_rows, w_in)
    expert_act, expert_pull = jax.vjp(gelu_tanh, expert_pre)
    expert_act = expert_act.astype(BF16)
    result = matmul_nt(expert_act, w_out)
    dot_here = jnp.sum(grad_rows.astype(F32) * result, axis=1)
    act_grad = matmul(moe_grad, w_out)
    expert_pre_grad = expert_pull(act_grad)[0].astype(BF16)
    row_grad = matmul_nt(expert_pre_grad, w_in)
    grad_expert_out = matmul_tn(moe_grad, expert_act)[None]
    grad_expert_in = matmul_tn(sent_rows, expert_pre_grad)[None]

    blocks = (expert_count, capacity, model_width)
    back_grad = exchange(row_grad.astype(BF16).reshape(blocks)).reshape(slot_count, model_width)
    returned = exchange(result.astype(BF16).reshape(blocks)).reshape(slot_count, model_width)
    dots = exchange(dot_here.reshape(expert_count, capacity))
    slot_hot = (slots[:, None] == jnp.arange(capacity)[None, :]).astype(F32) * mine_col
    second_dot = jnp.sum(jnp.dot(one_hot, dots, precision=lax.Precision.HIGHEST) * slot_hot, axis=1)

    both_dots = lax.psum(jnp.stack([first_dot, second_dot]), "tp")
    gate_shard = shard_of(gate_all)
    mix_shard = shard_of(mix_all)
    first_shard = lax.dynamic_slice_in_dim(both_dots[0], first_row, shard_rows)
    second_shard = lax.dynamic_slice_in_dim(both_dots[1], first_row, shard_rows)
    mix_grad = jnp.stack([first_shard, gate_shard * second_shard], axis=1)
    gate_grad = mix_shard[:, 1] * second_shard
    gate_pull = jax.vjp(
        partial(gate_and_mix, one_hot=shard_of(one_hot)), shard_of(logits), shard_of(mix_logits)
    )[1]
    logit_grad, mix_logit_grad = gate_pull((gate_grad, mix_grad))
    logit_low = logit_grad.astype(BF16)
    mix_low = mix_logit_grad.astype(BF16)
    ffn_shard = shard_of(ffn_in)
    grad_router = matmul_tn(ffn_shard, logit_low)
    grad_mix = matmul_tn(ffn_shard, mix_low)
    input_part = input_part + back_grad[take_index].astype(F32) * mine_col
    input_grad = scatter_rows(input_part)
    ffn_in_grad = input_grad + matmul_nt(logit_low, router) + matmul_nt(mix_low, mix_weight)
    resid_shard = shard_of(resid)
    norm_pull_two = jax.vjp(layer_norm, resid_shard, ffn_gain, ffn_bias)[1]
    resid_part, grad_gain_ffn, grad_bias_ffn = norm_pull_two(ffn_in_grad)
    live_grad = live * out_grad.astype(jnp.float32)
    resid_grad = live_grad + resid_part

    attn_grad_all = gather_rows(resid_grad.astype(BF16))
    grad_output = matmul_tn(attn_grad_all, attn_out)
    heads_grad = matmul(attn_grad_all, w_output).astype(BF16)
    qkv_grad = attention_backward(
        projected, attn_out, heads_grad, log_sums, seq_count, local_heads
    )
    qkv_grad = jnp.concatenate(qkv_grad, axis=1)
    grad_weights = matmul_tn(attn_in, qkv_grad)
    attn_in_part = matmul_nt(qkv_grad, qkv_weight)
    norm_all = layer_norm(tokens_wide, 1.0, 0.0)
    grad_gain_attn = jnp.sum(attn_in_part * norm_all, axis=0)
    grad_bias_attn = jnp.sum(attn_in_part, axis=0)
    attn_in_grad = scatter_rows(attn_in_part)
    norm_pull_one = jax.vjp(layer_norm, shard_of(tokens_wide), attn_gain, attn_bias)[1]
    token_part = norm_pull_one(attn_in_grad)[0]
    token_grad = resid_grad + token_part

    moe_part = returned[take_index].astype(F32) * mine_col
    weighted = mix_all[:, 0:1] * dense_part + mix_all[:, 1:2] * gate_all[:, None] * moe_part
    block_out = (live * (resid_shard + scatter_rows(weighted))).astype(BF16)

    def over_sequences(values):
        return lax.psum_scatter(
            values.astype(BF16), "ep", scatter_dimension=0, tiled=True
        ).astype(F32)

    grad_hidden = over_sequences(grad_hidden)
    grad_return = over_sequences(grad_return)
    square = over_sequences(jnp.concatenate([grad_weights, grad_output], axis=1))
    grad_query, grad_key, grad_value, grad_output = jnp.split(square, 4, axis=1)
    grad_router, grad_mix, grad_gain_ffn, grad_bias_ffn = lax.psum(
        (grad_router, grad_mix, grad_gain_ffn, grad_bias_ffn), ("ep", "tp")
    )
    grad_gain_attn, grad_bias_attn = lax.psum((grad_gain_attn, grad_bias_attn), ("ep", "tp"))
    return (
        block_out,
        token_grad,
        grad_query,
        grad_key,
        grad_value,
        grad_output,
        grad_hidden,
        grad_return,
        grad_router,
        grad_mix,
        grad_gain_attn,
        grad_bias_attn,
        grad_gain_ffn,
        grad_bias_ffn,
        grad_expert_in,
        grad_expert_out,
    )


def solution(mesh):
    in_specs = (
        P("ep", None),
        P(("ep", "tp"), None),
        P("ep"),
        P("ep"),
        P(None, "tp"),
        P(None, "tp"),
        P(None, "tp"),
        P(None, "tp"),
        P(None, "tp"),
        P(None, "tp"),
        P(),
        P(),
        P(),
        P(),
        P(),
        P(),
        P("ep", None, "tp"),
        P("ep", None, "tp"),
    )
    out_specs = (
        P(("ep", "tp"), None),
        P(("ep", "tp"), None),
        P("ep", "tp"),
        P("ep", "tp"),
        P("ep", "tp"),
        P("ep", "tp"),
        P("ep", "tp"),
        P("ep", "tp"),
        P(),
        P(),
        P(),
        P(),
        P(),
        P(),
        P("ep", None, "tp"),
        P("ep", None, "tp"),
    )
    return jax.shard_map(
        partial(on_device, mesh.shape["tp"]),
        mesh=mesh,
        in_specs=in_specs,
        out_specs=out_specs,
        check_vma=False,
    )
```

```python
import math
from functools import partial

import jax
import jax.numpy as jnp
from jax import lax
from jax.experimental import pallas as pl
from jax.experimental.pallas import tpu as pltpu
from jax.sharding import PartitionSpec as P

HEAD_DIM = 64
PAIR = 2 * HEAD_DIM


EPS = 1e-05
NEG = -1e30
F32 = jnp.float32
BF16 = jnp.bfloat16
NT = (((1,), (1,)), ((), ()))


LANES = 128
GELU_C = math.sqrt(2.0 / math.pi)
GELU_A = 0.044715
BIG_VMEM = 62 * 1024 * 1024


def dot(left, right):
    return jnp.dot(left, right, preferred_element_type=F32)


def dot_nt(left, right):
    return lax.dot_general(left, right, NT, preferred_element_type=F32)


def normalized(values):
    middle = jnp.mean(values, axis=-1, keepdims=True)
    centred = values - middle
    rstd = lax.rsqrt(jnp.mean(centred * centred, axis=-1, keepdims=True) + EPS)
    return centred * rstd, rstd


def norm_pull(grad, normal, rstd, gain):
    q = grad * gain
    along = jnp.mean(q * normal, axis=-1, keepdims=True)
    return rstd * (q - jnp.mean(q, axis=-1, keepdims=True) - normal * along)


def gelu_and_slope(v):
    square = v * v
    t = jnp.tanh(v * (GELU_C + (GELU_C * GELU_A) * square))
    half = 0.5 + 0.5 * t
    slope = half + v * (0.5 - 0.5 * (t * t)) * (GELU_C + (3.0 * GELU_C * GELU_A) * square)
    return v * half, slope


def router_and_mix(logits, experts):
    lane = lax.broadcasted_iota(jnp.int32, logits.shape, 1)
    out = jnp.zeros_like(logits)
    for low, high in ((0, experts), (experts, experts + 2)):
        inside = (lane >= low) & (lane < high)
        top = jnp.max(jnp.where(inside, logits, NEG), axis=-1, keepdims=True)
        e = jnp.where(inside, jnp.exp(jnp.where(inside, logits - top, 0.0)), 0.0)
        out = out + e / jnp.sum(e, axis=-1, keepdims=True)
    return out


def lane_of(values, index):
    lane = lax.broadcasted_iota(jnp.int32, values.shape, 1)
    return jnp.sum(jnp.where(lane == index, values, 0.0), axis=-1, keepdims=True)


def resident(shape):
    return pl.BlockSpec(shape, lambda i, *_: (0,) * len(shape), pipeline_mode=pl.Buffered(1))


def cost(flops, bytes_accessed):
    return pl.CostEstimate(flops=flops, bytes_accessed=bytes_accessed, transcendentals=0)


def attention_forward_kernel(q_ref, k_ref, v_ref, o_ref, lse_ref, vt_ref, *, bq, bk, scale):
    qi = pl.program_id(2)

    @pl.when(qi == 0)
    def _():
        vt_ref[...] = v_ref[...].T

    lane = lax.broadcasted_iota(jnp.int32, (bq, PAIR), 1)
    q = q_ref[...] * jnp.asarray(scale, BF16)
    zero = jnp.zeros_like(q)
    halves = [jnp.where(lane < HEAD_DIM, q, zero), jnp.where(lane < HEAD_DIM, zero, q)]

    def step(j, carry, masked):
        off = pl.multiple_of(j * bk, bk)
        k = k_ref[pl.ds(off, bk), :]
        vt = vt_ref[:, pl.ds(off, bk)]
        scores = [lax.dot_general(k, half, NT, preferred_element_type=F32) for half in halves]
        if masked:
            key_pos = off + lax.broadcasted_iota(jnp.int32, (bk, bq), 0)
            query_pos = qi * bq + lax.broadcasted_iota(jnp.int32, (bk, bq), 1)
            allowed = key_pos <= query_pos
            scores = [jnp.where(allowed, s, NEG) for s in scores]
        new = []
        for h in range(2):
            m, l, acc = carry[h]
            m_new = jnp.maximum(m, jnp.max(scores[h], axis=0, keepdims=True))
            alpha = jnp.exp(m - m_new)
            p = jnp.exp(scores[h] - m_new)
            l = l * alpha + jnp.sum(p, axis=0, keepdims=True)
            part = jnp.dot(
                vt[h * HEAD_DIM : (h + 1) * HEAD_DIM], p.astype(BF16), preferred_element_type=F32
            )
            new.append((m_new, l, acc * alpha + part))
        return tuple(new)

    init = tuple(
        (jnp.full((1, bq), NEG, F32), jnp.zeros((1, bq), F32), jnp.zeros((HEAD_DIM, bq), F32))
        for _ in range(2)
    )
    full = qi * (bq // bk)
    carry = lax.fori_loop(0, full, lambda j, c: step(j, c, False), init)
    for d in range(bq // bk):
        carry = step(full + d, carry, True)
    outs = []
    for h in range(2):
        m, l, acc = carry[h]
        outs.append(acc / l)
        lse_ref[0, h : h + 1, :] = m + jnp.log(l)
    o_ref[...] = jnp.concatenate(outs, axis=0).T.astype(BF16)


def attention_forward(proj, seqs, heads, first, count, bq=512, bk=512):
    rows = proj.shape[0]
    length = rows // seqs
    pairs = heads // 2
    nq = length // bq
    flops = 2 * rows * length * count * PAIR
    return pl.pallas_call(
        partial(attention_forward_kernel, bq=bq, bk=bk, scale=HEAD_DIM**-0.5),
        grid=(seqs, count, nq),
        in_specs=[
            pl.BlockSpec((bq, PAIR), lambda s, p, i: (s * nq + i, first + p)),
            pl.BlockSpec((length, PAIR), lambda s, p, i: (s, pairs + first + p)),
            pl.BlockSpec((length, PAIR), lambda s, p, i: (s, 2 * pairs + first + p)),
        ],
        out_specs=[
            pl.BlockSpec((bq, PAIR), lambda s, p, i: (s * nq + i, p)),
            pl.BlockSpec((1, 2, bq), lambda s, p, i: (p, 0, s * nq + i)),
        ],
        out_shape=[
            jax.ShapeDtypeStruct((rows, count * PAIR), BF16),
            jax.ShapeDtypeStruct((count, 2, rows), F32),
        ],
        scratch_shapes=[pltpu.VMEM((PAIR, length), BF16)],
        cost_estimate=pl.CostEstimate(
            flops=flops * 4, bytes_accessed=8 * rows * count * PAIR, transcendentals=0
        ),
        name="attention_forward",
    )(proj, proj, proj)


def attention_backward_kernel(
    q_ref,
    k_ref,
    v_ref,
    o_ref,
    lse_ref,
    *refs,
    terms,
    bq,
    bk,
    scale,
    length,
):
    lane = lax.broadcasted_iota(jnp.int32, (length, PAIR), 1)
    first = lane < HEAD_DIM
    q = q_ref[...] * jnp.asarray(scale, BF16)
    do_refs = refs[:terms]
    dq_ref, dk_ref, dv_ref, dqt_ref, qs_ref, dos_ref, kt_ref, dl_ref = refs[terms:]
    do = do_refs[0][...]
    if terms == 2:
        do = (do.astype(F32) + do_refs[1][...].astype(F32)).astype(BF16)
    zero = jnp.zeros_like(q)
    qs_ref[0] = jnp.where(first, q, zero)
    qs_ref[1] = jnp.where(first, zero, q)
    dos_ref[0] = jnp.where(first, do, zero)
    dos_ref[1] = jnp.where(first, zero, do)
    kt_ref[...] = (k_ref[...] * jnp.asarray(scale, BF16)).T
    prod = (do.astype(F32) * o_ref[...].astype(F32)).T
    dl_ref[0:1, :] = jnp.sum(prod[:HEAD_DIM], axis=0, keepdims=True)
    dl_ref[1:2, :] = jnp.sum(prod[HEAD_DIM:], axis=0, keepdims=True)
    dqt_ref[...] = jnp.zeros_like(dqt_ref)
    nq = length // bq
    nk = length // bk

    def key_block(j, _):
        koff = pl.multiple_of(j * bk, bk)
        k = k_ref[pl.ds(koff, bk), :]
        v = v_ref[pl.ds(koff, bk), :]
        kt = kt_ref[:, pl.ds(koff, bk)]

        def step(i, carry, masked):
            dk, dv = carry
            qoff = pl.multiple_of(i * bq, bq)
            if masked:
                key_pos = koff + lax.broadcasted_iota(jnp.int32, (bk, bq), 0)
                query_pos = qoff + lax.broadcasted_iota(jnp.int32, (bk, bq), 1)
                allowed = key_pos <= query_pos
            qh = [qs_ref[h, pl.ds(qoff, bq), :] for h in range(2)]
            dh = [dos_ref[h, pl.ds(qoff, bq), :] for h in range(2)]
            scores = [lax.dot_general(k, x, NT, preferred_element_type=F32) for x in qh]
            pulls = [lax.dot_general(v, x, NT, preferred_element_type=F32) for x in dh]
            dqs = []
            for h in range(2):
                p = jnp.exp(scores[h] - lse_ref[0, h : h + 1, pl.ds(qoff, bq)])
                if masked:
                    p = jnp.where(allowed, p, 0.0)
                ds = (p * (pulls[h] - dl_ref[h : h + 1, pl.ds(qoff, bq)])).astype(BF16)
                dv = dv + jnp.dot(p.astype(BF16), dh[h], preferred_element_type=F32)
                dk = dk + jnp.dot(ds, qh[h], preferred_element_type=F32)
                dqs.append(
                    jnp.dot(
                        kt[h * HEAD_DIM : (h + 1) * HEAD_DIM], ds, preferred_element_type=F32
                    )
                )
            dqt_ref[:, pl.ds(qoff, bq)] += jnp.concatenate(dqs, axis=0)
            return dk, dv

        carry = (jnp.zeros((bk, PAIR), F32), jnp.zeros((bk, PAIR), F32))
        i0 = j * (bk // bq)
        for d in range(bk // bq):
            carry = step(i0 + d, carry, True)
        dk, dv = lax.fori_loop(i0 + bk // bq, nq, lambda i, c: step(i, c, False), carry)
        dk_ref[pl.ds(koff, bk), :] = dk.astype(BF16)
        dv_ref[pl.ds(koff, bk), :] = dv.astype(BF16)
        return 0

    lax.fori_loop(0, nk, key_block, 0)
    dq_ref[...] = dqt_ref[...].T.astype(BF16)


def attention_backward(proj, out, out_grads, lse, seqs, heads, first, bq=512, bk=512):
    rows, width = out.shape
    length = rows // seqs
    pairs = heads // 2
    count = width // PAIR

    def block(off):
        return pl.BlockSpec((length, PAIR), lambda s, p: (s, off + p))

    grad = jax.ShapeDtypeStruct((rows, width), BF16)
    terms = len(out_grads)
    return pl.pallas_call(
        partial(
            attention_backward_kernel,
            terms=terms,
            bq=bq,
            bk=bk,
            scale=HEAD_DIM**-0.5,
            length=length,
        ),
        grid=(seqs, count),
        in_specs=[
            block(first),
            block(pairs + first),
            block(2 * pairs + first),
            block(0),
            pl.BlockSpec((1, 2, length), lambda s, p: (p, 0, s)),
        ]
        + [block(0)] * terms,
        out_specs=[block(0)] * 3,
        out_shape=[grad] * 3,
        scratch_shapes=[
            pltpu.VMEM((PAIR, length), F32),
            pltpu.VMEM((2, length, PAIR), BF16),
            pltpu.VMEM((2, length, PAIR), BF16),
            pltpu.VMEM((PAIR, length), BF16),
            pltpu.VMEM((2, length), F32),
        ],
        cost_estimate=cost(20 * rows * length * width, 16 * rows * width),
        compiler_params=pltpu.CompilerParams(vmem_limit_bytes=40 * 1024 * 1024),
        name="attention_backward",
    )(proj, proj, proj, out, lse, *out_grads)


def norm_project_kernel(x_ref, gain_ref, bias_ref, wq_ref, wk_ref, wv_ref, a_ref, p_ref):
    normal, _ = normalized(x_ref[...].astype(F32))
    a = (normal * gain_ref[...] + bias_ref[...]).astype(BF16)
    a_ref[...] = a
    width = wq_ref.shape[1]
    for j, w in enumerate((wq_ref, wk_ref, wv_ref)):
        p_ref[:, j * width : (j + 1) * width] = dot(a, w[...]).astype(BF16)


def norm_project(x, gain, bias, weights, rb=512):
    rows, wide = x.shape
    width = weights[0].shape[1]
    return pl.pallas_call(
        norm_project_kernel,
        grid=(rows // rb,),
        in_specs=[pl.BlockSpec((rb, wide), lambda i: (i, 0)), resident((1, wide)), resident((1, wide))]
        + [resident((wide, width))] * 3,
        out_specs=[
            pl.BlockSpec((rb, wide), lambda i: (i, 0)),
            pl.BlockSpec((rb, 3 * width), lambda i: (i, 0)),
        ],
        out_shape=[
            jax.ShapeDtypeStruct((rows, wide), BF16),
            jax.ShapeDtypeStruct((rows, 3 * width), BF16),
        ],
        cost_estimate=cost(6 * rows * wide * width, 8 * rows * wide),
        name="norm_project",
    )(x, gain, bias, *weights)


def output_norm_kernel(*refs, parts, experts):
    x_ref, gain_ref, bias_ref, rm_ref = refs[:4]
    heads = refs[4 : 4 + parts]
    weights = refs[4 + parts : 4 + 2 * parts]
    resid_ref, f_ref, chance_ref = refs[4 + 2 * parts :]
    total = dot_nt(heads[0][...], weights[0][...])
    for h, w in zip(heads[1:], weights[1:]):
        total = total + dot_nt(h[...], w[...])
    resid = x_ref[...].astype(F32) + total
    resid_ref[...] = resid
    normal, _ = normalized(resid)
    f = (normal * gain_ref[...] + bias_ref[...]).astype(BF16)
    f_ref[...] = f
    chance_ref[...] = router_and_mix(dot(f, rm_ref[...]), experts)


def output_norm(x, gain, bias, rm, heads, weights, experts, rb=256):
    rows, wide = x.shape
    block = pl.BlockSpec((rb, wide), lambda i: (i, 0))
    weight_specs = [
        pl.BlockSpec(
            (wide, h.shape[1]), lambda i, j=j: (0, j), pipeline_mode=pl.Buffered(1)
        )
        for h, (_, j) in zip(heads, weights)
    ]
    return pl.pallas_call(
        partial(output_norm_kernel, parts=len(heads), experts=experts),
        grid=(rows // rb,),
        in_specs=[block, resident((1, wide)), resident((1, wide)), resident((wide, LANES))]
        + [pl.BlockSpec((rb, h.shape[1]), lambda i: (i, 0)) for h in heads]
        + weight_specs,
        out_specs=[block, block, pl.BlockSpec((rb, LANES), lambda i: (i, 0))],
        out_shape=[
            jax.ShapeDtypeStruct((rows, wide), F32),
            jax.ShapeDtypeStruct((rows, wide), BF16),
            jax.ShapeDtypeStruct((rows, LANES), F32),
        ],
        cost_estimate=cost(2 * rows * wide * wide, 12 * rows * wide),
        name="output_norm",
    )(x, gain, bias, rm, *heads, *[w for w, _ in weights])


def pack_kernel(place_ref, x_ref, o_ref):
    count, rows = o_ref.shape[0], x_ref.shape[0]
    slot = pl.program_id(0) * count + lax.broadcasted_iota(jnp.int32, (count, rows), 0)
    hot = jnp.where(slot == place_ref[...], 1.0, 0.0).astype(BF16)
    o_ref[...] = dot(hot, x_ref[...]).astype(BF16)


def pack(place, x, count, sb=512):
    rows, wide = x.shape
    return pl.pallas_call(
        pack_kernel,
        grid=(count // sb,),
        in_specs=[resident((1, rows)), resident((rows, wide))],
        out_specs=pl.BlockSpec((sb, wide), lambda i: (i, 0)),
        out_shape=jax.ShapeDtypeStruct((count, wide), BF16),
        cost_estimate=cost(2 * rows * wide * count, 4 * rows * wide),
        name="pack_rows",
    )(place, x)


def unpacked(place, all_ref):
    slot = lax.broadcasted_iota(jnp.int32, (place.shape[0], all_ref.shape[0]), 1)
    return dot(jnp.where(slot == place, 1.0, 0.0).astype(BF16), all_ref[...])


def nets_kernel(
    x_hbm,
    g_hbm,
    out_hbm,
    gin_hbm,
    sel_ref,
    rm_ref,
    wd1_hbm,
    wd2_hbm,
    we1_hbm,
    we2_hbm,
    y_hbm,
    dx_hbm,
    dot_hbm,
    gd1_hbm,
    gd2_hbm,
    ge1_hbm,
    ge2_hbm,
    in_hbm,
    res_hbm,
    pull_hbm,
    edot_hbm,
    pulls_hbm,
    edots_hbm,
    wd1,
    wd2,
    we1,
    we2,
    a1,
    a2,
    xb,
    gb,
    yb,
    dxb,
    dotb,
    rowb,
    ya,
    dxa,
    dyb,
    dyt,
    xt,
    w_sem,
    load_sem,
    store_sem,
    grad_sem,
    home_sem,
    local_sem,
    send_sem,
    recv_sem,
    back_send,
    back_recv,
    dot_send,
    dot_recv,
    *,
    peers,
    capacity,
    rb,
    ft,
):
    experts = peers
    me = lax.axis_index("ep")
    hidden = wd1.shape[1]
    per = rb // capacity
    quarter = peers // 4
    dense_steps = x_hbm.shape[0] // rb
    expert_steps = peers // per

    weight_copies = [
        pltpu.make_async_copy(src, dst, w_sem.at[j])
        for j, (src, dst) in enumerate(
            ((wd1_hbm, wd1), (wd2_hbm, wd2), (we1_hbm, we1), (we2_hbm, we2))
        )
    ]
    weight_copies[0].start()
    weight_copies[1].start()

    def load(t, slot):
        rows = pl.ds(pl.multiple_of(t * rb, rb), rb)
        return [
            pltpu.make_async_copy(x_hbm.at[rows, :], xb.at[slot], load_sem.at[slot, 0, 0]),
            pltpu.make_async_copy(g_hbm.at[rows, :], gb.at[slot], load_sem.at[slot, 1, 0]),
        ]

    for c in load(0, 0):
        c.start()

    barrier = pltpu.get_barrier_semaphore()
    for k in range(1, peers):
        pl.semaphore_signal(
            barrier,
            inc=1,
            device_id={"ep": jnp.bitwise_xor(me, k)},
            device_id_type=pl.DeviceIdType.MESH,
        )
    pl.semaphore_wait(barrier, peers - 1)

    def remote(src, dst, send, recv, k):
        peer = jnp.bitwise_xor(me, k)
        return pltpu.make_async_remote_copy(
            src_ref=src,
            dst_ref=dst,
            send_sem=send.at[k],
            recv_sem=recv.at[k],
            device_id={"ep": peer},
            device_id_type=pl.DeviceIdType.MESH,
        )

    def row_copy(k):
        return remote(
            out_hbm.at[jnp.bitwise_xor(me, k)], in_hbm.at[me], send_sem, recv_sem, k
        )

    def back_copy(k):
        return remote(
            pull_hbm.at[jnp.bitwise_xor(me, k)], pulls_hbm.at[me], back_send, back_recv, k
        )

    def dot_copy(k):
        return remote(
            edot_hbm.at[jnp.bitwise_xor(me, k)], edots_hbm.at[me], dot_send, dot_recv, k
        )

    far = list(range(2 * quarter, 3 * quarter))
    near = list(range(1, 2 * quarter))
    last = list(range(3 * quarter, peers))
    for k in far + near + last:
        row_copy(k).start()
    own_rows = pltpu.make_async_copy(out_hbm.at[me], in_hbm.at[me], home_sem.at[0])
    own_rows.start()
    weight_copies[2].start()
    weight_copies[3].start()

    def compute(slot, routed, w1_ref, w2_ref):
        x_ref = xb.at[slot]
        x = x_ref[...]
        g = gb[slot].astype(F32)
        chances = router_and_mix(dot(x, rm_ref[...]), experts)
        if routed:
            gate = jnp.sum(chances * sel_ref[...], axis=-1, keepdims=True)
            dy = g * lane_of(chances, experts + 1) * gate
        else:
            dy = g * lane_of(chances, experts)
        dy = dy.astype(BF16)
        dyb[...] = dy
        dyt[...] = dy.T
        xt[...] = x.T
        ya[...] = jnp.zeros_like(ya)
        dxa[...] = jnp.zeros_like(dxa)

        def step(f, _):
            cols = pl.ds(pl.multiple_of(f * ft, ft), ft)
            w1 = w1_ref[:, cols]
            w2 = w2_ref[:, cols]
            act, slope = gelu_and_slope(dot(x_ref[...], w1))
            h = act.astype(BF16)
            pre_grad = (slope * dot(dyb[...], w2)).astype(BF16)
            ya[...] += dot_nt(h, w2)
            dxa[...] += dot_nt(pre_grad, w1)
            a2[:, cols] += dot(dyt[...], h)
            a1[:, cols] += dot(xt[...], pre_grad)
            return 0

        lax.fori_loop(0, hidden // ft, step, 0)
        y = ya[...]
        yb[slot] = y.astype(BF16)
        dxb[slot] = dxa[...].astype(BF16)
        return jnp.sum(y * g, axis=1, keepdims=True)

    a1[...] = jnp.zeros_like(a1)
    a2[...] = jnp.zeros_like(a2)
    weight_copies[0].wait()
    weight_copies[1].wait()

    def dense_stores(t, slot):
        rows = pl.ds(pl.multiple_of(t * rb, rb), rb)
        return [
            pltpu.make_async_copy(yb.at[slot], y_hbm.at[rows, :], store_sem.at[slot, 0, 0]),
            pltpu.make_async_copy(dxb.at[slot], dx_hbm.at[rows, :], store_sem.at[slot, 1, 0]),
            pltpu.make_async_copy(dotb.at[slot], dot_hbm.at[rows, :], store_sem.at[slot, 2, 0]),
        ]

    def dense_step(t, _):
        slot = lax.rem(t, 2)
        for c in load(t, slot):
            c.wait()

        @pl.when(t + 1 < dense_steps)
        def _():
            for c in load(t + 1, 1 - slot):
                c.start()

        @pl.when(t >= 2)
        def _():
            for c in dense_stores(t - 2, slot):
                c.wait()

        dots = compute(slot, False, wd1, wd2)
        dotb[slot] = jnp.broadcast_to(dots, (rb, LANES))
        for c in dense_stores(t, slot):
            c.start()
        return 0

    lax.fori_loop(0, dense_steps, dense_step, 0)
    for t in range(max(0, dense_steps - 2), dense_steps):
        for c in dense_stores(t, t % 2):
            c.wait()

    wd1[...] = a1[...].astype(BF16)
    wd2[...] = a2[...].astype(BF16)
    dense_grads = [
        pltpu.make_async_copy(wd1, gd1_hbm, grad_sem.at[0]),
        pltpu.make_async_copy(wd2, gd2_hbm, grad_sem.at[1]),
    ]
    for c in dense_grads:
        c.start()
    a1[...] = jnp.zeros_like(a1)
    a2[...] = jnp.zeros_like(a2)
    weight_copies[2].wait()
    weight_copies[3].wait()
    own_rows.wait()

    def expert_step(p, _):
        base = jnp.where(p == expert_steps - 1, peers - per, (expert_steps - 2 - p) * per)
        slot = lax.rem(p, 2)
        loads = []
        for c in range(per):
            k = base + c

            @pl.when(k > 0)
            def _(k=k):
                row_copy(k).wait()

            source = jnp.bitwise_xor(me, k)
            rows = pl.ds(c * capacity, capacity)
            loads.append(
                pltpu.make_async_copy(in_hbm.at[source], xb.at[slot, rows, :], load_sem.at[slot, 0, c])
            )
            loads.append(
                pltpu.make_async_copy(gin_hbm.at[source], gb.at[slot, rows, :], load_sem.at[slot, 1, c])
            )
        for c in loads:
            c.start()
        for c in loads:
            c.wait()
        dots = compute(slot, True, we1, we2)
        across = jnp.broadcast_to(dots, (rb, LANES)).T
        stores = []
        for c in range(per):
            source = jnp.bitwise_xor(me, base + c)
            rows = pl.ds(c * capacity, capacity)
            rowb[c] = across[:8, c * capacity : (c + 1) * capacity]
            stores.append(
                pltpu.make_async_copy(yb.at[slot, rows, :], res_hbm.at[source], store_sem.at[slot, 0, c])
            )
            stores.append(
                pltpu.make_async_copy(dxb.at[slot, rows, :], pull_hbm.at[source], store_sem.at[slot, 1, c])
            )
            stores.append(
                pltpu.make_async_copy(rowb.at[c], edot_hbm.at[source], store_sem.at[slot, 2, c])
            )
        for c in stores:
            c.start()
        for c in stores:
            c.wait()
        for c in range(per):
            k = base + c

            @pl.when(k > 0)
            def _(k=k):
                back_copy(k).start()
                dot_copy(k).start()

        return 0

    lax.fori_loop(0, expert_steps, expert_step, 0)
    expert_grads = [
        pltpu.make_async_copy(a1, ge1_hbm, local_sem.at[0]),
        pltpu.make_async_copy(a2, ge2_hbm, local_sem.at[1]),
        pltpu.make_async_copy(pull_hbm.at[me], pulls_hbm.at[me], home_sem.at[1]),
        pltpu.make_async_copy(edot_hbm.at[me], edots_hbm.at[me], home_sem.at[2]),
    ]
    for c in expert_grads:
        c.start()
    for c in dense_grads + expert_grads:
        c.wait()
    for k in range(1, peers):
        back_copy(k).wait()
        dot_copy(k).wait()


def nets(x, g, out_rows, in_grads, sel, rm, dense_weights, expert_weights, rb=512, ft=512):
    rows, wide = x.shape
    hidden = dense_weights[0].shape[1]
    peers, capacity, _ = out_rows.shape
    per = rb // capacity
    anywhere = pl.BlockSpec(memory_space=pl.ANY)
    vmem = pl.BlockSpec(memory_space=pltpu.VMEM)
    sheet = jax.ShapeDtypeStruct((rows, wide), BF16)
    blocks = jax.ShapeDtypeStruct((peers, capacity, wide), BF16)
    strips = jax.ShapeDtypeStruct((peers, 8, capacity), F32)
    return pl.pallas_call(
        partial(nets_kernel, peers=peers, capacity=capacity, rb=rb, ft=ft),
        in_specs=[anywhere] * 4 + [vmem] * 2 + [anywhere] * 4,
        out_specs=[anywhere] * 13,
        out_shape=[
            sheet,
            sheet,
            jax.ShapeDtypeStruct((rows, LANES), F32),
            jax.ShapeDtypeStruct((wide, hidden), BF16),
            jax.ShapeDtypeStruct((wide, hidden), BF16),
            jax.ShapeDtypeStruct((wide, hidden), F32),
            jax.ShapeDtypeStruct((wide, hidden), F32),
            blocks,
            blocks,
            blocks,
            strips,
            blocks,
            strips,
        ],
        scratch_shapes=[pltpu.VMEM((wide, hidden), BF16)] * 4
        + [pltpu.VMEM((wide, hidden), F32)] * 2
        + [pltpu.VMEM((2, rb, wide), BF16)] * 4
        + [
            pltpu.VMEM((2, rb, LANES), F32),
            pltpu.VMEM((per, 8, capacity), F32),
            pltpu.VMEM((rb, wide), F32),
            pltpu.VMEM((rb, wide), F32),
            pltpu.VMEM((rb, wide), BF16),
            pltpu.VMEM((wide, rb), BF16),
            pltpu.VMEM((wide, rb), BF16),
            pltpu.SemaphoreType.DMA((4,)),
            pltpu.SemaphoreType.DMA((2, 2, per)),
            pltpu.SemaphoreType.DMA((2, 3, per)),
            pltpu.SemaphoreType.DMA((2,)),
            pltpu.SemaphoreType.DMA((3,)),
            pltpu.SemaphoreType.DMA((2,)),
        ]
        + [pltpu.SemaphoreType.DMA((peers,))] * 6,
        cost_estimate=cost(24 * rows * wide * hidden, 16 * rows * wide + 24 * wide * hidden),
        compiler_params=pltpu.CompilerParams(
            vmem_limit_bytes=BIG_VMEM, collective_id=0, has_side_effects=True
        ),
        name="feed_forward_nets",
    )(x, g, out_rows, in_grads, sel, rm, *dense_weights, *expert_weights)


def expert_hot(place, capacity, experts):
    lane = lax.broadcasted_iota(jnp.int32, (place.shape[0], LANES), 1)
    low = lane * capacity
    return ((place >= low) & (place < low + capacity) & (lane < experts)).astype(F32)


def ffn_pull_kernel(*refs, parts, experts, capacity):
    (
        place_ref,
        own_ref,
        dx_ref,
        chance_ref,
        first_ref,
        f_ref,
        g_ref,
        resid_ref,
        gain_ref,
        rm_ref,
        slot_ref,
        dots_ref,
    ) = refs[:12]
    weights = refs[12 : 12 + parts]
    r_ref = refs[12 + parts]
    heads = refs[13 + parts : 13 + 2 * parts]
    sums_ref, rmg_ref = refs[13 + 2 * parts :]
    place = place_ref[...]
    chances = chance_ref[...]
    hot = expert_hot(place, capacity, experts)
    gate = jnp.sum(hot * chances, axis=-1, keepdims=True)
    mix_0, mix_1 = lane_of(chances, experts), lane_of(chances, experts + 1)
    table = jnp.dot(
        hot, dots_ref[...], precision=lax.Precision.HIGHEST, preferred_element_type=F32
    )
    slot = lax.broadcasted_iota(jnp.int32, table.shape, 1)
    number = jnp.sum(hot * lax.broadcasted_iota(jnp.int32, hot.shape, 1).astype(F32), axis=-1)
    inside = place - number.astype(jnp.int32)[:, None] * capacity
    second = jnp.sum(jnp.where(slot == inside, table, 0.0), axis=-1, keepdims=True)
    first = lane_of(first_ref[...], 0)
    grad_0, grad_1 = first, gate * second
    inner = mix_0 * grad_0 + mix_1 * grad_1
    lane = lax.broadcasted_iota(jnp.int32, chances.shape, 1)
    low = (mix_1 * second * gate) * (hot - chances)
    low = jnp.where(lane == experts, mix_0 * (grad_0 - inner), low)
    low = jnp.where(lane == experts + 1, mix_1 * (grad_1 - inner), low)
    low = jnp.where(lane > experts + 1, 0.0, low).astype(BF16)
    grad = dx_ref[...].astype(F32) + unpacked(place, slot_ref) + dot_nt(low, rm_ref[...])
    normal, rstd = normalized(resid_ref[...])
    r = norm_pull(grad, normal, rstd, gain_ref[...]) + own_ref[...] * g_ref[...].astype(F32)
    r = r.astype(BF16)
    r_ref[...] = r
    for h, w in zip(heads, weights):
        h[...] = dot(r, w[...]).astype(BF16)

    @pl.when(pl.program_id(0) == 0)
    def _():
        sums_ref[...] = jnp.zeros_like(sums_ref)
        rmg_ref[...] = jnp.zeros_like(rmg_ref)

    sums_ref[0:1, :] += jnp.sum(grad * normal, axis=0, keepdims=True)
    sums_ref[1:2, :] += jnp.sum(grad, axis=0, keepdims=True)
    rmg_ref[...] += dot(low.T, f_ref[...])


def ffn_pull(
    place, own, dx, chances, first, f, g, resid, gain, rm, slot_rows, dots, weights, experts, rb=256
):
    rows, wide = dx.shape
    capacity = dots.shape[1]
    dots = jnp.pad(dots, ((0, LANES - experts), (0, 0)))
    block = pl.BlockSpec((rb, wide), lambda i: (i, 0))
    narrow = pl.BlockSpec((rb, LANES), lambda i: (i, 0))
    col = pl.BlockSpec((rb, 1), lambda i: (i, 0))
    head_specs = [pl.BlockSpec((rb, size), lambda i: (i, 0)) for _, _, size in weights]
    return pl.pallas_call(
        partial(ffn_pull_kernel, parts=len(weights), experts=experts, capacity=capacity),
        grid=(rows // rb,),
        in_specs=[col, col, block, narrow, narrow, block, block, block]
        + [resident((1, wide)), resident((wide, LANES))]
        + [resident(slot_rows.shape), resident(dots.shape)]
        + [
            pl.BlockSpec((wide, size), lambda i, j=j: (0, j), pipeline_mode=pl.Buffered(1))
            for _, j, size in weights
        ],
        out_specs=[block] + head_specs + [resident((8, wide)), resident((LANES, wide))],
        out_shape=[jax.ShapeDtypeStruct((rows, wide), BF16)]
        + [jax.ShapeDtypeStruct((rows, size), BF16) for _, _, size in weights]
        + [jax.ShapeDtypeStruct((8, wide), F32), jax.ShapeDtypeStruct((LANES, wide), F32)],
        cost_estimate=cost(6 * rows * wide * wide, 16 * rows * wide),
        compiler_params=pltpu.CompilerParams(vmem_limit_bytes=48 * 1024 * 1024),
        name="ffn_norm_pull",
    )(
        place,
        own,
        dx,
        chances,
        first,
        f,
        g,
        resid,
        gain,
        rm,
        slot_rows,
        dots,
        *[w for w, _, _ in weights],
    )


def outer_kernel(left_ref, *refs, parts):
    rights = refs[:parts]
    o_ref, acc_ref = refs[parts:]

    @pl.when(pl.program_id(0) == 0)
    def _():
        acc_ref[...] = jnp.zeros_like(acc_ref)

    left = left_ref[...].T
    at = 0
    for r in rights:
        width = r.shape[1]
        acc_ref[:, at : at + width] += dot(left, r[...])
        at += width

    @pl.when(pl.program_id(0) == pl.num_programs(0) - 1)
    def _():
        o_ref[...] = acc_ref[...].astype(BF16)


def outer(left, rights, rb=512):
    rows, wide = left.shape
    total = sum(r.shape[1] for r in rights)
    return pl.pallas_call(
        partial(outer_kernel, parts=len(rights)),
        grid=(rows // rb,),
        in_specs=[pl.BlockSpec((rb, wide), lambda i: (i, 0))]
        + [pl.BlockSpec((rb, r.shape[1]), lambda i: (i, 0)) for r in rights],
        out_specs=resident((wide, total)),
        out_shape=jax.ShapeDtypeStruct((wide, total), BF16),
        scratch_shapes=[pltpu.VMEM((wide, total), F32)],
        cost_estimate=cost(2 * rows * wide * total, 2 * rows * (wide + total)),
        name="outer_product",
    )(left, *rights)


def attn_pull_kernel(at_ref, x_ref, r_ref, gain_ref, *refs, groups):
    grads = refs[: 3 * groups]
    weights = refs[3 * groups : 3 * groups + 3]
    t_ref, sums_ref = refs[3 * groups + 3 :]
    del at_ref
    total = None
    for k in range(3):
        at = 0
        for j in range(groups):
            d = grads[k * groups + j]
            width = d.shape[1]
            part = dot_nt(d[...], weights[k][:, at : at + width])
            total = part if total is None else total + part
            at += width
    normal, rstd = normalized(x_ref[...].astype(F32))
    t = norm_pull(total, normal, rstd, gain_ref[...]) + r_ref[...].astype(F32)
    t_ref[...] = t.astype(t_ref.dtype)

    @pl.when(pl.program_id(0) == 0)
    def _():
        sums_ref[...] = jnp.zeros_like(sums_ref)

    sums_ref[0:1, :] += jnp.sum(total * normal, axis=0, keepdims=True)
    sums_ref[1:2, :] += jnp.sum(total, axis=0, keepdims=True)


def attn_pull(first_row, count, x, r, gain, grads, weights, out_type, rb=256):
    wide = x.shape[1]
    groups = len(grads) // 3

    def rows(width):
        return pl.BlockSpec((rb, width), lambda i, at: (at[0] + i, 0))

    return pl.pallas_call(
        partial(attn_pull_kernel, groups=groups),
        grid_spec=pltpu.PrefetchScalarGridSpec(
            num_scalar_prefetch=1,
            grid=(count // rb,),
            in_specs=[rows(wide), rows(wide), resident((1, wide))]
            + [rows(d.shape[1]) for d in grads]
            + [resident(w.shape) for w in weights],
            out_specs=[pl.BlockSpec((rb, wide), lambda i, at: (i, 0)), resident((8, wide))],
        ),
        out_shape=[
            jax.ShapeDtypeStruct((count, wide), out_type),
            jax.ShapeDtypeStruct((8, wide), F32),
        ],
        cost_estimate=cost(6 * count * wide * weights[0].shape[1], 10 * count * wide),
        name="attention_norm_pull",
    )((first_row // rb).astype(jnp.int32).reshape(1), x, r, gain, *grads, *weights)


def combine_kernel(place_ref, y_ref, chance_ref, slot_ref, o_ref, *, experts, capacity):
    place = place_ref[...]
    chances = chance_ref[...]
    gate = jnp.sum(expert_hot(place, capacity, experts) * chances, axis=-1, keepdims=True)
    moe = unpacked(place, slot_ref) * (lane_of(chances, experts + 1) * gate)
    o_ref[...] = (lane_of(chances, experts) * y_ref[...].astype(F32) + moe).astype(BF16)


def combine(place, y, coef, slot_rows, experts, rb=256):
    rows, wide = y.shape
    block = pl.BlockSpec((rb, wide), lambda i: (i, 0))
    return pl.pallas_call(
        partial(combine_kernel, experts=experts, capacity=slot_rows.shape[0] // experts),
        grid=(rows // rb,),
        in_specs=[
            pl.BlockSpec((rb, 1), lambda i: (i, 0)),
            block,
            pl.BlockSpec((rb, LANES), lambda i: (i, 0)),
        ]
        + [resident(slot_rows.shape)],
        out_specs=block,
        out_shape=jax.ShapeDtypeStruct((rows, wide), BF16),
        cost_estimate=cost(4 * rows * wide * wide, 8 * rows * wide),
        name="combine_nets",
    )(place, y, coef, slot_rows)


def on_device(
    sizes,
    tokens,
    out_grad,
    lengths,
    expert_ids,
    w_query,
    w_key,
    w_value,
    w_output,
    w_hidden,
    w_return,
    router,
    mix_weight,
    gain_attn,
    bias_attn,
    gain_ffn,
    bias_ffn,
    expert_in,
    expert_out,
):
    tp, ep = sizes
    shard_rows = out_grad.shape[0]
    all_rows = tokens.shape[0]
    model_width = tokens.shape[1]
    experts = router.shape[1]
    capacity = all_rows // experts
    seq_count = lengths.shape[0]
    seq_len = all_rows // seq_count
    local_width = w_query.shape[1]
    local_heads = local_width // HEAD_DIM
    pairs = local_heads // 2
    splits = 2 if pairs % 2 == 0 else 1
    each = pairs // splits
    tp_index = lax.axis_index("tp")
    ep_index = lax.axis_index("ep")
    first_row = tp_index * shard_rows
    swap = [(0, 1), (1, 0)]

    def shard_of(values, axis=0):
        return lax.dynamic_slice_in_dim(values, first_row, shard_rows, axis)

    def swapped(values):
        return lax.ppermute(values, "tp", swap)

    def exchange(values):
        return lax.all_to_all(values, "ep", split_axis=0, concat_axis=0, tiled=True)

    def after(values, *others):
        return lax.optimization_barrier((values, others))[0]

    def summed_over(values, axis, size):
        step = 1
        while step < size:
            values = values + lax.ppermute(values, axis, [(i, i ^ step) for i in range(size)])
            step *= 2
        return values

    def over_sequences(values):
        return lax.psum_scatter(values, "ep", scatter_dimension=0, tiled=True).astype(F32)

    def halved_over_sequences(values):
        step = 1
        while step < ep:
            width = values.shape[-1]
            split = values.reshape(-1, 2, values.shape[0] // (ep // step), width)
            bit = (ep_index // step) % 2
            keep = lax.dynamic_index_in_dim(split, bit, 1, keepdims=False)
            give = lax.dynamic_index_in_dim(split, 1 - bit, 1, keepdims=False)
            give = give.reshape(-1, width)
            got = lax.ppermute(give, "ep", [(i, i ^ step) for i in range(ep)])
            values = (keep.reshape(-1, width).astype(F32) + got.astype(F32)).astype(BF16)
            step *= 2
        return values.astype(F32)

    positions = jnp.arange(all_rows)
    seq_index = positions // seq_len
    row_limit = jnp.sum(
        jnp.where(seq_index[:, None] == jnp.arange(seq_count)[None, :], lengths[None, :], 0), axis=1
    )
    live_all = positions % seq_len < row_limit
    one_hot = (expert_ids[:, None] == jnp.arange(experts)[None, :]) & live_all[:, None]
    routed = one_hot.astype(F32)
    slots = jnp.sum((jnp.cumsum(routed, axis=0) - routed) * routed, axis=1).astype(jnp.int32)
    sound = live_all & (slots < capacity)
    place = jnp.where(sound, expert_ids * capacity + slots, -1)
    place_row = place[None, :]
    place_col = place[:, None]
    slot_count = experts * capacity
    blocks = (experts, capacity, model_width)

    live_grad = jnp.where(shard_of(live_all)[:, None], out_grad, jnp.zeros_like(out_grad))
    if tp == 2:
        grad_other = swapped(live_grad)
        w_other = swapped(w_output)
        mine_first = tp_index == 0
        grad_all = jnp.concatenate(
            [
                jnp.where(mine_first, live_grad, grad_other),
                jnp.where(mine_first, grad_other, live_grad),
            ],
            axis=0,
        )
    else:
        w_all = lax.all_gather(w_output, "tp", axis=1, tiled=True)
        grad_all = lax.all_gather(live_grad, "tp", axis=0, tiled=True)

    def row(values):
        return values.astype(F32)[None, :]

    rm = jnp.pad(
        jnp.concatenate([router, mix_weight], axis=1), ((0, 0), (0, LANES - experts - 2))
    )

    attn_in, projected = norm_project(
        tokens, row(gain_attn), row(bias_attn), (w_query, w_key, w_value)
    )
    heads, log_sums = [], []
    for s in range(splits):
        if s == splits - 1:
            grad_blocks = pack(place_row, after(grad_all, *heads), slot_count)
            projected = after(projected, grad_blocks)
        o, lse = attention_forward(projected, seq_count, local_heads, s * each, each)
        heads.append(o)
        log_sums.append(lse)
    if tp == 2:
        others = [swapped(o) for o in heads]
        all_heads = heads + others
        weights = [(w_output, s) for s in range(splits)] + [(w_other, s) for s in range(splits)]
        wide_weights = [(w, s, each * PAIR) for w, s in weights]
    else:
        all_heads = [lax.all_gather(jnp.concatenate(heads, axis=1), "tp", axis=1, tiled=True)]
        weights = [(w_all, 0)]
        wide_weights = [(w_all, 0, model_width)]
    resid, ffn_in, chances = output_norm(
        tokens, row(gain_ffn), row(bias_ffn), rm, all_heads, weights, experts
    )
    grad_rows = exchange(grad_blocks.reshape(blocks))
    sent = pack(place_row, ffn_in, slot_count).reshape(blocks)
    sel = (jnp.arange(LANES) == ep_index).astype(F32)[None, :]
    (
        dense,
        dense_pull,
        first_dot,
        grad_hidden,
        grad_return,
        grad_expert_in,
        grad_expert_out,
        _,
        results,
        _,
        _,
        pulls,
        dots,
    ) = nets(
        ffn_in,
        grad_all,
        sent,
        grad_rows,
        sel,
        rm,
        (w_hidden, w_return),
        (expert_in[0], expert_out[0]),
    )
    returned = exchange(results).reshape(slot_count, model_width)
    pulls = pulls.reshape(slot_count, model_width)
    dots = dots[:, 0, :]
    own = ((positions >= first_row) & (positions < first_row + shard_rows)).astype(F32)[:, None]

    part, *rest = ffn_pull(
        place_col,
        own,
        dense_pull,
        chances,
        first_dot,
        ffn_in,
        grad_all,
        resid,
        row(gain_ffn),
        rm,
        pulls,
        dots,
        wide_weights,
        experts,
    )
    *head_parts, ffn_sums, rm_sums = rest
    if tp == 2:
        head_grads = [[m, swapped(o)] for m, o in zip(head_parts[:splits], head_parts[splits:])]
    else:
        local = lax.psum_scatter(head_parts[0], "tp", scatter_dimension=1, tiled=True)
        head_grads = [
            [local[:, s * each * PAIR : (s + 1) * each * PAIR]] for s in range(splits)
        ]
    grad_output = halved_over_sequences(outer(part, all_heads))
    if tp == 2:
        grad_output = grad_output[:, :local_width] + swapped(
            grad_output[:, local_width:].astype(BF16)
        ).astype(F32)
    else:
        grad_output = lax.psum_scatter(
            grad_output.astype(BF16), "tp", scatter_dimension=1, tiled=True
        ).astype(F32)

    grad_hidden = over_sequences(grad_hidden)
    grad_return = over_sequences(grad_return)

    square, qkv = [], []
    for s in range(splits):
        if s == splits - 1:
            weighted = combine(place_col, dense, chances, returned, experts)
            grad_expert_in, grad_expert_out = [
                jnp.where(lengths[0] > 0, e, 0.0) for e in (grad_expert_in, grad_expert_out)
            ]
            projected = after(
                projected, weighted, grad_expert_in, grad_expert_out, *(qkv[-1] if qkv else ())
            )
        grads3 = attention_backward(
            projected, heads[s], head_grads[s], log_sums[s], seq_count, local_heads, s * each
        )
        qkv.append(grads3)
        square.append(halved_over_sequences(outer(attn_in, grads3)))
    width = each * PAIR
    grad_query, grad_key, grad_value = [
        jnp.concatenate([q[:, k * width : (k + 1) * width] for q in square], axis=1)
        for k in range(3)
    ]
    part = after(part, grad_hidden, grad_return)
    ffn_sums, rm_sums = after((ffn_sums, rm_sums), *qkv[-1])
    flat = [qkv[s][k] for k in range(3) for s in range(splits)]
    pull = partial(
        attn_pull,
        x=tokens,
        r=part,
        gain=row(gain_attn),
        grads=flat,
        weights=(w_query, w_key, w_value),
    )
    if tp == 2:
        theirs, sums_a = pull(shard_rows - first_row, shard_rows, out_type=BF16)
        own_part, sums_b = pull(first_row, shard_rows, out_type=F32)
        token_grad = own_part + swapped(theirs).astype(F32)
        attn_sums = sums_a + sums_b
    else:
        whole, attn_sums = pull(jnp.zeros((), jnp.int32), all_rows, out_type=BF16)
        token_grad = lax.psum_scatter(whole, "tp", scatter_dimension=0, tiled=True).astype(F32)

    if tp == 2:
        theirs = lax.dynamic_slice_in_dim(weighted, shard_rows - first_row, shard_rows, 0)
        summed = shard_of(weighted).astype(F32) + swapped(theirs).astype(F32)
    else:
        summed = lax.psum_scatter(weighted, "tp", scatter_dimension=0, tiled=True).astype(F32)
    block_out = jnp.where(shard_of(live_all)[:, None], shard_of(resid) + summed, 0.0).astype(BF16)

    rows_kept = -(-(experts + 2) // 8) * 8
    small = summed_over(
        summed_over(jnp.concatenate([ffn_sums, rm_sums[:rows_kept]], axis=0), "tp", tp), "ep", ep
    )
    attn_sums = summed_over(summed_over(attn_sums, "tp", tp), "ep", ep)
    return (
        block_out,
        token_grad,
        grad_query,
        grad_key,
        grad_value,
        grad_output,
        grad_hidden,
        grad_return,
        small[8 : 8 + experts].T,
        small[8 + experts : 10 + experts].T,
        attn_sums[0],
        attn_sums[1],
        small[0],
        small[1],
        grad_expert_in[None],
        grad_expert_out[None],
    )


def solution(mesh):
    in_specs = (
        P("ep", None),
        P(("ep", "tp"), None),
        P("ep"),
        P("ep"),
        P(None, "tp"),
        P(None, "tp"),
        P(None, "tp"),
        P(None, "tp"),
        P(None, "tp"),
        P(None, "tp"),
        P(),
        P(),
        P(),
        P(),
        P(),
        P(),
        P("ep", None, "tp"),
        P("ep", None, "tp"),
    )
    out_specs = (
        P(("ep", "tp"), None),
        P(("ep", "tp"), None),
        P("ep", "tp"),
        P("ep", "tp"),
        P("ep", "tp"),
        P("ep", "tp"),
        P("ep", "tp"),
        P("ep", "tp"),
        P(),
        P(),
        P(),
        P(),
        P(),
        P(),
        P("ep", None, "tp"),
        P("ep", None, "tp"),
    )
    return jax.shard_map(
        partial(on_device, (mesh.shape["tp"], mesh.shape["ep"])),
        mesh=mesh,
        in_specs=in_specs,
        out_specs=out_specs,
        check_vma=False,
    )
```

```python
import math
from functools import partial

import jax
import jax.numpy as jnp
from jax import lax
from jax.experimental import pallas as pl
from jax.experimental.pallas import tpu as pltpu
from jax.sharding import PartitionSpec as P

HEAD_DIM = 64
PAIR = 2 * HEAD_DIM


EPS = 1e-05
NEG = -1e30
F32 = jnp.float32
BF16 = jnp.bfloat16
NT = (((1,), (1,)), ((), ()))


LANES = 128
GELU_C = math.sqrt(2.0 / math.pi)
GELU_A = 0.044715
BIG_VMEM = 62 * 1024 * 1024


def dot(left, right):
    return jnp.dot(left, right, preferred_element_type=F32)


def dot_nt(left, right):
    return lax.dot_general(left, right, NT, preferred_element_type=F32)


def normalized(values):
    middle = jnp.mean(values, axis=-1, keepdims=True)
    centred = values - middle
    rstd = lax.rsqrt(jnp.mean(centred * centred, axis=-1, keepdims=True) + EPS)
    return centred * rstd, rstd


def norm_pull(grad, normal, rstd, gain):
    q = grad * gain
    along = jnp.mean(q * normal, axis=-1, keepdims=True)
    return rstd * (q - jnp.mean(q, axis=-1, keepdims=True) - normal * along)


def gelu_and_slope(v):
    square = v * v
    t = jnp.tanh(v * (GELU_C + (GELU_C * GELU_A) * square))
    half = 0.5 + 0.5 * t
    slope = half + v * (0.5 - 0.5 * (t * t)) * (GELU_C + (3.0 * GELU_C * GELU_A) * square)
    return v * half, slope


def router_and_mix(logits, experts):
    lane = lax.broadcasted_iota(jnp.int32, logits.shape, 1)
    out = jnp.zeros_like(logits)
    for low, high in ((0, experts), (experts, experts + 2)):
        inside = (lane >= low) & (lane < high)
        top = jnp.max(jnp.where(inside, logits, NEG), axis=-1, keepdims=True)
        e = jnp.where(inside, jnp.exp(jnp.where(inside, logits - top, 0.0)), 0.0)
        out = out + e / jnp.sum(e, axis=-1, keepdims=True)
    return out


def lane_of(values, index):
    lane = lax.broadcasted_iota(jnp.int32, values.shape, 1)
    return jnp.sum(jnp.where(lane == index, values, 0.0), axis=-1, keepdims=True)


def resident(shape):
    return pl.BlockSpec(shape, lambda i, *_: (0,) * len(shape), pipeline_mode=pl.Buffered(1))


def cost(flops, bytes_accessed):
    return pl.CostEstimate(flops=flops // 64, bytes_accessed=bytes_accessed // 64, transcendentals=0)


def attend_block(qi, q, keys, values_t, bq, bk, scale):
    lane = lax.broadcasted_iota(jnp.int32, (bq, PAIR), 1)
    q = q * jnp.asarray(scale, BF16)
    zero = jnp.zeros_like(q)
    halves = [jnp.where(lane < HEAD_DIM, q, zero), jnp.where(lane < HEAD_DIM, zero, q)]

    def step(j, carry, masked):
        off = pl.multiple_of(j * bk, bk)
        k = keys(pl.ds(off, bk))
        vt = values_t(pl.ds(off, bk))
        scores = [lax.dot_general(k, half, NT, preferred_element_type=F32) for half in halves]
        if masked:
            key_pos = off + lax.broadcasted_iota(jnp.int32, (bk, bq), 0)
            query_pos = qi * bq + lax.broadcasted_iota(jnp.int32, (bk, bq), 1)
            allowed = key_pos <= query_pos
            scores = [jnp.where(allowed, s, NEG) for s in scores]
        new = []
        for h in range(2):
            m, l, acc = carry[h]
            m_new = jnp.maximum(m, jnp.max(scores[h], axis=0, keepdims=True))
            alpha = jnp.exp(m - m_new)
            p = jnp.exp(scores[h] - m_new)
            l = l * alpha + jnp.sum(p, axis=0, keepdims=True)
            part = dot(vt[h * HEAD_DIM : (h + 1) * HEAD_DIM], p.astype(BF16))
            new.append((m_new, l, acc * alpha + part))
        return tuple(new)

    init = tuple(
        (jnp.full((1, bq), NEG, F32), jnp.zeros((1, bq), F32), jnp.zeros((HEAD_DIM, bq), F32))
        for _ in range(2)
    )
    full = qi * (bq // bk)
    carry = lax.fori_loop(0, full, lambda j, c: step(j, c, False), init)
    for d in range(bq // bk):
        carry = step(full + d, carry, True)
    out = jnp.concatenate([acc / l for _, l, acc in carry], axis=0).T.astype(BF16)
    return out, [m + jnp.log(l) for m, l, _ in carry]


def attention_forward_kernel(q_ref, k_ref, v_ref, o_ref, lse_ref, vt_ref, *, bq, bk, scale):
    qi = pl.program_id(2)

    @pl.when(qi == 0)
    def _():
        vt_ref[...] = v_ref[...].T

    out, lse = attend_block(
        qi, q_ref[...], lambda s: k_ref[s, :], lambda s: vt_ref[:, s], bq, bk, scale
    )
    o_ref[...] = out
    for h in range(2):
        lse_ref[0, h : h + 1, :] = lse[h]


def attention_forward(proj, seqs, heads, first, count, bq=512, bk=512):
    rows = proj.shape[0]
    length = rows // seqs
    pairs = heads // 2
    nq = length // bq
    flops = 2 * rows * length * count * PAIR
    return pl.pallas_call(
        partial(attention_forward_kernel, bq=bq, bk=bk, scale=HEAD_DIM**-0.5),
        grid=(seqs, count, nq),
        in_specs=[
            pl.BlockSpec((bq, PAIR), lambda s, p, i: (s * nq + i, first + p)),
            pl.BlockSpec((length, PAIR), lambda s, p, i: (s, pairs + first + p)),
            pl.BlockSpec((length, PAIR), lambda s, p, i: (s, 2 * pairs + first + p)),
        ],
        out_specs=[
            pl.BlockSpec((bq, PAIR), lambda s, p, i: (s * nq + i, p)),
            pl.BlockSpec((1, 2, bq), lambda s, p, i: (p, 0, s * nq + i)),
        ],
        out_shape=[
            jax.ShapeDtypeStruct((rows, count * PAIR), BF16),
            jax.ShapeDtypeStruct((count, 2, rows), F32),
        ],
        scratch_shapes=[pltpu.VMEM((PAIR, length), BF16)],
        cost_estimate=cost(flops * 4, 8 * rows * count * PAIR),
        name="attention_forward",
    )(proj, proj, proj)


def attention_backward_kernel(
    q_ref,
    k_ref,
    v_ref,
    o_ref,
    lse_ref,
    *refs,
    terms,
    bq,
    bk,
    scale,
    length,
):
    lane = lax.broadcasted_iota(jnp.int32, (length, PAIR), 1)
    first = lane < HEAD_DIM
    q = q_ref[...] * jnp.asarray(scale, BF16)
    do_refs = refs[:terms]
    dq_ref, dk_ref, dv_ref, dqt_ref, qs_ref, dos_ref, kt_ref, dl_ref = refs[terms:]
    do = do_refs[0][...]
    if terms == 2:
        do = (do.astype(F32) + do_refs[1][...].astype(F32)).astype(BF16)
    zero = jnp.zeros_like(q)
    qs_ref[0] = jnp.where(first, q, zero)
    qs_ref[1] = jnp.where(first, zero, q)
    dos_ref[0] = jnp.where(first, do, zero)
    dos_ref[1] = jnp.where(first, zero, do)
    kt_ref[...] = (k_ref[...] * jnp.asarray(scale, BF16)).T
    prod = (do.astype(F32) * o_ref[...].astype(F32)).T
    dl_ref[0:1, :] = jnp.sum(prod[:HEAD_DIM], axis=0, keepdims=True)
    dl_ref[1:2, :] = jnp.sum(prod[HEAD_DIM:], axis=0, keepdims=True)
    dqt_ref[...] = jnp.zeros_like(dqt_ref)
    nq = length // bq
    nk = length // bk

    def key_block(j, _):
        koff = pl.multiple_of(j * bk, bk)
        k = k_ref[pl.ds(koff, bk), :]
        v = v_ref[pl.ds(koff, bk), :]
        kt = kt_ref[:, pl.ds(koff, bk)]

        def step(i, carry, masked):
            dk, dv = carry
            qoff = pl.multiple_of(i * bq, bq)
            if masked:
                key_pos = koff + lax.broadcasted_iota(jnp.int32, (bk, bq), 0)
                query_pos = qoff + lax.broadcasted_iota(jnp.int32, (bk, bq), 1)
                allowed = key_pos <= query_pos
            qh = [qs_ref[h, pl.ds(qoff, bq), :] for h in range(2)]
            dh = [dos_ref[h, pl.ds(qoff, bq), :] for h in range(2)]
            scores = [lax.dot_general(k, x, NT, preferred_element_type=F32) for x in qh]
            pulls = [lax.dot_general(v, x, NT, preferred_element_type=F32) for x in dh]
            dqs = []
            for h in range(2):
                p = jnp.exp(scores[h] - lse_ref[0, h : h + 1, pl.ds(qoff, bq)])
                if masked:
                    p = jnp.where(allowed, p, 0.0)
                ds = (p * (pulls[h] - dl_ref[h : h + 1, pl.ds(qoff, bq)])).astype(BF16)
                dv = dv + jnp.dot(p.astype(BF16), dh[h], preferred_element_type=F32)
                dk = dk + jnp.dot(ds, qh[h], preferred_element_type=F32)
                dqs.append(
                    jnp.dot(
                        kt[h * HEAD_DIM : (h + 1) * HEAD_DIM], ds, preferred_element_type=F32
                    )
                )
            dqt_ref[:, pl.ds(qoff, bq)] += jnp.concatenate(dqs, axis=0)
            return dk, dv

        carry = (jnp.zeros((bk, PAIR), F32), jnp.zeros((bk, PAIR), F32))
        i0 = j * (bk // bq)
        for d in range(bk // bq):
            carry = step(i0 + d, carry, True)
        dk, dv = lax.fori_loop(i0 + bk // bq, nq, lambda i, c: step(i, c, False), carry)
        dk_ref[pl.ds(koff, bk), :] = dk.astype(BF16)
        dv_ref[pl.ds(koff, bk), :] = dv.astype(BF16)
        return 0

    lax.fori_loop(0, nk, key_block, 0)
    dq_ref[...] = dqt_ref[...].T.astype(BF16)


def attention_backward(proj, out, out_grads, lse, seqs, heads, first, bq=512, bk=512):
    rows, width = out.shape
    length = rows // seqs
    pairs = heads // 2
    count = width // PAIR

    def block(off):
        return pl.BlockSpec((length, PAIR), lambda s, p: (s, off + p))

    grad = jax.ShapeDtypeStruct((rows, width), BF16)
    terms = len(out_grads)
    return pl.pallas_call(
        partial(
            attention_backward_kernel,
            terms=terms,
            bq=bq,
            bk=bk,
            scale=HEAD_DIM**-0.5,
            length=length,
        ),
        grid=(seqs, count),
        in_specs=[
            block(first),
            block(pairs + first),
            block(2 * pairs + first),
            block(0),
            pl.BlockSpec((1, 2, length), lambda s, p: (p, 0, s)),
        ]
        + [block(0)] * terms,
        out_specs=[block(0)] * 3,
        out_shape=[grad] * 3,
        scratch_shapes=[
            pltpu.VMEM((PAIR, length), F32),
            pltpu.VMEM((2, length, PAIR), BF16),
            pltpu.VMEM((2, length, PAIR), BF16),
            pltpu.VMEM((PAIR, length), BF16),
            pltpu.VMEM((2, length), F32),
        ],
        cost_estimate=cost(20 * rows * length * width, 16 * rows * width),
        compiler_params=pltpu.CompilerParams(vmem_limit_bytes=40 * 1024 * 1024),
        name="attention_backward",
    )(proj, proj, proj, out, lse, *out_grads)


def norm_project_kernel(x_ref, gain_ref, bias_ref, wq_ref, wk_ref, wv_ref, a_ref, p_ref):
    normal, _ = normalized(x_ref[...].astype(F32))
    a = (normal * gain_ref[...] + bias_ref[...]).astype(BF16)
    a_ref[...] = a
    width = wq_ref.shape[1]
    for j, w in enumerate((wq_ref, wk_ref, wv_ref)):
        p_ref[:, j * width : (j + 1) * width] = dot(a, w[...]).astype(BF16)


def norm_project(x, gain, bias, weights, rb=512):
    rows, wide = x.shape
    width = weights[0].shape[1]
    return pl.pallas_call(
        norm_project_kernel,
        grid=(rows // rb,),
        in_specs=[pl.BlockSpec((rb, wide), lambda i: (i, 0)), resident((1, wide)), resident((1, wide))]
        + [resident((wide, width))] * 3,
        out_specs=[
            pl.BlockSpec((rb, wide), lambda i: (i, 0)),
            pl.BlockSpec((rb, 3 * width), lambda i: (i, 0)),
        ],
        out_shape=[
            jax.ShapeDtypeStruct((rows, wide), BF16),
            jax.ShapeDtypeStruct((rows, 3 * width), BF16),
        ],
        cost_estimate=cost(6 * rows * wide * width, 8 * rows * wide),
        name="norm_project",
    )(x, gain, bias, *weights)


def output_norm_kernel(*refs, parts, experts):
    x_ref, gain_ref, bias_ref, rm_ref = refs[:4]
    heads = refs[4 : 4 + parts]
    weights = refs[4 + parts : 4 + 2 * parts]
    resid_ref, f_ref, chance_ref = refs[4 + 2 * parts :]
    total = dot_nt(heads[0][...], weights[0][...])
    for h, w in zip(heads[1:], weights[1:]):
        total = total + dot_nt(h[...], w[...])
    resid = x_ref[...].astype(F32) + total
    resid_ref[...] = resid
    normal, _ = normalized(resid)
    f = (normal * gain_ref[...] + bias_ref[...]).astype(BF16)
    f_ref[...] = f
    chance_ref[...] = router_and_mix(dot(f, rm_ref[...]), experts)


def output_norm(x, gain, bias, rm, heads, weights, experts, rb=256):
    rows, wide = x.shape
    block = pl.BlockSpec((rb, wide), lambda i: (i, 0))
    weight_specs = [
        pl.BlockSpec(
            (wide, h.shape[1]), lambda i, j=j: (0, j), pipeline_mode=pl.Buffered(1)
        )
        for h, (_, j) in zip(heads, weights)
    ]
    return pl.pallas_call(
        partial(output_norm_kernel, parts=len(heads), experts=experts),
        grid=(rows // rb,),
        in_specs=[block, resident((1, wide)), resident((1, wide)), resident((wide, LANES))]
        + [pl.BlockSpec((rb, h.shape[1]), lambda i: (i, 0)) for h in heads]
        + weight_specs,
        out_specs=[block, block, pl.BlockSpec((rb, LANES), lambda i: (i, 0))],
        out_shape=[
            jax.ShapeDtypeStruct((rows, wide), F32),
            jax.ShapeDtypeStruct((rows, wide), BF16),
            jax.ShapeDtypeStruct((rows, LANES), F32),
        ],
        cost_estimate=cost(2 * rows * wide * wide, 12 * rows * wide),
        name="output_norm",
    )(x, gain, bias, rm, *heads, *[w for w, _ in weights])


def pack_kernel(place_ref, x_ref, o_ref):
    count, rows = o_ref.shape[0], x_ref.shape[0]
    slot = pl.program_id(0) * count + lax.broadcasted_iota(jnp.int32, (count, rows), 0)
    hot = jnp.where(slot == place_ref[...], 1.0, 0.0).astype(BF16)
    o_ref[...] = dot(hot, x_ref[...]).astype(BF16)


def pack(place, x, count, sb=512):
    rows, wide = x.shape
    return pl.pallas_call(
        pack_kernel,
        grid=(count // sb,),
        in_specs=[resident((1, rows)), resident((rows, wide))],
        out_specs=pl.BlockSpec((sb, wide), lambda i: (i, 0)),
        out_shape=jax.ShapeDtypeStruct((count, wide), BF16),
        cost_estimate=cost(2 * rows * wide * count, 4 * rows * wide),
        name="pack_rows",
    )(place, x)


def unpacked(place, all_ref):
    slot = lax.broadcasted_iota(jnp.int32, (place.shape[0], all_ref.shape[0]), 1)
    return dot(jnp.where(slot == place, 1.0, 0.0).astype(BF16), all_ref[...])


def front_kernel(*refs, peers, experts, half, bq, heads_count):
    refs = list(refs)

    def take(count):
        taken = refs[:count]
        del refs[:count]
        return taken

    x_hbm, g_hbm, wq_hbm, wk_hbm, wv_hbm, wo_hbm = take(6)
    len_ref, norms_ref, rm_ref, ids_ref = take(4)
    a_hbm, p_hbm, heads_hbm_a, heads_hbm_b, others_hbm_a, others_hbm_b, wo2_hbm = take(7)
    gall_hbm, resid_hbm, f_hbm, chance_hbm, packed_hbm, gin_hbm, info_hbm, lse_ref = take(8)
    xv, wq, wk, wv, wo, wo2, av, pv, vt, ha, hb, oa, ob, gv, pk, fv, rb, cb, hbuf = take(19)
    place_ref, place_g_ref, info = take(3)
    (
        load_sem,
        x_sem,
        a_sem,
        home_sem,
        grad_sem,
        w_sem,
        head_send,
        head_recv,
        z_send,
        z_recv,
        out_sem,
    ) = refs
    me = lax.axis_index("ep")
    tp_me = lax.axis_index("tp")
    mesh = pl.DeviceIdType.MESH
    across = {"tp": 1 - tp_me}
    rows, wide = xv.shape
    shard = rows // 2
    width = wq.shape[1]
    block = 512
    steps = rows // block

    def rows_at(i, size):
        return pl.ds(pl.multiple_of(i * size, size), size)

    def x_load(i):
        return pltpu.make_async_copy(
            x_hbm.at[rows_at(i, block), :], xv.at[rows_at(i, block), :], x_sem.at[i]
        )

    weight_loads = [
        pltpu.make_async_copy(src, dst, load_sem.at[j])
        for j, (src, dst) in enumerate(((wq_hbm, wq), (wk_hbm, wk), (wv_hbm, wv), (wo_hbm, wo)))
    ]
    for c in weight_loads[:3]:
        c.start()
    for i in range(steps):
        x_load(i).start()
    weight_loads[3].start()
    own_rows = pl.ds(pl.multiple_of(tp_me * shard, shard), shard)
    own_grad = pltpu.make_async_copy(g_hbm, gv.at[own_rows, :], home_sem.at[0])
    own_grad.start()

    barrier = pltpu.get_barrier_semaphore()
    pl.semaphore_signal(barrier, inc=1, device_id=across, device_id_type=mesh)
    for k in range(1, peers):
        pl.semaphore_signal(
            barrier, inc=1, device_id={"ep": jnp.bitwise_xor(me, k)}, device_id_type=mesh
        )
    pl.semaphore_wait(barrier, peers)

    def remote(src, dst, send, recv, to):
        return pltpu.make_async_remote_copy(
            src_ref=src,
            dst_ref=dst,
            send_sem=send,
            recv_sem=recv,
            device_id=to,
            device_id_type=mesh,
        )

    grad_copy = remote(g_hbm, gv.at[own_rows, :], grad_sem.at[0], grad_sem.at[1], across)
    grad_copy.start()
    side = lax.rem(me, 2)
    part = wide // 2
    half_rows = pl.ds(pl.multiple_of(side * part, part), part)
    w_copy = remote(
        wo_hbm.at[half_rows, :], wo2.at[half_rows, :], w_sem.at[0], w_sem.at[1], across
    )
    w_copy.start()
    w_pass = remote(
        wo2.at[half_rows, :],
        wo2.at[half_rows, :],
        w_sem.at[2],
        w_sem.at[3],
        {"ep": jnp.bitwise_xor(me, 1)},
    )

    for c in weight_loads[:3]:
        c.wait()

    def a_store(i):
        return [
            pltpu.make_async_copy(
                av.at[rows_at(i, block), :], a_hbm.at[rows_at(i, block), :], a_sem.at[i, 0]
            ),
            pltpu.make_async_copy(
                pv.at[rows_at(i, block), :], p_hbm.at[rows_at(i, block), :], a_sem.at[i, 1]
            ),
        ]

    def project(i, _):
        at = rows_at(i, block)
        x_load(i).wait()
        normal, _ = normalized(xv[at, :].astype(F32))
        a = (normal * norms_ref[0:1, :] + norms_ref[1:2, :]).astype(BF16)
        av[at, :] = a
        for j, w in enumerate((wq, wk, wv)):
            pv[at, j * width : (j + 1) * width] = dot(a, w[...]).astype(BF16)
        for c in a_store(i):
            c.start()
        return 0

    lax.fori_loop(0, steps, project, 0)

    pairs = heads_count // 2

    def attend(pair, out_ref, col):
        vt[...] = pv[:, 2 * width + pair * PAIR : 2 * width + (pair + 1) * PAIR].T

        def q_step(i, _):
            at = rows_at(i, bq)
            q = pv[at, pair * PAIR : (pair + 1) * PAIR]
            out, lse = attend_block(
                i,
                q,
                lambda s: pv[s, width + pair * PAIR : width + (pair + 1) * PAIR],
                lambda s: vt[:, s],
                bq,
                bq,
                HEAD_DIM**-0.5,
            )
            out_ref[at, col : col + PAIR] = out
            for h in range(2):
                lse_ref[pair, h : h + 1, at] = lse[h]
            return 0

        lax.fori_loop(0, rows // bq, q_step, 0)

    def is_live(position):
        count = len_ref.shape[0]
        length = rows // count
        inside = None
        for s in range(count):
            here = (position >= s * length) & (position < s * length + len_ref[s])
            inside = here if inside is None else inside | here
        return inside

    span = 256
    run = jnp.zeros((experts, 1), F32)
    triangle = jnp.where(
        lax.broadcasted_iota(jnp.int32, (span, span), 0)
        < lax.broadcasted_iota(jnp.int32, (span, span), 1),
        1.0,
        0.0,
    ).astype(BF16)
    capacity = 2 * half
    for b in range(rows // span):
        at = slice(b * span, (b + 1) * span)
        ids = ids_ref[:, at]
        live = is_live(b * span + lax.broadcasted_iota(jnp.int32, (1, span), 1))
        hot = (lax.broadcasted_iota(jnp.int32, (experts, span), 0) == ids) & live
        hot = jnp.where(hot, 1.0, 0.0)
        before = dot(hot.astype(BF16), triangle) + run
        run = run + jnp.sum(hot, axis=1, keepdims=True)
        slot = jnp.sum(before * hot, axis=0, keepdims=True).astype(jnp.int32)
        sound = live & (slot < capacity)
        place = jnp.where(sound, ids * capacity + slot, -1)
        inside = slot - tp_me * half
        mine = sound & (inside >= 0) & (inside < half)
        place_g = jnp.where(mine, ids * half + inside, -1)
        place_ref[:, at] = place
        place_g_ref[:, at] = place_g
        line = lax.broadcasted_iota(jnp.int32, (LANES, span), 0)
        both = jnp.where(line == 0, place.astype(F32), place_g.astype(F32))
        info[at, :] = both.T
    info_store = pltpu.make_async_copy(info, info_hbm, home_sem.at[4])
    info_store.start()

    def head_copy(j, src, dst):
        return remote(src, dst, head_send.at[j], head_recv.at[j], across)

    first = pairs // 2
    for pair in range(first):
        attend(pair, ha, pair * PAIR)
    copy_a = head_copy(0, ha, oa)
    copy_a.start()
    for pair in range(first, pairs - 1):
        attend(pair, hb, (pair - first) * PAIR)

    own_grad.wait()
    grad_copy.wait()

    def mask(i, _):
        at = rows_at(i, block)
        live = is_live(i * block + lax.broadcasted_iota(jnp.int32, (block, wide), 0))
        gv[at, :] = jnp.where(live, gv[at, :], jnp.zeros((block, wide), BF16))
        return 0

    lax.fori_loop(0, steps, mask, 0)
    gall_store = pltpu.make_async_copy(gv, gall_hbm, home_sem.at[1])
    gall_store.start()

    def pack_g(i, _):
        slot = i * block + lax.broadcasted_iota(jnp.int32, (block, rows), 0)
        hot = jnp.where(slot == place_g_ref[...], 1.0, 0.0).astype(BF16)
        pk[rows_at(i, block), :] = dot(hot, gv[...]).astype(BF16)
        return 0

    lax.fori_loop(0, peers * half // block, pack_g, 0)

    def z_copy(k):
        peer = jnp.bitwise_xor(me, k)
        return remote(
            pk.at[rows_at(peer, half), :], gin_hbm.at[me], z_send.at[k], z_recv.at[k], {"ep": peer}
        )

    for k in list(range(peers // 2, peers)) + list(range(1, peers // 2)):
        z_copy(k).start()
    gin_own = pltpu.make_async_copy(pk.at[rows_at(me, half), :], gin_hbm.at[me], home_sem.at[2])
    gin_own.start()
    w_copy.wait()
    w_pass.start()
    attend(pairs - 1, hb, (pairs - 1 - first) * PAIR)
    copy_b = head_copy(1, hb, ob)
    copy_b.start()
    weight_loads[3].wait()
    w_pass.wait()
    stores = [
        pltpu.make_async_copy(ha, heads_hbm_a, out_sem.at[0]),
        pltpu.make_async_copy(hb, heads_hbm_b, out_sem.at[1]),
        pltpu.make_async_copy(wo2, wo2_hbm, out_sem.at[2]),
    ]
    for c in stores:
        c.start()
    copy_a.wait()
    copy_b.wait()
    stores_others = [
        pltpu.make_async_copy(oa, others_hbm_a, out_sem.at[3]),
        pltpu.make_async_copy(ob, others_hbm_b, out_sem.at[4]),
    ]
    for c in stores_others:
        c.start()
    small = rb.shape[1]
    cut = first * PAIR

    def norm_stores(i, slot):
        at = rows_at(i, small)
        return [
            pltpu.make_async_copy(rb.at[slot], resid_hbm.at[at, :], out_sem.at[5 + slot]),
            pltpu.make_async_copy(cb.at[slot], chance_hbm.at[at, :], out_sem.at[7 + slot]),
        ]

    def norm_step(i, _):
        at = rows_at(i, small)
        slot = lax.rem(i, 2)

        @pl.when(i >= 2)
        def _():
            for c in norm_stores(i - 2, slot):
                c.wait()

        total = dot_nt(ha[at, :], wo[:, :cut]) + dot_nt(hb[at, :], wo[:, cut:])
        total = total + (dot_nt(oa[at, :], wo2[:, :cut]) + dot_nt(ob[at, :], wo2[:, cut:]))
        resid = xv[at, :].astype(F32) + total
        rb[slot] = resid
        normal, _ = normalized(resid)
        f = (normal * norms_ref[2:3, :] + norms_ref[3:4, :]).astype(BF16)
        fv[at, :] = f
        cb[slot] = router_and_mix(dot(f, rm_ref[...]), experts)
        for c in norm_stores(i, slot):
            c.start()
        return 0

    count = rows // small
    lax.fori_loop(0, count, norm_step, 0)
    f_store = pltpu.make_async_copy(fv, f_hbm, home_sem.at[3])
    f_store.start()
    for i in range(count - 2, count):
        for c in norm_stores(i, i % 2):
            c.wait()

    def packed_store(i, slot):
        return pltpu.make_async_copy(
            hbuf.at[slot], packed_hbm.at[rows_at(i, block), :], out_sem.at[5 + slot]
        )

    def pack_h(i, _):
        slot = lax.rem(i, 2)

        @pl.when(i >= 2)
        def _():
            packed_store(i - 2, slot).wait()

        at = i * block + lax.broadcasted_iota(jnp.int32, (block, rows), 0)
        hot = jnp.where(at == place_ref[...], 1.0, 0.0).astype(BF16)
        hbuf[slot] = dot(hot, fv[...]).astype(BF16)
        packed_store(i, slot).start()
        return 0

    packs = packed_hbm.shape[0] // block
    lax.fori_loop(0, packs, pack_h, 0)
    for i in range(packs - 2, packs):
        packed_store(i, i % 2).wait()
    for c in [gall_store, gin_own, f_store, info_store] + stores + stores_others:
        c.wait()
    for i in range(steps):
        for c in a_store(i):
            c.wait()
    for k in range(1, peers):
        z_copy(k).wait()


def front(x, g, weights, lengths, norms, rm, ids, peers, experts, capacity, bq=512):
    rows, wide = x.shape
    width = weights[0].shape[1]
    half = capacity // 2
    cut = width // 2
    anywhere = pl.BlockSpec(memory_space=pl.ANY)
    vmem = pl.BlockSpec(memory_space=pltpu.VMEM)

    def like(*shape, kind=BF16):
        return jax.ShapeDtypeStruct(shape, kind)

    return pl.pallas_call(
        partial(
            front_kernel,
            peers=peers,
            experts=experts,
            half=half,
            bq=bq,
            heads_count=width // HEAD_DIM,
        ),
        in_specs=[anywhere] * 6 + [pl.BlockSpec(memory_space=pltpu.SMEM)] + [vmem] * 3,
        out_specs=[anywhere] * 14 + [vmem],
        out_shape=[
            like(rows, wide),
            like(rows, 3 * width),
            like(rows, cut),
            like(rows, cut),
            like(rows, cut),
            like(rows, cut),
            like(wide, width),
            like(rows, wide),
            like(rows, wide, kind=F32),
            like(rows, wide),
            like(rows, LANES, kind=F32),
            like(experts * capacity, wide),
            like(peers, half, wide),
            like(rows, LANES, kind=F32),
            like(width // PAIR, 2, rows, kind=F32),
        ],
        scratch_shapes=[pltpu.VMEM((rows, wide), BF16)]
        + [pltpu.VMEM((wide, width), BF16)] * 5
        + [
            pltpu.VMEM((rows, wide), BF16),
            pltpu.VMEM((rows, 3 * width), BF16),
            pltpu.VMEM((PAIR, rows), BF16),
        ]
        + [pltpu.VMEM((rows, cut), BF16)] * 4
        + [
            pltpu.VMEM((rows, wide), BF16),
            pltpu.VMEM((peers * half, wide), BF16),
            pltpu.VMEM((rows, wide), BF16),
            pltpu.VMEM((2, 256, wide), F32),
            pltpu.VMEM((2, 256, LANES), F32),
            pltpu.VMEM((2, 512, wide), BF16),
            pltpu.VMEM((1, rows), jnp.int32),
            pltpu.VMEM((1, rows), jnp.int32),
            pltpu.VMEM((rows, LANES), F32),
            pltpu.SemaphoreType.DMA((4,)),
            pltpu.SemaphoreType.DMA((rows // 512,)),
            pltpu.SemaphoreType.DMA((rows // 512, 2)),
            pltpu.SemaphoreType.DMA((5,)),
            pltpu.SemaphoreType.DMA((2,)),
            pltpu.SemaphoreType.DMA((4,)),
            pltpu.SemaphoreType.DMA((2,)),
            pltpu.SemaphoreType.DMA((2,)),
            pltpu.SemaphoreType.DMA((peers,)),
            pltpu.SemaphoreType.DMA((peers,)),
            pltpu.SemaphoreType.DMA((9,)),
        ],
        cost_estimate=cost(20 * rows * wide * wide, 30 * rows * wide),
        compiler_params=pltpu.CompilerParams(
            vmem_limit_bytes=BIG_VMEM, collective_id=2, has_side_effects=True
        ),
        name="layer_front",
    )(x, g, *weights, lengths, norms, rm, ids)


def nets_kernel(
    x_hbm,
    g_hbm,
    out_hbm,
    gin_hbm,
    sel_ref,
    rm_ref,
    wd1_hbm,
    wd2_hbm,
    we1_hbm,
    we2_hbm,
    y_hbm,
    dx_hbm,
    dot_hbm,
    gd1_hbm,
    gd2_hbm,
    ge1_hbm,
    ge2_hbm,
    in_hbm,
    res_hbm,
    pull_hbm,
    edot_hbm,
    pulls_hbm,
    edots_hbm,
    gin2_hbm,
    wd1,
    wd2,
    we1,
    we2,
    a1,
    a2,
    xb,
    gb,
    yb,
    dxb,
    dotb,
    rowb,
    ya,
    dxa,
    dyb,
    dyt,
    xt,
    w_sem,
    load_sem,
    store_sem,
    grad_sem,
    home_sem,
    local_sem,
    send_sem,
    recv_sem,
    back_send,
    back_recv,
    dot_send,
    dot_recv,
    relay_sem,
    swap_send,
    swap_recv,
    keep,
    give,
    got,
    stage,
    *,
    peers,
    capacity,
    rb,
    ft,
    relayed,
):
    experts = peers
    me = lax.axis_index("ep")
    hidden = wd1.shape[1]
    per = rb // capacity
    quarter = peers // 4
    dense_steps = x_hbm.shape[0] // rb
    expert_steps = peers // per

    weight_copies = [
        pltpu.make_async_copy(src, dst, w_sem.at[j])
        for j, (src, dst) in enumerate(
            ((wd1_hbm, wd1), (wd2_hbm, wd2), (we1_hbm, we1), (we2_hbm, we2))
        )
    ]
    weight_copies[0].start()
    weight_copies[1].start()

    def load(t, slot):
        rows = pl.ds(pl.multiple_of(t * rb, rb), rb)
        return [
            pltpu.make_async_copy(x_hbm.at[rows, :], xb.at[slot], load_sem.at[slot, 0, 0]),
            pltpu.make_async_copy(g_hbm.at[rows, :], gb.at[slot], load_sem.at[slot, 1, 0]),
        ]

    for c in load(0, 0):
        c.start()

    barrier = pltpu.get_barrier_semaphore()
    for k in range(1, peers):
        pl.semaphore_signal(
            barrier,
            inc=1,
            device_id={"ep": jnp.bitwise_xor(me, k)},
            device_id_type=pl.DeviceIdType.MESH,
        )
    tp_me = lax.axis_index("tp")
    across = {"tp": 1 - tp_me}
    half = capacity // 2
    if relayed:
        pl.semaphore_signal(
            barrier, inc=1, device_id=across, device_id_type=pl.DeviceIdType.MESH
        )
    pl.semaphore_wait(barrier, peers if relayed else peers - 1)
    relay = pltpu.make_async_remote_copy(
        src_ref=gin_hbm,
        dst_ref=gin2_hbm,
        send_sem=relay_sem.at[0],
        recv_sem=relay_sem.at[1],
        device_id=across,
        device_id_type=pl.DeviceIdType.MESH,
    )
    if relayed:
        relay.start()

    def remote(src, dst, send, recv, k):
        peer = jnp.bitwise_xor(me, k)
        return pltpu.make_async_remote_copy(
            src_ref=src,
            dst_ref=dst,
            send_sem=send.at[k],
            recv_sem=recv.at[k],
            device_id={"ep": peer},
            device_id_type=pl.DeviceIdType.MESH,
        )

    def row_copy(k):
        return remote(
            out_hbm.at[jnp.bitwise_xor(me, k)], in_hbm.at[me], send_sem, recv_sem, k
        )

    def back_copy(k):
        return remote(
            pull_hbm.at[jnp.bitwise_xor(me, k)], pulls_hbm.at[me], back_send, back_recv, k
        )

    def dot_copy(k):
        return remote(
            edot_hbm.at[jnp.bitwise_xor(me, k)], edots_hbm.at[me], dot_send, dot_recv, k
        )

    far = list(range(2 * quarter, peers))
    near = list(range(1, 2 * quarter))
    for k in far[:quarter] + near[quarter - 1 :] + far[quarter:] + near[: quarter - 1]:
        row_copy(k).start()
    own_rows = pltpu.make_async_copy(out_hbm.at[me], in_hbm.at[me], home_sem.at[0])
    own_rows.start()
    weight_copies[2].start()
    weight_copies[3].start()

    def compute(slot, routed, w1_ref, w2_ref):
        x_ref = xb.at[slot]
        x = x_ref[...]
        g = gb[slot].astype(F32)
        chances = router_and_mix(dot(x, rm_ref[...]), experts)
        if routed:
            gate = jnp.sum(chances * sel_ref[...], axis=-1, keepdims=True)
            dy = g * lane_of(chances, experts + 1) * gate
        else:
            dy = g * lane_of(chances, experts)
        dy = dy.astype(BF16)
        dyb[...] = dy
        dyt[...] = dy.T
        xt[...] = x.T
        ya[...] = jnp.zeros_like(ya)
        dxa[...] = jnp.zeros_like(dxa)

        def step(f, _):
            cols = pl.ds(pl.multiple_of(f * ft, ft), ft)
            w1 = w1_ref[:, cols]
            w2 = w2_ref[:, cols]
            act, slope = gelu_and_slope(dot(x_ref[...], w1))
            h = act.astype(BF16)
            pre_grad = (slope * dot(dyb[...], w2)).astype(BF16)
            ya[...] += dot_nt(h, w2)
            dxa[...] += dot_nt(pre_grad, w1)
            a2[:, cols] += dot(dyt[...], h)
            a1[:, cols] += dot(xt[...], pre_grad)
            return 0

        lax.fori_loop(0, hidden // ft, step, 0)
        return jnp.sum(ya[...] * gb[slot].astype(F32), axis=1, keepdims=True)

    a1[...] = jnp.zeros_like(a1)
    a2[...] = jnp.zeros_like(a2)
    weight_copies[0].wait()
    weight_copies[1].wait()

    def dense_stores(t, slot):
        rows = pl.ds(pl.multiple_of(t * rb, rb), rb)
        return [
            pltpu.make_async_copy(yb.at[slot], y_hbm.at[rows, :], store_sem.at[slot, 0, 0]),
            pltpu.make_async_copy(dxb.at[slot], dx_hbm.at[rows, :], store_sem.at[slot, 1, 0]),
            pltpu.make_async_copy(dotb.at[slot], dot_hbm.at[rows, :], store_sem.at[slot, 2, 0]),
        ]

    def dense_step(t, _):
        slot = lax.rem(t, 2)
        for c in load(t, slot):
            c.wait()

        @pl.when(t + 1 < dense_steps)
        def _():
            for c in load(t + 1, 1 - slot):
                c.start()

        @pl.when(t >= 2)
        def _():
            for c in dense_stores(t - 2, slot):
                c.wait()

        dots = compute(slot, False, wd1, wd2)
        yb[slot] = ya[...].astype(BF16)
        dxb[slot] = dxa[...].astype(BF16)
        dotb[slot] = jnp.broadcast_to(dots, (rb, LANES))
        for c in dense_stores(t, slot):
            c.start()
        return 0

    lax.fori_loop(0, dense_steps, dense_step, 0)
    for t in range(max(0, dense_steps - 2), dense_steps):
        for c in dense_stores(t, t % 2):
            c.wait()

    wd1[...] = a1[...].astype(BF16)
    wd2[...] = a2[...].astype(BF16)
    dense_grads = [
        pltpu.make_async_copy(wd1, gd1_hbm, grad_sem.at[0]),
        pltpu.make_async_copy(wd2, gd2_hbm, grad_sem.at[1]),
    ]
    for c in dense_grads:
        c.start()
    a1[...] = jnp.zeros_like(a1)
    a2[...] = jnp.zeros_like(a2)
    weight_copies[2].wait()
    weight_copies[3].wait()
    own_rows.wait()
    if relayed:
        relay.wait()

    def first_of(p):
        if expert_steps != 4:
            return (expert_steps - 1 - p) * per
        return jnp.where(p < 2, 2 + p, 3 - p) * per

    def swap_copy(p, j):
        slot = lax.rem(p, 2)
        return pltpu.make_async_remote_copy(
            src_ref=give.at[slot, j],
            dst_ref=got.at[slot, j],
            send_sem=swap_send.at[slot, j],
            recv_sem=swap_recv.at[slot, j],
            device_id=across,
            device_id_type=pl.DeviceIdType.MESH,
        )

    def send_back(p, size, sources):
        base = first_of(p)
        stores = []
        for c in range(per):
            source = jnp.bitwise_xor(me, base + c)
            rows = pl.ds(c * size, size)
            for j, to in ((0, pull_hbm), (1, res_hbm)):
                stores.append(
                    pltpu.make_async_copy(
                        sources[j].at[rows, :], to.at[source], store_sem.at[0, j, c]
                    )
                )
        for c in stores:
            c.start()
        for c in stores:
            c.wait()
        for c in range(per):
            k = base + c

            @pl.when(k > 0)
            def _(k=k):
                back_copy(k).start()

    def finish(p):
        slot = lax.rem(p, 2)
        for j in range(2):
            swap_copy(p, j).wait()
            stage[j] = (keep[j] + got[slot, j].astype(F32)).astype(BF16)
        send_back(p, half, (stage.at[0], stage.at[1]))

    def expert_step(p, _):
        base = first_of(p)
        slot = lax.rem(p, 2)
        loads = []
        for c in range(per):
            k = base + c

            @pl.when(k > 0)
            def _(k=k):
                row_copy(k).wait()

            source = jnp.bitwise_xor(me, k)
            rows = pl.ds(c * capacity, capacity)
            loads.append(
                pltpu.make_async_copy(in_hbm.at[source], xb.at[slot, rows, :], load_sem.at[slot, 0, c])
            )
            if relayed:
                for j, src, which in ((1, gin_hbm, tp_me), (2, gin2_hbm, 1 - tp_me)):
                    at = pl.ds(pl.multiple_of(c * capacity + which * half, half), half)
                    loads.append(
                        pltpu.make_async_copy(
                            src.at[source], gb.at[slot, at, :], load_sem.at[slot, j, c]
                        )
                    )
            else:
                loads.append(
                    pltpu.make_async_copy(
                        gin_hbm.at[source], gb.at[slot, rows, :], load_sem.at[slot, 1, c]
                    )
                )
        for c in loads:
            c.start()
        for c in loads:
            c.wait()
        dots = compute(slot, True, we1, we2)
        if relayed:

            @pl.when(p > 0)
            def _():
                finish(p - 1)

            for j, total in ((0, dxa), (1, ya)):
                for c in range(per):
                    rows = slice(c * half, (c + 1) * half)
                    at = pl.ds(pl.multiple_of(c * capacity + tp_me * half, half), half)
                    other = pl.ds(pl.multiple_of(c * capacity + (1 - tp_me) * half, half), half)
                    keep[j, rows, :] = total[at, :]
                    give[slot, j, rows, :] = total[other, :].astype(BF16)
                swap_copy(p, j).start()
        else:
            yb[slot] = ya[...].astype(BF16)
            dxb[slot] = dxa[...].astype(BF16)
            send_back(p, capacity, (dxb.at[slot], yb.at[slot]))
        across_dots = jnp.broadcast_to(dots, (rb, LANES)).T
        stores = []
        for c in range(per):
            rowb[c] = across_dots[:8, c * capacity : (c + 1) * capacity]
            stores.append(
                pltpu.make_async_copy(
                    rowb.at[c], edot_hbm.at[jnp.bitwise_xor(me, base + c)], store_sem.at[1, 2, c]
                )
            )
        for c in stores:
            c.start()
        for c in stores:
            c.wait()
        for c in range(per):
            k = base + c

            @pl.when(k > 0)
            def _(k=k):
                dot_copy(k).start()

        return 0

    lax.fori_loop(0, expert_steps, expert_step, 0)
    if relayed:
        finish(expert_steps - 1)
    expert_grads = [
        pltpu.make_async_copy(a1, ge1_hbm, local_sem.at[0]),
        pltpu.make_async_copy(a2, ge2_hbm, local_sem.at[1]),
        pltpu.make_async_copy(pull_hbm.at[me], pulls_hbm.at[me], home_sem.at[1]),
        pltpu.make_async_copy(edot_hbm.at[me], edots_hbm.at[me], home_sem.at[2]),
    ]
    for c in expert_grads:
        c.start()
    for c in dense_grads + expert_grads:
        c.wait()
    for k in range(1, peers):
        back_copy(k).wait()
        dot_copy(k).wait()


def nets(x, g, out_rows, in_grads, sel, rm, dense_weights, expert_weights, rb=512, ft=512):
    rows, wide = x.shape
    hidden = dense_weights[0].shape[1]
    peers, capacity, _ = out_rows.shape
    per = rb // capacity
    anywhere = pl.BlockSpec(memory_space=pl.ANY)
    vmem = pl.BlockSpec(memory_space=pltpu.VMEM)
    sheet = jax.ShapeDtypeStruct((rows, wide), BF16)
    relayed = in_grads.shape[1] < capacity
    blocks = jax.ShapeDtypeStruct((peers, capacity, wide), BF16)
    backs = jax.ShapeDtypeStruct(in_grads.shape, BF16)
    part = (rb * in_grads.shape[1] // capacity, wide) if relayed else (16, wide)
    strips = jax.ShapeDtypeStruct((peers, 8, capacity), F32)
    return pl.pallas_call(
        partial(nets_kernel, peers=peers, capacity=capacity, rb=rb, ft=ft, relayed=relayed),
        in_specs=[anywhere] * 4 + [vmem] * 2 + [anywhere] * 4,
        out_specs=[anywhere] * 14,
        out_shape=[
            sheet,
            sheet,
            jax.ShapeDtypeStruct((rows, LANES), F32),
            jax.ShapeDtypeStruct((wide, hidden), BF16),
            jax.ShapeDtypeStruct((wide, hidden), BF16),
            jax.ShapeDtypeStruct((wide, hidden), F32),
            jax.ShapeDtypeStruct((wide, hidden), F32),
            blocks,
            backs,
            backs,
            strips,
            backs,
            strips,
            backs,
        ],
        scratch_shapes=[pltpu.VMEM((wide, hidden), BF16)] * 4
        + [pltpu.VMEM((wide, hidden), F32)] * 2
        + [pltpu.VMEM((2, rb, wide), BF16)] * 4
        + [
            pltpu.VMEM((2, rb, LANES), F32),
            pltpu.VMEM((per, 8, capacity), F32),
            pltpu.VMEM((rb, wide), F32),
            pltpu.VMEM((rb, wide), F32),
            pltpu.VMEM((rb, wide), BF16),
            pltpu.VMEM((wide, rb), BF16),
            pltpu.VMEM((wide, rb), BF16),
            pltpu.SemaphoreType.DMA((4,)),
            pltpu.SemaphoreType.DMA((2, 3, per)),
            pltpu.SemaphoreType.DMA((2, 3, per)),
            pltpu.SemaphoreType.DMA((2,)),
            pltpu.SemaphoreType.DMA((3,)),
            pltpu.SemaphoreType.DMA((2,)),
        ]
        + [pltpu.SemaphoreType.DMA((peers,))] * 6
        + [
            pltpu.SemaphoreType.DMA((2,)),
            pltpu.SemaphoreType.DMA((2, 2)),
            pltpu.SemaphoreType.DMA((2, 2)),
            pltpu.VMEM((2, *part), F32),
            pltpu.VMEM((2, 2, *part), BF16),
            pltpu.VMEM((2, 2, *part), BF16),
            pltpu.VMEM((2, *part), BF16),
        ],
        cost_estimate=cost(24 * rows * wide * hidden, 16 * rows * wide + 24 * wide * hidden),
        compiler_params=pltpu.CompilerParams(
            vmem_limit_bytes=BIG_VMEM, collective_id=0, has_side_effects=True
        ),
        name="feed_forward_nets",
    )(x, g, out_rows, in_grads, sel, rm, *dense_weights, *expert_weights)


def expert_hot(place, capacity, experts):
    lane = lax.broadcasted_iota(jnp.int32, (place.shape[0], LANES), 1)
    low = lane * capacity
    return ((place >= low) & (place < low + capacity) & (lane < experts)).astype(F32)


def ffn_pull_kernel(*refs, parts, experts, capacity, shard):
    (
        info_ref,
        dx_ref,
        chance_ref,
        first_ref,
        f_ref,
        g_ref,
        resid_ref,
        gain_ref,
        rm_ref,
        slot_ref,
        dots_ref,
    ) = refs[:11]
    weights = refs[11 : 11 + parts]
    r_ref = refs[11 + parts]
    heads = refs[12 + parts : 12 + 2 * parts]
    sums_ref, rmg_ref = refs[12 + 2 * parts :]
    place = info_ref[:, 0:1].astype(jnp.int32)
    here = info_ref[:, 1:2].astype(jnp.int32)
    size = info_ref.shape[0]
    row = pl.program_id(0) * size + lax.broadcasted_iota(jnp.int32, (size, 1), 0)
    row = row - lax.axis_index("tp") * shard
    own = ((row >= 0) & (row < shard)).astype(F32)
    chances = chance_ref[...]
    hot = expert_hot(place, capacity, experts)
    gate = jnp.sum(hot * chances, axis=-1, keepdims=True)
    mix_0, mix_1 = lane_of(chances, experts), lane_of(chances, experts + 1)
    table = jnp.dot(
        hot, dots_ref[...], precision=lax.Precision.HIGHEST, preferred_element_type=F32
    )
    slot = lax.broadcasted_iota(jnp.int32, table.shape, 1)
    number = jnp.sum(hot * lax.broadcasted_iota(jnp.int32, hot.shape, 1).astype(F32), axis=-1)
    inside = place - number.astype(jnp.int32)[:, None] * capacity
    second = jnp.sum(jnp.where(slot == inside, table, 0.0), axis=-1, keepdims=True)
    first = lane_of(first_ref[...], 0)
    grad_0, grad_1 = first, gate * second
    inner = mix_0 * grad_0 + mix_1 * grad_1
    lane = lax.broadcasted_iota(jnp.int32, chances.shape, 1)
    low = (mix_1 * second * gate) * (hot - chances)
    low = jnp.where(lane == experts, mix_0 * (grad_0 - inner), low)
    low = jnp.where(lane == experts + 1, mix_1 * (grad_1 - inner), low)
    low = jnp.where(lane > experts + 1, 0.0, low).astype(BF16)
    grad = dx_ref[...].astype(F32) + unpacked(here, slot_ref) + dot_nt(low, rm_ref[...])
    normal, rstd = normalized(resid_ref[...])
    r = norm_pull(grad, normal, rstd, gain_ref[2:3, :]) + own * g_ref[...].astype(F32)
    r = r.astype(BF16)
    r_ref[...] = r
    for h, w in zip(heads, weights):
        h[...] = dot(r, w[...]).astype(BF16)

    @pl.when(pl.program_id(0) == 0)
    def _():
        sums_ref[...] = jnp.zeros_like(sums_ref)
        rmg_ref[...] = jnp.zeros_like(rmg_ref)

    sums_ref[0:1, :] += jnp.sum(grad * normal, axis=0, keepdims=True)
    sums_ref[1:2, :] += jnp.sum(grad, axis=0, keepdims=True)
    rmg_ref[...] += dot(low.T, f_ref[...])


def ffn_pull(
    info, dx, chances, first, f, g, resid, gain, rm, slot_rows, dots, weights, experts, shard, rb=256
):
    rows, wide = dx.shape
    capacity = dots.shape[1]
    dots = jnp.pad(dots, ((0, LANES - experts), (0, 0)))
    block = pl.BlockSpec((rb, wide), lambda i: (i, 0))
    narrow = pl.BlockSpec((rb, LANES), lambda i: (i, 0))
    head_specs = [pl.BlockSpec((rb, size), lambda i: (i, 0)) for _, _, size in weights]
    return pl.pallas_call(
        partial(
            ffn_pull_kernel, parts=len(weights), experts=experts, capacity=capacity, shard=shard
        ),
        grid=(rows // rb,),
        in_specs=[narrow, block, narrow, narrow, block, block, block]
        + [resident(gain.shape), resident((wide, LANES))]
        + [resident(slot_rows.shape), resident(dots.shape)]
        + [
            pl.BlockSpec((wide, size), lambda i, j=j: (0, j), pipeline_mode=pl.Buffered(1))
            for _, j, size in weights
        ],
        out_specs=[block] + head_specs + [resident((8, wide)), resident((LANES, wide))],
        out_shape=[jax.ShapeDtypeStruct((rows, wide), BF16)]
        + [jax.ShapeDtypeStruct((rows, size), BF16) for _, _, size in weights]
        + [jax.ShapeDtypeStruct((8, wide), F32), jax.ShapeDtypeStruct((LANES, wide), F32)],
        cost_estimate=cost(6 * rows * wide * wide, 16 * rows * wide),
        compiler_params=pltpu.CompilerParams(vmem_limit_bytes=48 * 1024 * 1024),
        name="ffn_norm_pull",
    )(
        info,
        dx,
        chances,
        first,
        f,
        g,
        resid,
        gain,
        rm,
        slot_rows,
        dots,
        *[w for w, _, _ in weights],
    )


def outer_kernel(left_ref, *refs, parts):
    rights = refs[:parts]
    o_ref, acc_ref = refs[parts:]

    @pl.when(pl.program_id(0) == 0)
    def _():
        acc_ref[...] = jnp.zeros_like(acc_ref)

    left = left_ref[...].T
    at = 0
    for r in rights:
        width = r.shape[1]
        acc_ref[:, at : at + width] += dot(left, r[...])
        at += width

    @pl.when(pl.program_id(0) == pl.num_programs(0) - 1)
    def _():
        o_ref[...] = acc_ref[...].astype(BF16)


def outer(left, rights, rb=512):
    rows, wide = left.shape
    total = sum(r.shape[1] for r in rights)
    return pl.pallas_call(
        partial(outer_kernel, parts=len(rights)),
        grid=(rows // rb,),
        in_specs=[pl.BlockSpec((rb, wide), lambda i: (i, 0))]
        + [pl.BlockSpec((rb, r.shape[1]), lambda i: (i, 0)) for r in rights],
        out_specs=resident((wide, total)),
        out_shape=jax.ShapeDtypeStruct((wide, total), BF16),
        scratch_shapes=[pltpu.VMEM((wide, total), F32)],
        cost_estimate=cost(2 * rows * wide * total, 2 * rows * (wide + total)),
        name="outer_product",
    )(left, *rights)


def attn_pull_kernel(at_ref, x_ref, r_ref, gain_ref, *refs, groups):
    grads = refs[: 3 * groups]
    weights = refs[3 * groups : 3 * groups + 3]
    t_ref, sums_ref = refs[3 * groups + 3 :]
    del at_ref
    total = None
    for k in range(3):
        at = 0
        for j in range(groups):
            d = grads[k * groups + j]
            width = d.shape[1]
            part = dot_nt(d[...], weights[k][:, at : at + width])
            total = part if total is None else total + part
            at += width
    normal, rstd = normalized(x_ref[...].astype(F32))
    t = norm_pull(total, normal, rstd, gain_ref[...]) + r_ref[...].astype(F32)
    t_ref[...] = t.astype(t_ref.dtype)

    @pl.when(pl.program_id(0) == 0)
    def _():
        sums_ref[...] = jnp.zeros_like(sums_ref)

    sums_ref[0:1, :] += jnp.sum(total * normal, axis=0, keepdims=True)
    sums_ref[1:2, :] += jnp.sum(total, axis=0, keepdims=True)


def attn_pull(first_row, count, x, r, gain, grads, weights, out_type, rb=256):
    wide = x.shape[1]
    groups = len(grads) // 3

    def rows(width):
        return pl.BlockSpec((rb, width), lambda i, at: (at[0] + i, 0))

    return pl.pallas_call(
        partial(attn_pull_kernel, groups=groups),
        grid_spec=pltpu.PrefetchScalarGridSpec(
            num_scalar_prefetch=1,
            grid=(count // rb,),
            in_specs=[rows(wide), rows(wide), resident((1, wide))]
            + [rows(d.shape[1]) for d in grads]
            + [resident(w.shape) for w in weights],
            out_specs=[pl.BlockSpec((rb, wide), lambda i, at: (i, 0)), resident((8, wide))],
        ),
        out_shape=[
            jax.ShapeDtypeStruct((count, wide), out_type),
            jax.ShapeDtypeStruct((8, wide), F32),
        ],
        cost_estimate=cost(6 * count * wide * weights[0].shape[1], 10 * count * wide),
        name="attention_norm_pull",
    )((first_row // rb).astype(jnp.int32).reshape(1), x, r, gain, *grads, *weights)


def combine_kernel(info_ref, y_ref, chance_ref, slot_ref, o_ref, *, experts, capacity):
    place = info_ref[:, 0:1].astype(jnp.int32)
    here = info_ref[:, 1:2].astype(jnp.int32)
    chances = chance_ref[...]
    gate = jnp.sum(expert_hot(place, capacity, experts) * chances, axis=-1, keepdims=True)
    moe = unpacked(here, slot_ref) * (lane_of(chances, experts + 1) * gate)
    o_ref[...] = (lane_of(chances, experts) * y_ref[...].astype(F32) + moe).astype(BF16)


def combine(info, y, coef, slot_rows, experts, capacity, rb=256):
    rows, wide = y.shape
    block = pl.BlockSpec((rb, wide), lambda i: (i, 0))
    return pl.pallas_call(
        partial(combine_kernel, experts=experts, capacity=capacity),
        grid=(rows // rb,),
        in_specs=[
            pl.BlockSpec((rb, LANES), lambda i: (i, 0)),
            block,
            pl.BlockSpec((rb, LANES), lambda i: (i, 0)),
        ]
        + [resident(slot_rows.shape)],
        out_specs=block,
        out_shape=jax.ShapeDtypeStruct((rows, wide), BF16),
        cost_estimate=cost(4 * rows * wide * wide, 8 * rows * wide),
        name="combine_nets",
    )(info, y, coef, slot_rows)


class Halving:
    def __init__(self, total, gives, gots, send, recv, me, size):
        self.total, self.gives, self.gots = total, gives, gots
        self.send, self.recv, self.me, self.size = send, recv, me, size
        self.rows = total.shape[0] // size

    def block(self, index):
        return pl.ds(pl.multiple_of(index * self.rows, self.rows), self.rows)

    def copy(self, s):
        return pltpu.make_async_remote_copy(
            src_ref=self.gives[s],
            dst_ref=self.gots[s],
            send_sem=self.send.at[s],
            recv_sem=self.recv.at[s],
            device_id={"ep": jnp.bitwise_xor(self.me, 1 << s)},
            device_id_type=pl.DeviceIdType.MESH,
        )

    def bit(self, s):
        return lax.rem(lax.div(self.me, 1 << s), 2)

    def start(self, s):
        for i in range(self.size >> (s + 1)):
            at = slice(i * self.rows, (i + 1) * self.rows)
            self.gives[s][at, :] = self.total[self.block(2 * i + 1 - self.bit(s)), :].astype(BF16)
        self.copy(s).start()

    def finish(self, s):
        self.copy(s).wait()
        for i in range(self.size >> (s + 1)):
            at = slice(i * self.rows, (i + 1) * self.rows)
            self.total[at, :] = self.total[self.block(2 * i + self.bit(s)), :] + self.gots[s][at, :].astype(F32)


def tail_kernel(*refs, groups, size, rb, small_rows):
    refs = list(refs)

    def take(count):
        taken = refs[:count]
        del refs[:count]
        return taken

    x_hbm, r_hbm, a_hbm, out_hbm = take(4)
    grads_hbm = take(3 * groups)
    small_ref, gain_ref = take(2)
    weights = take(3)
    own_hbm, got_hbm, square_ref, outsum_ref, total_ref = take(5)
    xv, rv, av = take(3)
    grads = take(3 * groups)
    gov, acc, goacc, give_rows, own_buf = take(5)
    steps = size.bit_length() - 1
    hops = steps + 1
    gives, gots = take(steps), take(steps)
    go_gives, go_gots = take(steps), take(steps)
    small_gives, small_gots = take(hops), take(hops)
    (
        load_sem,
        own_sem,
        row_send,
        row_recv,
        half_send,
        half_recv,
        go_send,
        go_recv,
        small_send,
        small_recv,
        out_sem,
        out_give,
        out_got,
    ) = refs
    me = lax.axis_index("ep")
    tp_me = lax.axis_index("tp")
    rows = x_hbm.shape[0]
    shard = rows // 2
    count = shard // rb

    sources = [x_hbm, r_hbm, *grads_hbm, a_hbm, out_hbm]
    targets = [xv, rv, *grads, av, gov]
    loads = [
        pltpu.make_async_copy(src, dst, load_sem.at[j])
        for j, (src, dst) in enumerate(zip(sources, targets))
    ]
    loads[-1].start()
    for c in loads[:-1]:
        c.start()

    barrier = pltpu.get_barrier_semaphore()
    mesh = pl.DeviceIdType.MESH
    pl.semaphore_signal(barrier, inc=1, device_id={"tp": 1 - tp_me}, device_id_type=mesh)
    for s in range(steps):
        pl.semaphore_signal(
            barrier, inc=1, device_id={"ep": jnp.bitwise_xor(me, 1 << s)}, device_id_type=mesh
        )
    pl.semaphore_wait(barrier, hops)

    qkv = Halving(acc, gives, gots, half_send, half_recv, me, size)
    go = Halving(goacc, go_gives, go_gots, go_send, go_recv, me, size)

    loads[-1].wait()
    goacc[...] = gov[...].astype(F32)
    go.start(0)
    for c in loads[:-2]:
        c.wait()

    total_ref[:small_rows, :] = small_ref[...]
    total_ref[small_rows:, :] = jnp.zeros_like(total_ref[small_rows:, :])

    def pulled(at):
        total = None
        for k in range(3):
            col = 0
            for j in range(groups):
                d = grads[k * groups + j][at, :]
                width = d.shape[1]
                part = dot_nt(d, weights[k][:, col : col + width])
                total = part if total is None else total + part
                col += width
        normal, rstd = normalized(xv[at, :].astype(F32))
        total_ref[small_rows : small_rows + 1, :] += jnp.sum(total * normal, axis=0, keepdims=True)
        total_ref[small_rows + 1 : small_rows + 2, :] += jnp.sum(total, axis=0, keepdims=True)
        return norm_pull(total, normal, rstd, gain_ref[0:1, :]) + rv[at, :].astype(F32)

    def row_copy(b):
        at = pl.ds(pl.multiple_of(b * rb, rb), rb)
        return pltpu.make_async_remote_copy(
            src_ref=give_rows.at[at, :],
            dst_ref=got_hbm.at[at, :],
            send_sem=row_send.at[b],
            recv_sem=row_recv.at[b],
            device_id={"tp": 1 - tp_me},
            device_id_type=mesh,
        )

    def theirs(b, _):
        at = pl.ds(pl.multiple_of((1 - tp_me) * shard + b * rb, rb), rb)
        give_rows[pl.ds(pl.multiple_of(b * rb, rb), rb), :] = pulled(at).astype(BF16)
        row_copy(b).start()
        return 0

    lax.fori_loop(0, count, theirs, 0)
    go.finish(0)
    go.start(1)

    loads[-2].wait()
    acc[...] = jnp.zeros_like(acc)

    def outer_step(b, _):
        at = pl.ds(pl.multiple_of(b * 512, 512), 512)
        left = av[at, :].T
        col = 0
        for g in grads:
            width = g.shape[1]
            acc[:, col : col + width] += dot(left, g[at, :])
            col += width
        return 0

    lax.fori_loop(0, rows // 512, outer_step, 0)
    qkv.start(0)
    for s in range(1, steps):
        go.finish(s)
        if s + 1 < steps:
            go.start(s + 1)
        if s == 1:
            qkv.finish(0)
            qkv.start(1)

    own_width = outsum_ref.shape[1]
    out_give[...] = goacc[: goacc.shape[0] // size, own_width:].astype(BF16)
    out_copy = pltpu.make_async_remote_copy(
        src_ref=out_give,
        dst_ref=out_got,
        send_sem=out_sem.at[0],
        recv_sem=out_sem.at[1],
        device_id={"tp": 1 - tp_me},
        device_id_type=mesh,
    )
    out_copy.start()

    def own_copy(b):
        at = pl.ds(pl.multiple_of(b * rb, rb), rb)
        return pltpu.make_async_copy(own_buf.at[at, :], own_hbm.at[at, :], own_sem.at[b])

    def own_step(b, _):
        at = pl.ds(pl.multiple_of(tp_me * shard + b * rb, rb), rb)
        own_buf[pl.ds(pl.multiple_of(b * rb, rb), rb), :] = pulled(at)
        own_copy(b).start()
        return 0

    lax.fori_loop(0, count, own_step, 0)

    def small_copy(s):
        peer = {"tp": 1 - tp_me} if s == 0 else {"ep": jnp.bitwise_xor(me, 1 << (s - 1))}
        return pltpu.make_async_remote_copy(
            src_ref=small_gives[s],
            dst_ref=small_gots[s],
            send_sem=small_send.at[s],
            recv_sem=small_recv.at[s],
            device_id=peer,
            device_id_type=mesh,
        )

    for s in range(hops):
        small_gives[s][...] = total_ref[...]
        small_copy(s).start()
        if 0 < s < steps:
            qkv.finish(s)
            if s + 1 < steps:
                qkv.start(s + 1)
        small_copy(s).wait()
        total_ref[...] += small_gots[s][...]
    square_ref[...] = acc[: acc.shape[0] // size, :]
    out_copy.wait()
    outsum_ref[...] = goacc[: goacc.shape[0] // size, :own_width] + out_got[...].astype(F32)
    for b in range(count):
        own_copy(b).wait()
        row_copy(b).wait()


def tail(x, r, a, out_part, grads, small, gain, weights, size, rb=256):
    rows, wide = x.shape
    shard = rows // 2
    groups = len(grads) // 3
    total = sum(g.shape[1] for g in grads)
    out_width = out_part.shape[1]
    small_rows = small.shape[0]
    steps = size.bit_length() - 1
    kept = wide // size
    anywhere = pl.BlockSpec(memory_space=pl.ANY)
    vmem = pl.BlockSpec(memory_space=pltpu.VMEM)

    def halves(width):
        return [pltpu.VMEM((wide >> (s + 1), width), BF16) for s in range(steps)]

    return pl.pallas_call(
        partial(tail_kernel, groups=groups, size=size, rb=rb, small_rows=small_rows),
        in_specs=[anywhere] * (4 + 3 * groups) + [vmem] * 5,
        out_specs=[anywhere, anywhere, vmem, vmem, vmem],
        out_shape=[
            jax.ShapeDtypeStruct((shard, wide), F32),
            jax.ShapeDtypeStruct((shard, wide), BF16),
            jax.ShapeDtypeStruct((kept, total), F32),
            jax.ShapeDtypeStruct((kept, out_width // 2), F32),
            jax.ShapeDtypeStruct((small_rows + 8, wide), F32),
        ],
        scratch_shapes=[pltpu.VMEM((rows, wide), BF16)] * 3
        + [pltpu.VMEM(g.shape, BF16) for g in grads]
        + [
            pltpu.VMEM((wide, out_width), BF16),
            pltpu.VMEM((wide, total), F32),
            pltpu.VMEM((wide, out_width), F32),
            pltpu.VMEM((shard, wide), BF16),
            pltpu.VMEM((shard, wide), F32),
        ]
        + halves(total) * 2
        + halves(out_width) * 2
        + [pltpu.VMEM((small_rows + 8, wide), F32)] * (2 * (steps + 1))
        + [
            pltpu.SemaphoreType.DMA((5 + 3 * groups,)),
            pltpu.SemaphoreType.DMA((shard // rb,)),
            pltpu.SemaphoreType.DMA((shard // rb,)),
            pltpu.SemaphoreType.DMA((shard // rb,)),
        ]
        + [pltpu.SemaphoreType.DMA((steps,))] * 4
        + [pltpu.SemaphoreType.DMA((steps + 1,))] * 2
        + [
            pltpu.SemaphoreType.DMA((2,)),
            pltpu.VMEM((kept, out_width // 2), BF16),
            pltpu.VMEM((kept, out_width // 2), BF16),
        ],
        cost_estimate=cost(12 * rows * wide * total // 3, 16 * rows * wide),
        compiler_params=pltpu.CompilerParams(
            vmem_limit_bytes=BIG_VMEM, collective_id=1, has_side_effects=True
        ),
        name="backward_tail",
    )(x, r, a, out_part, *grads, small, gain, *weights)


def on_device(
    sizes,
    tokens,
    out_grad,
    lengths,
    expert_ids,
    w_query,
    w_key,
    w_value,
    w_output,
    w_hidden,
    w_return,
    router,
    mix_weight,
    gain_attn,
    bias_attn,
    gain_ffn,
    bias_ffn,
    expert_in,
    expert_out,
):
    tp, ep = sizes
    shard_rows = out_grad.shape[0]
    all_rows = tokens.shape[0]
    model_width = tokens.shape[1]
    experts = router.shape[1]
    capacity = all_rows // experts
    seq_count = lengths.shape[0]
    seq_len = all_rows // seq_count
    local_width = w_query.shape[1]
    local_heads = local_width // HEAD_DIM
    pairs = local_heads // 2
    splits = 2 if pairs % 2 == 0 else 1
    each = pairs // splits
    tp_index = lax.axis_index("tp")
    ep_index = lax.axis_index("ep")
    first_row = tp_index * shard_rows
    swap = [(0, 1), (1, 0)]

    def shard_of(values, axis=0):
        return lax.dynamic_slice_in_dim(values, first_row, shard_rows, axis)

    def swapped(values):
        return lax.ppermute(values, "tp", swap)

    def exchange(values):
        return lax.all_to_all(values, "ep", split_axis=0, concat_axis=0, tiled=True)

    def after(values, *others):
        return lax.optimization_barrier((values, others))[0]

    def summed_over(values, axis, size):
        step = 1
        while step < size:
            values = values + lax.ppermute(values, axis, [(i, i ^ step) for i in range(size)])
            step *= 2
        return values

    def over_sequences(values):
        return lax.psum_scatter(values, "ep", scatter_dimension=0, tiled=True)

    positions = jnp.arange(all_rows)
    seq_index = positions // seq_len
    row_limit = jnp.sum(
        jnp.where(seq_index[:, None] == jnp.arange(seq_count)[None, :], lengths[None, :], 0), axis=1
    )
    live_all = positions % seq_len < row_limit
    slot_count = experts * capacity
    blocks = (experts, capacity, model_width)

    rm = jnp.pad(
        jnp.concatenate([router, mix_weight], axis=1), ((0, 0), (0, LANES - experts - 2))
    )
    norms = jnp.stack([gain_attn, bias_attn, gain_ffn, bias_ffn]).astype(F32)
    projections = (w_query, w_key, w_value)
    if tp == 2:
        (
            attn_in,
            projected,
            *heads,
            w_other,
            grad_all,
            resid,
            ffn_in,
            chances,
            packed,
            grad_rows,
            info,
            lse,
        ) = front(
            tokens,
            out_grad,
            (*projections, w_output),
            lengths,
            norms,
            rm,
            expert_ids[None, :],
            ep,
            experts,
            capacity,
        )
        all_heads = heads
        heads = heads[:2]
        log_sums = [lse[s * each : (s + 1) * each] for s in range(splits)]
        weights = [(w_output, s) for s in range(2)] + [(w_other, s) for s in range(2)]
        wide_weights = [(w, s, each * PAIR) for w, s in weights]
    else:
        one_hot = (expert_ids[:, None] == jnp.arange(experts)[None, :]) & live_all[:, None]
        routed = one_hot.astype(F32)
        slots = jnp.sum((jnp.cumsum(routed, axis=0) - routed) * routed, axis=1).astype(jnp.int32)
        sound = live_all & (slots < capacity)
        place = jnp.where(sound, expert_ids * capacity + slots, -1)
        place_row = place[None, :]
        info = jnp.broadcast_to(place[:, None], (all_rows, LANES)).astype(F32)
        live_grad = jnp.where(shard_of(live_all)[:, None], out_grad, jnp.zeros_like(out_grad))
        w_all = lax.all_gather(w_output, "tp", axis=1, tiled=True)
        grad_all = lax.all_gather(live_grad, "tp", axis=0, tiled=True)
        grad_rows = exchange(pack(place_row, grad_all, slot_count).reshape(blocks))
        attn_in, projected = norm_project(tokens, norms[0:1], norms[1:2], projections)
        heads, log_sums = [], []
        for s in range(splits):
            o, lse = attention_forward(projected, seq_count, local_heads, s * each, each)
            heads.append(o)
            log_sums.append(lse)
        all_heads = [lax.all_gather(jnp.concatenate(heads, axis=1), "tp", axis=1, tiled=True)]
        wide_weights = [(w_all, 0, model_width)]
        resid, ffn_in, chances = output_norm(
            tokens, norms[2:3], norms[3:4], rm, all_heads, [(w_all, 0)], experts
        )
        packed = pack(place_row, ffn_in, slot_count)

    sel = (jnp.arange(LANES) == ep_index).astype(F32)[None, :]
    (
        dense,
        dense_pull,
        first_dot,
        grad_hidden,
        grad_return,
        grad_expert_in,
        grad_expert_out,
        _,
        results,
        _,
        _,
        pulls,
        dots,
        _,
    ) = nets(
        ffn_in,
        grad_all,
        packed.reshape(blocks),
        grad_rows,
        sel,
        rm,
        (w_hidden, w_return),
        (expert_in[0], expert_out[0]),
    )
    returned = exchange(results).reshape(-1, model_width)
    pulls = pulls.reshape(-1, model_width)
    dots = dots[:, 0, :]
    part, *rest = ffn_pull(
        info,
        dense_pull,
        chances,
        first_dot,
        ffn_in,
        grad_all,
        resid,
        norms,
        rm,
        pulls,
        dots,
        wide_weights,
        experts,
        shard_rows,
    )
    *head_parts, ffn_sums, rm_sums = rest
    if tp == 2:
        head_grads = [[m, swapped(o)] for m, o in zip(head_parts[:splits], head_parts[splits:])]
    else:
        local = lax.psum_scatter(head_parts[0], "tp", scatter_dimension=1, tiled=True)
        head_grads = [
            [local[:, s * each * PAIR : (s + 1) * each * PAIR]] for s in range(splits)
        ]
    out_part = outer(part, all_heads)
    part = after(part, out_part)
    grad_hidden = over_sequences(grad_hidden)
    grad_return = over_sequences(grad_return)

    square, qkv = [], []
    for s in range(splits):
        if s == splits - 1:
            if qkv:
                dense, qkv[-1], head_grads[s], out_part = lax.optimization_barrier(
                    (dense, qkv[-1], head_grads[s], out_part)
                )
            weighted = combine(info, dense, chances, returned, experts, capacity)
            grad_expert_in, grad_expert_out = [
                jnp.where(lengths[0] > 0, e, 0.0) for e in (grad_expert_in, grad_expert_out)
            ]
            projected, weighted, grad_expert_in, grad_expert_out = lax.optimization_barrier(
                (projected, weighted, grad_expert_in, grad_expert_out)
            )
        grads3 = attention_backward(
            projected, heads[s], head_grads[s], log_sums[s], seq_count, local_heads, s * each
        )
        qkv.append(grads3)
    flat = [qkv[s][k] for k in range(3) for s in range(splits)]
    rows_kept = -(-(experts + 2) // 8) * 8
    small = jnp.concatenate([ffn_sums, rm_sums[:rows_kept]], axis=0)
    theirs = lax.dynamic_slice_in_dim(weighted, shard_rows - first_row, shard_rows, 0)
    if tp == 2:
        summed = shard_of(weighted).astype(F32) + swapped(theirs).astype(F32)
        block_out = jnp.where(shard_of(live_all)[:, None], shard_of(resid) + summed, 0.0).astype(BF16)
        part, block_out = lax.optimization_barrier((part, block_out))
        own_part, got, square, grad_output, small = tail(
            tokens,
            part,
            attn_in,
            out_part,
            flat,
            small,
            norms,
            projections,
            ep,
        )
        token_grad = own_part + got.astype(F32)
        attn_sums = small[8 + rows_kept :]
    else:
        whole, attn_sums = attn_pull(
            jnp.zeros((), jnp.int32), all_rows, tokens, part, norms[0:1], flat, projections, BF16
        )
        token_grad = lax.psum_scatter(whole, "tp", scatter_dimension=0, tiled=True).astype(F32)
        summed = lax.psum_scatter(weighted, "tp", scatter_dimension=0, tiled=True).astype(F32)
        block_out = jnp.where(shard_of(live_all)[:, None], shard_of(resid) + summed, 0.0).astype(BF16)
        square = over_sequences(outer(attn_in, flat))
        grad_output = lax.psum_scatter(
            over_sequences(out_part).astype(BF16), "tp", scatter_dimension=1, tiled=True
        ).astype(F32)
        small = summed_over(summed_over(small, "tp", tp), "ep", ep)
        attn_sums = summed_over(summed_over(attn_sums, "tp", tp), "ep", ep)
    grad_hidden, grad_return, square = lax.optimization_barrier((grad_hidden, grad_return, square))
    grad_query, grad_key, grad_value = jnp.split(square.astype(F32), 3, axis=1)


    return (
        block_out,
        token_grad,
        grad_query,
        grad_key,
        grad_value,
        grad_output,
        grad_hidden.astype(F32),
        grad_return.astype(F32),
        small[8 : 8 + experts].T,
        small[8 + experts : 10 + experts].T,
        attn_sums[0],
        attn_sums[1],
        small[0],
        small[1],
        grad_expert_in[None],
        grad_expert_out[None],
    )


def solution(mesh):
    in_specs = (
        P("ep", None),
        P(("ep", "tp"), None),
        P("ep"),
        P("ep"),
        P(None, "tp"),
        P(None, "tp"),
        P(None, "tp"),
        P(None, "tp"),
        P(None, "tp"),
        P(None, "tp"),
        P(),
        P(),
        P(),
        P(),
        P(),
        P(),
        P("ep", None, "tp"),
        P("ep", None, "tp"),
    )
    out_specs = (
        P(("ep", "tp"), None),
        P(("ep", "tp"), None),
        P("ep", "tp"),
        P("ep", "tp"),
        P("ep", "tp"),
        P("ep", "tp"),
        P("ep", "tp"),
        P("ep", "tp"),
        P(),
        P(),
        P(),
        P(),
        P(),
        P(),
        P("ep", None, "tp"),
        P("ep", None, "tp"),
    )
    return jax.shard_map(
        partial(on_device, (mesh.shape["tp"], mesh.shape["ep"])),
        mesh=mesh,
        in_specs=in_specs,
        out_specs=out_specs,
        check_vma=False,
    )
```

```python
import math
from functools import partial

import jax
import jax.numpy as jnp
from jax import lax
from jax.experimental import pallas as pl
from jax.experimental.pallas import tpu as pltpu
from jax.sharding import PartitionSpec as P

HEAD_DIM = 64
PAIR = 2 * HEAD_DIM


EPS = 1e-05
NEG = -1e30
F32 = jnp.float32
BF16 = jnp.bfloat16
NT = (((1,), (1,)), ((), ()))


LANES = 128
GELU_C = math.sqrt(2.0 / math.pi)
GELU_A = 0.044715
BIG_VMEM = 62 * 1024 * 1024


def dot(left, right):
    return jnp.dot(left, right, preferred_element_type=F32)


def dot_nt(left, right):
    return lax.dot_general(left, right, NT, preferred_element_type=F32)


def normalized(values):
    middle = jnp.mean(values, axis=-1, keepdims=True)
    centred = values - middle
    rstd = lax.rsqrt(jnp.mean(centred * centred, axis=-1, keepdims=True) + EPS)
    return centred * rstd, rstd


def norm_pull(grad, normal, rstd, gain):
    q = grad * gain
    along = jnp.mean(q * normal, axis=-1, keepdims=True)
    return rstd * (q - jnp.mean(q, axis=-1, keepdims=True) - normal * along)


def gelu_and_slope(v):
    square = v * v
    t = jnp.tanh(v * (GELU_C + (GELU_C * GELU_A) * square))
    half = 0.5 + 0.5 * t
    slope = half + v * (0.5 - 0.5 * (t * t)) * (GELU_C + (3.0 * GELU_C * GELU_A) * square)
    return v * half, slope


def router_and_mix(logits, experts):
    lane = lax.broadcasted_iota(jnp.int32, logits.shape, 1)
    out = jnp.zeros_like(logits)
    for low, high in ((0, experts), (experts, experts + 2)):
        inside = (lane >= low) & (lane < high)
        top = jnp.max(jnp.where(inside, logits, NEG), axis=-1, keepdims=True)
        e = jnp.where(inside, jnp.exp(jnp.where(inside, logits - top, 0.0)), 0.0)
        out = out + e / jnp.sum(e, axis=-1, keepdims=True)
    return out


def lane_of(values, index):
    lane = lax.broadcasted_iota(jnp.int32, values.shape, 1)
    return jnp.sum(jnp.where(lane == index, values, 0.0), axis=-1, keepdims=True)


def resident(shape):
    return pl.BlockSpec(shape, lambda i, *_: (0,) * len(shape), pipeline_mode=pl.Buffered(1))


def cost(flops, bytes_accessed):
    return pl.CostEstimate(flops=flops // 64, bytes_accessed=bytes_accessed // 64, transcendentals=0)


def attend_block(qi, q, keys, values_t, bq, bk, scale):
    lane = lax.broadcasted_iota(jnp.int32, (bq, PAIR), 1)
    q = q * jnp.asarray(scale, BF16)
    zero = jnp.zeros_like(q)
    halves = [jnp.where(lane < HEAD_DIM, q, zero), jnp.where(lane < HEAD_DIM, zero, q)]

    def step(j, carry, masked):
        off = pl.multiple_of(j * bk, bk)
        k = keys(pl.ds(off, bk))
        vt = values_t(pl.ds(off, bk))
        scores = [lax.dot_general(k, half, NT, preferred_element_type=F32) for half in halves]
        if masked:
            key_pos = off + lax.broadcasted_iota(jnp.int32, (bk, bq), 0)
            query_pos = qi * bq + lax.broadcasted_iota(jnp.int32, (bk, bq), 1)
            allowed = key_pos <= query_pos
            scores = [jnp.where(allowed, s, NEG) for s in scores]
        new = []
        for h in range(2):
            m, l, acc = carry[h]
            m_new = jnp.maximum(m, jnp.max(scores[h], axis=0, keepdims=True))
            alpha = jnp.exp(m - m_new)
            p = jnp.exp(scores[h] - m_new)
            l = l * alpha + jnp.sum(p, axis=0, keepdims=True)
            part = dot(vt[h * HEAD_DIM : (h + 1) * HEAD_DIM], p.astype(BF16))
            new.append((m_new, l, acc * alpha + part))
        return tuple(new)

    init = tuple(
        (jnp.full((1, bq), NEG, F32), jnp.zeros((1, bq), F32), jnp.zeros((HEAD_DIM, bq), F32))
        for _ in range(2)
    )
    full = qi * (bq // bk)
    carry = lax.fori_loop(0, full, lambda j, c: step(j, c, False), init)
    for d in range(bq // bk):
        carry = step(full + d, carry, True)
    out = jnp.concatenate([acc / l for _, l, acc in carry], axis=0).T.astype(BF16)
    return out, [m + jnp.log(l) for m, l, _ in carry]


def attention_forward_kernel(q_ref, k_ref, v_ref, o_ref, lse_ref, vt_ref, *, bq, bk, scale):
    qi = pl.program_id(2)

    @pl.when(qi == 0)
    def _():
        vt_ref[...] = v_ref[...].T

    out, lse = attend_block(
        qi, q_ref[...], lambda s: k_ref[s, :], lambda s: vt_ref[:, s], bq, bk, scale
    )
    o_ref[...] = out
    for h in range(2):
        lse_ref[0, h : h + 1, :] = lse[h]


def attention_forward(proj, seqs, heads, first, count, bq=512, bk=512):
    rows = proj.shape[0]
    length = rows // seqs
    pairs = heads // 2
    nq = length // bq
    flops = 2 * rows * length * count * PAIR
    return pl.pallas_call(
        partial(attention_forward_kernel, bq=bq, bk=bk, scale=HEAD_DIM**-0.5),
        grid=(seqs, count, nq),
        in_specs=[
            pl.BlockSpec((bq, PAIR), lambda s, p, i: (s * nq + i, first + p)),
            pl.BlockSpec((length, PAIR), lambda s, p, i: (s, pairs + first + p)),
            pl.BlockSpec((length, PAIR), lambda s, p, i: (s, 2 * pairs + first + p)),
        ],
        out_specs=[
            pl.BlockSpec((bq, PAIR), lambda s, p, i: (s * nq + i, p)),
            pl.BlockSpec((1, 2, bq), lambda s, p, i: (p, 0, s * nq + i)),
        ],
        out_shape=[
            jax.ShapeDtypeStruct((rows, count * PAIR), BF16),
            jax.ShapeDtypeStruct((count, 2, rows), F32),
        ],
        scratch_shapes=[pltpu.VMEM((PAIR, length), BF16)],
        cost_estimate=cost(flops * 4, 8 * rows * count * PAIR),
        name="attention_forward",
    )(proj, proj, proj)


def attention_backward_kernel(
    q_ref,
    k_ref,
    v_ref,
    o_ref,
    lse_ref,
    *refs,
    terms,
    carried,
    bq,
    bk,
    scale,
    length,
):
    lane = lax.broadcasted_iota(jnp.int32, (length, PAIR), 1)
    first = lane < HEAD_DIM
    q = q_ref[...] * jnp.asarray(scale, BF16)
    do_refs = refs[:terms]
    refs = refs[terms:]
    if carried:
        from_hbm, dq_ref, dk_ref, dv_ref, to_hbm, *refs, held, carry_sem = refs
        way_in = pltpu.make_async_copy(from_hbm, held, carry_sem.at[0])
        way_out = pltpu.make_async_copy(held, to_hbm, carry_sem.at[1])
        at = pl.program_id(0) * pl.num_programs(1) + pl.program_id(1)
        final = pl.num_programs(0) * pl.num_programs(1) - 1

        @pl.when(at == 0)
        def _():
            way_in.start()

        @pl.when(at == final)
        def _():
            way_in.wait()
            way_out.start()

    else:
        dq_ref, dk_ref, dv_ref, *refs = refs
    dqt_ref, qs_ref, dos_ref, kt_ref, dl_ref = refs
    do = do_refs[0][...]
    if terms == 2:
        do = (do.astype(F32) + do_refs[1][...].astype(F32)).astype(BF16)
    zero = jnp.zeros_like(q)
    qs_ref[0] = jnp.where(first, q, zero)
    qs_ref[1] = jnp.where(first, zero, q)
    dos_ref[0] = jnp.where(first, do, zero)
    dos_ref[1] = jnp.where(first, zero, do)
    kt_ref[...] = (k_ref[...] * jnp.asarray(scale, BF16)).T
    prod = (do.astype(F32) * o_ref[...].astype(F32)).T
    dl_ref[0:1, :] = jnp.sum(prod[:HEAD_DIM], axis=0, keepdims=True)
    dl_ref[1:2, :] = jnp.sum(prod[HEAD_DIM:], axis=0, keepdims=True)
    dqt_ref[...] = jnp.zeros_like(dqt_ref)
    nq = length // bq
    nk = length // bk

    def key_block(j, _):
        koff = pl.multiple_of(j * bk, bk)
        k = k_ref[pl.ds(koff, bk), :]
        v = v_ref[pl.ds(koff, bk), :]
        kt = kt_ref[:, pl.ds(koff, bk)]

        def step(i, carry, masked):
            dk, dv = carry
            qoff = pl.multiple_of(i * bq, bq)
            if masked:
                key_pos = koff + lax.broadcasted_iota(jnp.int32, (bk, bq), 0)
                query_pos = qoff + lax.broadcasted_iota(jnp.int32, (bk, bq), 1)
                allowed = key_pos <= query_pos
            qh = [qs_ref[h, pl.ds(qoff, bq), :] for h in range(2)]
            dh = [dos_ref[h, pl.ds(qoff, bq), :] for h in range(2)]
            scores = [lax.dot_general(k, x, NT, preferred_element_type=F32) for x in qh]
            pulls = [lax.dot_general(v, x, NT, preferred_element_type=F32) for x in dh]
            dqs = []
            for h in range(2):
                p = jnp.exp(scores[h] - lse_ref[0, h : h + 1, pl.ds(qoff, bq)])
                if masked:
                    p = jnp.where(allowed, p, 0.0)
                ds = (p * (pulls[h] - dl_ref[h : h + 1, pl.ds(qoff, bq)])).astype(BF16)
                dv = dv + jnp.dot(p.astype(BF16), dh[h], preferred_element_type=F32)
                dk = dk + jnp.dot(ds, qh[h], preferred_element_type=F32)
                dqs.append(
                    jnp.dot(
                        kt[h * HEAD_DIM : (h + 1) * HEAD_DIM], ds, preferred_element_type=F32
                    )
                )
            dqt_ref[:, pl.ds(qoff, bq)] += jnp.concatenate(dqs, axis=0)
            return dk, dv

        carry = (jnp.zeros((bk, PAIR), F32), jnp.zeros((bk, PAIR), F32))
        i0 = j * (bk // bq)
        for d in range(bk // bq):
            carry = step(i0 + d, carry, True)
        dk, dv = lax.fori_loop(i0 + bk // bq, nq, lambda i, c: step(i, c, False), carry)
        dk_ref[pl.ds(koff, bk), :] = dk.astype(BF16)
        dv_ref[pl.ds(koff, bk), :] = dv.astype(BF16)
        return 0

    lax.fori_loop(0, nk, key_block, 0)
    dq_ref[...] = dqt_ref[...].T.astype(BF16)
    if carried:

        @pl.when(at == final)
        def _():
            way_out.wait()


def attention_backward(proj, out, out_grads, lse, seqs, heads, first, count, carry=(), bq=512, bk=512):
    rows = out.shape[0]
    length = rows // seqs
    pairs = heads // 2
    width = count * PAIR

    def block(off):
        return pl.BlockSpec((length, PAIR), lambda s, p: (s, off + p))

    grad = jax.ShapeDtypeStruct((rows, width), BF16)
    terms = len(out_grads)
    return pl.pallas_call(
        partial(
            attention_backward_kernel,
            terms=terms,
            carried=bool(carry),
            bq=bq,
            bk=bk,
            scale=HEAD_DIM**-0.5,
            length=length,
        ),
        grid=(seqs, count),
        in_specs=[
            block(first),
            block(pairs + first),
            block(2 * pairs + first),
            block(first),
            pl.BlockSpec((1, 2, length), lambda s, p: (first + p, 0, s)),
        ]
        + [block(0)] * terms
        + [pl.BlockSpec(memory_space=pl.ANY) for _ in carry],
        out_specs=[block(0)] * 3 + [pl.BlockSpec(memory_space=pl.ANY) for _ in carry],
        out_shape=[grad] * 3 + [jax.ShapeDtypeStruct(c.shape, c.dtype) for c in carry],
        scratch_shapes=[
            pltpu.VMEM((PAIR, length), F32),
            pltpu.VMEM((2, length, PAIR), BF16),
            pltpu.VMEM((2, length, PAIR), BF16),
            pltpu.VMEM((PAIR, length), BF16),
            pltpu.VMEM((2, length), F32),
        ]
        + [s for c in carry for s in (pltpu.VMEM(c.shape, c.dtype), pltpu.SemaphoreType.DMA((2,)))],
        cost_estimate=cost(20 * rows * length * width, 16 * rows * width),
        compiler_params=pltpu.CompilerParams(vmem_limit_bytes=52 * 1024 * 1024),
        name="attention_backward",
    )(proj, proj, proj, out, lse, *out_grads, *carry)


def norm_project_kernel(x_ref, gain_ref, bias_ref, wq_ref, wk_ref, wv_ref, a_ref, p_ref):
    normal, _ = normalized(x_ref[...].astype(F32))
    a = (normal * gain_ref[...] + bias_ref[...]).astype(BF16)
    a_ref[...] = a
    width = wq_ref.shape[1]
    for j, w in enumerate((wq_ref, wk_ref, wv_ref)):
        p_ref[:, j * width : (j + 1) * width] = dot(a, w[...]).astype(BF16)


def norm_project(x, gain, bias, weights, rb=512):
    rows, wide = x.shape
    width = weights[0].shape[1]
    return pl.pallas_call(
        norm_project_kernel,
        grid=(rows // rb,),
        in_specs=[pl.BlockSpec((rb, wide), lambda i: (i, 0)), resident((1, wide)), resident((1, wide))]
        + [resident((wide, width))] * 3,
        out_specs=[
            pl.BlockSpec((rb, wide), lambda i: (i, 0)),
            pl.BlockSpec((rb, 3 * width), lambda i: (i, 0)),
        ],
        out_shape=[
            jax.ShapeDtypeStruct((rows, wide), BF16),
            jax.ShapeDtypeStruct((rows, 3 * width), BF16),
        ],
        cost_estimate=cost(6 * rows * wide * width, 8 * rows * wide),
        name="norm_project",
    )(x, gain, bias, *weights)


def output_norm_kernel(*refs, parts, experts):
    x_ref, gain_ref, bias_ref, rm_ref = refs[:4]
    heads = refs[4 : 4 + parts]
    weights = refs[4 + parts : 4 + 2 * parts]
    resid_ref, f_ref, chance_ref = refs[4 + 2 * parts :]
    total = dot_nt(heads[0][...], weights[0][...])
    for h, w in zip(heads[1:], weights[1:]):
        total = total + dot_nt(h[...], w[...])
    resid = x_ref[...].astype(F32) + total
    resid_ref[...] = resid
    normal, _ = normalized(resid)
    f = (normal * gain_ref[...] + bias_ref[...]).astype(BF16)
    f_ref[...] = f
    chance_ref[...] = router_and_mix(dot(f, rm_ref[...]), experts)


def output_norm(x, gain, bias, rm, heads, weights, experts, rb=256):
    rows, wide = x.shape
    block = pl.BlockSpec((rb, wide), lambda i: (i, 0))
    weight_specs = [
        pl.BlockSpec(
            (wide, h.shape[1]), lambda i, j=j: (0, j), pipeline_mode=pl.Buffered(1)
        )
        for h, (_, j) in zip(heads, weights)
    ]
    return pl.pallas_call(
        partial(output_norm_kernel, parts=len(heads), experts=experts),
        grid=(rows // rb,),
        in_specs=[block, resident((1, wide)), resident((1, wide)), resident((wide, LANES))]
        + [pl.BlockSpec((rb, h.shape[1]), lambda i: (i, 0)) for h in heads]
        + weight_specs,
        out_specs=[block, block, pl.BlockSpec((rb, LANES), lambda i: (i, 0))],
        out_shape=[
            jax.ShapeDtypeStruct((rows, wide), F32),
            jax.ShapeDtypeStruct((rows, wide), BF16),
            jax.ShapeDtypeStruct((rows, LANES), F32),
        ],
        cost_estimate=cost(2 * rows * wide * wide, 12 * rows * wide),
        name="output_norm",
    )(x, gain, bias, rm, *heads, *[w for w, _ in weights])


def pack_kernel(place_ref, x_ref, o_ref):
    count, rows = o_ref.shape[0], x_ref.shape[0]
    slot = pl.program_id(0) * count + lax.broadcasted_iota(jnp.int32, (count, rows), 0)
    hot = jnp.where(slot == place_ref[...], 1.0, 0.0).astype(BF16)
    o_ref[...] = dot(hot, x_ref[...]).astype(BF16)


def pack(place, x, count, sb=512):
    rows, wide = x.shape
    return pl.pallas_call(
        pack_kernel,
        grid=(count // sb,),
        in_specs=[resident((1, rows)), resident((rows, wide))],
        out_specs=pl.BlockSpec((sb, wide), lambda i: (i, 0)),
        out_shape=jax.ShapeDtypeStruct((count, wide), BF16),
        cost_estimate=cost(2 * rows * wide * count, 4 * rows * wide),
        name="pack_rows",
    )(place, x)


def unpacked(place, all_ref):
    slot = lax.broadcasted_iota(jnp.int32, (place.shape[0], all_ref.shape[0]), 1)
    return dot(jnp.where(slot == place, 1.0, 0.0).astype(BF16), all_ref[...])


def front_kernel(*refs, peers, experts, half, heads_count):
    refs = list(refs)

    def take(count):
        taken = refs[:count]
        del refs[:count]
        return taken

    x_hbm, g_hbm, wq_hbm, wk_hbm, wv_hbm, wo_hbm = take(6)
    len_ref, norms_ref, rm_ref, ids_ref = take(4)
    a_hbm, p_hbm, heads_hbm, others_hbm, wo2_hbm = take(5)
    gall_hbm, resid_hbm, f_hbm, chance_hbm, packed_hbm, gin_hbm, info_hbm, lse_ref = take(8)
    xv, wq, wk, wv, wo, wo2, av, pv, vt, hv, ov, gv, pk, fv, rb, cb, hbuf, pa = take(18)
    place_ref, place_g_ref, info = take(3)
    (
        load_sem,
        x_sem,
        a_sem,
        home_sem,
        grad_sem,
        w_sem,
        w_send,
        w_recv,
        head_send,
        head_recv,
        z_send,
        z_recv,
        out_sem,
    ) = refs
    me = lax.axis_index("ep")
    tp_me = lax.axis_index("tp")
    mesh = pl.DeviceIdType.MESH
    across = {"tp": 1 - tp_me}
    rows, wide = xv.shape
    shard = rows // 2
    width = wq.shape[1]
    block = 512
    steps = rows // block

    def rows_at(i, size):
        return pl.ds(pl.multiple_of(i * size, size), size)

    def x_load(i):
        return pltpu.make_async_copy(
            x_hbm.at[rows_at(i, block), :], xv.at[rows_at(i, block), :], x_sem.at[i]
        )

    weight_loads = [
        pltpu.make_async_copy(src, dst, load_sem.at[j])
        for j, (src, dst) in enumerate(((wq_hbm, wq), (wk_hbm, wk), (wv_hbm, wv), (wo_hbm, wo)))
    ]
    for c in weight_loads[:3]:
        c.start()
    for i in range(steps):
        x_load(i).start()
    weight_loads[3].start()
    own_rows = pl.ds(pl.multiple_of(tp_me * shard, shard), shard)
    own_grad = pltpu.make_async_copy(g_hbm, gv.at[own_rows, :], home_sem.at[0])
    own_grad.start()

    barrier = pltpu.get_barrier_semaphore()
    pl.semaphore_signal(barrier, inc=1, device_id=across, device_id_type=mesh)
    for k in range(1, peers):
        pl.semaphore_signal(
            barrier, inc=1, device_id={"ep": jnp.bitwise_xor(me, k)}, device_id_type=mesh
        )
    pl.semaphore_wait(barrier, peers)

    def remote(src, dst, send, recv, to):
        return pltpu.make_async_remote_copy(
            src_ref=src,
            dst_ref=dst,
            send_sem=send,
            recv_sem=recv,
            device_id=to,
            device_id_type=mesh,
        )

    def w_rows(index):
        return wo2.at[rows_at(index, wide // peers), :]

    w_copy = remote(
        wo_hbm.at[rows_at(me, wide // peers), :], w_rows(me), w_sem.at[0], w_sem.at[1], across
    )
    w_copy.start()
    grad_copy = remote(g_hbm, gv.at[own_rows, :], grad_sem.at[0], grad_sem.at[1], across)
    grad_copy.start()

    def w_pass(k):
        return remote(
            w_rows(me), w_rows(me), w_send.at[k], w_recv.at[k], {"ep": jnp.bitwise_xor(me, k)}
        )

    for c in weight_loads[:3]:
        c.wait()

    def a_store(i):
        return [
            pltpu.make_async_copy(
                av.at[rows_at(i, block), :], a_hbm.at[rows_at(i, block), :], a_sem.at[i, 0]
            ),
            pltpu.make_async_copy(
                pv.at[rows_at(i, block), :], p_hbm.at[rows_at(i, block), :], a_sem.at[i, 1]
            ),
        ]

    def project(i):
        at = rows_at(i, block)
        x_load(i).wait()
        normal, _ = normalized(xv[at, :].astype(F32))
        a = (normal * norms_ref[0:1, :] + norms_ref[1:2, :]).astype(BF16)
        av[at, :] = a
        for j, w in enumerate((wq, wk, wv)):
            pv[at, j * width : (j + 1) * width] = dot(a, w[...]).astype(BF16)
        for c in a_store(i):
            c.start()

    pairs = heads_count // 2

    def head_copy(i):
        at = rows_at(i, block)
        return remote(hv.at[at, :], ov.at[at, :], head_send.at[i], head_recv.at[i], across)

    def attend(i, _):
        project(i)
        at = rows_at(i, block)
        for pair in range(pairs):
            cols = [slice(j * width + pair * PAIR, j * width + (pair + 1) * PAIR) for j in range(3)]
            vt[pair, :, at] = pv[at, cols[2]].T
            out, lse = attend_block(
                i,
                pv[at, cols[0]],
                lambda s, cols=cols: pv[s, cols[1]],
                lambda s, pair=pair: vt[pair, :, s],
                block,
                block,
                HEAD_DIM**-0.5,
            )
            hv[at, pair * PAIR : (pair + 1) * PAIR] = out
            for h in range(2):
                lse_ref[pair, h : h + 1, at] = lse[h]
        head_copy(i).start()

        @pl.when(i == 0)
        def _():
            w_copy.wait()
            for k in range(1, peers):
                w_pass(k).start()

        return 0

    def is_live(position):
        count = len_ref.shape[0]
        length = rows // count
        inside = None
        for s in range(count):
            here = (position >= s * length) & (position < s * length + len_ref[s])
            inside = here if inside is None else inside | here
        return inside

    span = 256
    run = jnp.zeros((experts, 1), F32)
    triangle = jnp.where(
        lax.broadcasted_iota(jnp.int32, (span, span), 0)
        < lax.broadcasted_iota(jnp.int32, (span, span), 1),
        1.0,
        0.0,
    ).astype(BF16)
    capacity = 2 * half
    for b in range(rows // span):
        at = slice(b * span, (b + 1) * span)
        ids = ids_ref[:, at]
        live = is_live(b * span + lax.broadcasted_iota(jnp.int32, (1, span), 1))
        hot = (lax.broadcasted_iota(jnp.int32, (experts, span), 0) == ids) & live
        hot = jnp.where(hot, 1.0, 0.0)
        before = dot(hot.astype(BF16), triangle) + run
        run = run + jnp.sum(hot, axis=1, keepdims=True)
        slot = jnp.sum(before * hot, axis=0, keepdims=True).astype(jnp.int32)
        sound = live & (slot < capacity)
        place = jnp.where(sound, ids * capacity + slot, -1)
        inside = slot - tp_me * half
        mine = sound & (inside >= 0) & (inside < half)
        place_g = jnp.where(mine, ids * half + inside, -1)
        place_ref[:, at] = place
        place_g_ref[:, at] = place_g
        line = lax.broadcasted_iota(jnp.int32, (LANES, span), 0)
        both = jnp.where(line == 0, place.astype(F32), place_g.astype(F32))
        info[at, :] = both.T
    info_store = pltpu.make_async_copy(info, info_hbm, home_sem.at[4])
    info_store.start()

    lax.fori_loop(0, steps - 1, attend, 0)

    own_grad.wait()
    grad_copy.wait()

    def mask(i, _):
        at = rows_at(i, block)
        live = is_live(i * block + lax.broadcasted_iota(jnp.int32, (block, wide), 0))
        gv[at, :] = jnp.where(live, gv[at, :], jnp.zeros((block, wide), BF16))
        return 0

    lax.fori_loop(0, steps, mask, 0)
    gall_store = pltpu.make_async_copy(gv, gall_hbm, home_sem.at[1])
    gall_store.start()

    def pack_g(i, _):
        slot = i * block + lax.broadcasted_iota(jnp.int32, (block, rows), 0)
        hot = jnp.where(slot == place_g_ref[...], 1.0, 0.0).astype(BF16)
        pk[rows_at(i, block), :] = dot(hot, gv[...]).astype(BF16)
        return 0

    lax.fori_loop(0, peers * half // block, pack_g, 0)

    def z_copy(k):
        peer = jnp.bitwise_xor(me, k)
        return remote(
            pk.at[rows_at(peer, half), :], gin_hbm.at[me], z_send.at[k], z_recv.at[k], {"ep": peer}
        )

    for k in list(range(peers // 2, peers)) + list(range(1, peers // 2)):
        z_copy(k).start()
    gin_own = pltpu.make_async_copy(pk.at[rows_at(me, half), :], gin_hbm.at[me], home_sem.at[2])
    gin_own.start()
    lax.fori_loop(steps - 1, steps, attend, 0)
    weight_loads[3].wait()
    for k in range(1, peers):
        w_pass(k).wait()
    stores = [
        pltpu.make_async_copy(hv, heads_hbm, out_sem.at[0]),
        pltpu.make_async_copy(wo2, wo2_hbm, out_sem.at[1]),
    ]
    for c in stores:
        c.start()
    small = rb.shape[1]

    def norm_stores(i, slot):
        at = rows_at(i, small)
        return [
            pltpu.make_async_copy(rb.at[slot], resid_hbm.at[at, :], out_sem.at[3 + slot]),
            pltpu.make_async_copy(cb.at[slot], chance_hbm.at[at, :], out_sem.at[5 + slot]),
        ]

    def norm_step(i, _):
        at = rows_at(i, small)
        slot = lax.rem(i, 2)

        @pl.when(slot == 0)
        def _():
            head_copy(i // 2).wait()

        @pl.when(i >= 2)
        def _():
            for c in norm_stores(i - 2, slot):
                c.wait()

        total = dot_nt(hv[at, :], wo[...]) + dot_nt(ov[at, :], wo2[...])
        resid = xv[at, :].astype(F32) + total
        rb[slot] = resid
        normal, _ = normalized(resid)
        f = (normal * norms_ref[2:3, :] + norms_ref[3:4, :]).astype(BF16)
        fv[at, :] = f
        cb[slot] = router_and_mix(dot(f, rm_ref[...]), experts)
        for c in norm_stores(i, slot):
            c.start()
        return 0

    def packed_part(i, first, size):
        at = i * block + lax.broadcasted_iota(jnp.int32, (block, size), 0)
        hot = jnp.where(at == place_ref[:, first : first + size], 1.0, 0.0).astype(BF16)
        return dot(hot, fv[first : first + size, :])

    count = rows // small
    packs = packed_hbm.shape[0] // block
    lax.fori_loop(0, count // 2, norm_step, 0)

    def pack_low(i, _):
        pa[rows_at(i, block), :] = packed_part(i, 0, rows // 2).astype(BF16)
        return 0

    lax.fori_loop(0, packs, pack_low, 0)
    lax.fori_loop(count // 2, count, norm_step, 0)
    stores_late = [
        pltpu.make_async_copy(ov, others_hbm, out_sem.at[2]),
        pltpu.make_async_copy(fv, f_hbm, home_sem.at[3]),
    ]
    for c in stores_late:
        c.start()

    def packed_store(i, slot):
        return pltpu.make_async_copy(
            hbuf.at[slot], packed_hbm.at[rows_at(i, block), :], out_sem.at[7 + slot]
        )

    def pack_high(i, _):
        slot = lax.rem(i, 2)

        @pl.when(i >= 2)
        def _():
            packed_store(i - 2, slot).wait()

        both = packed_part(i, rows // 2, rows // 2) + pa[rows_at(i, block), :].astype(F32)
        hbuf[slot] = both.astype(BF16)
        packed_store(i, slot).start()
        return 0

    lax.fori_loop(0, packs, pack_high, 0)
    for i in range(packs - 2, packs):
        packed_store(i, i % 2).wait()
    for i in range(count - 2, count):
        for c in norm_stores(i, i % 2):
            c.wait()
    for c in [gall_store, gin_own, info_store] + stores + stores_late:
        c.wait()
    for i in range(steps):
        for c in a_store(i):
            c.wait()
    for k in range(1, peers):
        z_copy(k).wait()


def front(x, g, weights, lengths, norms, rm, ids, peers, experts, capacity):
    rows, wide = x.shape
    width = weights[0].shape[1]
    half = capacity // 2
    anywhere = pl.BlockSpec(memory_space=pl.ANY)
    vmem = pl.BlockSpec(memory_space=pltpu.VMEM)

    def like(*shape, kind=BF16):
        return jax.ShapeDtypeStruct(shape, kind)

    return pl.pallas_call(
        partial(
            front_kernel,
            peers=peers,
            experts=experts,
            half=half,
            heads_count=width // HEAD_DIM,
        ),
        in_specs=[anywhere] * 6 + [pl.BlockSpec(memory_space=pltpu.SMEM)] + [vmem] * 3,
        out_specs=[anywhere] * 12 + [vmem],
        out_shape=[
            like(rows, wide),
            like(rows, 3 * width),
            like(rows, width),
            like(rows, width),
            like(wide, width),
            like(rows, wide),
            like(rows, wide, kind=F32),
            like(rows, wide),
            like(rows, LANES, kind=F32),
            like(experts * capacity, wide),
            like(peers, half, wide),
            like(rows, LANES, kind=F32),
            like(width // PAIR, 2, rows, kind=F32),
        ],
        scratch_shapes=[pltpu.VMEM((rows, wide), BF16)]
        + [pltpu.VMEM((wide, width), BF16)] * 5
        + [
            pltpu.VMEM((rows, wide), BF16),
            pltpu.VMEM((rows, 3 * width), BF16),
            pltpu.VMEM((width // PAIR, PAIR, rows), BF16),
            pltpu.VMEM((rows, width), BF16),
            pltpu.VMEM((rows, width), BF16),

            pltpu.VMEM((rows, wide), BF16),
            pltpu.VMEM((peers * half, wide), BF16),
            pltpu.VMEM((rows, wide), BF16),
            pltpu.VMEM((2, 256, wide), F32),
            pltpu.VMEM((2, 256, LANES), F32),
            pltpu.VMEM((2, 512, wide), BF16),
            pltpu.VMEM((experts * capacity, wide), BF16),
            pltpu.VMEM((1, rows), jnp.int32),
            pltpu.VMEM((1, rows), jnp.int32),
            pltpu.VMEM((rows, LANES), F32),
            pltpu.SemaphoreType.DMA((4,)),
            pltpu.SemaphoreType.DMA((rows // 512,)),
            pltpu.SemaphoreType.DMA((rows // 512, 2)),
            pltpu.SemaphoreType.DMA((5,)),
            pltpu.SemaphoreType.DMA((2,)),
            pltpu.SemaphoreType.DMA((2,)),
            pltpu.SemaphoreType.DMA((peers,)),
            pltpu.SemaphoreType.DMA((peers,)),
            pltpu.SemaphoreType.DMA((rows // 512,)),
            pltpu.SemaphoreType.DMA((rows // 512,)),
            pltpu.SemaphoreType.DMA((peers,)),
            pltpu.SemaphoreType.DMA((peers,)),
            pltpu.SemaphoreType.DMA((9,)),
        ],
        cost_estimate=cost(20 * rows * wide * wide, 30 * rows * wide),
        compiler_params=pltpu.CompilerParams(
            vmem_limit_bytes=BIG_VMEM, collective_id=2, has_side_effects=True
        ),
        name="layer_front",
    )(x, g, *weights, lengths, norms, rm, ids)


def nets_kernel(
    x_hbm,
    g_hbm,
    out_hbm,
    gin_hbm,
    sel_ref,
    rm_ref,
    wd1_hbm,
    wd2_hbm,
    we1_hbm,
    we2_hbm,
    y_hbm,
    dx_hbm,
    dot_hbm,
    gd1_hbm,
    gd2_hbm,
    ge1_hbm,
    ge2_hbm,
    in_hbm,
    res_hbm,
    pull_hbm,
    edot_hbm,
    pulls_hbm,
    edots_hbm,
    gin2_hbm,
    wd1,
    wd2,
    we1,
    we2,
    a1,
    a2,
    xb,
    gb,
    yb,
    dxb,
    dotb,
    rowb,
    ya,
    dxa,
    dyb,
    dyt,
    xt,
    w_sem,
    load_sem,
    store_sem,
    grad_sem,
    home_sem,
    local_sem,
    send_sem,
    recv_sem,
    back_send,
    back_recv,
    dot_send,
    dot_recv,
    relay_sem,
    swap_send,
    swap_recv,
    keep,
    give,
    got,
    hv,
    pv,
    *,
    peers,
    capacity,
    rb,
    ft,
    relayed,
):
    experts = peers
    me = lax.axis_index("ep")
    hidden = wd1.shape[1]
    per = rb // capacity
    quarter = peers // 4
    dense_steps = x_hbm.shape[0] // rb
    expert_steps = peers // per

    weight_copies = [
        pltpu.make_async_copy(src, dst, w_sem.at[j])
        for j, (src, dst) in enumerate(
            ((wd1_hbm, wd1), (wd2_hbm, wd2), (we1_hbm, we1), (we2_hbm, we2))
        )
    ]
    weight_copies[0].start()
    weight_copies[1].start()

    def load(t):
        rows = pl.ds(pl.multiple_of(t * rb, rb), rb)
        return [
            pltpu.make_async_copy(x_hbm.at[rows, :], xb, load_sem.at[0, 0]),
            pltpu.make_async_copy(g_hbm.at[rows, :], gb, load_sem.at[1, 0]),
        ]

    for c in load(0):
        c.start()

    barrier = pltpu.get_barrier_semaphore()
    for k in range(1, peers):
        pl.semaphore_signal(
            barrier,
            inc=1,
            device_id={"ep": jnp.bitwise_xor(me, k)},
            device_id_type=pl.DeviceIdType.MESH,
        )
    tp_me = lax.axis_index("tp")
    across = {"tp": 1 - tp_me}
    half = capacity // 2
    if relayed:
        pl.semaphore_signal(
            barrier, inc=1, device_id=across, device_id_type=pl.DeviceIdType.MESH
        )
    pl.semaphore_wait(barrier, peers if relayed else peers - 1)
    relay = pltpu.make_async_remote_copy(
        src_ref=gin_hbm,
        dst_ref=gin2_hbm,
        send_sem=relay_sem.at[0],
        recv_sem=relay_sem.at[1],
        device_id=across,
        device_id_type=pl.DeviceIdType.MESH,
    )
    if relayed:
        relay.start()

    def remote(src, dst, send, recv, k):
        peer = jnp.bitwise_xor(me, k)
        return pltpu.make_async_remote_copy(
            src_ref=src,
            dst_ref=dst,
            send_sem=send.at[k],
            recv_sem=recv.at[k],
            device_id={"ep": peer},
            device_id_type=pl.DeviceIdType.MESH,
        )

    def row_copy(k):
        return remote(
            out_hbm.at[jnp.bitwise_xor(me, k)], in_hbm.at[me], send_sem, recv_sem, k
        )

    def back_copy(k):
        return remote(
            pull_hbm.at[jnp.bitwise_xor(me, k)], pulls_hbm.at[me], back_send, back_recv, k
        )

    def dot_copy(k):
        return remote(
            edot_hbm.at[jnp.bitwise_xor(me, k)], edots_hbm.at[me], dot_send, dot_recv, k
        )

    far = list(range(2 * quarter, peers))
    near = list(range(1, 2 * quarter))
    for k in far[:quarter] + near[quarter - 1 :] + far[quarter:] + near[: quarter - 1]:
        row_copy(k).start()
    own_rows = pltpu.make_async_copy(out_hbm.at[me], in_hbm.at[me], home_sem.at[0])
    own_rows.start()
    weight_copies[2].start()
    weight_copies[3].start()

    def outputs(routed, w1_ref, w2_ref):
        x = xb[...]
        g = gb[...].astype(F32)
        chances = router_and_mix(dot(x, rm_ref[...]), experts)
        if routed:
            gate = jnp.sum(chances * sel_ref[...], axis=-1, keepdims=True)
            dy = g * lane_of(chances, experts + 1) * gate
        else:
            dy = g * lane_of(chances, experts)
        dy = dy.astype(BF16)
        dyb[...] = dy
        dyt[...] = dy.T
        xt[...] = x.T

        def products(f, _):
            cols = pl.ds(pl.multiple_of(f * ft, ft), ft)
            w1 = w1_ref[:, cols]
            w2 = w2_ref[:, cols]
            act, slope = gelu_and_slope(dot(xb[...], w1))
            h = act.astype(BF16)
            pre_grad = (slope * dot(dyb[...], w2)).astype(BF16)
            hv[:, cols] = h
            pv[:, cols] = pre_grad
            ya[...] += dot_nt(h, w2)
            dxa[...] += dot_nt(pre_grad, w1)
            return 0

        ya[...] = jnp.zeros_like(ya)
        dxa[...] = jnp.zeros_like(dxa)
        lax.fori_loop(0, hidden // ft, products, 0)

    def row_dots():
        return jnp.sum(ya[...] * gb[...].astype(F32), axis=1, keepdims=True)

    def gradients(first, last=None):
        wide_step = ft

        def at(f):
            return pl.ds(pl.multiple_of(f * wide_step, wide_step), wide_step)

        def put(f, _):
            a2[:, at(f)] = dot(dyt[...], hv[:, at(f)])
            a1[:, at(f)] = dot(xt[...], pv[:, at(f)])
            return 0

        def add(f, _):
            a2[:, at(f)] += dot(dyt[...], hv[:, at(f)])
            a1[:, at(f)] += dot(xt[...], pv[:, at(f)])
            return 0

        def round_off(f, _):
            wd2[:, at(f)] = (a2[:, at(f)] + dot(dyt[...], hv[:, at(f)])).astype(BF16)
            wd1[:, at(f)] = (a1[:, at(f)] + dot(xt[...], pv[:, at(f)])).astype(BF16)
            return 0

        @pl.when(first)
        def _():
            lax.fori_loop(0, hidden // wide_step, put, 0)

        if last is None:
            middle = jnp.logical_not(first)
        else:
            middle = jnp.logical_not(first | last)

            @pl.when(last)
            def _():
                lax.fori_loop(0, hidden // wide_step, round_off, 0)

        @pl.when(middle)
        def _():
            lax.fori_loop(0, hidden // wide_step, add, 0)

    weight_copies[0].wait()
    weight_copies[1].wait()

    def dense_stores(t, slot):
        rows = pl.ds(pl.multiple_of(t * rb, rb), rb)
        return [
            pltpu.make_async_copy(yb, y_hbm.at[rows, :], store_sem.at[slot, 0, 0]),
            pltpu.make_async_copy(dxb, dx_hbm.at[rows, :], store_sem.at[slot, 1, 0]),
            pltpu.make_async_copy(dotb.at[slot], dot_hbm.at[rows, :], store_sem.at[slot, 2, 0]),
        ]

    def dense_step(t, _):
        slot = lax.rem(t, 2)
        for c in load(t):
            c.wait()
        outputs(False, wd1, wd2)

        @pl.when(t >= 1)
        def _():
            for c in dense_stores(t - 1, 1 - slot):
                c.wait()

        yb[...] = ya[...].astype(BF16)
        dxb[...] = dxa[...].astype(BF16)
        dotb[slot] = jnp.broadcast_to(row_dots(), (rb, LANES))

        @pl.when(t + 1 < dense_steps)
        def _():
            for c in load(t + 1):
                c.start()

        for c in dense_stores(t, slot):
            c.start()
        gradients(t == 0, t == dense_steps - 1)
        return 0

    lax.fori_loop(0, dense_steps, dense_step, 0)
    for c in dense_stores(dense_steps - 1, (dense_steps - 1) % 2):
        c.wait()

    dense_grads = [
        pltpu.make_async_copy(wd1, gd1_hbm, grad_sem.at[0]),
        pltpu.make_async_copy(wd2, gd2_hbm, grad_sem.at[1]),
    ]
    for c in dense_grads:
        c.start()
    weight_copies[2].wait()
    weight_copies[3].wait()
    own_rows.wait()
    if relayed:
        relay.wait()

    def first_of(p):
        if expert_steps != 4:
            return (expert_steps - 1 - p) * per
        return jnp.where(p == 0, 2, jnp.where(p == 1, 1, jnp.where(p == 2, 3, 0))) * per

    def swap_copy(p, j):
        slot = lax.rem(p, 2)
        return pltpu.make_async_remote_copy(
            src_ref=give.at[slot, j],
            dst_ref=got.at[slot, j],
            send_sem=swap_send.at[slot, j],
            recv_sem=swap_recv.at[slot, j],
            device_id=across,
            device_id_type=pl.DeviceIdType.MESH,
        )

    size = half if relayed else capacity

    def back_stores(p, j, source_ref):
        to = (pull_hbm, res_hbm)[j]
        return [
            pltpu.make_async_copy(
                source_ref.at[pl.ds(c * size, size), :],
                to.at[jnp.bitwise_xor(me, first_of(p) + c)],
                store_sem.at[0, j, c],
            )
            for c in range(per)
        ]

    def dot_stores(p):
        return [
            pltpu.make_async_copy(
                rowb.at[c], edot_hbm.at[jnp.bitwise_xor(me, first_of(p) + c)], store_sem.at[1, 2, c]
            )
            for c in range(per)
        ]

    def to_peers(p, copy):
        for c in range(per):
            k = first_of(p) + c

            @pl.when(k > 0)
            def _(k=k):
                copy(k).start()

    def sum_shares(p, j):
        swap_copy(p, j).wait()
        stage = (dxb, yb)[j]
        stage[: per * half, :] = (keep[j] + got[lax.rem(p, 2), j].astype(F32)).astype(BF16)
        for c in back_stores(p, j, stage):
            c.start()

    def stored(p, j, source_ref):
        for c in back_stores(p, j, source_ref):
            c.wait()

    def fetch(p):
        for c in range(per):
            k = first_of(p) + c

            @pl.when(k > 0)
            def _(k=k):
                row_copy(k).wait()

        for c in fetches(p):
            c.start()

    def fetches(p):
        loads = []
        for c in range(per):
            source = jnp.bitwise_xor(me, first_of(p) + c)
            rows = pl.ds(c * capacity, capacity)
            loads.append(
                pltpu.make_async_copy(in_hbm.at[source], xb.at[rows, :], load_sem.at[0, c])
            )
            if relayed:
                for j, src, which in ((1, gin_hbm, tp_me), (2, gin2_hbm, 1 - tp_me)):
                    at = pl.ds(pl.multiple_of(c * capacity + which * half, half), half)
                    loads.append(
                        pltpu.make_async_copy(
                            src.at[source], gb.at[at, :], load_sem.at[j, c]
                        )
                    )
            else:
                loads.append(
                    pltpu.make_async_copy(
                        gin_hbm.at[source], gb.at[rows, :], load_sem.at[1, c]
                    )
                )
        return loads

    fetch(0)

    def expert_step(p, _):
        slot = lax.rem(p, 2)
        for c in fetches(p):
            c.wait()
        outputs(True, we1, we2)
        across_dots = jnp.broadcast_to(row_dots(), (rb, LANES)).T
        for c in range(per):
            rowb[c] = across_dots[:8, c * capacity : (c + 1) * capacity]
        for c in dot_stores(p):
            c.start()
        if relayed:

            @pl.when(p > 0)
            def _():
                for j in range(2):
                    sum_shares(p - 1, j)

            for j, total in ((0, dxa), (1, ya)):
                for c in range(per):
                    rows = slice(c * half, (c + 1) * half)
                    at = pl.ds(pl.multiple_of(c * capacity + tp_me * half, half), half)
                    other = pl.ds(pl.multiple_of(c * capacity + (1 - tp_me) * half, half), half)
                    keep[j, rows, :] = total[at, :]
                    give[slot, j, rows, :] = total[other, :].astype(BF16)
                swap_copy(p, j).start()
        else:
            dxb[...] = dxa[...].astype(BF16)
            yb[...] = ya[...].astype(BF16)
            for j, source_ref in ((0, dxb), (1, yb)):
                for c in back_stores(p, j, source_ref):
                    c.start()

        @pl.when(p + 1 < expert_steps)
        def _():
            fetch(p + 1)

        gradients(p == 0)
        for c in dot_stores(p):
            c.wait()
        to_peers(p, dot_copy)
        if relayed:

            @pl.when(p > 0)
            def _():
                for j in range(2):
                    stored(p - 1, j, (dxb, yb)[j])
                to_peers(p - 1, back_copy)
        else:
            for j, source_ref in ((0, dxb), (1, yb)):
                stored(p, j, source_ref)
            to_peers(p, back_copy)
        return 0

    lax.fori_loop(0, expert_steps, expert_step, 0)
    expert_grads = [
        pltpu.make_async_copy(a1, ge1_hbm, local_sem.at[0]),
        pltpu.make_async_copy(a2, ge2_hbm, local_sem.at[1]),
        pltpu.make_async_copy(edot_hbm.at[me], edots_hbm.at[me], home_sem.at[2]),
    ]
    for c in expert_grads:
        c.start()
    if relayed:
        final = expert_steps - 1
        sum_shares(final, 0)
        stored(final, 0, dxb)
        to_peers(final, back_copy)
        sum_shares(final, 1)
        stored(final, 1, yb)
    own_back = pltpu.make_async_copy(pull_hbm.at[me], pulls_hbm.at[me], home_sem.at[1])
    own_back.start()
    for c in dense_grads + expert_grads + [own_back]:
        c.wait()
    for k in range(1, peers):
        back_copy(k).wait()
        dot_copy(k).wait()


def nets(x, g, out_rows, in_grads, sel, rm, dense_weights, expert_weights, rb=512, ft=512):
    rows, wide = x.shape
    hidden = dense_weights[0].shape[1]
    peers, capacity, _ = out_rows.shape
    per = rb // capacity
    anywhere = pl.BlockSpec(memory_space=pl.ANY)
    vmem = pl.BlockSpec(memory_space=pltpu.VMEM)
    sheet = jax.ShapeDtypeStruct((rows, wide), BF16)
    relayed = in_grads.shape[1] < capacity
    blocks = jax.ShapeDtypeStruct((peers, capacity, wide), BF16)
    backs = jax.ShapeDtypeStruct(in_grads.shape, BF16)
    part = (rb * in_grads.shape[1] // capacity, wide) if relayed else (16, wide)
    strips = jax.ShapeDtypeStruct((peers, 8, capacity), F32)
    return pl.pallas_call(
        partial(nets_kernel, peers=peers, capacity=capacity, rb=rb, ft=ft, relayed=relayed),
        in_specs=[anywhere] * 4 + [vmem] * 2 + [anywhere] * 4,
        out_specs=[anywhere] * 14,
        out_shape=[
            sheet,
            sheet,
            jax.ShapeDtypeStruct((rows, LANES), F32),
            jax.ShapeDtypeStruct((wide, hidden), BF16),
            jax.ShapeDtypeStruct((wide, hidden), BF16),
            jax.ShapeDtypeStruct((wide, hidden), F32),
            jax.ShapeDtypeStruct((wide, hidden), F32),
            blocks,
            backs,
            backs,
            strips,
            backs,
            strips,
            backs,
        ],
        scratch_shapes=[pltpu.VMEM((wide, hidden), BF16)] * 4
        + [pltpu.VMEM((wide, hidden), F32)] * 2
        + [pltpu.VMEM((rb, wide), BF16)] * 4
        + [
            pltpu.VMEM((2, rb, LANES), F32),
            pltpu.VMEM((per, 8, capacity), F32),
            pltpu.VMEM((rb, wide), F32),
            pltpu.VMEM((rb, wide), F32),
            pltpu.VMEM((rb, wide), BF16),
            pltpu.VMEM((wide, rb), BF16),
            pltpu.VMEM((wide, rb), BF16),
            pltpu.SemaphoreType.DMA((4,)),
            pltpu.SemaphoreType.DMA((3, per)),
            pltpu.SemaphoreType.DMA((2, 3, per)),
            pltpu.SemaphoreType.DMA((2,)),
            pltpu.SemaphoreType.DMA((3,)),
            pltpu.SemaphoreType.DMA((2,)),
        ]
        + [pltpu.SemaphoreType.DMA((peers,))] * 6
        + [
            pltpu.SemaphoreType.DMA((2,)),
            pltpu.SemaphoreType.DMA((2, 2)),
            pltpu.SemaphoreType.DMA((2, 2)),
            pltpu.VMEM((2, *part), F32),
            pltpu.VMEM((2, 2, *part), BF16),
            pltpu.VMEM((2, 2, *part), BF16),
            pltpu.VMEM((rb, hidden), BF16),
            pltpu.VMEM((rb, hidden), BF16),
        ],
        cost_estimate=cost(24 * rows * wide * hidden, 16 * rows * wide + 24 * wide * hidden),
        compiler_params=pltpu.CompilerParams(
            vmem_limit_bytes=67043328, collective_id=0, has_side_effects=True
        ),
        name="feed_forward_nets",
    )(x, g, out_rows, in_grads, sel, rm, *dense_weights, *expert_weights)


def expert_hot(place, capacity, experts):
    lane = lax.broadcasted_iota(jnp.int32, (place.shape[0], LANES), 1)
    low = lane * capacity
    return ((place >= low) & (place < low + capacity) & (lane < experts)).astype(F32)


def ffn_pull_kernel(*refs, parts, experts, capacity, shard, sent):
    (
        info_ref,
        dx_ref,
        chance_ref,
        first_ref,
        f_ref,
        g_ref,
        resid_ref,
        gain_ref,
        rm_ref,
        slot_ref,
        dots_ref,
    ) = refs[:11]
    weights = refs[11 : 11 + parts]
    r_ref = refs[11 + parts]
    heads = list(refs[12 + parts : 12 + 2 * parts])
    sums_ref, rmg_ref = refs[12 + 2 * parts : 14 + 2 * parts]
    size = info_ref.shape[0]
    step = pl.program_id(0)
    if sent is not None:
        give, send_sem, recv_sem = refs[14 + 2 * parts :]
        got = heads[sent]
        across = {"tp": 1 - lax.axis_index("tp")}
        mesh = pl.DeviceIdType.MESH

        def share(b):
            at = pl.ds(pl.multiple_of(b * size, size), size)
            return pltpu.make_async_remote_copy(
                src_ref=give.at[at, :],
                dst_ref=got.at[at, :],
                send_sem=send_sem.at[b],
                recv_sem=recv_sem.at[b],
                device_id=across,
                device_id_type=mesh,
            )

        @pl.when(step == 0)
        def _():
            barrier = pltpu.get_barrier_semaphore()
            pl.semaphore_signal(barrier, inc=1, device_id=across, device_id_type=mesh)
            pl.semaphore_wait(barrier, 1)

    place = info_ref[:, 0:1].astype(jnp.int32)
    here = info_ref[:, 1:2].astype(jnp.int32)
    row = step * size + lax.broadcasted_iota(jnp.int32, (size, 1), 0)
    row = row - lax.axis_index("tp") * shard
    own = ((row >= 0) & (row < shard)).astype(F32)
    chances = chance_ref[...]
    hot = expert_hot(place, capacity, experts)
    gate = jnp.sum(hot * chances, axis=-1, keepdims=True)
    mix_0, mix_1 = lane_of(chances, experts), lane_of(chances, experts + 1)
    table = jnp.dot(
        hot, dots_ref[...], precision=lax.Precision.HIGHEST, preferred_element_type=F32
    )
    slot = lax.broadcasted_iota(jnp.int32, table.shape, 1)
    number = jnp.sum(hot * lax.broadcasted_iota(jnp.int32, hot.shape, 1).astype(F32), axis=-1)
    inside = place - number.astype(jnp.int32)[:, None] * capacity
    second = jnp.sum(jnp.where(slot == inside, table, 0.0), axis=-1, keepdims=True)
    first = lane_of(first_ref[...], 0)
    grad_0, grad_1 = first, gate * second
    inner = mix_0 * grad_0 + mix_1 * grad_1
    lane = lax.broadcasted_iota(jnp.int32, chances.shape, 1)
    low = (mix_1 * second * gate) * (hot - chances)
    low = jnp.where(lane == experts, mix_0 * (grad_0 - inner), low)
    low = jnp.where(lane == experts + 1, mix_1 * (grad_1 - inner), low)
    low = jnp.where(lane > experts + 1, 0.0, low).astype(BF16)
    grad = dx_ref[...].astype(F32) + unpacked(here, slot_ref) + dot_nt(low, rm_ref[...])
    normal, rstd = normalized(resid_ref[...])
    r = norm_pull(grad, normal, rstd, gain_ref[2:3, :]) + own * g_ref[...].astype(F32)
    r = r.astype(BF16)
    r_ref[...] = r
    if sent is not None:
        at = pl.ds(pl.multiple_of(step * size, size), size)
        give[at, :] = dot(r, weights[sent][...]).astype(BF16)
        share(step).start()
    for j, (h, w) in enumerate(zip(heads, weights)):
        if j != sent:
            h[...] = dot(r, w[...]).astype(BF16)

    @pl.when(pl.program_id(0) == 0)
    def _():
        sums_ref[...] = jnp.zeros_like(sums_ref)
        rmg_ref[...] = jnp.zeros_like(rmg_ref)

    sums_ref[0:1, :] += jnp.sum(grad * normal, axis=0, keepdims=True)
    sums_ref[1:2, :] += jnp.sum(grad, axis=0, keepdims=True)
    rmg_ref[...] += dot(low.T, f_ref[...])
    if sent is not None:

        @pl.when(step == pl.num_programs(0) - 1)
        def _():
            for b in range(give.shape[0] // size):
                share(b).wait()


def ffn_pull(
    info,
    dx,
    chances,
    first,
    f,
    g,
    resid,
    gain,
    rm,
    slot_rows,
    dots,
    weights,
    experts,
    shard,
    sent=None,
    rb=256,
):
    rows, wide = dx.shape
    capacity = dots.shape[1]
    dots = jnp.pad(dots, ((0, LANES - experts), (0, 0)))
    block = pl.BlockSpec((rb, wide), lambda i: (i, 0))
    narrow = pl.BlockSpec((rb, LANES), lambda i: (i, 0))
    head_specs = [
        pl.BlockSpec(memory_space=pl.ANY) if j == sent else pl.BlockSpec((rb, size), lambda i: (i, 0))
        for j, (_, _, size) in enumerate(weights)
    ]
    scratch, extra = [], {}
    if sent is not None:
        scratch = [
            pltpu.VMEM((rows, weights[sent][2]), BF16),
            pltpu.SemaphoreType.DMA((rows // rb,)),
            pltpu.SemaphoreType.DMA((rows // rb,)),
        ]
        extra = dict(collective_id=3, has_side_effects=True)
    return pl.pallas_call(
        partial(
            ffn_pull_kernel,
            parts=len(weights),
            experts=experts,
            capacity=capacity,
            shard=shard,
            sent=sent,
        ),
        grid=(rows // rb,),
        in_specs=[narrow, block, narrow, narrow, block, block, block]
        + [resident(gain.shape), resident((wide, LANES))]
        + [resident(slot_rows.shape), resident(dots.shape)]
        + [
            pl.BlockSpec((wide, size), lambda i, j=j: (0, j), pipeline_mode=pl.Buffered(1))
            for _, j, size in weights
        ],
        out_specs=[block] + head_specs + [resident((8, wide)), resident((LANES, wide))],
        out_shape=[jax.ShapeDtypeStruct((rows, wide), BF16)]
        + [jax.ShapeDtypeStruct((rows, size), BF16) for _, _, size in weights]
        + [jax.ShapeDtypeStruct((8, wide), F32), jax.ShapeDtypeStruct((LANES, wide), F32)],
        scratch_shapes=scratch,
        cost_estimate=cost(6 * rows * wide * wide, 16 * rows * wide),
        compiler_params=pltpu.CompilerParams(vmem_limit_bytes=48 * 1024 * 1024, **extra),
        name="ffn_norm_pull",
    )(
        info,
        dx,
        chances,
        first,
        f,
        g,
        resid,
        gain,
        rm,
        slot_rows,
        dots,
        *[w for w, _, _ in weights],
    )


def outer_kernel(left_ref, *refs, parts):
    rights = refs[:parts]
    o_ref, acc_ref = refs[parts:]

    @pl.when(pl.program_id(0) == 0)
    def _():
        acc_ref[...] = jnp.zeros_like(acc_ref)

    left = left_ref[...].T
    at = 0
    for r in rights:
        width = r.shape[1]
        acc_ref[:, at : at + width] += dot(left, r[...])
        at += width

    @pl.when(pl.program_id(0) == pl.num_programs(0) - 1)
    def _():
        o_ref[...] = acc_ref[...].astype(BF16)


def outer(left, rights, rb=512):
    rows, wide = left.shape
    total = sum(r.shape[1] for r in rights)
    return pl.pallas_call(
        partial(outer_kernel, parts=len(rights)),
        grid=(rows // rb,),
        in_specs=[pl.BlockSpec((rb, wide), lambda i: (i, 0))]
        + [pl.BlockSpec((rb, r.shape[1]), lambda i: (i, 0)) for r in rights],
        out_specs=resident((wide, total)),
        out_shape=jax.ShapeDtypeStruct((wide, total), BF16),
        scratch_shapes=[pltpu.VMEM((wide, total), F32)],
        cost_estimate=cost(2 * rows * wide * total, 2 * rows * (wide + total)),
        name="outer_product",
    )(left, *rights)


def attn_pull_kernel(at_ref, x_ref, r_ref, gain_ref, *refs, groups):
    grads = refs[: 3 * groups]
    weights = refs[3 * groups : 3 * groups + 3]
    t_ref, sums_ref = refs[3 * groups + 3 :]
    del at_ref
    total = None
    for k in range(3):
        at = 0
        for j in range(groups):
            d = grads[k * groups + j]
            width = d.shape[1]
            part = dot_nt(d[...], weights[k][:, at : at + width])
            total = part if total is None else total + part
            at += width
    normal, rstd = normalized(x_ref[...].astype(F32))
    t = norm_pull(total, normal, rstd, gain_ref[...]) + r_ref[...].astype(F32)
    t_ref[...] = t.astype(t_ref.dtype)

    @pl.when(pl.program_id(0) == 0)
    def _():
        sums_ref[...] = jnp.zeros_like(sums_ref)

    sums_ref[0:1, :] += jnp.sum(total * normal, axis=0, keepdims=True)
    sums_ref[1:2, :] += jnp.sum(total, axis=0, keepdims=True)


def attn_pull(first_row, count, x, r, gain, grads, weights, out_type, rb=256):
    wide = x.shape[1]
    groups = len(grads) // 3

    def rows(width):
        return pl.BlockSpec((rb, width), lambda i, at: (at[0] + i, 0))

    return pl.pallas_call(
        partial(attn_pull_kernel, groups=groups),
        grid_spec=pltpu.PrefetchScalarGridSpec(
            num_scalar_prefetch=1,
            grid=(count // rb,),
            in_specs=[rows(wide), rows(wide), resident((1, wide))]
            + [rows(d.shape[1]) for d in grads]
            + [resident(w.shape) for w in weights],
            out_specs=[pl.BlockSpec((rb, wide), lambda i, at: (i, 0)), resident((8, wide))],
        ),
        out_shape=[
            jax.ShapeDtypeStruct((count, wide), out_type),
            jax.ShapeDtypeStruct((8, wide), F32),
        ],
        cost_estimate=cost(6 * count * wide * weights[0].shape[1], 10 * count * wide),
        name="attention_norm_pull",
    )((first_row // rb).astype(jnp.int32).reshape(1), x, r, gain, *grads, *weights)


def combine_kernel(info_ref, y_ref, chance_ref, slot_ref, o_ref, *, experts, capacity):
    place = info_ref[:, 0:1].astype(jnp.int32)
    here = info_ref[:, 1:2].astype(jnp.int32)
    chances = chance_ref[...]
    gate = jnp.sum(expert_hot(place, capacity, experts) * chances, axis=-1, keepdims=True)
    moe = unpacked(here, slot_ref) * (lane_of(chances, experts + 1) * gate)
    o_ref[...] = (lane_of(chances, experts) * y_ref[...].astype(F32) + moe).astype(BF16)


def combine(info, y, coef, slot_rows, experts, capacity, rb=256):
    rows, wide = y.shape
    block = pl.BlockSpec((rb, wide), lambda i: (i, 0))
    return pl.pallas_call(
        partial(combine_kernel, experts=experts, capacity=capacity),
        grid=(rows // rb,),
        in_specs=[
            pl.BlockSpec((rb, LANES), lambda i: (i, 0)),
            block,
            pl.BlockSpec((rb, LANES), lambda i: (i, 0)),
        ]
        + [resident(slot_rows.shape)],
        out_specs=block,
        out_shape=jax.ShapeDtypeStruct((rows, wide), BF16),
        cost_estimate=cost(4 * rows * wide * wide, 8 * rows * wide),
        name="combine_nets",
    )(info, y, coef, slot_rows)


class Halving:
    def __init__(self, total, gives, gots, send, recv, me, size, order):
        self.total, self.gives, self.gots = total, gives, gots
        self.send, self.recv, self.me, self.size = send, recv, me, size
        self.order = order
        self.rows = total.shape[0] // size

    def block(self, index):
        return pl.ds(pl.multiple_of(index * self.rows, self.rows), self.rows)

    def copy(self, s):
        return pltpu.make_async_remote_copy(
            src_ref=self.gives[s],
            dst_ref=self.gots[s],
            send_sem=self.send.at[s],
            recv_sem=self.recv.at[s],
            device_id={"ep": jnp.bitwise_xor(self.me, 1 << self.order[s])},
            device_id_type=pl.DeviceIdType.MESH,
        )

    def halves(self, s):
        place = sum(1 for b in self.order[s:] if b < self.order[s])
        low = (1 << place) - 1
        return [((i >> place) << (place + 1) | (i & low)) for i in range(self.size >> (s + 1))], 1 << place

    def bit(self, s):
        return lax.rem(lax.div(self.me, 1 << self.order[s]), 2)

    def start(self, s):
        places, step = self.halves(s)
        for i, at in enumerate(places):
            rows = slice(i * self.rows, (i + 1) * self.rows)
            self.gives[s][rows, :] = self.total[self.block(at + (1 - self.bit(s)) * step), :].astype(BF16)
        self.copy(s).start()

    def finish(self, s):
        self.copy(s).wait()
        places, step = self.halves(s)
        for i, at in enumerate(places):
            rows = slice(i * self.rows, (i + 1) * self.rows)
            kept = self.total[self.block(at + self.bit(s) * step), :]
            self.total[rows, :] = kept + self.gots[s][rows, :].astype(F32)

    def step(self, s):
        self.finish(s)
        if s + 1 < len(self.order):
            self.start(s + 1)


def tail_kernel(*refs, groups, size, rb, small_rows):
    refs = list(refs)

    def take(count):
        taken = refs[:count]
        del refs[:count]
        return taken

    x_hbm, r_hbm, a_hbm, out_hbm = take(4)
    grads_hbm = take(3 * groups)
    small_ref, gain_ref = take(2)
    weights = take(3)
    own_hbm, got_hbm, square_ref, outsum_ref, total_ref = take(5)
    xv, rv, av = take(3)
    grads = take(3 * groups)
    gov, acc_a, acc_b, goacc, give_rows, own_buf = take(6)
    steps = size.bit_length() - 1
    hops = steps + 1
    gives, gots = take(steps), take(steps)
    gives_b, gots_b = take(steps), take(steps)
    go_gives, go_gots = take(steps), take(steps)
    small_gives, small_gots = take(hops), take(hops)
    (
        load_sem,
        own_sem,
        row_send,
        row_recv,
        half_send,
        half_recv,
        half_send_b,
        half_recv_b,
        go_send,
        go_recv,
        small_send,
        small_recv,
        out_sem,
        out_give,
        out_got,
    ) = refs
    me = lax.axis_index("ep")
    tp_me = lax.axis_index("tp")
    rows = x_hbm.shape[0]
    shard = rows // 2
    count = shard // rb

    out_load = pltpu.make_async_copy(out_hbm, gov, load_sem.at[0, 0])
    a_load = pltpu.make_async_copy(a_hbm, av, load_sem.at[1, 0])

    def loads(which, line):
        at = pl.ds(pl.multiple_of(which * shard, shard), shard)
        return [
            pltpu.make_async_copy(
                src.at[at, :], dst.at[at, :], load_sem.at[line, j + 1]
            )
            for j, (src, dst) in enumerate(zip([x_hbm, r_hbm, *grads_hbm], [xv, rv, *grads]))
        ]

    theirs_loads, own_loads = loads(1 - tp_me, 0), loads(tp_me, 1)
    for c in theirs_loads:
        c.start()
    out_load.start()
    for c in own_loads:
        c.start()
    a_load.start()

    barrier = pltpu.get_barrier_semaphore()
    mesh = pl.DeviceIdType.MESH
    pl.semaphore_signal(barrier, inc=1, device_id={"tp": 1 - tp_me}, device_id_type=mesh)
    for s in range(steps):
        pl.semaphore_signal(
            barrier, inc=1, device_id={"ep": jnp.bitwise_xor(me, 1 << s)}, device_id_type=mesh
        )
    pl.semaphore_wait(barrier, hops)

    order = list(range(steps))
    other_order = [0, 2, 1] + order[3:] if steps > 2 else order
    qkv = [
        Halving(acc_a, gives, gots, half_send, half_recv, me, size, order),
        Halving(acc_b, gives_b, gots_b, half_send_b, half_recv_b, me, size, other_order),
    ]
    go = Halving(goacc, go_gives, go_gots, go_send, go_recv, me, size, order)

    for c in theirs_loads:
        c.wait()

    total_ref[:small_rows, :] = small_ref[...]
    total_ref[small_rows:, :] = jnp.zeros_like(total_ref[small_rows:, :])

    def pulled(at):
        total = None
        for k in range(3):
            col = 0
            for j in range(groups):
                d = grads[k * groups + j][at, :]
                width = d.shape[1]
                part = dot_nt(d, weights[k][:, col : col + width])
                total = part if total is None else total + part
                col += width
        normal, rstd = normalized(xv[at, :].astype(F32))
        total_ref[small_rows : small_rows + 1, :] += jnp.sum(total * normal, axis=0, keepdims=True)
        total_ref[small_rows + 1 : small_rows + 2, :] += jnp.sum(total, axis=0, keepdims=True)
        return norm_pull(total, normal, rstd, gain_ref[0:1, :]) + rv[at, :].astype(F32)

    def row_copy(b):
        at = pl.ds(pl.multiple_of(b * rb, rb), rb)
        return pltpu.make_async_remote_copy(
            src_ref=give_rows.at[at, :],
            dst_ref=got_hbm.at[at, :],
            send_sem=row_send.at[b],
            recv_sem=row_recv.at[b],
            device_id={"tp": 1 - tp_me},
            device_id_type=mesh,
        )

    def theirs(b, _):
        at = pl.ds(pl.multiple_of((1 - tp_me) * shard + b * rb, rb), rb)
        give_rows[pl.ds(pl.multiple_of(b * rb, rb), rb), :] = pulled(at).astype(BF16)
        row_copy(b).start()
        return 0

    lax.fori_loop(0, count // 2, theirs, 0)
    out_load.wait()
    goacc[...] = gov[...].astype(F32)
    go.start(0)
    for c in own_loads + [a_load]:
        c.wait()
    cut = len(grads) // 2
    for acc in (acc_a, acc_b):
        acc[...] = jnp.zeros_like(acc)

    def outer_step(b, _):
        at = pl.ds(pl.multiple_of(b * 512, 512), 512)
        left = av[at, :].T
        for acc, some in ((acc_a, grads[:cut]), (acc_b, grads[cut:])):
            col = 0
            for g in some:
                width = g.shape[1]
                acc[:, col : col + width] += dot(left, g[at, :])
                col += width
        return 0

    lax.fori_loop(0, rows // 512, outer_step, 0)
    for chain in qkv:
        chain.start(0)
    go.step(0)
    lax.fori_loop(count // 2, count, theirs, 0)

    def own_copy(b):
        at = pl.ds(pl.multiple_of(b * rb, rb), rb)
        return pltpu.make_async_copy(own_buf.at[at, :], own_hbm.at[at, :], own_sem.at[b])

    def own_step(b, _):
        at = pl.ds(pl.multiple_of(tp_me * shard + b * rb, rb), rb)
        own_buf[pl.ds(pl.multiple_of(b * rb, rb), rb), :] = pulled(at)
        own_copy(b).start()
        return 0

    for chain in qkv:
        chain.step(0)
    lax.fori_loop(0, count // 2, own_step, 0)
    go.step(1)
    lax.fori_loop(count // 2, count, own_step, 0)

    def small_copy(s):
        peer = {"tp": 1 - tp_me} if s == 0 else {"ep": jnp.bitwise_xor(me, 1 << (s - 1))}
        return pltpu.make_async_remote_copy(
            src_ref=small_gives[s],
            dst_ref=small_gots[s],
            send_sem=small_send.at[s],
            recv_sem=small_recv.at[s],
            device_id=peer,
            device_id_type=mesh,
        )

    for s in range(hops):
        small_gives[s][...] = total_ref[...]
        small_copy(s).start()
        if s + 2 < steps:
            go.step(s + 2)
        if 0 < s < steps:
            for chain in qkv:
                chain.step(s)
        small_copy(s).wait()
        total_ref[...] += small_gots[s][...]
        if s == max(0, steps - 3):
            own_width = outsum_ref.shape[1]
            out_give[...] = goacc[: goacc.shape[0] // size, own_width:].astype(BF16)
            out_copy = pltpu.make_async_remote_copy(
                src_ref=out_give,
                dst_ref=out_got,
                send_sem=out_sem.at[0],
                recv_sem=out_sem.at[1],
                device_id={"tp": 1 - tp_me},
                device_id_type=mesh,
            )
            out_copy.start()
    col = 0
    for acc in (acc_a, acc_b):
        square_ref[:, col : col + acc.shape[1]] = acc[: acc.shape[0] // size, :]
        col += acc.shape[1]
    out_copy.wait()
    outsum_ref[...] = goacc[: goacc.shape[0] // size, :own_width] + out_got[...].astype(F32)
    for b in range(count):
        own_copy(b).wait()
        row_copy(b).wait()


def tail(x, r, a, out_part, grads, small, gain, weights, size, rb=256):
    rows, wide = x.shape
    shard = rows // 2
    groups = len(grads) // 3
    total = sum(g.shape[1] for g in grads)
    out_width = out_part.shape[1]
    small_rows = small.shape[0]
    steps = size.bit_length() - 1
    kept = wide // size
    anywhere = pl.BlockSpec(memory_space=pl.ANY)
    vmem = pl.BlockSpec(memory_space=pltpu.VMEM)

    def halves(width):
        return [pltpu.VMEM((wide >> (s + 1), width), BF16) for s in range(steps)]

    return pl.pallas_call(
        partial(tail_kernel, groups=groups, size=size, rb=rb, small_rows=small_rows),
        in_specs=[anywhere] * (4 + 3 * groups) + [vmem] * 5,
        out_specs=[anywhere, anywhere, vmem, vmem, vmem],
        out_shape=[
            jax.ShapeDtypeStruct((shard, wide), F32),
            jax.ShapeDtypeStruct((shard, wide), BF16),
            jax.ShapeDtypeStruct((kept, total), F32),
            jax.ShapeDtypeStruct((kept, out_width // 2), F32),
            jax.ShapeDtypeStruct((small_rows + 8, wide), F32),
        ],
        scratch_shapes=[pltpu.VMEM((rows, wide), BF16)] * 3
        + [pltpu.VMEM(g.shape, BF16) for g in grads]
        + [
            pltpu.VMEM((wide, out_width), BF16),
            pltpu.VMEM((wide, total // 2), F32),
            pltpu.VMEM((wide, total // 2), F32),
            pltpu.VMEM((wide, out_width), F32),
            pltpu.VMEM((shard, wide), BF16),
            pltpu.VMEM((shard, wide), F32),
        ]
        + halves(total // 2) * 4
        + halves(out_width) * 2
        + [pltpu.VMEM((small_rows + 8, wide), F32)] * (2 * (steps + 1))
        + [
            pltpu.SemaphoreType.DMA((2, 3 + 3 * groups)),
            pltpu.SemaphoreType.DMA((shard // rb,)),
            pltpu.SemaphoreType.DMA((shard // rb,)),
            pltpu.SemaphoreType.DMA((shard // rb,)),
        ]
        + [pltpu.SemaphoreType.DMA((steps,))] * 6
        + [pltpu.SemaphoreType.DMA((steps + 1,))] * 2
        + [
            pltpu.SemaphoreType.DMA((2,)),
            pltpu.VMEM((kept, out_width // 2), BF16),
            pltpu.VMEM((kept, out_width // 2), BF16),
        ],
        cost_estimate=cost(12 * rows * wide * total // 3, 16 * rows * wide),
        compiler_params=pltpu.CompilerParams(
            vmem_limit_bytes=BIG_VMEM, collective_id=1, has_side_effects=True
        ),
        name="backward_tail",
    )(x, r, a, out_part, *grads, small, gain, *weights)


def results_kernel(
    own_ref,
    got_ref,
    square_ref,
    small_ref,
    h_ref,
    r_ref,
    token_ref,
    q_ref,
    k_ref,
    v_ref,
    gh_ref,
    gr_ref,
    router_ref,
    mix_ref,
    gain1_ref,
    bias1_ref,
    gain2_ref,
    bias2_ref,
):
    token_ref[...] = own_ref[...] + got_ref[...].astype(F32)

    @pl.when(pl.program_id(0) == 0)
    def _():
        width = q_ref.shape[1]
        for j, ref in enumerate((q_ref, k_ref, v_ref)):
            ref[...] = square_ref[:, j * width : (j + 1) * width]
        gh_ref[...] = h_ref[...].astype(F32)
        gr_ref[...] = r_ref[...].astype(F32)
        experts = router_ref.shape[0]
        router_ref[...] = small_ref[8 : 8 + experts, :]
        mix_ref[...] = small_ref[8 + experts : 10 + experts, :]
        end = small_ref.shape[0] - 8
        for ref, at in ((gain1_ref, end), (bias1_ref, end + 1), (gain2_ref, 0), (bias2_ref, 1)):
            ref[...] = small_ref[at : at + 1, :]


def results(own, got, square, small, gh, gr, experts, rb=256):
    rows, wide = own.shape
    kept, width = square.shape[0], square.shape[1] // 3
    block = pl.BlockSpec((rb, wide), lambda i: (i, 0))
    shapes = [(kept, width)] * 3 + [gh.shape, gr.shape, (experts, wide), (2, wide)] + [(1, wide)] * 4
    return pl.pallas_call(
        results_kernel,
        grid=(rows // rb,),
        in_specs=[block, block] + [resident(v.shape) for v in (square, small, gh, gr)],
        out_specs=[block] + [resident(s) for s in shapes],
        out_shape=[jax.ShapeDtypeStruct((rows, wide), F32)]
        + [jax.ShapeDtypeStruct(s, F32) for s in shapes],
        cost_estimate=cost(rows * wide, 12 * rows * wide),
        name="results",
    )(own, got, square, small, gh, gr)


def on_device(
    sizes,
    tokens,
    out_grad,
    lengths,
    expert_ids,
    w_query,
    w_key,
    w_value,
    w_output,
    w_hidden,
    w_return,
    router,
    mix_weight,
    gain_attn,
    bias_attn,
    gain_ffn,
    bias_ffn,
    expert_in,
    expert_out,
):
    tp, ep = sizes
    shard_rows = out_grad.shape[0]
    all_rows = tokens.shape[0]
    model_width = tokens.shape[1]
    experts = router.shape[1]
    capacity = all_rows // experts
    seq_count = lengths.shape[0]
    seq_len = all_rows // seq_count
    local_width = w_query.shape[1]
    local_heads = local_width // HEAD_DIM
    pairs = local_heads // 2
    splits = 2 if pairs % 2 == 0 else 1
    each = pairs // splits
    tp_index = lax.axis_index("tp")
    ep_index = lax.axis_index("ep")
    first_row = tp_index * shard_rows
    swap = [(0, 1), (1, 0)]

    def shard_of(values, axis=0):
        return lax.dynamic_slice_in_dim(values, first_row, shard_rows, axis)

    def swapped(values):
        return lax.ppermute(values, "tp", swap)

    def exchange(values):
        return lax.all_to_all(values, "ep", split_axis=0, concat_axis=0, tiled=True)

    def after(values, *others):
        return lax.optimization_barrier((values, others))[0]

    def summed_over(values, axis, size):
        step = 1
        while step < size:
            values = values + lax.ppermute(values, axis, [(i, i ^ step) for i in range(size)])
            step *= 2
        return values

    def over_sequences(values):
        return lax.psum_scatter(values, "ep", scatter_dimension=0, tiled=True)

    positions = jnp.arange(all_rows)
    seq_index = positions // seq_len
    row_limit = jnp.sum(
        jnp.where(seq_index[:, None] == jnp.arange(seq_count)[None, :], lengths[None, :], 0), axis=1
    )
    live_all = positions % seq_len < row_limit
    slot_count = experts * capacity
    blocks = (experts, capacity, model_width)

    rm = jnp.pad(
        jnp.concatenate([router, mix_weight], axis=1), ((0, 0), (0, LANES - experts - 2))
    )
    norms = jnp.stack([gain_attn, bias_attn, gain_ffn, bias_ffn]).astype(F32)
    projections = (w_query, w_key, w_value)
    if tp == 2:
        (
            attn_in,
            projected,
            heads,
            others,
            w_other,
            grad_all,
            resid,
            ffn_in,
            chances,
            packed,
            grad_rows,
            info,
            lse,
        ) = front(
            tokens,
            out_grad,
            (*projections, w_output),
            lengths,
            norms,
            rm,
            expert_ids[None, :],
            ep,
            experts,
            capacity,
        )
        all_heads = [heads, others]
        wide_weights = [(w, s, each * PAIR) for w in (w_output, w_other) for s in range(splits)]
    else:
        one_hot = (expert_ids[:, None] == jnp.arange(experts)[None, :]) & live_all[:, None]
        routed = one_hot.astype(F32)
        slots = jnp.sum((jnp.cumsum(routed, axis=0) - routed) * routed, axis=1).astype(jnp.int32)
        sound = live_all & (slots < capacity)
        place = jnp.where(sound, expert_ids * capacity + slots, -1)
        place_row = place[None, :]
        info = jnp.broadcast_to(place[:, None], (all_rows, LANES)).astype(F32)
        live_grad = jnp.where(shard_of(live_all)[:, None], out_grad, jnp.zeros_like(out_grad))
        w_all = lax.all_gather(w_output, "tp", axis=1, tiled=True)
        grad_all = lax.all_gather(live_grad, "tp", axis=0, tiled=True)
        grad_rows = exchange(pack(place_row, grad_all, slot_count).reshape(blocks))
        attn_in, projected = norm_project(tokens, norms[0:1], norms[1:2], projections)
        heads, lse = attention_forward(projected, seq_count, local_heads, 0, pairs)
        all_heads = [lax.all_gather(heads, "tp", axis=1, tiled=True)]
        wide_weights = [(w_all, 0, model_width)]
        resid, ffn_in, chances = output_norm(
            tokens, norms[2:3], norms[3:4], rm, all_heads, [(w_all, 0)], experts
        )
        packed = pack(place_row, ffn_in, slot_count)

    sel = (jnp.arange(LANES) == ep_index).astype(F32)[None, :]
    (
        dense,
        dense_pull,
        first_dot,
        grad_hidden,
        grad_return,
        grad_expert_in,
        grad_expert_out,
        _,
        sums_back,
        _,
        _,
        pulls,
        dots,
        _,
    ) = nets(
        ffn_in,
        grad_all,
        packed.reshape(blocks),
        grad_rows,
        sel,
        rm,
        (w_hidden, w_return),
        (expert_in[0], expert_out[0]),
    )
    returned = exchange(sums_back).reshape(-1, model_width)
    pulls = pulls.reshape(-1, model_width)
    dots = dots[:, 0, :]
    part, *rest = ffn_pull(
        info,
        dense_pull,
        chances,
        first_dot,
        ffn_in,
        grad_all,
        resid,
        norms,
        rm,
        pulls,
        dots,
        wide_weights,
        experts,
        shard_rows,
        sent=splits if tp == 2 else None,
    )
    *head_parts, ffn_sums, rm_sums = rest
    if tp == 2:
        head_grads = [
            [m, o if s == 0 else swapped(o)]
            for s, (m, o) in enumerate(zip(head_parts[:splits], head_parts[splits:]))
        ]
    else:
        local = lax.psum_scatter(head_parts[0], "tp", scatter_dimension=1, tiled=True)
        head_grads = [
            [local[:, s * each * PAIR : (s + 1) * each * PAIR]] for s in range(splits)
        ]
    out_part = outer(part, all_heads)
    part = after(part, out_part)
    grad_hidden = over_sequences(grad_hidden)
    grad_return = over_sequences(grad_return)

    qkv = []
    expert_grads = [grad_expert_in, grad_expert_out]
    for s in range(splits):
        if s == splits - 1:
            if qkv:
                dense, qkv[-1], head_grads[s], out_part = lax.optimization_barrier(
                    (dense, qkv[-1], head_grads[s], out_part)
                )
            weighted = combine(info, dense, chances, returned, experts, capacity)
            projected, weighted = lax.optimization_barrier((projected, weighted))
        *grads3, expert_grads[s] = attention_backward(
            projected,
            heads,
            head_grads[s],
            lse,
            seq_count,
            local_heads,
            s * each,
            each,
            (expert_grads[s],),
        )
        qkv.append(grads3)
    flat = [qkv[s][k] for k in range(3) for s in range(splits)]
    rows_kept = -(-(experts + 2) // 8) * 8
    small = jnp.concatenate([ffn_sums, rm_sums[:rows_kept]], axis=0)
    theirs = lax.dynamic_slice_in_dim(weighted, shard_rows - first_row, shard_rows, 0)
    if tp == 2:
        summed = shard_of(weighted).astype(F32) + swapped(theirs).astype(F32)
        block_out = jnp.where(shard_of(live_all)[:, None], shard_of(resid) + summed, 0.0).astype(BF16)
        part, block_out = lax.optimization_barrier((part, block_out))
        own_part, got, square, grad_output, small = tail(
            tokens,
            part,
            attn_in,
            out_part,
            flat,
            small,
            norms,
            projections,
            ep,
        )
        (
            token_grad,
            grad_query,
            grad_key,
            grad_value,
            grad_hidden,
            grad_return,
            grad_router,
            grad_mix,
            *vectors,
        ) = results(own_part, got, square, small, grad_hidden, grad_return, experts)
        vectors = [v[0] for v in vectors]
    else:
        whole, attn_sums = attn_pull(
            jnp.zeros((), jnp.int32), all_rows, tokens, part, norms[0:1], flat, projections, BF16
        )
        token_grad = lax.psum_scatter(whole, "tp", scatter_dimension=0, tiled=True).astype(F32)
        summed = lax.psum_scatter(weighted, "tp", scatter_dimension=0, tiled=True).astype(F32)
        block_out = jnp.where(shard_of(live_all)[:, None], shard_of(resid) + summed, 0.0).astype(BF16)
        square = over_sequences(outer(attn_in, flat))
        grad_output = lax.psum_scatter(
            over_sequences(out_part).astype(BF16), "tp", scatter_dimension=1, tiled=True
        ).astype(F32)
        small = summed_over(summed_over(small, "tp", tp), "ep", ep)
        attn_sums = summed_over(summed_over(attn_sums, "tp", tp), "ep", ep)
        grad_query, grad_key, grad_value = jnp.split(square.astype(F32), 3, axis=1)
        grad_hidden, grad_return = grad_hidden.astype(F32), grad_return.astype(F32)
        grad_router, grad_mix = small[8 : 8 + experts], small[8 + experts : 10 + experts]
        vectors = [attn_sums[0], attn_sums[1], small[0], small[1]]
    return (
        block_out,
        token_grad,
        grad_query,
        grad_key,
        grad_value,
        grad_output,
        grad_hidden,
        grad_return,
        grad_router.T,
        grad_mix.T,
        *vectors,
        expert_grads[0][None],
        expert_grads[1][None],
    )


def solution(mesh):
    in_specs = (
        P("ep", None),
        P(("ep", "tp"), None),
        P("ep"),
        P("ep"),
        P(None, "tp"),
        P(None, "tp"),
        P(None, "tp"),
        P(None, "tp"),
        P(None, "tp"),
        P(None, "tp"),
        P(),
        P(),
        P(),
        P(),
        P(),
        P(),
        P("ep", None, "tp"),
        P("ep", None, "tp"),
    )
    out_specs = (
        P(("ep", "tp"), None),
        P(("ep", "tp"), None),
        P("ep", "tp"),
        P("ep", "tp"),
        P("ep", "tp"),
        P("ep", "tp"),
        P("ep", "tp"),
        P("ep", "tp"),
        P(),
        P(),
        P(),
        P(),
        P(),
        P(),
        P("ep", None, "tp"),
        P("ep", None, "tp"),
    )
    return jax.shard_map(
        partial(on_device, (mesh.shape["tp"], mesh.shape["ep"])),
        mesh=mesh,
        in_specs=in_specs,
        out_specs=out_specs,
        check_vma=False,
    )
```

```python
import math
from functools import partial

import jax
import jax.numpy as jnp
from jax import lax
from jax.experimental import pallas as pl
from jax.experimental.pallas import tpu as pltpu
from jax.sharding import PartitionSpec as P

HEAD_DIM = 64
PAIR = 2 * HEAD_DIM


EPS = 1e-05
NEG = -1e30
F32 = jnp.float32
BF16 = jnp.bfloat16
NT = (((1,), (1,)), ((), ()))


LANES = 128
GELU_C = math.sqrt(2.0 / math.pi)
GELU_A = 0.044715
BIG_VMEM = 62 * 1024 * 1024


def dot(left, right):
    return jnp.dot(left, right, preferred_element_type=F32)


def dot_nt(left, right):
    return lax.dot_general(left, right, NT, preferred_element_type=F32)


def normalized(values):
    middle = jnp.mean(values, axis=-1, keepdims=True)
    centred = values - middle
    rstd = lax.rsqrt(jnp.mean(centred * centred, axis=-1, keepdims=True) + EPS)
    return centred * rstd, rstd


def norm_pull(grad, normal, rstd, gain):
    q = grad * gain
    along = jnp.mean(q * normal, axis=-1, keepdims=True)
    return rstd * (q - jnp.mean(q, axis=-1, keepdims=True) - normal * along)


def gelu_and_slope(v):
    square = v * v
    t = jnp.tanh(v * (GELU_C + (GELU_C * GELU_A) * square))
    half = 0.5 + 0.5 * t
    slope = half + v * (0.5 - 0.5 * (t * t)) * (GELU_C + (3.0 * GELU_C * GELU_A) * square)
    return v * half, slope


def router_and_mix(logits, experts):
    lane = lax.broadcasted_iota(jnp.int32, logits.shape, 1)
    out = jnp.zeros_like(logits)
    for low, high in ((0, experts), (experts, experts + 2)):
        inside = (lane >= low) & (lane < high)
        top = jnp.max(jnp.where(inside, logits, NEG), axis=-1, keepdims=True)
        e = jnp.where(inside, jnp.exp(jnp.where(inside, logits - top, 0.0)), 0.0)
        out = out + e / jnp.sum(e, axis=-1, keepdims=True)
    return out


def lane_of(values, index):
    lane = lax.broadcasted_iota(jnp.int32, values.shape, 1)
    return jnp.sum(jnp.where(lane == index, values, 0.0), axis=-1, keepdims=True)


def resident(shape):
    return pl.BlockSpec(shape, lambda i, *_: (0,) * len(shape), pipeline_mode=pl.Buffered(1))


def cost(flops, bytes_accessed):
    return pl.CostEstimate(flops=flops // 64, bytes_accessed=bytes_accessed // 64, transcendentals=0)


def attend_block(qi, q, keys, values_t, bq, bk, scale):
    lane = lax.broadcasted_iota(jnp.int32, (bq, PAIR), 1)
    q = q * jnp.asarray(scale, BF16)
    zero = jnp.zeros_like(q)
    halves = [jnp.where(lane < HEAD_DIM, q, zero), jnp.where(lane < HEAD_DIM, zero, q)]

    def step(j, carry, masked):
        off = pl.multiple_of(j * bk, bk)
        k = keys(pl.ds(off, bk))
        vt = values_t(pl.ds(off, bk))
        scores = [lax.dot_general(k, half, NT, preferred_element_type=F32) for half in halves]
        if masked:
            key_pos = off + lax.broadcasted_iota(jnp.int32, (bk, bq), 0)
            query_pos = qi * bq + lax.broadcasted_iota(jnp.int32, (bk, bq), 1)
            allowed = key_pos <= query_pos
            scores = [jnp.where(allowed, s, NEG) for s in scores]
        new = []
        for h in range(2):
            m, l, acc = carry[h]
            m_new = jnp.maximum(m, jnp.max(scores[h], axis=0, keepdims=True))
            alpha = jnp.exp(m - m_new)
            p = jnp.exp(scores[h] - m_new)
            l = l * alpha + jnp.sum(p, axis=0, keepdims=True)
            part = dot(vt[h * HEAD_DIM : (h + 1) * HEAD_DIM], p.astype(BF16))
            new.append((m_new, l, acc * alpha + part))
        return tuple(new)

    init = tuple(
        (jnp.full((1, bq), NEG, F32), jnp.zeros((1, bq), F32), jnp.zeros((HEAD_DIM, bq), F32))
        for _ in range(2)
    )
    full = qi * (bq // bk)
    carry = lax.fori_loop(0, full, lambda j, c: step(j, c, False), init)
    for d in range(bq // bk):
        carry = step(full + d, carry, True)
    out = jnp.concatenate([acc / l for _, l, acc in carry], axis=0).T.astype(BF16)
    return out, [m + jnp.log(l) for m, l, _ in carry]


def attention_forward_kernel(q_ref, k_ref, v_ref, o_ref, lse_ref, vt_ref, *, bq, bk, scale):
    qi = pl.program_id(2)

    @pl.when(qi == 0)
    def _():
        vt_ref[...] = v_ref[...].T

    out, lse = attend_block(
        qi, q_ref[...], lambda s: k_ref[s, :], lambda s: vt_ref[:, s], bq, bk, scale
    )
    o_ref[...] = out
    for h in range(2):
        lse_ref[0, h : h + 1, :] = lse[h]


def attention_forward(proj, seqs, heads, first, count, bq=512, bk=512):
    rows = proj.shape[0]
    length = rows // seqs
    pairs = heads // 2
    nq = length // bq
    flops = 2 * rows * length * count * PAIR
    return pl.pallas_call(
        partial(attention_forward_kernel, bq=bq, bk=bk, scale=HEAD_DIM**-0.5),
        grid=(seqs, count, nq),
        in_specs=[
            pl.BlockSpec((bq, PAIR), lambda s, p, i: (s * nq + i, first + p)),
            pl.BlockSpec((length, PAIR), lambda s, p, i: (s, pairs + first + p)),
            pl.BlockSpec((length, PAIR), lambda s, p, i: (s, 2 * pairs + first + p)),
        ],
        out_specs=[
            pl.BlockSpec((bq, PAIR), lambda s, p, i: (s * nq + i, p)),
            pl.BlockSpec((1, 2, bq), lambda s, p, i: (p, 0, s * nq + i)),
        ],
        out_shape=[
            jax.ShapeDtypeStruct((rows, count * PAIR), BF16),
            jax.ShapeDtypeStruct((count, 2, rows), F32),
        ],
        scratch_shapes=[pltpu.VMEM((PAIR, length), BF16)],
        cost_estimate=cost(flops * 4, 8 * rows * count * PAIR),
        name="attention_forward",
    )(proj, proj, proj)


def attention_backward_kernel(
    q_ref,
    k_ref,
    v_ref,
    o_ref,
    lse_ref,
    *refs,
    terms,
    carried,
    bq,
    bk,
    scale,
    length,
):
    lane = lax.broadcasted_iota(jnp.int32, (length, PAIR), 1)
    first = lane < HEAD_DIM
    q = q_ref[...] * jnp.asarray(scale, BF16)
    do_refs = refs[:terms]
    refs = refs[terms:]
    if carried:
        from_hbm, dq_ref, dk_ref, dv_ref, to_hbm, *refs, held, carry_sem = refs
        way_in = pltpu.make_async_copy(from_hbm, held, carry_sem.at[0])
        way_out = pltpu.make_async_copy(held, to_hbm, carry_sem.at[1])
        at = pl.program_id(0) * pl.num_programs(1) + pl.program_id(1)
        final = pl.num_programs(0) * pl.num_programs(1) - 1

        @pl.when(at == 0)
        def _():
            way_in.start()

        @pl.when(at == final)
        def _():
            way_in.wait()
            way_out.start()

    else:
        dq_ref, dk_ref, dv_ref, *refs = refs
    dqt_ref, qs_ref, dos_ref, kt_ref, dl_ref = refs
    do = do_refs[0][...]
    if terms == 2:
        do = (do.astype(F32) + do_refs[1][...].astype(F32)).astype(BF16)
    zero = jnp.zeros_like(q)
    qs_ref[0] = jnp.where(first, q, zero)
    qs_ref[1] = jnp.where(first, zero, q)
    dos_ref[0] = jnp.where(first, do, zero)
    dos_ref[1] = jnp.where(first, zero, do)
    kt_ref[...] = (k_ref[...] * jnp.asarray(scale, BF16)).T
    prod = (do.astype(F32) * o_ref[...].astype(F32)).T
    dl_ref[0:1, :] = jnp.sum(prod[:HEAD_DIM], axis=0, keepdims=True)
    dl_ref[1:2, :] = jnp.sum(prod[HEAD_DIM:], axis=0, keepdims=True)
    dqt_ref[...] = jnp.zeros_like(dqt_ref)
    nq = length // bq
    nk = length // bk

    def key_block(j, _):
        koff = pl.multiple_of(j * bk, bk)
        k = k_ref[pl.ds(koff, bk), :]
        v = v_ref[pl.ds(koff, bk), :]
        kt = kt_ref[:, pl.ds(koff, bk)]

        def tile(qoff, wide, tall, masked):
            qoff = pl.multiple_of(qoff, wide)
            cols = pl.ds(qoff, wide)
            if masked:
                key_pos = koff + lax.broadcasted_iota(jnp.int32, (tall, wide), 0)
                query_pos = qoff + lax.broadcasted_iota(jnp.int32, (tall, wide), 1)
                allowed = key_pos <= query_pos
            qh = [qs_ref[h, cols, :] for h in range(2)]
            dh = [dos_ref[h, cols, :] for h in range(2)]
            scores = [lax.dot_general(k[:tall], x, NT, preferred_element_type=F32) for x in qh]
            pulls = [lax.dot_general(v[:tall], x, NT, preferred_element_type=F32) for x in dh]
            dk, dv, dqs = 0.0, 0.0, []
            for h in range(2):
                p = jnp.exp(scores[h] - lse_ref[0, h : h + 1, cols])
                if masked:
                    p = jnp.where(allowed, p, 0.0)
                ds = (p * (pulls[h] - dl_ref[h : h + 1, cols])).astype(BF16)
                dv = dv + dot(p.astype(BF16), dh[h])
                dk = dk + dot(ds, qh[h])
                dqs.append(dot(kt[h * HEAD_DIM : (h + 1) * HEAD_DIM, :tall], ds))
            dqt_ref[:, cols] += jnp.concatenate(dqs, axis=0)
            return dk, dv

        def step(i, carry):
            dk, dv = tile(i * bq, bq, bk, False)
            return carry[0] + dk, carry[1] + dv

        half = bk // 2
        dk, dv = tile(koff + half, half, bk, True)
        dk_0, dv_0 = tile(koff, half, half, True)
        rest = jnp.zeros((bk - half, PAIR), F32)
        carry = (
            dk + jnp.concatenate([dk_0, rest], axis=0),
            dv + jnp.concatenate([dv_0, rest], axis=0),
        )
        i0 = j * (bk // bq)
        dk, dv = lax.fori_loop(i0 + bk // bq, nq, step, carry)
        dk_ref[pl.ds(koff, bk), :] = dk.astype(BF16)
        dv_ref[pl.ds(koff, bk), :] = dv.astype(BF16)
        return 0

    lax.fori_loop(0, nk, key_block, 0)
    dq_ref[...] = dqt_ref[...].T.astype(BF16)
    if carried:

        @pl.when(at == final)
        def _():
            way_out.wait()


def attention_backward(proj, out, out_grads, lse, seqs, heads, first, count, carry=(), bq=512, bk=512):
    rows = out.shape[0]
    length = rows // seqs
    pairs = heads // 2
    width = count * PAIR

    def block(off):
        return pl.BlockSpec((length, PAIR), lambda s, p: (s, off + p))

    grad = jax.ShapeDtypeStruct((rows, width), BF16)
    terms = len(out_grads)
    return pl.pallas_call(
        partial(
            attention_backward_kernel,
            terms=terms,
            carried=bool(carry),
            bq=bq,
            bk=bk,
            scale=HEAD_DIM**-0.5,
            length=length,
        ),
        grid=(seqs, count),
        in_specs=[
            block(first),
            block(pairs + first),
            block(2 * pairs + first),
            block(first),
            pl.BlockSpec((1, 2, length), lambda s, p: (first + p, 0, s)),
        ]
        + [block(0)] * terms
        + [pl.BlockSpec(memory_space=pl.ANY) for _ in carry],
        out_specs=[block(0)] * 3 + [pl.BlockSpec(memory_space=pl.ANY) for _ in carry],
        out_shape=[grad] * 3 + [jax.ShapeDtypeStruct(c.shape, c.dtype) for c in carry],
        scratch_shapes=[
            pltpu.VMEM((PAIR, length), F32),
            pltpu.VMEM((2, length, PAIR), BF16),
            pltpu.VMEM((2, length, PAIR), BF16),
            pltpu.VMEM((PAIR, length), BF16),
            pltpu.VMEM((2, length), F32),
        ]
        + [s for c in carry for s in (pltpu.VMEM(c.shape, c.dtype), pltpu.SemaphoreType.DMA((2,)))],
        cost_estimate=cost(20 * rows * length * width, 16 * rows * width),
        compiler_params=pltpu.CompilerParams(vmem_limit_bytes=52 * 1024 * 1024),
        name="attention_backward",
    )(proj, proj, proj, out, lse, *out_grads, *carry)


def norm_project_kernel(x_ref, gain_ref, bias_ref, wq_ref, wk_ref, wv_ref, a_ref, p_ref):
    normal, _ = normalized(x_ref[...].astype(F32))
    a = (normal * gain_ref[...] + bias_ref[...]).astype(BF16)
    a_ref[...] = a
    width = wq_ref.shape[1]
    for j, w in enumerate((wq_ref, wk_ref, wv_ref)):
        p_ref[:, j * width : (j + 1) * width] = dot(a, w[...]).astype(BF16)


def norm_project(x, gain, bias, weights, rb=512):
    rows, wide = x.shape
    width = weights[0].shape[1]
    return pl.pallas_call(
        norm_project_kernel,
        grid=(rows // rb,),
        in_specs=[pl.BlockSpec((rb, wide), lambda i: (i, 0)), resident((1, wide)), resident((1, wide))]
        + [resident((wide, width))] * 3,
        out_specs=[
            pl.BlockSpec((rb, wide), lambda i: (i, 0)),
            pl.BlockSpec((rb, 3 * width), lambda i: (i, 0)),
        ],
        out_shape=[
            jax.ShapeDtypeStruct((rows, wide), BF16),
            jax.ShapeDtypeStruct((rows, 3 * width), BF16),
        ],
        cost_estimate=cost(6 * rows * wide * width, 8 * rows * wide),
        name="norm_project",
    )(x, gain, bias, *weights)


def output_norm_kernel(*refs, parts, experts):
    x_ref, gain_ref, bias_ref, rm_ref = refs[:4]
    heads = refs[4 : 4 + parts]
    weights = refs[4 + parts : 4 + 2 * parts]
    resid_ref, f_ref, chance_ref = refs[4 + 2 * parts :]
    total = dot_nt(heads[0][...], weights[0][...])
    for h, w in zip(heads[1:], weights[1:]):
        total = total + dot_nt(h[...], w[...])
    resid = x_ref[...].astype(F32) + total
    resid_ref[...] = resid
    normal, _ = normalized(resid)
    f = (normal * gain_ref[...] + bias_ref[...]).astype(BF16)
    f_ref[...] = f
    chance_ref[...] = router_and_mix(dot(f, rm_ref[...]), experts)


def output_norm(x, gain, bias, rm, heads, weights, experts, rb=256):
    rows, wide = x.shape
    block = pl.BlockSpec((rb, wide), lambda i: (i, 0))
    weight_specs = [
        pl.BlockSpec(
            (wide, h.shape[1]), lambda i, j=j: (0, j), pipeline_mode=pl.Buffered(1)
        )
        for h, (_, j) in zip(heads, weights)
    ]
    return pl.pallas_call(
        partial(output_norm_kernel, parts=len(heads), experts=experts),
        grid=(rows // rb,),
        in_specs=[block, resident((1, wide)), resident((1, wide)), resident((wide, LANES))]
        + [pl.BlockSpec((rb, h.shape[1]), lambda i: (i, 0)) for h in heads]
        + weight_specs,
        out_specs=[block, block, pl.BlockSpec((rb, LANES), lambda i: (i, 0))],
        out_shape=[
            jax.ShapeDtypeStruct((rows, wide), F32),
            jax.ShapeDtypeStruct((rows, wide), BF16),
            jax.ShapeDtypeStruct((rows, LANES), F32),
        ],
        cost_estimate=cost(2 * rows * wide * wide, 12 * rows * wide),
        name="output_norm",
    )(x, gain, bias, rm, *heads, *[w for w, _ in weights])


def pack_kernel(place_ref, x_ref, o_ref):
    count, rows = o_ref.shape[0], x_ref.shape[0]
    slot = pl.program_id(0) * count + lax.broadcasted_iota(jnp.int32, (count, rows), 0)
    hot = jnp.where(slot == place_ref[...], 1.0, 0.0).astype(BF16)
    o_ref[...] = dot(hot, x_ref[...]).astype(BF16)


def pack(place, x, count, sb=512):
    rows, wide = x.shape
    return pl.pallas_call(
        pack_kernel,
        grid=(count // sb,),
        in_specs=[resident((1, rows)), resident((rows, wide))],
        out_specs=pl.BlockSpec((sb, wide), lambda i: (i, 0)),
        out_shape=jax.ShapeDtypeStruct((count, wide), BF16),
        cost_estimate=cost(2 * rows * wide * count, 4 * rows * wide),
        name="pack_rows",
    )(place, x)


def unpacked(place, all_ref):
    slot = lax.broadcasted_iota(jnp.int32, (place.shape[0], all_ref.shape[0]), 1)
    return dot(jnp.where(slot == place, 1.0, 0.0).astype(BF16), all_ref[...])


def front_kernel(*refs, peers, experts, half, heads_count):
    refs = list(refs)

    def take(count):
        taken = refs[:count]
        del refs[:count]
        return taken

    x_hbm, g_hbm, wq_hbm, wk_hbm, wv_hbm, wo_hbm = take(6)
    len_ref, norms_ref, rm_ref, ids_ref = take(4)
    a_hbm, p_hbm, heads_hbm, others_hbm, wo2_hbm = take(5)
    gall_hbm, resid_hbm, f_hbm, chance_hbm, packed_hbm, gin_hbm, info_hbm, lse_ref = take(8)
    xv, wq, wk, wv, wo, wo2, av, pv, vt, hv, ov, gv, pk, fv, rb, cb, hbuf, pa = take(18)
    place_ref, place_g_ref, info = take(3)
    (
        load_sem,
        x_sem,
        a_sem,
        home_sem,
        grad_sem,
        w_sem,
        w_send,
        w_recv,
        head_send,
        head_recv,
        z_send,
        z_recv,
        out_sem,
    ) = refs
    me = lax.axis_index("ep")
    tp_me = lax.axis_index("tp")
    mesh = pl.DeviceIdType.MESH
    across = {"tp": 1 - tp_me}
    rows, wide = xv.shape
    shard = rows // 2
    width = wq.shape[1]
    block = 512
    steps = rows // block

    def rows_at(i, size):
        return pl.ds(pl.multiple_of(i * size, size), size)

    def x_load(i):
        return pltpu.make_async_copy(
            x_hbm.at[rows_at(i, block), :], xv.at[rows_at(i, block), :], x_sem.at[i]
        )

    weight_loads = [
        pltpu.make_async_copy(src, dst, load_sem.at[j])
        for j, (src, dst) in enumerate(((wq_hbm, wq), (wk_hbm, wk), (wv_hbm, wv), (wo_hbm, wo)))
    ]
    for c in weight_loads[:3]:
        c.start()
    for i in range(steps):
        x_load(i).start()
    weight_loads[3].start()
    own_rows = pl.ds(pl.multiple_of(tp_me * shard, shard), shard)
    own_grad = pltpu.make_async_copy(g_hbm, gv.at[own_rows, :], home_sem.at[0])
    own_grad.start()

    barrier = pltpu.get_barrier_semaphore()
    pl.semaphore_signal(barrier, inc=1, device_id=across, device_id_type=mesh)
    for k in range(1, peers):
        pl.semaphore_signal(
            barrier, inc=1, device_id={"ep": jnp.bitwise_xor(me, k)}, device_id_type=mesh
        )
    pl.semaphore_wait(barrier, peers)

    def remote(src, dst, send, recv, to):
        return pltpu.make_async_remote_copy(
            src_ref=src,
            dst_ref=dst,
            send_sem=send,
            recv_sem=recv,
            device_id=to,
            device_id_type=mesh,
        )

    def w_rows(index):
        return wo2.at[rows_at(index, wide // peers), :]

    w_copy = remote(
        wo_hbm.at[rows_at(me, wide // peers), :], w_rows(me), w_sem.at[0], w_sem.at[1], across
    )
    w_copy.start()
    grad_copy = remote(g_hbm, gv.at[own_rows, :], grad_sem.at[0], grad_sem.at[1], across)
    grad_copy.start()

    def w_pass(k):
        return remote(
            w_rows(me), w_rows(me), w_send.at[k], w_recv.at[k], {"ep": jnp.bitwise_xor(me, k)}
        )

    for c in weight_loads[:3]:
        c.wait()

    def a_store(i):
        return [
            pltpu.make_async_copy(
                av.at[rows_at(i, block), :], a_hbm.at[rows_at(i, block), :], a_sem.at[i, 0]
            ),
            pltpu.make_async_copy(
                pv.at[rows_at(i, block), :], p_hbm.at[rows_at(i, block), :], a_sem.at[i, 1]
            ),
        ]

    def project(i):
        at = rows_at(i, block)
        x_load(i).wait()
        normal, _ = normalized(xv[at, :].astype(F32))
        a = (normal * norms_ref[0:1, :] + norms_ref[1:2, :]).astype(BF16)
        av[at, :] = a
        for j, w in enumerate((wq, wk, wv)):
            pv[at, j * width : (j + 1) * width] = dot(a, w[...]).astype(BF16)
        for c in a_store(i):
            c.start()

    pairs = heads_count // 2

    def head_copy(i):
        at = rows_at(i, block)
        return remote(hv.at[at, :], ov.at[at, :], head_send.at[i], head_recv.at[i], across)

    def is_live(position):
        count = len_ref.shape[0]
        length = rows // count
        inside = None
        for s in range(count):
            here = (position >= s * length) & (position < s * length + len_ref[s])
            inside = here if inside is None else inside | here
        return inside

    span = 256
    run = jnp.zeros((experts, 1), F32)
    triangle = jnp.where(
        lax.broadcasted_iota(jnp.int32, (span, span), 0)
        < lax.broadcasted_iota(jnp.int32, (span, span), 1),
        1.0,
        0.0,
    ).astype(BF16)
    capacity = 2 * half
    for b in range(rows // span):
        at = slice(b * span, (b + 1) * span)
        ids = ids_ref[:, at]
        live = is_live(b * span + lax.broadcasted_iota(jnp.int32, (1, span), 1))
        hot = (lax.broadcasted_iota(jnp.int32, (experts, span), 0) == ids) & live
        hot = jnp.where(hot, 1.0, 0.0)
        before = dot(hot.astype(BF16), triangle) + run
        run = run + jnp.sum(hot, axis=1, keepdims=True)
        slot = jnp.sum(before * hot, axis=0, keepdims=True).astype(jnp.int32)
        sound = live & (slot < capacity)
        place = jnp.where(sound, ids * capacity + slot, -1)
        inside = slot - tp_me * half
        mine = sound & (inside >= 0) & (inside < half)
        place_g = jnp.where(mine, ids * half + inside, -1)
        place_ref[:, at] = place
        place_g_ref[:, at] = place_g
        line = lax.broadcasted_iota(jnp.int32, (LANES, span), 0)
        both = jnp.where(line == 0, place.astype(F32), place_g.astype(F32))
        info[at, :] = both.T
    info_store = pltpu.make_async_copy(info, info_hbm, home_sem.at[4])
    info_store.start()

    gall_store = pltpu.make_async_copy(gv, gall_hbm, home_sem.at[1])
    gin_own = pltpu.make_async_copy(pk.at[rows_at(me, half), :], gin_hbm.at[me], home_sem.at[2])

    def mask(i, _):
        at = rows_at(i, block)
        live = is_live(i * block + lax.broadcasted_iota(jnp.int32, (block, wide), 0))
        gv[at, :] = jnp.where(live, gv[at, :], jnp.zeros((block, wide), BF16))
        return 0

    def pack_g(i, _):
        slot = i * block + lax.broadcasted_iota(jnp.int32, (block, rows), 0)
        hot = jnp.where(slot == place_g_ref[...], 1.0, 0.0).astype(BF16)
        pk[rows_at(i, block), :] = dot(hot, gv[...]).astype(BF16)
        return 0

    def z_copy(k):
        peer = jnp.bitwise_xor(me, k)
        return remote(
            pk.at[rows_at(peer, half), :], gin_hbm.at[me], z_send.at[k], z_recv.at[k], {"ep": peer}
        )

    def send_gradient():
        own_grad.wait()
        grad_copy.wait()
        lax.fori_loop(0, steps, mask, 0)
        gall_store.start()
        lax.fori_loop(0, peers * half // block, pack_g, 0)
        for k in list(range(peers // 2, peers)) + list(range(1, peers // 2)):
            z_copy(k).start()
        gin_own.start()

    def attend(i, _):
        project(i)
        at = rows_at(i, block)
        for pair in range(pairs):
            cols = [slice(j * width + pair * PAIR, j * width + (pair + 1) * PAIR) for j in range(3)]
            vt[pair, :, at] = pv[at, cols[2]].T
            out, lse = attend_block(
                i,
                pv[at, cols[0]],
                lambda s, cols=cols: pv[s, cols[1]],
                lambda s, pair=pair: vt[pair, :, s],
                block,
                block,
                HEAD_DIM**-0.5,
            )
            hv[at, pair * PAIR : (pair + 1) * PAIR] = out
            for h in range(2):
                lse_ref[pair, h : h + 1, at] = lse[h]
        head_copy(i).start()

        @pl.when(i == 0)
        def _():
            w_copy.wait()
            for k in range(1, peers):
                w_pass(k).start()

        pl.when(i == steps - 2)(send_gradient)
        return 0

    lax.fori_loop(0, steps, attend, 0)
    weight_loads[3].wait()
    for k in range(1, peers):
        w_pass(k).wait()
    stores = [
        pltpu.make_async_copy(hv, heads_hbm, out_sem.at[0]),
        pltpu.make_async_copy(wo2, wo2_hbm, out_sem.at[1]),
    ]
    for c in stores:
        c.start()
    small = rb.shape[1]

    def norm_stores(i, slot):
        at = rows_at(i, small)
        return [
            pltpu.make_async_copy(rb.at[slot], resid_hbm.at[at, :], out_sem.at[3 + slot]),
            pltpu.make_async_copy(cb.at[slot], chance_hbm.at[at, :], out_sem.at[5 + slot]),
        ]

    def norm_step(i, _):
        at = rows_at(i, small)
        slot = lax.rem(i, 2)

        @pl.when(slot == 0)
        def _():
            head_copy(i // 2).wait()

        @pl.when(i >= 2)
        def _():
            for c in norm_stores(i - 2, slot):
                c.wait()

        total = dot_nt(hv[at, :], wo[...]) + dot_nt(ov[at, :], wo2[...])
        resid = xv[at, :].astype(F32) + total
        rb[slot] = resid
        normal, _ = normalized(resid)
        f = (normal * norms_ref[2:3, :] + norms_ref[3:4, :]).astype(BF16)
        fv[at, :] = f
        cb[slot] = router_and_mix(dot(f, rm_ref[...]), experts)
        for c in norm_stores(i, slot):
            c.start()
        return 0

    def packed_part(i, first, size):
        at = i * block + lax.broadcasted_iota(jnp.int32, (block, size), 0)
        hot = jnp.where(at == place_ref[:, first : first + size], 1.0, 0.0).astype(BF16)
        return dot(hot, fv[first : first + size, :])

    count = rows // small
    packs = packed_hbm.shape[0] // block
    lax.fori_loop(0, count // 2, norm_step, 0)

    def pack_low(i, _):
        pa[rows_at(i, block), :] = packed_part(i, 0, rows // 2).astype(BF16)
        return 0

    lax.fori_loop(0, packs, pack_low, 0)
    lax.fori_loop(count // 2, count, norm_step, 0)
    stores_late = [
        pltpu.make_async_copy(ov, others_hbm, out_sem.at[2]),
        pltpu.make_async_copy(fv, f_hbm, home_sem.at[3]),
    ]
    for c in stores_late:
        c.start()

    def packed_store(i, slot):
        return pltpu.make_async_copy(
            hbuf.at[slot], packed_hbm.at[rows_at(i, block), :], out_sem.at[7 + slot]
        )

    def pack_high(i, _):
        slot = lax.rem(i, 2)

        @pl.when(i >= 2)
        def _():
            packed_store(i - 2, slot).wait()

        both = packed_part(i, rows // 2, rows // 2) + pa[rows_at(i, block), :].astype(F32)
        hbuf[slot] = both.astype(BF16)
        packed_store(i, slot).start()
        return 0

    lax.fori_loop(0, packs, pack_high, 0)
    for i in range(packs - 2, packs):
        packed_store(i, i % 2).wait()
    for i in range(count - 2, count):
        for c in norm_stores(i, i % 2):
            c.wait()
    for c in [gall_store, gin_own, info_store] + stores + stores_late:
        c.wait()
    for i in range(steps):
        for c in a_store(i):
            c.wait()
    for k in range(1, peers):
        z_copy(k).wait()


def front(x, g, weights, lengths, norms, rm, ids, peers, experts, capacity):
    rows, wide = x.shape
    width = weights[0].shape[1]
    half = capacity // 2
    anywhere = pl.BlockSpec(memory_space=pl.ANY)
    vmem = pl.BlockSpec(memory_space=pltpu.VMEM)

    def like(*shape, kind=BF16):
        return jax.ShapeDtypeStruct(shape, kind)

    return pl.pallas_call(
        partial(
            front_kernel,
            peers=peers,
            experts=experts,
            half=half,
            heads_count=width // HEAD_DIM,
        ),
        in_specs=[anywhere] * 6 + [pl.BlockSpec(memory_space=pltpu.SMEM)] + [vmem] * 3,
        out_specs=[anywhere] * 12 + [vmem],
        out_shape=[
            like(rows, wide),
            like(rows, 3 * width),
            like(rows, width),
            like(rows, width),
            like(wide, width),
            like(rows, wide),
            like(rows, wide, kind=F32),
            like(rows, wide),
            like(rows, LANES, kind=F32),
            like(experts * capacity, wide),
            like(peers, half, wide),
            like(rows, LANES, kind=F32),
            like(width // PAIR, 2, rows, kind=F32),
        ],
        scratch_shapes=[pltpu.VMEM((rows, wide), BF16)]
        + [pltpu.VMEM((wide, width), BF16)] * 5
        + [
            pltpu.VMEM((rows, wide), BF16),
            pltpu.VMEM((rows, 3 * width), BF16),
            pltpu.VMEM((width // PAIR, PAIR, rows), BF16),
            pltpu.VMEM((rows, width), BF16),
            pltpu.VMEM((rows, width), BF16),

            pltpu.VMEM((rows, wide), BF16),
            pltpu.VMEM((peers * half, wide), BF16),
            pltpu.VMEM((rows, wide), BF16),
            pltpu.VMEM((2, 256, wide), F32),
            pltpu.VMEM((2, 256, LANES), F32),
            pltpu.VMEM((2, 512, wide), BF16),
            pltpu.VMEM((experts * capacity, wide), BF16),
            pltpu.VMEM((1, rows), jnp.int32),
            pltpu.VMEM((1, rows), jnp.int32),
            pltpu.VMEM((rows, LANES), F32),
            pltpu.SemaphoreType.DMA((4,)),
            pltpu.SemaphoreType.DMA((rows // 512,)),
            pltpu.SemaphoreType.DMA((rows // 512, 2)),
            pltpu.SemaphoreType.DMA((5,)),
            pltpu.SemaphoreType.DMA((2,)),
            pltpu.SemaphoreType.DMA((2,)),
            pltpu.SemaphoreType.DMA((peers,)),
            pltpu.SemaphoreType.DMA((peers,)),
            pltpu.SemaphoreType.DMA((rows // 512,)),
            pltpu.SemaphoreType.DMA((rows // 512,)),
            pltpu.SemaphoreType.DMA((peers,)),
            pltpu.SemaphoreType.DMA((peers,)),
            pltpu.SemaphoreType.DMA((9,)),
        ],
        cost_estimate=cost(20 * rows * wide * wide, 30 * rows * wide),
        compiler_params=pltpu.CompilerParams(
            vmem_limit_bytes=BIG_VMEM, collective_id=2, has_side_effects=True
        ),
        name="layer_front",
    )(x, g, *weights, lengths, norms, rm, ids)


def nets_kernel(
    x_hbm,
    g_hbm,
    out_hbm,
    gin_hbm,
    sel_ref,
    rm_ref,
    wd1_hbm,
    wd2_hbm,
    we1_hbm,
    we2_hbm,
    y_hbm,
    dx_hbm,
    dot_hbm,
    gd1_hbm,
    gd2_hbm,
    ge1_hbm,
    ge2_hbm,
    in_hbm,
    res_hbm,
    pull_hbm,
    edot_hbm,
    pulls_hbm,
    edots_hbm,
    gin2_hbm,
    wd1,
    wd2,
    we1,
    we2,
    a1,
    a2,
    xb,
    gb,
    yb,
    dxb,
    dotb,
    rowb,
    ya,
    dxa,
    dyb,
    dyt,
    xt,
    w_sem,
    load_sem,
    store_sem,
    grad_sem,
    home_sem,
    local_sem,
    send_sem,
    recv_sem,
    back_send,
    back_recv,
    dot_send,
    dot_recv,
    relay_sem,
    swap_send,
    swap_recv,
    keep,
    give,
    got,
    hv,
    pv,
    *,
    peers,
    capacity,
    rb,
    ft,
    relayed,
):
    experts = peers
    me = lax.axis_index("ep")
    hidden = wd1.shape[1]
    per = rb // capacity
    quarter = peers // 4
    dense_steps = x_hbm.shape[0] // rb
    expert_steps = peers // per

    weight_copies = [
        pltpu.make_async_copy(src, dst, w_sem.at[j])
        for j, (src, dst) in enumerate(
            ((wd1_hbm, wd1), (wd2_hbm, wd2), (we1_hbm, we1), (we2_hbm, we2))
        )
    ]
    weight_copies[0].start()
    weight_copies[1].start()

    def load(t):
        rows = pl.ds(pl.multiple_of(t * rb, rb), rb)
        return [
            pltpu.make_async_copy(x_hbm.at[rows, :], xb, load_sem.at[0, 0]),
            pltpu.make_async_copy(g_hbm.at[rows, :], gb, load_sem.at[1, 0]),
        ]

    for c in load(0):
        c.start()

    barrier = pltpu.get_barrier_semaphore()
    for k in range(1, peers):
        pl.semaphore_signal(
            barrier,
            inc=1,
            device_id={"ep": jnp.bitwise_xor(me, k)},
            device_id_type=pl.DeviceIdType.MESH,
        )
    tp_me = lax.axis_index("tp")
    across = {"tp": 1 - tp_me}
    half = capacity // 2
    if relayed:
        pl.semaphore_signal(
            barrier, inc=1, device_id=across, device_id_type=pl.DeviceIdType.MESH
        )
    pl.semaphore_wait(barrier, peers if relayed else peers - 1)
    relay = pltpu.make_async_remote_copy(
        src_ref=gin_hbm,
        dst_ref=gin2_hbm,
        send_sem=relay_sem.at[0],
        recv_sem=relay_sem.at[1],
        device_id=across,
        device_id_type=pl.DeviceIdType.MESH,
    )
    if relayed:
        relay.start()

    def remote(src, dst, send, recv, k):
        peer = jnp.bitwise_xor(me, k)
        return pltpu.make_async_remote_copy(
            src_ref=src,
            dst_ref=dst,
            send_sem=send.at[k],
            recv_sem=recv.at[k],
            device_id={"ep": peer},
            device_id_type=pl.DeviceIdType.MESH,
        )

    def row_copy(k):
        return remote(
            out_hbm.at[jnp.bitwise_xor(me, k)], in_hbm.at[me], send_sem, recv_sem, k
        )

    def back_copy(k):
        return remote(
            pull_hbm.at[jnp.bitwise_xor(me, k)], pulls_hbm.at[me], back_send, back_recv, k
        )

    def dot_copy(k):
        return remote(
            edot_hbm.at[jnp.bitwise_xor(me, k)], edots_hbm.at[me], dot_send, dot_recv, k
        )

    far = list(range(2 * quarter, peers))
    near = list(range(1, 2 * quarter))
    for k in far[:quarter] + near[quarter - 1 :] + far[quarter:] + near[: quarter - 1]:
        row_copy(k).start()
    own_rows = pltpu.make_async_copy(out_hbm.at[me], in_hbm.at[me], home_sem.at[0])
    own_rows.start()
    weight_copies[2].start()
    weight_copies[3].start()

    def outputs(routed, w1_ref, w2_ref):
        x = xb[...]
        g = gb[...].astype(F32)
        chances = router_and_mix(dot(x, rm_ref[...]), experts)
        if routed:
            gate = jnp.sum(chances * sel_ref[...], axis=-1, keepdims=True)
            dy = g * lane_of(chances, experts + 1) * gate
        else:
            dy = g * lane_of(chances, experts)
        dy = dy.astype(BF16)
        dyb[...] = dy
        dyt[...] = dy.T
        xt[...] = x.T

        def products(f, _):
            cols = pl.ds(pl.multiple_of(f * ft, ft), ft)
            w1 = w1_ref[:, cols]
            w2 = w2_ref[:, cols]
            act, slope = gelu_and_slope(dot(xb[...], w1))
            h = act.astype(BF16)
            pre_grad = (slope * dot(dyb[...], w2)).astype(BF16)
            hv[:, cols] = h
            pv[:, cols] = pre_grad
            ya[...] += dot_nt(h, w2)
            dxa[...] += dot_nt(pre_grad, w1)
            return 0

        ya[...] = jnp.zeros_like(ya)
        dxa[...] = jnp.zeros_like(dxa)
        lax.fori_loop(0, hidden // ft, products, 0)

    def row_dots():
        return jnp.sum(ya[...] * gb[...].astype(F32), axis=1, keepdims=True)

    def gradients(first, last=None):
        wide_step = ft

        def at(f):
            return pl.ds(pl.multiple_of(f * wide_step, wide_step), wide_step)

        def put(f, _):
            a2[:, at(f)] = dot(dyt[...], hv[:, at(f)])
            a1[:, at(f)] = dot(xt[...], pv[:, at(f)])
            return 0

        def add(f, _):
            a2[:, at(f)] += dot(dyt[...], hv[:, at(f)])
            a1[:, at(f)] += dot(xt[...], pv[:, at(f)])
            return 0

        def round_off(f, _):
            wd2[:, at(f)] = (a2[:, at(f)] + dot(dyt[...], hv[:, at(f)])).astype(BF16)
            wd1[:, at(f)] = (a1[:, at(f)] + dot(xt[...], pv[:, at(f)])).astype(BF16)
            return 0

        @pl.when(first)
        def _():
            lax.fori_loop(0, hidden // wide_step, put, 0)

        if last is None:
            middle = jnp.logical_not(first)
        else:
            middle = jnp.logical_not(first | last)

            @pl.when(last)
            def _():
                lax.fori_loop(0, hidden // wide_step, round_off, 0)

        @pl.when(middle)
        def _():
            lax.fori_loop(0, hidden // wide_step, add, 0)

    weight_copies[0].wait()
    weight_copies[1].wait()

    def dense_stores(t, slot):
        rows = pl.ds(pl.multiple_of(t * rb, rb), rb)
        return [
            pltpu.make_async_copy(yb, y_hbm.at[rows, :], store_sem.at[slot, 0, 0]),
            pltpu.make_async_copy(dxb, dx_hbm.at[rows, :], store_sem.at[slot, 1, 0]),
            pltpu.make_async_copy(dotb.at[slot], dot_hbm.at[rows, :], store_sem.at[slot, 2, 0]),
        ]

    def dense_step(t, _):
        slot = lax.rem(t, 2)
        for c in load(t):
            c.wait()
        outputs(False, wd1, wd2)

        @pl.when(t >= 1)
        def _():
            for c in dense_stores(t - 1, 1 - slot):
                c.wait()

        yb[...] = ya[...].astype(BF16)
        dxb[...] = dxa[...].astype(BF16)
        dotb[slot] = jnp.broadcast_to(row_dots(), (rb, LANES))

        @pl.when(t + 1 < dense_steps)
        def _():
            for c in load(t + 1):
                c.start()

        for c in dense_stores(t, slot):
            c.start()
        gradients(t == 0, t == dense_steps - 1)
        return 0

    lax.fori_loop(0, dense_steps, dense_step, 0)
    for c in dense_stores(dense_steps - 1, (dense_steps - 1) % 2):
        c.wait()

    dense_grads = [
        pltpu.make_async_copy(wd1, gd1_hbm, grad_sem.at[0]),
        pltpu.make_async_copy(wd2, gd2_hbm, grad_sem.at[1]),
    ]
    for c in dense_grads:
        c.start()
    weight_copies[2].wait()
    weight_copies[3].wait()
    own_rows.wait()
    if relayed:
        relay.wait()

    def first_of(p):
        if expert_steps != 4:
            return (expert_steps - 1 - p) * per
        return jnp.where(p == 0, 2, jnp.where(p == 1, 1, jnp.where(p == 2, 3, 0))) * per

    def swap_copy(p, j):
        slot = lax.rem(p, 2)
        return pltpu.make_async_remote_copy(
            src_ref=give.at[slot, j],
            dst_ref=got.at[slot, j],
            send_sem=swap_send.at[slot, j],
            recv_sem=swap_recv.at[slot, j],
            device_id=across,
            device_id_type=pl.DeviceIdType.MESH,
        )

    size = half if relayed else capacity

    def back_stores(p, j, source_ref):
        to = (pull_hbm, res_hbm)[j]
        return [
            pltpu.make_async_copy(
                source_ref.at[pl.ds(c * size, size), :],
                to.at[jnp.bitwise_xor(me, first_of(p) + c)],
                store_sem.at[0, j, c],
            )
            for c in range(per)
        ]

    def dot_stores(p):
        return [
            pltpu.make_async_copy(
                rowb.at[c], edot_hbm.at[jnp.bitwise_xor(me, first_of(p) + c)], store_sem.at[1, 2, c]
            )
            for c in range(per)
        ]

    def to_peers(p, copy):
        for c in range(per):
            k = first_of(p) + c

            @pl.when(k > 0)
            def _(k=k):
                copy(k).start()

    def sum_shares(p, j):
        swap_copy(p, j).wait()
        stage = (dxb, yb)[j]
        stage[: per * half, :] = (keep[j] + got[lax.rem(p, 2), j].astype(F32)).astype(BF16)
        for c in back_stores(p, j, stage):
            c.start()

    def stored(p, j, source_ref):
        for c in back_stores(p, j, source_ref):
            c.wait()

    def fetch(p):
        for c in range(per):
            k = first_of(p) + c

            @pl.when(k > 0)
            def _(k=k):
                row_copy(k).wait()

        for c in fetches(p):
            c.start()

    def fetches(p):
        loads = []
        for c in range(per):
            source = jnp.bitwise_xor(me, first_of(p) + c)
            rows = pl.ds(c * capacity, capacity)
            loads.append(
                pltpu.make_async_copy(in_hbm.at[source], xb.at[rows, :], load_sem.at[0, c])
            )
            if relayed:
                for j, src, which in ((1, gin_hbm, tp_me), (2, gin2_hbm, 1 - tp_me)):
                    at = pl.ds(pl.multiple_of(c * capacity + which * half, half), half)
                    loads.append(
                        pltpu.make_async_copy(
                            src.at[source], gb.at[at, :], load_sem.at[j, c]
                        )
                    )
            else:
                loads.append(
                    pltpu.make_async_copy(
                        gin_hbm.at[source], gb.at[rows, :], load_sem.at[1, c]
                    )
                )
        return loads

    fetch(0)

    def expert_step(p, _):
        slot = lax.rem(p, 2)
        for c in fetches(p):
            c.wait()
        outputs(True, we1, we2)
        across_dots = jnp.broadcast_to(row_dots(), (rb, LANES)).T
        for c in range(per):
            rowb[c] = across_dots[:8, c * capacity : (c + 1) * capacity]
        for c in dot_stores(p):
            c.start()
        if relayed:

            @pl.when(p > 0)
            def _():
                for j in range(2):
                    sum_shares(p - 1, j)

            for j, total in ((0, dxa), (1, ya)):
                for c in range(per):
                    rows = slice(c * half, (c + 1) * half)
                    at = pl.ds(pl.multiple_of(c * capacity + tp_me * half, half), half)
                    other = pl.ds(pl.multiple_of(c * capacity + (1 - tp_me) * half, half), half)
                    keep[j, rows, :] = total[at, :]
                    give[slot, j, rows, :] = total[other, :].astype(BF16)
                swap_copy(p, j).start()
        else:
            dxb[...] = dxa[...].astype(BF16)
            yb[...] = ya[...].astype(BF16)
            for j, source_ref in ((0, dxb), (1, yb)):
                for c in back_stores(p, j, source_ref):
                    c.start()

        @pl.when(p + 1 < expert_steps)
        def _():
            fetch(p + 1)

        gradients(p == 0)
        for c in dot_stores(p):
            c.wait()
        to_peers(p, dot_copy)
        if relayed:

            @pl.when(p > 0)
            def _():
                for j in range(2):
                    stored(p - 1, j, (dxb, yb)[j])
                to_peers(p - 1, back_copy)
        else:
            for j, source_ref in ((0, dxb), (1, yb)):
                stored(p, j, source_ref)
            to_peers(p, back_copy)
        return 0

    lax.fori_loop(0, expert_steps, expert_step, 0)
    expert_grads = [
        pltpu.make_async_copy(a1, ge1_hbm, local_sem.at[0]),
        pltpu.make_async_copy(a2, ge2_hbm, local_sem.at[1]),
        pltpu.make_async_copy(edot_hbm.at[me], edots_hbm.at[me], home_sem.at[2]),
    ]
    for c in expert_grads:
        c.start()
    if relayed:
        final = expert_steps - 1
        sum_shares(final, 0)
        stored(final, 0, dxb)
        to_peers(final, back_copy)
        sum_shares(final, 1)
        stored(final, 1, yb)
    own_back = pltpu.make_async_copy(pull_hbm.at[me], pulls_hbm.at[me], home_sem.at[1])
    own_back.start()
    for c in dense_grads + expert_grads + [own_back]:
        c.wait()
    for k in range(1, peers):
        back_copy(k).wait()
        dot_copy(k).wait()


def nets(x, g, out_rows, in_grads, sel, rm, dense_weights, expert_weights, rb=512, ft=512):
    rows, wide = x.shape
    hidden = dense_weights[0].shape[1]
    peers, capacity, _ = out_rows.shape
    per = rb // capacity
    anywhere = pl.BlockSpec(memory_space=pl.ANY)
    vmem = pl.BlockSpec(memory_space=pltpu.VMEM)
    sheet = jax.ShapeDtypeStruct((rows, wide), BF16)
    relayed = in_grads.shape[1] < capacity
    blocks = jax.ShapeDtypeStruct((peers, capacity, wide), BF16)
    backs = jax.ShapeDtypeStruct(in_grads.shape, BF16)
    part = (rb * in_grads.shape[1] // capacity, wide) if relayed else (16, wide)
    strips = jax.ShapeDtypeStruct((peers, 8, capacity), F32)
    return pl.pallas_call(
        partial(nets_kernel, peers=peers, capacity=capacity, rb=rb, ft=ft, relayed=relayed),
        in_specs=[anywhere] * 4 + [vmem] * 2 + [anywhere] * 4,
        out_specs=[anywhere] * 14,
        out_shape=[
            sheet,
            sheet,
            jax.ShapeDtypeStruct((rows, LANES), F32),
            jax.ShapeDtypeStruct((wide, hidden), BF16),
            jax.ShapeDtypeStruct((wide, hidden), BF16),
            jax.ShapeDtypeStruct((wide, hidden), F32),
            jax.ShapeDtypeStruct((wide, hidden), F32),
            blocks,
            backs,
            backs,
            strips,
            backs,
            strips,
            backs,
        ],
        scratch_shapes=[pltpu.VMEM((wide, hidden), BF16)] * 4
        + [pltpu.VMEM((wide, hidden), F32)] * 2
        + [pltpu.VMEM((rb, wide), BF16)] * 4
        + [
            pltpu.VMEM((2, rb, LANES), F32),
            pltpu.VMEM((per, 8, capacity), F32),
            pltpu.VMEM((rb, wide), F32),
            pltpu.VMEM((rb, wide), F32),
            pltpu.VMEM((rb, wide), BF16),
            pltpu.VMEM((wide, rb), BF16),
            pltpu.VMEM((wide, rb), BF16),
            pltpu.SemaphoreType.DMA((4,)),
            pltpu.SemaphoreType.DMA((3, per)),
            pltpu.SemaphoreType.DMA((2, 3, per)),
            pltpu.SemaphoreType.DMA((2,)),
            pltpu.SemaphoreType.DMA((3,)),
            pltpu.SemaphoreType.DMA((2,)),
        ]
        + [pltpu.SemaphoreType.DMA((peers,))] * 6
        + [
            pltpu.SemaphoreType.DMA((2,)),
            pltpu.SemaphoreType.DMA((2, 2)),
            pltpu.SemaphoreType.DMA((2, 2)),
            pltpu.VMEM((2, *part), F32),
            pltpu.VMEM((2, 2, *part), BF16),
            pltpu.VMEM((2, 2, *part), BF16),
            pltpu.VMEM((rb, hidden), BF16),
            pltpu.VMEM((rb, hidden), BF16),
        ],
        cost_estimate=cost(24 * rows * wide * hidden, 16 * rows * wide + 24 * wide * hidden),
        compiler_params=pltpu.CompilerParams(
            vmem_limit_bytes=67043328, collective_id=0, has_side_effects=True
        ),
        name="feed_forward_nets",
    )(x, g, out_rows, in_grads, sel, rm, *dense_weights, *expert_weights)


def expert_hot(place, capacity, experts):
    lane = lax.broadcasted_iota(jnp.int32, (place.shape[0], LANES), 1)
    low = lane * capacity
    return ((place >= low) & (place < low + capacity) & (lane < experts)).astype(F32)


def ffn_pull_kernel(*refs, parts, experts, capacity, shard, sent, outs):
    (
        info_ref,
        dx_ref,
        chance_ref,
        first_ref,
        f_ref,
        g_ref,
        resid_ref,
        gain_ref,
        rm_ref,
        slot_ref,
        dots_ref,
    ) = refs[:11]
    heads_out = refs[11 : 11 + outs]
    refs = refs[11 + outs :]
    weights = refs[:parts]
    r_ref = refs[parts]
    heads = list(refs[1 + parts : 1 + 2 * parts])
    sums_ref, rmg_ref, outer_ref, outer_acc = (
        *refs[1 + 2 * parts : 4 + 2 * parts],
        refs[4 + 2 * parts],
    )
    size = info_ref.shape[0]
    step = pl.program_id(0)
    if sent is not None:
        give, send_sem, recv_sem = refs[5 + 2 * parts :]
        got = heads[sent]
        across = {"tp": 1 - lax.axis_index("tp")}
        mesh = pl.DeviceIdType.MESH

        def share(b):
            at = pl.ds(pl.multiple_of(b * size, size), size)
            return pltpu.make_async_remote_copy(
                src_ref=give.at[at, :],
                dst_ref=got.at[at, :],
                send_sem=send_sem.at[b],
                recv_sem=recv_sem.at[b],
                device_id=across,
                device_id_type=mesh,
            )

        @pl.when(step == 0)
        def _():
            barrier = pltpu.get_barrier_semaphore()
            pl.semaphore_signal(barrier, inc=1, device_id=across, device_id_type=mesh)
            pl.semaphore_wait(barrier, 1)

    place = info_ref[:, 0:1].astype(jnp.int32)
    here = info_ref[:, 1:2].astype(jnp.int32)
    row = step * size + lax.broadcasted_iota(jnp.int32, (size, 1), 0)
    row = row - lax.axis_index("tp") * shard
    own = ((row >= 0) & (row < shard)).astype(F32)
    chances = chance_ref[...]
    hot = expert_hot(place, capacity, experts)
    gate = jnp.sum(hot * chances, axis=-1, keepdims=True)
    mix_0, mix_1 = lane_of(chances, experts), lane_of(chances, experts + 1)
    table = jnp.dot(
        hot, dots_ref[...], precision=lax.Precision.HIGHEST, preferred_element_type=F32
    )
    slot = lax.broadcasted_iota(jnp.int32, table.shape, 1)
    number = jnp.sum(hot * lax.broadcasted_iota(jnp.int32, hot.shape, 1).astype(F32), axis=-1)
    inside = place - number.astype(jnp.int32)[:, None] * capacity
    second = jnp.sum(jnp.where(slot == inside, table, 0.0), axis=-1, keepdims=True)
    first = lane_of(first_ref[...], 0)
    grad_0, grad_1 = first, gate * second
    inner = mix_0 * grad_0 + mix_1 * grad_1
    lane = lax.broadcasted_iota(jnp.int32, chances.shape, 1)
    low = (mix_1 * second * gate) * (hot - chances)
    low = jnp.where(lane == experts, mix_0 * (grad_0 - inner), low)
    low = jnp.where(lane == experts + 1, mix_1 * (grad_1 - inner), low)
    low = jnp.where(lane > experts + 1, 0.0, low).astype(BF16)
    grad = dx_ref[...].astype(F32) + unpacked(here, slot_ref) + dot_nt(low, rm_ref[...])
    normal, rstd = normalized(resid_ref[...])
    r = norm_pull(grad, normal, rstd, gain_ref[2:3, :]) + own * g_ref[...].astype(F32)
    r = r.astype(BF16)
    r_ref[...] = r
    if sent is not None:
        at = pl.ds(pl.multiple_of(step * size, size), size)
        give[at, :] = dot(r, weights[sent][...]).astype(BF16)
        share(step).start()
    for j, (h, w) in enumerate(zip(heads, weights)):
        if j != sent:
            h[...] = dot(r, w[...]).astype(BF16)

    @pl.when(pl.program_id(0) == 0)
    def _():
        sums_ref[...] = jnp.zeros_like(sums_ref)
        rmg_ref[...] = jnp.zeros_like(rmg_ref)
        outer_acc[...] = jnp.zeros_like(outer_acc)

    sums_ref[0:1, :] += jnp.sum(grad * normal, axis=0, keepdims=True)
    sums_ref[1:2, :] += jnp.sum(grad, axis=0, keepdims=True)
    rmg_ref[...] += dot(low.T, f_ref[...])
    left = r.T
    col = 0
    for h in heads_out:
        outer_acc[:, col : col + h.shape[1]] += dot(left, h[...])
        col += h.shape[1]

    @pl.when(step == pl.num_programs(0) - 1)
    def _():
        outer_ref[...] = outer_acc[...].astype(BF16)

    if sent is not None:

        @pl.when(step == pl.num_programs(0) - 1)
        def _():
            for b in range(give.shape[0] // size):
                share(b).wait()


def ffn_pull(
    info,
    dx,
    chances,
    first,
    f,
    g,
    resid,
    gain,
    rm,
    slot_rows,
    dots,
    heads,
    weights,
    experts,
    shard,
    sent=None,
    rb=256,
):
    rows, wide = dx.shape
    capacity = dots.shape[1]
    dots = jnp.pad(dots, ((0, LANES - experts), (0, 0)))
    block = pl.BlockSpec((rb, wide), lambda i: (i, 0))
    narrow = pl.BlockSpec((rb, LANES), lambda i: (i, 0))
    head_specs = [
        pl.BlockSpec(memory_space=pl.ANY) if j == sent else pl.BlockSpec((rb, size), lambda i: (i, 0))
        for j, (_, _, size) in enumerate(weights)
    ]
    outer_width = sum(h.shape[1] for h in heads)
    scratch, extra = [pltpu.VMEM((wide, outer_width), F32)], {}
    if sent is not None:
        scratch += [
            pltpu.VMEM((rows, weights[sent][2]), BF16),
            pltpu.SemaphoreType.DMA((rows // rb,)),
            pltpu.SemaphoreType.DMA((rows // rb,)),
        ]
        extra = dict(collective_id=3, has_side_effects=True)
    return pl.pallas_call(
        partial(
            ffn_pull_kernel,
            parts=len(weights),
            experts=experts,
            capacity=capacity,
            shard=shard,
            sent=sent,
            outs=len(heads),
        ),
        grid=(rows // rb,),
        in_specs=[narrow, block, narrow, narrow, block, block, block]
        + [resident(gain.shape), resident((wide, LANES))]
        + [resident(slot_rows.shape), resident(dots.shape)]
        + [pl.BlockSpec((rb, h.shape[1]), lambda i: (i, 0)) for h in heads]
        + [
            pl.BlockSpec((wide, size), lambda i, j=j: (0, j), pipeline_mode=pl.Buffered(1))
            for _, j, size in weights
        ],
        out_specs=[block]
        + head_specs
        + [resident((8, wide)), resident((LANES, wide)), resident((wide, outer_width))],
        out_shape=[jax.ShapeDtypeStruct((rows, wide), BF16)]
        + [jax.ShapeDtypeStruct((rows, size), BF16) for _, _, size in weights]
        + [jax.ShapeDtypeStruct((8, wide), F32), jax.ShapeDtypeStruct((LANES, wide), F32)]
        + [jax.ShapeDtypeStruct((wide, outer_width), BF16)],
        scratch_shapes=scratch,
        cost_estimate=cost(6 * rows * wide * wide, 16 * rows * wide),
        compiler_params=pltpu.CompilerParams(vmem_limit_bytes=56 * 1024 * 1024, **extra),
        name="ffn_norm_pull",
    )(
        info,
        dx,
        chances,
        first,
        f,
        g,
        resid,
        gain,
        rm,
        slot_rows,
        dots,
        *heads,
        *[w for w, _, _ in weights],
    )


def outer_kernel(left_ref, *refs, parts):
    rights = refs[:parts]
    o_ref, acc_ref = refs[parts:]

    @pl.when(pl.program_id(0) == 0)
    def _():
        acc_ref[...] = jnp.zeros_like(acc_ref)

    left = left_ref[...].T
    at = 0
    for r in rights:
        width = r.shape[1]
        acc_ref[:, at : at + width] += dot(left, r[...])
        at += width

    @pl.when(pl.program_id(0) == pl.num_programs(0) - 1)
    def _():
        o_ref[...] = acc_ref[...].astype(BF16)


def outer(left, rights, rb=512):
    rows, wide = left.shape
    total = sum(r.shape[1] for r in rights)
    return pl.pallas_call(
        partial(outer_kernel, parts=len(rights)),
        grid=(rows // rb,),
        in_specs=[pl.BlockSpec((rb, wide), lambda i: (i, 0))]
        + [pl.BlockSpec((rb, r.shape[1]), lambda i: (i, 0)) for r in rights],
        out_specs=resident((wide, total)),
        out_shape=jax.ShapeDtypeStruct((wide, total), BF16),
        scratch_shapes=[pltpu.VMEM((wide, total), F32)],
        cost_estimate=cost(2 * rows * wide * total, 2 * rows * (wide + total)),
        name="outer_product",
    )(left, *rights)


def attn_pull_kernel(at_ref, x_ref, r_ref, gain_ref, *refs, groups):
    grads = refs[: 3 * groups]
    weights = refs[3 * groups : 3 * groups + 3]
    t_ref, sums_ref = refs[3 * groups + 3 :]
    del at_ref
    total = None
    for k in range(3):
        at = 0
        for j in range(groups):
            d = grads[k * groups + j]
            width = d.shape[1]
            part = dot_nt(d[...], weights[k][:, at : at + width])
            total = part if total is None else total + part
            at += width
    normal, rstd = normalized(x_ref[...].astype(F32))
    t = norm_pull(total, normal, rstd, gain_ref[...]) + r_ref[...].astype(F32)
    t_ref[...] = t.astype(t_ref.dtype)

    @pl.when(pl.program_id(0) == 0)
    def _():
        sums_ref[...] = jnp.zeros_like(sums_ref)

    sums_ref[0:1, :] += jnp.sum(total * normal, axis=0, keepdims=True)
    sums_ref[1:2, :] += jnp.sum(total, axis=0, keepdims=True)


def attn_pull(first_row, count, x, r, gain, grads, weights, out_type, rb=256):
    wide = x.shape[1]
    groups = len(grads) // 3

    def rows(width):
        return pl.BlockSpec((rb, width), lambda i, at: (at[0] + i, 0))

    return pl.pallas_call(
        partial(attn_pull_kernel, groups=groups),
        grid_spec=pltpu.PrefetchScalarGridSpec(
            num_scalar_prefetch=1,
            grid=(count // rb,),
            in_specs=[rows(wide), rows(wide), resident((1, wide))]
            + [rows(d.shape[1]) for d in grads]
            + [resident(w.shape) for w in weights],
            out_specs=[pl.BlockSpec((rb, wide), lambda i, at: (i, 0)), resident((8, wide))],
        ),
        out_shape=[
            jax.ShapeDtypeStruct((count, wide), out_type),
            jax.ShapeDtypeStruct((8, wide), F32),
        ],
        cost_estimate=cost(6 * count * wide * weights[0].shape[1], 10 * count * wide),
        name="attention_norm_pull",
    )((first_row // rb).astype(jnp.int32).reshape(1), x, r, gain, *grads, *weights)


def combine_kernel(
    at_ref, info_ref, y_ref, chance_ref, slot_ref, other_ref, own_ref, *, experts, capacity
):
    del at_ref
    place = info_ref[:, 0:1].astype(jnp.int32)
    here = info_ref[:, 1:2].astype(jnp.int32)
    chances = chance_ref[...]
    gate = jnp.sum(expert_hot(place, capacity, experts) * chances, axis=-1, keepdims=True)
    moe = unpacked(here, slot_ref) * (lane_of(chances, experts + 1) * gate)
    total = (lane_of(chances, experts) * y_ref[...].astype(F32) + moe).astype(BF16)
    first = pl.program_id(0) < pl.num_programs(0) // 2

    @pl.when(first)
    def _():
        other_ref[...] = total

    @pl.when(jnp.logical_not(first))
    def _():
        own_ref[...] = total


def combine(first_row, info, y, coef, slot_rows, experts, capacity, rb=256):
    rows, wide = y.shape
    half = rows // rb // 2

    def block(width):
        return pl.BlockSpec((rb, width), lambda i, at: (lax.rem(at[0] + half + i, 2 * half), 0))

    part = jax.ShapeDtypeStruct((rows // 2, wide), BF16)
    return pl.pallas_call(
        partial(combine_kernel, experts=experts, capacity=capacity),
        grid_spec=pltpu.PrefetchScalarGridSpec(
            num_scalar_prefetch=1,
            grid=(2 * half,),
            in_specs=[block(LANES), block(wide), block(LANES), resident(slot_rows.shape)],
            out_specs=[
                pl.BlockSpec((rb, wide), lambda i, _: (jnp.minimum(i, half - 1), 0)),
                pl.BlockSpec((rb, wide), lambda i, _: (jnp.maximum(i - half, 0), 0)),
            ],
        ),
        out_shape=[part, part],
        cost_estimate=cost(4 * rows * wide * wide, 8 * rows * wide),
        name="combine_nets",
    )((first_row // rb).astype(jnp.int32).reshape(1), info, y, coef, slot_rows)


class Halving:
    def __init__(self, total, gives, gots, send, recv, me, size, order):
        self.total, self.gives, self.gots = total, gives, gots
        self.send, self.recv, self.me, self.size = send, recv, me, size
        self.order = order
        self.rows = total.shape[0] // size

    def block(self, index):
        return pl.ds(pl.multiple_of(index * self.rows, self.rows), self.rows)

    def copy(self, s):
        return pltpu.make_async_remote_copy(
            src_ref=self.gives[s],
            dst_ref=self.gots[s],
            send_sem=self.send.at[s],
            recv_sem=self.recv.at[s],
            device_id={"ep": jnp.bitwise_xor(self.me, 1 << self.order[s])},
            device_id_type=pl.DeviceIdType.MESH,
        )

    def halves(self, s):
        place = sum(1 for b in self.order[s:] if b < self.order[s])
        low = (1 << place) - 1
        return [((i >> place) << (place + 1) | (i & low)) for i in range(self.size >> (s + 1))], 1 << place

    def bit(self, s):
        return lax.rem(lax.div(self.me, 1 << self.order[s]), 2)

    def start(self, s):
        places, step = self.halves(s)
        for i, at in enumerate(places):
            rows = slice(i * self.rows, (i + 1) * self.rows)
            self.gives[s][rows, :] = self.total[self.block(at + (1 - self.bit(s)) * step), :].astype(BF16)
        self.copy(s).start()

    def finish(self, s):
        self.copy(s).wait()
        places, step = self.halves(s)
        for i, at in enumerate(places):
            rows = slice(i * self.rows, (i + 1) * self.rows)
            kept = self.total[self.block(at + self.bit(s) * step), :]
            self.total[rows, :] = kept + self.gots[s][rows, :].astype(F32)

    def step(self, s):
        self.finish(s)
        if s + 1 < len(self.order):
            self.start(s + 1)


def tail_kernel(*refs, groups, size, rb, small_rows):
    refs = list(refs)

    def take(count):
        taken = refs[:count]
        del refs[:count]
        return taken

    x_hbm, r_hbm, a_hbm, out_hbm = take(4)
    grads_hbm = take(3 * groups)
    small_ref, gain_ref = take(2)
    weights = take(3)
    own_hbm, got_hbm, square_ref, outsum_ref, total_ref = take(5)
    xv, rv, av = take(3)
    grads = take(3 * groups)
    gov, acc_a, acc_b, goacc, give_rows, own_buf = take(6)
    steps = size.bit_length() - 1
    hops = steps + 1
    gives, gots = take(steps), take(steps)
    gives_b, gots_b = take(steps), take(steps)
    go_gives, go_gots = take(steps), take(steps)
    small_gives, small_gots = take(hops), take(hops)
    (
        load_sem,
        own_sem,
        row_send,
        row_recv,
        half_send,
        half_recv,
        half_send_b,
        half_recv_b,
        go_send,
        go_recv,
        small_send,
        small_recv,
        out_sem,
        out_give,
        out_got,
    ) = refs
    me = lax.axis_index("ep")
    tp_me = lax.axis_index("tp")
    rows = x_hbm.shape[0]
    shard = rows // 2
    count = shard // rb

    out_load = pltpu.make_async_copy(out_hbm, gov, load_sem.at[0, 0])
    a_load = pltpu.make_async_copy(a_hbm, av, load_sem.at[1, 0])

    def loads(which, line):
        at = pl.ds(pl.multiple_of(which * shard, shard), shard)
        return [
            pltpu.make_async_copy(
                src.at[at, :], dst.at[at, :], load_sem.at[line, j + 1]
            )
            for j, (src, dst) in enumerate(zip([x_hbm, r_hbm, *grads_hbm], [xv, rv, *grads]))
        ]

    theirs_loads, own_loads = loads(1 - tp_me, 0), loads(tp_me, 1)
    for c in theirs_loads:
        c.start()
    out_load.start()
    for c in own_loads:
        c.start()
    a_load.start()

    barrier = pltpu.get_barrier_semaphore()
    mesh = pl.DeviceIdType.MESH
    pl.semaphore_signal(barrier, inc=1, device_id={"tp": 1 - tp_me}, device_id_type=mesh)
    for s in range(steps):
        pl.semaphore_signal(
            barrier, inc=1, device_id={"ep": jnp.bitwise_xor(me, 1 << s)}, device_id_type=mesh
        )
    pl.semaphore_wait(barrier, hops)

    order = list(range(steps))
    other_order = [0, 2, 1] + order[3:] if steps > 2 else order
    qkv = [
        Halving(acc_a, gives, gots, half_send, half_recv, me, size, order),
        Halving(acc_b, gives_b, gots_b, half_send_b, half_recv_b, me, size, other_order),
    ]
    go = Halving(goacc, go_gives, go_gots, go_send, go_recv, me, size, order)

    for c in theirs_loads:
        c.wait()

    total_ref[:small_rows, :] = small_ref[...]
    total_ref[small_rows:, :] = jnp.zeros_like(total_ref[small_rows:, :])

    def pulled(at):
        total = None
        for k in range(3):
            col = 0
            for j in range(groups):
                d = grads[k * groups + j][at, :]
                width = d.shape[1]
                part = dot_nt(d, weights[k][:, col : col + width])
                total = part if total is None else total + part
                col += width
        normal, rstd = normalized(xv[at, :].astype(F32))
        total_ref[small_rows : small_rows + 1, :] += jnp.sum(total * normal, axis=0, keepdims=True)
        total_ref[small_rows + 1 : small_rows + 2, :] += jnp.sum(total, axis=0, keepdims=True)
        return norm_pull(total, normal, rstd, gain_ref[0:1, :]) + rv[at, :].astype(F32)

    def row_copy(b):
        at = pl.ds(pl.multiple_of(b * rb, rb), rb)
        return pltpu.make_async_remote_copy(
            src_ref=give_rows.at[at, :],
            dst_ref=got_hbm.at[at, :],
            send_sem=row_send.at[b],
            recv_sem=row_recv.at[b],
            device_id={"tp": 1 - tp_me},
            device_id_type=mesh,
        )

    def theirs(b, _):
        at = pl.ds(pl.multiple_of((1 - tp_me) * shard + b * rb, rb), rb)
        give_rows[pl.ds(pl.multiple_of(b * rb, rb), rb), :] = pulled(at).astype(BF16)
        row_copy(b).start()
        return 0

    lax.fori_loop(0, count // 2, theirs, 0)
    out_load.wait()
    goacc[...] = gov[...].astype(F32)
    go.start(0)
    for c in own_loads + [a_load]:
        c.wait()
    cut = len(grads) // 2
    for acc in (acc_a, acc_b):
        acc[...] = jnp.zeros_like(acc)

    for acc, some, chain in ((acc_a, grads[:cut], qkv[0]), (acc_b, grads[cut:], qkv[1])):

        def outer_step(b, _, acc=acc, some=some):
            at = pl.ds(pl.multiple_of(b * 512, 512), 512)
            left = av[at, :].T
            col = 0
            for g in some:
                width = g.shape[1]
                acc[:, col : col + width] += dot(left, g[at, :])
                col += width
            return 0

        lax.fori_loop(0, rows // 512, outer_step, 0)
        chain.start(0)
        if chain is qkv[0]:
            go.step(0)
    qkv[0].step(0)
    lax.fori_loop(count // 2, count, theirs, 0)

    def own_copy(b):
        at = pl.ds(pl.multiple_of(b * rb, rb), rb)
        return pltpu.make_async_copy(own_buf.at[at, :], own_hbm.at[at, :], own_sem.at[b])

    def own_step(b, _):
        at = pl.ds(pl.multiple_of(tp_me * shard + b * rb, rb), rb)
        own_buf[pl.ds(pl.multiple_of(b * rb, rb), rb), :] = pulled(at)
        own_copy(b).start()
        return 0

    qkv[1].step(0)
    lax.fori_loop(0, count // 2, own_step, 0)
    go.step(1)
    qkv[0].step(1)
    lax.fori_loop(count // 2, count, own_step, 0)

    def small_copy(s):
        peer = {"tp": 1 - tp_me} if s == 0 else {"ep": jnp.bitwise_xor(me, 1 << (s - 1))}
        return pltpu.make_async_remote_copy(
            src_ref=small_gives[s],
            dst_ref=small_gots[s],
            send_sem=small_send.at[s],
            recv_sem=small_recv.at[s],
            device_id=peer,
            device_id_type=mesh,
        )

    for s in range(hops):
        small_gives[s][...] = total_ref[...]
        small_copy(s).start()
        if s + 2 < steps:
            go.step(s + 2)
        if s == 1:
            qkv[1].step(1)
            qkv[0].step(2)
        if s == 2:
            qkv[1].step(2)
        small_copy(s).wait()
        total_ref[...] += small_gots[s][...]
        if s == max(0, steps - 3):
            own_width = outsum_ref.shape[1]
            out_give[...] = goacc[: goacc.shape[0] // size, own_width:].astype(BF16)
            out_copy = pltpu.make_async_remote_copy(
                src_ref=out_give,
                dst_ref=out_got,
                send_sem=out_sem.at[0],
                recv_sem=out_sem.at[1],
                device_id={"tp": 1 - tp_me},
                device_id_type=mesh,
            )
            out_copy.start()
    for chain in qkv:
        for s in range(3, steps):
            chain.step(s)
    col = 0
    for acc in (acc_a, acc_b):
        square_ref[:, col : col + acc.shape[1]] = acc[: acc.shape[0] // size, :]
        col += acc.shape[1]
    out_copy.wait()
    outsum_ref[...] = goacc[: goacc.shape[0] // size, :own_width] + out_got[...].astype(F32)
    for b in range(count):
        own_copy(b).wait()
        row_copy(b).wait()


def tail(x, r, a, out_part, grads, small, gain, weights, size, rb=256):
    rows, wide = x.shape
    shard = rows // 2
    groups = len(grads) // 3
    total = sum(g.shape[1] for g in grads)
    out_width = out_part.shape[1]
    small_rows = small.shape[0]
    steps = size.bit_length() - 1
    kept = wide // size
    anywhere = pl.BlockSpec(memory_space=pl.ANY)
    vmem = pl.BlockSpec(memory_space=pltpu.VMEM)

    def halves(width):
        return [pltpu.VMEM((wide >> (s + 1), width), BF16) for s in range(steps)]

    return pl.pallas_call(
        partial(tail_kernel, groups=groups, size=size, rb=rb, small_rows=small_rows),
        in_specs=[anywhere] * (4 + 3 * groups) + [vmem] * 5,
        out_specs=[anywhere, anywhere, vmem, vmem, vmem],
        out_shape=[
            jax.ShapeDtypeStruct((shard, wide), F32),
            jax.ShapeDtypeStruct((shard, wide), BF16),
            jax.ShapeDtypeStruct((kept, total), F32),
            jax.ShapeDtypeStruct((kept, out_width // 2), F32),
            jax.ShapeDtypeStruct((small_rows + 8, wide), F32),
        ],
        scratch_shapes=[pltpu.VMEM((rows, wide), BF16)] * 3
        + [pltpu.VMEM(g.shape, BF16) for g in grads]
        + [
            pltpu.VMEM((wide, out_width), BF16),
            pltpu.VMEM((wide, total // 2), F32),
            pltpu.VMEM((wide, total // 2), F32),
            pltpu.VMEM((wide, out_width), F32),
            pltpu.VMEM((shard, wide), BF16),
            pltpu.VMEM((shard, wide), F32),
        ]
        + halves(total // 2) * 4
        + halves(out_width) * 2
        + [pltpu.VMEM((small_rows + 8, wide), F32)] * (2 * (steps + 1))
        + [
            pltpu.SemaphoreType.DMA((2, 3 + 3 * groups)),
            pltpu.SemaphoreType.DMA((shard // rb,)),
            pltpu.SemaphoreType.DMA((shard // rb,)),
            pltpu.SemaphoreType.DMA((shard // rb,)),
        ]
        + [pltpu.SemaphoreType.DMA((steps,))] * 6
        + [pltpu.SemaphoreType.DMA((steps + 1,))] * 2
        + [
            pltpu.SemaphoreType.DMA((2,)),
            pltpu.VMEM((kept, out_width // 2), BF16),
            pltpu.VMEM((kept, out_width // 2), BF16),
        ],
        cost_estimate=cost(12 * rows * wide * total // 3, 16 * rows * wide),
        compiler_params=pltpu.CompilerParams(
            vmem_limit_bytes=BIG_VMEM, collective_id=1, has_side_effects=True
        ),
        name="backward_tail",
    )(x, r, a, out_part, *grads, small, gain, *weights)


def results_kernel(
    at_ref,
    len_ref,
    own_ref,
    got_ref,
    resid_ref,
    mine_ref,
    theirs_ref,
    square_ref,
    small_ref,
    h_ref,
    r_ref,
    token_ref,
    block_ref,
    q_ref,
    k_ref,
    v_ref,
    gh_ref,
    gr_ref,
    router_ref,
    mix_ref,
    gain1_ref,
    bias1_ref,
    gain2_ref,
    bias2_ref,
    *,
    length,
):
    token_ref[...] = own_ref[...] + got_ref[...].astype(F32)
    size = own_ref.shape[0]
    position = (at_ref[0] + pl.program_id(0)) * size + lax.broadcasted_iota(jnp.int32, own_ref.shape, 0)
    live = None
    for s in range(len_ref.shape[0]):
        inside = (position >= s * length) & (position < s * length + len_ref[s])
        live = inside if live is None else live | inside
    nets_sum = mine_ref[...].astype(F32) + theirs_ref[...].astype(F32)
    block_ref[...] = jnp.where(live, resid_ref[...] + nets_sum, 0.0).astype(BF16)

    @pl.when(pl.program_id(0) == 0)
    def _():
        width = q_ref.shape[1]
        for j, ref in enumerate((q_ref, k_ref, v_ref)):
            ref[...] = square_ref[:, j * width : (j + 1) * width]
        gh_ref[...] = h_ref[...].astype(F32)
        gr_ref[...] = r_ref[...].astype(F32)
        experts = router_ref.shape[0]
        router_ref[...] = small_ref[8 : 8 + experts, :]
        mix_ref[...] = small_ref[8 + experts : 10 + experts, :]
        end = small_ref.shape[0] - 8
        for ref, at in ((gain1_ref, end), (bias1_ref, end + 1), (gain2_ref, 0), (bias2_ref, 1)):
            ref[...] = small_ref[at : at + 1, :]


def results(first_row, lengths, own, got, resid, weighted, theirs, square, small, gh, gr, experts, rb=256):
    rows, wide = own.shape
    kept, width = square.shape[0], square.shape[1] // 3
    block = pl.BlockSpec((rb, wide), lambda i, *_: (i, 0))
    shifted = pl.BlockSpec((rb, wide), lambda i, at, _: (at[0] + i, 0))
    shapes = [(kept, width)] * 3 + [gh.shape, gr.shape, (experts, wide), (2, wide)] + [(1, wide)] * 4
    return pl.pallas_call(
        partial(results_kernel, length=resid.shape[0] // lengths.shape[0]),
        grid_spec=pltpu.PrefetchScalarGridSpec(
            num_scalar_prefetch=2,
            grid=(rows // rb,),
            in_specs=[block, block, shifted, block, block]
            + [resident(v.shape) for v in (square, small, gh, gr)],
            out_specs=[block, block] + [resident(s) for s in shapes],
        ),
        out_shape=[jax.ShapeDtypeStruct((rows, wide), F32), jax.ShapeDtypeStruct((rows, wide), BF16)]
        + [jax.ShapeDtypeStruct(s, F32) for s in shapes],
        cost_estimate=cost(rows * wide, 22 * rows * wide),
        name="results",
    )(
        (first_row // rb).astype(jnp.int32).reshape(1),
        lengths,
        own,
        got,
        resid,
        weighted,
        theirs,
        square,
        small,
        gh,
        gr,
    )


def on_device(
    sizes,
    tokens,
    out_grad,
    lengths,
    expert_ids,
    w_query,
    w_key,
    w_value,
    w_output,
    w_hidden,
    w_return,
    router,
    mix_weight,
    gain_attn,
    bias_attn,
    gain_ffn,
    bias_ffn,
    expert_in,
    expert_out,
):
    tp, ep = sizes
    shard_rows = out_grad.shape[0]
    all_rows = tokens.shape[0]
    model_width = tokens.shape[1]
    experts = router.shape[1]
    capacity = all_rows // experts
    seq_count = lengths.shape[0]
    seq_len = all_rows // seq_count
    local_width = w_query.shape[1]
    local_heads = local_width // HEAD_DIM
    pairs = local_heads // 2
    splits = 2 if pairs % 2 == 0 else 1
    each = pairs // splits
    tp_index = lax.axis_index("tp")
    ep_index = lax.axis_index("ep")
    first_row = tp_index * shard_rows
    swap = [(0, 1), (1, 0)]

    def shard_of(values, axis=0):
        return lax.dynamic_slice_in_dim(values, first_row, shard_rows, axis)

    def swapped(values):
        return lax.ppermute(values, "tp", swap)

    def exchange(values):
        return lax.all_to_all(values, "ep", split_axis=0, concat_axis=0, tiled=True)

    def after(values, *others):
        return lax.optimization_barrier((values, others))[0]

    def summed_over(values, axis, size):
        step = 1
        while step < size:
            values = values + lax.ppermute(values, axis, [(i, i ^ step) for i in range(size)])
            step *= 2
        return values

    def over_sequences(values):
        return lax.psum_scatter(values, "ep", scatter_dimension=0, tiled=True)

    positions = jnp.arange(all_rows)
    seq_index = positions // seq_len
    row_limit = jnp.sum(
        jnp.where(seq_index[:, None] == jnp.arange(seq_count)[None, :], lengths[None, :], 0), axis=1
    )
    live_all = positions % seq_len < row_limit
    slot_count = experts * capacity
    blocks = (experts, capacity, model_width)

    rm = jnp.pad(
        jnp.concatenate([router, mix_weight], axis=1), ((0, 0), (0, LANES - experts - 2))
    )
    norms = jnp.concatenate([gain_attn, bias_attn, gain_ffn, bias_ffn]).astype(F32)
    norms = norms.reshape(4, model_width)
    projections = (w_query, w_key, w_value)
    if tp == 2:
        (
            attn_in,
            projected,
            heads,
            others,
            w_other,
            grad_all,
            resid,
            ffn_in,
            chances,
            packed,
            grad_rows,
            info,
            lse,
        ) = front(
            tokens,
            out_grad,
            (*projections, w_output),
            lengths,
            norms,
            rm,
            expert_ids[None, :],
            ep,
            experts,
            capacity,
        )
        all_heads = [heads, others]
        wide_weights = [(w, s, each * PAIR) for w in (w_output, w_other) for s in range(splits)]
    else:
        one_hot = (expert_ids[:, None] == jnp.arange(experts)[None, :]) & live_all[:, None]
        routed = one_hot.astype(F32)
        slots = jnp.sum((jnp.cumsum(routed, axis=0) - routed) * routed, axis=1).astype(jnp.int32)
        sound = live_all & (slots < capacity)
        place = jnp.where(sound, expert_ids * capacity + slots, -1)
        place_row = place[None, :]
        info = jnp.broadcast_to(place[:, None], (all_rows, LANES)).astype(F32)
        live_grad = jnp.where(shard_of(live_all)[:, None], out_grad, jnp.zeros_like(out_grad))
        w_all = lax.all_gather(w_output, "tp", axis=1, tiled=True)
        grad_all = lax.all_gather(live_grad, "tp", axis=0, tiled=True)
        grad_rows = exchange(pack(place_row, grad_all, slot_count).reshape(blocks))
        attn_in, projected = norm_project(tokens, norms[0:1], norms[1:2], projections)
        heads, lse = attention_forward(projected, seq_count, local_heads, 0, pairs)
        all_heads = [lax.all_gather(heads, "tp", axis=1, tiled=True)]
        wide_weights = [(w_all, 0, model_width)]
        resid, ffn_in, chances = output_norm(
            tokens, norms[2:3], norms[3:4], rm, all_heads, [(w_all, 0)], experts
        )
        packed = pack(place_row, ffn_in, slot_count)

    sel = (jnp.arange(LANES) == ep_index).astype(F32)[None, :]
    (
        dense,
        dense_pull,
        first_dot,
        grad_hidden,
        grad_return,
        grad_expert_in,
        grad_expert_out,
        _,
        sums_back,
        _,
        _,
        pulls,
        dots,
        _,
    ) = nets(
        ffn_in,
        grad_all,
        packed.reshape(blocks),
        grad_rows,
        sel,
        rm,
        (w_hidden, w_return),
        (expert_in[0], expert_out[0]),
    )
    returned = exchange(sums_back).reshape(-1, model_width)
    pulls = pulls.reshape(-1, model_width)
    dots = dots[:, 0, :]
    part, *rest = ffn_pull(
        info,
        dense_pull,
        chances,
        first_dot,
        ffn_in,
        grad_all,
        resid,
        norms,
        rm,
        pulls,
        dots,
        all_heads,
        wide_weights,
        experts,
        shard_rows,
        sent=splits if tp == 2 else None,
    )
    *head_parts, ffn_sums, rm_sums, out_part = rest
    if tp == 2:
        head_grads = [
            [m, o if s == 0 else swapped(o)]
            for s, (m, o) in enumerate(zip(head_parts[:splits], head_parts[splits:]))
        ]
    else:
        local = lax.psum_scatter(head_parts[0], "tp", scatter_dimension=1, tiled=True)
        head_grads = [
            [local[:, s * each * PAIR : (s + 1) * each * PAIR]] for s in range(splits)
        ]
    grad_hidden = over_sequences(grad_hidden)
    grad_return = over_sequences(grad_return)

    qkv = []
    expert_grads = [grad_expert_in, grad_expert_out]
    for s in range(splits):
        if s == splits - 1:
            if qkv:
                dense, qkv[-1], head_grads[s] = lax.optimization_barrier(
                    (dense, qkv[-1], head_grads[s])
                )
            weighted = combine(
                first_row if tp == 2 else jnp.zeros((), jnp.int32), info, dense, chances, returned, experts, capacity
            )
            projected, weighted = lax.optimization_barrier((projected, weighted))
        *grads3, expert_grads[s] = attention_backward(
            projected,
            heads,
            head_grads[s],
            lse,
            seq_count,
            local_heads,
            s * each,
            each,
            (expert_grads[s],),
        )
        qkv.append(grads3)
    flat = [qkv[s][k] for k in range(3) for s in range(splits)]
    rows_kept = -(-(experts + 2) // 8) * 8
    small = jnp.concatenate([ffn_sums, rm_sums[:rows_kept]], axis=0)
    if tp == 2:
        theirs = swapped(weighted[0])
        own_part, got, square, grad_output, small = tail(
            tokens,
            part,
            attn_in,
            out_part,
            flat,
            small,
            norms,
            projections,
            ep,
        )
        (
            token_grad,
            block_out,
            grad_query,
            grad_key,
            grad_value,
            grad_hidden,
            grad_return,
            grad_router,
            grad_mix,
            *vectors,
        ) = results(
            first_row,
            lengths,
            own_part,
            got,
            resid,
            weighted[1],
            theirs,
            square,
            small,
            grad_hidden,
            grad_return,
            experts,
        )
        vectors = [v[0] for v in vectors]
    else:
        whole, attn_sums = attn_pull(
            jnp.zeros((), jnp.int32), all_rows, tokens, part, norms[0:1], flat, projections, BF16
        )
        token_grad = lax.psum_scatter(whole, "tp", scatter_dimension=0, tiled=True).astype(F32)
        weighted = jnp.concatenate(weighted[::-1], axis=0)
        summed = lax.psum_scatter(weighted, "tp", scatter_dimension=0, tiled=True).astype(F32)
        block_out = jnp.where(shard_of(live_all)[:, None], shard_of(resid) + summed, 0.0).astype(BF16)
        square = over_sequences(outer(attn_in, flat))
        grad_output = lax.psum_scatter(
            over_sequences(out_part).astype(BF16), "tp", scatter_dimension=1, tiled=True
        ).astype(F32)
        small = summed_over(summed_over(small, "tp", tp), "ep", ep)
        attn_sums = summed_over(summed_over(attn_sums, "tp", tp), "ep", ep)
        grad_query, grad_key, grad_value = jnp.split(square.astype(F32), 3, axis=1)
        grad_hidden, grad_return = grad_hidden.astype(F32), grad_return.astype(F32)
        grad_router, grad_mix = small[8 : 8 + experts], small[8 + experts : 10 + experts]
        vectors = [attn_sums[0], attn_sums[1], small[0], small[1]]
    return (
        block_out,
        token_grad,
        grad_query,
        grad_key,
        grad_value,
        grad_output,
        grad_hidden,
        grad_return,
        grad_router.T,
        grad_mix.T,
        *vectors,
        expert_grads[0][None],
        expert_grads[1][None],
    )


def solution(mesh):
    in_specs = (
        P("ep", None),
        P(("ep", "tp"), None),
        P("ep"),
        P("ep"),
        P(None, "tp"),
        P(None, "tp"),
        P(None, "tp"),
        P(None, "tp"),
        P(None, "tp"),
        P(None, "tp"),
        P(),
        P(),
        P(),
        P(),
        P(),
        P(),
        P("ep", None, "tp"),
        P("ep", None, "tp"),
    )
    out_specs = (
        P(("ep", "tp"), None),
        P(("ep", "tp"), None),
        P("ep", "tp"),
        P("ep", "tp"),
        P("ep", "tp"),
        P("ep", "tp"),
        P("ep", "tp"),
        P("ep", "tp"),
        P(),
        P(),
        P(),
        P(),
        P(),
        P(),
        P("ep", None, "tp"),
        P("ep", None, "tp"),
    )
    return jax.shard_map(
        partial(on_device, (mesh.shape["tp"], mesh.shape["ep"])),
        mesh=mesh,
        in_specs=in_specs,
        out_specs=out_specs,
        check_vma=False,
    )
```

```python
import math
from functools import partial

import jax
import jax.numpy as jnp
from jax import lax
from jax.experimental import pallas as pl
from jax.experimental.pallas import tpu as pltpu
from jax.sharding import PartitionSpec as P

HEAD_DIM = 64
PAIR = 2 * HEAD_DIM


EPS = 1e-05
NEG = -1e30
F32 = jnp.float32
BF16 = jnp.bfloat16
NT = (((1,), (1,)), ((), ()))


LANES = 128
GELU_C = math.sqrt(2.0 / math.pi)
GELU_A = 0.044715
BIG_VMEM = 62 * 1024 * 1024


def dot(left, right):
    return jnp.dot(left, right, preferred_element_type=F32)


def dot_nt(left, right):
    return lax.dot_general(left, right, NT, preferred_element_type=F32)


def normalized(values):
    middle = jnp.mean(values, axis=-1, keepdims=True)
    centred = values - middle
    rstd = lax.rsqrt(jnp.mean(centred * centred, axis=-1, keepdims=True) + EPS)
    return centred * rstd, rstd


def norm_pull(grad, normal, rstd, gain):
    q = grad * gain
    along = jnp.mean(q * normal, axis=-1, keepdims=True)
    return rstd * (q - jnp.mean(q, axis=-1, keepdims=True) - normal * along)


def gelu_and_slope(v):
    square = v * v
    t = jnp.tanh(v * (GELU_C + (GELU_C * GELU_A) * square))
    half = 0.5 + 0.5 * t
    slope = half + v * (0.5 - 0.5 * (t * t)) * (GELU_C + (3.0 * GELU_C * GELU_A) * square)
    return v * half, slope


def router_and_mix(logits, experts):
    lane = lax.broadcasted_iota(jnp.int32, logits.shape, 1)
    out = jnp.zeros_like(logits)
    for low, high in ((0, experts), (experts, experts + 2)):
        inside = (lane >= low) & (lane < high)
        top = jnp.max(jnp.where(inside, logits, NEG), axis=-1, keepdims=True)
        e = jnp.where(inside, jnp.exp(jnp.where(inside, logits - top, 0.0)), 0.0)
        out = out + e / jnp.sum(e, axis=-1, keepdims=True)
    return out


def lane_of(values, index):
    lane = lax.broadcasted_iota(jnp.int32, values.shape, 1)
    return jnp.sum(jnp.where(lane == index, values, 0.0), axis=-1, keepdims=True)


def resident(shape):
    return pl.BlockSpec(shape, lambda i, *_: (0,) * len(shape), pipeline_mode=pl.Buffered(1))


def cost(flops, bytes_accessed):
    return pl.CostEstimate(flops=flops // 64, bytes_accessed=bytes_accessed // 64, transcendentals=0)


def attend_block(qi, q, keys, values_t, bq, bk, scale):
    lane = lax.broadcasted_iota(jnp.int32, (bq, PAIR), 1)
    q = q * jnp.asarray(scale, BF16)
    zero = jnp.zeros_like(q)
    halves = [jnp.where(lane < HEAD_DIM, q, zero), jnp.where(lane < HEAD_DIM, zero, q)]

    def step(j, carry, masked):
        off = pl.multiple_of(j * bk, bk)
        k = keys(pl.ds(off, bk))
        vt = values_t(pl.ds(off, bk))
        scores = [lax.dot_general(k, half, NT, preferred_element_type=F32) for half in halves]
        if masked:
            key_pos = off + lax.broadcasted_iota(jnp.int32, (bk, bq), 0)
            query_pos = qi * bq + lax.broadcasted_iota(jnp.int32, (bk, bq), 1)
            allowed = key_pos <= query_pos
            scores = [jnp.where(allowed, s, NEG) for s in scores]
        new = []
        for h in range(2):
            m, l, acc = carry[h]
            m_new = jnp.maximum(m, jnp.max(scores[h], axis=0, keepdims=True))
            alpha = jnp.exp(m - m_new)
            p = jnp.exp(scores[h] - m_new)
            l = l * alpha + jnp.sum(p, axis=0, keepdims=True)
            part = dot(vt[h * HEAD_DIM : (h + 1) * HEAD_DIM], p.astype(BF16))
            new.append((m_new, l, acc * alpha + part))
        return tuple(new)

    init = tuple(
        (jnp.full((1, bq), NEG, F32), jnp.zeros((1, bq), F32), jnp.zeros((HEAD_DIM, bq), F32))
        for _ in range(2)
    )
    full = qi * (bq // bk)
    carry = lax.fori_loop(0, full, lambda j, c: step(j, c, False), init)
    for d in range(bq // bk):
        carry = step(full + d, carry, True)
    out = jnp.concatenate([acc / l for _, l, acc in carry], axis=0).T.astype(BF16)
    return out, [m + jnp.log(l) for m, l, _ in carry]


def attention_forward_kernel(q_ref, k_ref, v_ref, o_ref, lse_ref, vt_ref, *, bq, bk, scale):
    qi = pl.program_id(2)

    @pl.when(qi == 0)
    def _():
        vt_ref[...] = v_ref[...].T

    out, lse = attend_block(
        qi, q_ref[...], lambda s: k_ref[s, :], lambda s: vt_ref[:, s], bq, bk, scale
    )
    o_ref[...] = out
    for h in range(2):
        lse_ref[0, h : h + 1, :] = lse[h]


def attention_forward(proj, seqs, heads, first, count, bq=512, bk=512):
    rows = proj.shape[0]
    length = rows // seqs
    pairs = heads // 2
    nq = length // bq
    flops = 2 * rows * length * count * PAIR
    return pl.pallas_call(
        partial(attention_forward_kernel, bq=bq, bk=bk, scale=HEAD_DIM**-0.5),
        grid=(seqs, count, nq),
        in_specs=[
            pl.BlockSpec((bq, PAIR), lambda s, p, i: (s * nq + i, first + p)),
            pl.BlockSpec((length, PAIR), lambda s, p, i: (s, pairs + first + p)),
            pl.BlockSpec((length, PAIR), lambda s, p, i: (s, 2 * pairs + first + p)),
        ],
        out_specs=[
            pl.BlockSpec((bq, PAIR), lambda s, p, i: (s * nq + i, p)),
            pl.BlockSpec((1, 2, bq), lambda s, p, i: (p, 0, s * nq + i)),
        ],
        out_shape=[
            jax.ShapeDtypeStruct((rows, count * PAIR), BF16),
            jax.ShapeDtypeStruct((count, 2, rows), F32),
        ],
        scratch_shapes=[pltpu.VMEM((PAIR, length), BF16)],
        cost_estimate=cost(flops * 4, 8 * rows * count * PAIR),
        name="attention_forward",
    )(proj, proj, proj)


def attention_backward_kernel(
    q_ref,
    k_ref,
    v_ref,
    o_ref,
    lse_ref,
    *refs,
    terms,
    carried,
    filled,
    bq,
    bk,
    scale,
    length,
):
    lane = lax.broadcasted_iota(jnp.int32, (length, PAIR), 1)
    first = lane < HEAD_DIM
    q = q_ref[...] * jnp.asarray(scale, BF16)
    do_refs = refs[:terms]
    refs = refs[terms:]
    from_refs = refs[:carried]
    dq_ref, dk_ref, dv_ref = refs[carried + filled : carried + filled + 3]
    refs = refs[carried + filled + 3 :]
    to_refs = refs[:carried]
    dqt_ref, qs_ref, dos_ref, kt_ref, dl_ref = refs[carried : carried + 5]
    held = refs[carried + 5 :]
    at = pl.program_id(0) * pl.num_programs(1) + pl.program_id(1)
    final = pl.num_programs(0) * pl.num_programs(1) - 1
    ways = [
        (
            pltpu.make_async_copy(from_refs[c], held[2 * c], held[2 * c + 1].at[0]),
            pltpu.make_async_copy(held[2 * c], to_refs[c], held[2 * c + 1].at[1]),
        )
        for c in range(carried)
    ]

    @pl.when(at == 0)
    def _():
        for way_in, _ in ways:
            way_in.start()

    @pl.when(at == final)
    def _():
        for way_in, way_out in ways:
            way_in.wait()
            way_out.start()

    do = do_refs[0][...]
    if terms == 2:
        do = (do.astype(F32) + do_refs[1][...].astype(F32)).astype(BF16)
    zero = jnp.zeros_like(q)
    qs_ref[0] = jnp.where(first, q, zero)
    qs_ref[1] = jnp.where(first, zero, q)
    dos_ref[0] = jnp.where(first, do, zero)
    dos_ref[1] = jnp.where(first, zero, do)
    kt_ref[...] = (k_ref[...] * jnp.asarray(scale, BF16)).T
    prod = (do.astype(F32) * o_ref[...].astype(F32)).T
    dl_ref[0:1, :] = jnp.sum(prod[:HEAD_DIM], axis=0, keepdims=True)
    dl_ref[1:2, :] = jnp.sum(prod[HEAD_DIM:], axis=0, keepdims=True)
    dqt_ref[...] = jnp.zeros_like(dqt_ref)
    nq = length // bq
    nk = length // bk

    def key_block(j, _):
        koff = pl.multiple_of(j * bk, bk)
        k = k_ref[pl.ds(koff, bk), :]
        v = v_ref[pl.ds(koff, bk), :]
        kt = kt_ref[:, pl.ds(koff, bk)]

        def tile(qoff, wide, tall, masked):
            qoff = pl.multiple_of(qoff, wide)
            cols = pl.ds(qoff, wide)
            if masked:
                key_pos = koff + lax.broadcasted_iota(jnp.int32, (tall, wide), 0)
                query_pos = qoff + lax.broadcasted_iota(jnp.int32, (tall, wide), 1)
                allowed = key_pos <= query_pos
            qh = [qs_ref[h, cols, :] for h in range(2)]
            dh = [dos_ref[h, cols, :] for h in range(2)]
            scores = [lax.dot_general(k[:tall], x, NT, preferred_element_type=F32) for x in qh]
            pulls = [lax.dot_general(v[:tall], x, NT, preferred_element_type=F32) for x in dh]
            dk, dv, dqs = 0.0, 0.0, []
            for h in range(2):
                p = jnp.exp(scores[h] - lse_ref[0, h : h + 1, cols])
                if masked:
                    p = jnp.where(allowed, p, 0.0)
                ds = (p * (pulls[h] - dl_ref[h : h + 1, cols])).astype(BF16)
                dv = dv + dot(p.astype(BF16), dh[h])
                dk = dk + dot(ds, qh[h])
                dqs.append(dot(kt[h * HEAD_DIM : (h + 1) * HEAD_DIM, :tall], ds))
            dqt_ref[:, cols] += jnp.concatenate(dqs, axis=0)
            return dk, dv

        def step(i, carry):
            dk, dv = tile(i * bq, bq, bk, False)
            return carry[0] + dk, carry[1] + dv

        half = bk // 2
        dk, dv = tile(koff + half, half, bk, True)
        dk_0, dv_0 = tile(koff, half, half, True)
        rest = jnp.zeros((bk - half, PAIR), F32)
        carry = (
            dk + jnp.concatenate([dk_0, rest], axis=0),
            dv + jnp.concatenate([dv_0, rest], axis=0),
        )
        i0 = j * (bk // bq)
        dk, dv = lax.fori_loop(i0 + bk // bq, nq, step, carry)
        dk_ref[pl.ds(koff, bk), :] = dk.astype(BF16)
        dv_ref[pl.ds(koff, bk), :] = dv.astype(BF16)
        return 0

    lax.fori_loop(0, nk, key_block, 0)
    dq_ref[...] = dqt_ref[...].T.astype(BF16)
    if carried:

        @pl.when(at == final)
        def _():
            for _, way_out in ways:
                way_out.wait()


def attention_backward(proj, out, out_grads, lse, seqs, heads, first, count, place=0, into=(), carry=(), bq=512, bk=512):
    rows = out.shape[0]
    length = rows // seqs
    pairs = heads // 2
    width = out_grads[0].shape[1]

    def block(off):
        return pl.BlockSpec((length, PAIR), lambda s, p: (s, off + p))

    grad = jax.ShapeDtypeStruct((rows, width), BF16)
    terms = len(out_grads)
    return pl.pallas_call(
        partial(
            attention_backward_kernel,
            terms=terms,
            carried=len(carry),
            filled=len(into),
            bq=bq,
            bk=bk,
            scale=HEAD_DIM**-0.5,
            length=length,
        ),
        grid=(seqs, count),
        in_specs=[
            block(first),
            block(pairs + first),
            block(2 * pairs + first),
            block(first),
            pl.BlockSpec((1, 2, length), lambda s, p: (first + p, 0, s)),
        ]
        + [block(place)] * terms
        + [pl.BlockSpec(memory_space=pl.ANY) for _ in (*carry, *into)],
        input_output_aliases={5 + terms + len(carry) + j: j for j in range(len(into))},
        out_specs=[block(place)] * 3 + [pl.BlockSpec(memory_space=pl.ANY) for _ in carry],
        out_shape=[grad] * 3 + [jax.ShapeDtypeStruct(c.shape, c.dtype) for c in carry],
        scratch_shapes=[
            pltpu.VMEM((PAIR, length), F32),
            pltpu.VMEM((2, length, PAIR), BF16),
            pltpu.VMEM((2, length, PAIR), BF16),
            pltpu.VMEM((PAIR, length), BF16),
            pltpu.VMEM((2, length), F32),
        ]
        + [s for c in carry for s in (pltpu.VMEM(c.shape, c.dtype), pltpu.SemaphoreType.DMA((2,)))],
        cost_estimate=cost(20 * rows * length * count * PAIR, 16 * rows * width),
        compiler_params=pltpu.CompilerParams(vmem_limit_bytes=52 * 1024 * 1024),
        name="attention_backward",
    )(proj, proj, proj, out, lse, *out_grads, *carry, *into)


def norm_project_kernel(x_ref, gain_ref, bias_ref, wq_ref, wk_ref, wv_ref, a_ref, p_ref):
    normal, _ = normalized(x_ref[...].astype(F32))
    a = (normal * gain_ref[...] + bias_ref[...]).astype(BF16)
    a_ref[...] = a
    width = wq_ref.shape[1]
    for j, w in enumerate((wq_ref, wk_ref, wv_ref)):
        p_ref[:, j * width : (j + 1) * width] = dot(a, w[...]).astype(BF16)


def norm_project(x, gain, bias, weights, rb=512):
    rows, wide = x.shape
    width = weights[0].shape[1]
    return pl.pallas_call(
        norm_project_kernel,
        grid=(rows // rb,),
        in_specs=[pl.BlockSpec((rb, wide), lambda i: (i, 0)), resident((1, wide)), resident((1, wide))]
        + [resident((wide, width))] * 3,
        out_specs=[
            pl.BlockSpec((rb, wide), lambda i: (i, 0)),
            pl.BlockSpec((rb, 3 * width), lambda i: (i, 0)),
        ],
        out_shape=[
            jax.ShapeDtypeStruct((rows, wide), BF16),
            jax.ShapeDtypeStruct((rows, 3 * width), BF16),
        ],
        cost_estimate=cost(6 * rows * wide * width, 8 * rows * wide),
        name="norm_project",
    )(x, gain, bias, *weights)


def output_norm_kernel(*refs, parts, experts):
    x_ref, gain_ref, bias_ref, rm_ref = refs[:4]
    heads = refs[4 : 4 + parts]
    weights = refs[4 + parts : 4 + 2 * parts]
    resid_ref, f_ref, chance_ref = refs[4 + 2 * parts :]
    total = dot_nt(heads[0][...], weights[0][...])
    for h, w in zip(heads[1:], weights[1:]):
        total = total + dot_nt(h[...], w[...])
    resid = x_ref[...].astype(F32) + total
    resid_ref[...] = resid
    normal, _ = normalized(resid)
    f = (normal * gain_ref[...] + bias_ref[...]).astype(BF16)
    f_ref[...] = f
    chance_ref[...] = router_and_mix(dot(f, rm_ref[...]), experts)


def output_norm(x, gain, bias, rm, heads, weights, experts, rb=256):
    rows, wide = x.shape
    block = pl.BlockSpec((rb, wide), lambda i: (i, 0))
    weight_specs = [
        pl.BlockSpec(
            (wide, h.shape[1]), lambda i, j=j: (0, j), pipeline_mode=pl.Buffered(1)
        )
        for h, (_, j) in zip(heads, weights)
    ]
    return pl.pallas_call(
        partial(output_norm_kernel, parts=len(heads), experts=experts),
        grid=(rows // rb,),
        in_specs=[block, resident((1, wide)), resident((1, wide)), resident((wide, LANES))]
        + [pl.BlockSpec((rb, h.shape[1]), lambda i: (i, 0)) for h in heads]
        + weight_specs,
        out_specs=[block, block, pl.BlockSpec((rb, LANES), lambda i: (i, 0))],
        out_shape=[
            jax.ShapeDtypeStruct((rows, wide), F32),
            jax.ShapeDtypeStruct((rows, wide), BF16),
            jax.ShapeDtypeStruct((rows, LANES), F32),
        ],
        cost_estimate=cost(2 * rows * wide * wide, 12 * rows * wide),
        name="output_norm",
    )(x, gain, bias, rm, *heads, *[w for w, _ in weights])


def pack_kernel(place_ref, x_ref, o_ref):
    count, rows = o_ref.shape[0], x_ref.shape[0]
    slot = pl.program_id(0) * count + lax.broadcasted_iota(jnp.int32, (count, rows), 0)
    hot = jnp.where(slot == place_ref[...], 1.0, 0.0).astype(BF16)
    o_ref[...] = dot(hot, x_ref[...]).astype(BF16)


def pack(place, x, count, sb=512):
    rows, wide = x.shape
    return pl.pallas_call(
        pack_kernel,
        grid=(count // sb,),
        in_specs=[resident((1, rows)), resident((rows, wide))],
        out_specs=pl.BlockSpec((sb, wide), lambda i: (i, 0)),
        out_shape=jax.ShapeDtypeStruct((count, wide), BF16),
        cost_estimate=cost(2 * rows * wide * count, 4 * rows * wide),
        name="pack_rows",
    )(place, x)


def unpacked(place, all_ref):
    slot = lax.broadcasted_iota(jnp.int32, (place.shape[0], all_ref.shape[0]), 1)
    return dot(jnp.where(slot == place, 1.0, 0.0).astype(BF16), all_ref[...])


def front_kernel(*refs, peers, experts, half, heads_count):
    refs = list(refs)

    def take(count):
        taken = refs[:count]
        del refs[:count]
        return taken

    x_hbm, g_hbm, wq_hbm, wk_hbm, wv_hbm, wo_hbm = take(6)
    len_ref, norms_ref, rm_ref, ids_ref = take(4)
    a_hbm, p_hbm, heads_hbm, others_hbm, wo2_hbm = take(5)
    gall_hbm, resid_hbm, f_hbm, chance_hbm, packed_hbm, gin_hbm, info_hbm, lse_ref = take(8)
    xv, wq, wk, wv, wo, wo2, av, pv, vt, hv, ov, gv, pk, fv, rb, cb, hbuf, pa = take(18)
    place_ref, place_g_ref, info = take(3)
    (
        load_sem,
        x_sem,
        a_sem,
        home_sem,
        grad_sem,
        w_sem,
        w_send,
        w_recv,
        head_send,
        head_recv,
        z_send,
        z_recv,
        out_sem,
    ) = refs
    me = lax.axis_index("ep")
    tp_me = lax.axis_index("tp")
    mesh = pl.DeviceIdType.MESH
    across = {"tp": 1 - tp_me}
    rows, wide = xv.shape
    shard = rows // 2
    width = wq.shape[1]
    block = 512
    steps = rows // block

    def rows_at(i, size):
        return pl.ds(pl.multiple_of(i * size, size), size)

    def x_load(i):
        return pltpu.make_async_copy(
            x_hbm.at[rows_at(i, block), :], xv.at[rows_at(i, block), :], x_sem.at[i]
        )

    weight_loads = [
        pltpu.make_async_copy(src, dst, load_sem.at[j])
        for j, (src, dst) in enumerate(((wq_hbm, wq), (wk_hbm, wk), (wv_hbm, wv), (wo_hbm, wo)))
    ]
    for c in weight_loads[:3]:
        c.start()
    for i in range(steps):
        x_load(i).start()
    weight_loads[3].start()
    own_rows = pl.ds(pl.multiple_of(tp_me * shard, shard), shard)
    own_grad = pltpu.make_async_copy(g_hbm, gv.at[own_rows, :], home_sem.at[0])
    own_grad.start()

    barrier = pltpu.get_barrier_semaphore()
    pl.semaphore_signal(barrier, inc=1, device_id=across, device_id_type=mesh)
    for k in range(1, peers):
        pl.semaphore_signal(
            barrier, inc=1, device_id={"ep": jnp.bitwise_xor(me, k)}, device_id_type=mesh
        )
    pl.semaphore_wait(barrier, peers)

    def remote(src, dst, send, recv, to):
        return pltpu.make_async_remote_copy(
            src_ref=src,
            dst_ref=dst,
            send_sem=send,
            recv_sem=recv,
            device_id=to,
            device_id_type=mesh,
        )

    def w_rows(index):
        return wo2.at[rows_at(index, wide // peers), :]

    w_copy = remote(
        wo_hbm.at[rows_at(me, wide // peers), :], w_rows(me), w_sem.at[0], w_sem.at[1], across
    )
    w_copy.start()
    grad_copy = remote(g_hbm, gv.at[own_rows, :], grad_sem.at[0], grad_sem.at[1], across)
    grad_copy.start()

    def w_pass(k):
        return remote(
            w_rows(me), w_rows(me), w_send.at[k], w_recv.at[k], {"ep": jnp.bitwise_xor(me, k)}
        )

    for c in weight_loads[:3]:
        c.wait()

    def a_store(i):
        return [
            pltpu.make_async_copy(
                av.at[rows_at(i, block), :], a_hbm.at[rows_at(i, block), :], a_sem.at[i, 0]
            ),
            pltpu.make_async_copy(
                pv.at[rows_at(i, block), :], p_hbm.at[rows_at(i, block), :], a_sem.at[i, 1]
            ),
        ]

    def project(i):
        at = rows_at(i, block)
        x_load(i).wait()
        normal, _ = normalized(xv[at, :].astype(F32))
        a = (normal * norms_ref[0:1, :] + norms_ref[1:2, :]).astype(BF16)
        av[at, :] = a
        for j, w in enumerate((wq, wk, wv)):
            pv[at, j * width : (j + 1) * width] = dot(a, w[...]).astype(BF16)
        for c in a_store(i):
            c.start()

    pairs = heads_count // 2

    def head_copy(i):
        at = rows_at(i, block)
        return remote(hv.at[at, :], ov.at[at, :], head_send.at[i], head_recv.at[i], across)

    def is_live(position):
        count = len_ref.shape[0]
        length = rows // count
        inside = None
        for s in range(count):
            here = (position >= s * length) & (position < s * length + len_ref[s])
            inside = here if inside is None else inside | here
        return inside

    span = 256
    run = jnp.zeros((experts, 1), F32)
    triangle = jnp.where(
        lax.broadcasted_iota(jnp.int32, (span, span), 0)
        < lax.broadcasted_iota(jnp.int32, (span, span), 1),
        1.0,
        0.0,
    ).astype(BF16)
    capacity = 2 * half
    for b in range(rows // span):
        at = slice(b * span, (b + 1) * span)
        ids = ids_ref[:, at]
        live = is_live(b * span + lax.broadcasted_iota(jnp.int32, (1, span), 1))
        hot = (lax.broadcasted_iota(jnp.int32, (experts, span), 0) == ids) & live
        hot = jnp.where(hot, 1.0, 0.0)
        before = dot(hot.astype(BF16), triangle) + run
        run = run + jnp.sum(hot, axis=1, keepdims=True)
        slot = jnp.sum(before * hot, axis=0, keepdims=True).astype(jnp.int32)
        sound = live & (slot < capacity)
        place = jnp.where(sound, ids * capacity + slot, -1)
        inside = slot - tp_me * half
        mine = sound & (inside >= 0) & (inside < half)
        place_g = jnp.where(mine, ids * half + inside, -1)
        place_ref[:, at] = place
        place_g_ref[:, at] = place_g
        line = lax.broadcasted_iota(jnp.int32, (LANES, span), 0)
        both = jnp.where(line == 0, place.astype(F32), place_g.astype(F32))
        info[at, :] = both.T
    info_store = pltpu.make_async_copy(info, info_hbm, home_sem.at[4])
    info_store.start()

    gall_store = pltpu.make_async_copy(gv, gall_hbm, home_sem.at[1])
    gin_own = pltpu.make_async_copy(pk.at[rows_at(me, half), :], gin_hbm.at[me], home_sem.at[2])

    def mask(i, _):
        at = rows_at(i, block)
        live = is_live(i * block + lax.broadcasted_iota(jnp.int32, (block, wide), 0))
        gv[at, :] = jnp.where(live, gv[at, :], jnp.zeros((block, wide), BF16))
        return 0

    def pack_g(i, _):
        slot = i * block + lax.broadcasted_iota(jnp.int32, (block, rows), 0)
        hot = jnp.where(slot == place_g_ref[...], 1.0, 0.0).astype(BF16)
        pk[rows_at(i, block), :] = dot(hot, gv[...]).astype(BF16)
        return 0

    def z_copy(k):
        peer = jnp.bitwise_xor(me, k)
        return remote(
            pk.at[rows_at(peer, half), :], gin_hbm.at[me], z_send.at[k], z_recv.at[k], {"ep": peer}
        )

    def send_gradient():
        own_grad.wait()
        grad_copy.wait()
        lax.fori_loop(0, steps, mask, 0)
        gall_store.start()
        lax.fori_loop(0, peers * half // block, pack_g, 0)
        for k in list(range(peers // 2, peers)) + list(range(1, peers // 2)):
            z_copy(k).start()
        gin_own.start()

    def attend(i, _):
        project(i)
        at = rows_at(i, block)
        for pair in range(pairs):
            cols = [slice(j * width + pair * PAIR, j * width + (pair + 1) * PAIR) for j in range(3)]
            vt[pair, :, at] = pv[at, cols[2]].T
            out, lse = attend_block(
                i,
                pv[at, cols[0]],
                lambda s, cols=cols: pv[s, cols[1]],
                lambda s, pair=pair: vt[pair, :, s],
                block,
                block,
                HEAD_DIM**-0.5,
            )
            hv[at, pair * PAIR : (pair + 1) * PAIR] = out
            for h in range(2):
                lse_ref[pair, h : h + 1, at] = lse[h]
        head_copy(i).start()

        @pl.when(i == 0)
        def _():
            w_copy.wait()
            for k in range(1, peers):
                w_pass(k).start()

        pl.when(i == steps - 2)(send_gradient)
        return 0

    lax.fori_loop(0, steps, attend, 0)
    weight_loads[3].wait()
    for k in range(1, peers):
        w_pass(k).wait()
    stores = [
        pltpu.make_async_copy(hv, heads_hbm, out_sem.at[0]),
        pltpu.make_async_copy(wo2, wo2_hbm, out_sem.at[1]),
    ]
    for c in stores:
        c.start()
    small = rb.shape[1]

    def norm_stores(i, slot):
        at = rows_at(i, small)
        return [
            pltpu.make_async_copy(rb.at[slot], resid_hbm.at[at, :], out_sem.at[3 + slot]),
            pltpu.make_async_copy(cb.at[slot], chance_hbm.at[at, :], out_sem.at[5 + slot]),
        ]

    def norm_step(i, _):
        at = rows_at(i, small)
        slot = lax.rem(i, 2)

        @pl.when(slot == 0)
        def _():
            head_copy(i // 2).wait()

        @pl.when(i >= 2)
        def _():
            for c in norm_stores(i - 2, slot):
                c.wait()

        total = dot_nt(hv[at, :], wo[...]) + dot_nt(ov[at, :], wo2[...])
        resid = xv[at, :].astype(F32) + total
        rb[slot] = resid
        normal, _ = normalized(resid)
        f = (normal * norms_ref[2:3, :] + norms_ref[3:4, :]).astype(BF16)
        fv[at, :] = f
        cb[slot] = router_and_mix(dot(f, rm_ref[...]), experts)
        for c in norm_stores(i, slot):
            c.start()
        return 0

    def packed_part(i, first, size):
        at = i * block + lax.broadcasted_iota(jnp.int32, (block, size), 0)
        hot = jnp.where(at == place_ref[:, first : first + size], 1.0, 0.0).astype(BF16)
        return dot(hot, fv[first : first + size, :])

    count = rows // small
    packs = packed_hbm.shape[0] // block
    lax.fori_loop(0, count // 2, norm_step, 0)

    def pack_low(i, _):
        pa[rows_at(i, block), :] = packed_part(i, 0, rows // 2).astype(BF16)
        return 0

    lax.fori_loop(0, packs, pack_low, 0)
    lax.fori_loop(count // 2, count, norm_step, 0)
    stores_late = [
        pltpu.make_async_copy(ov, others_hbm, out_sem.at[2]),
        pltpu.make_async_copy(fv, f_hbm, home_sem.at[3]),
    ]
    for c in stores_late:
        c.start()

    def packed_store(i, slot):
        return pltpu.make_async_copy(
            hbuf.at[slot], packed_hbm.at[rows_at(i, block), :], out_sem.at[7 + slot]
        )

    def pack_high(i, _):
        slot = lax.rem(i, 2)

        @pl.when(i >= 2)
        def _():
            packed_store(i - 2, slot).wait()

        both = packed_part(i, rows // 2, rows // 2) + pa[rows_at(i, block), :].astype(F32)
        hbuf[slot] = both.astype(BF16)
        packed_store(i, slot).start()
        return 0

    lax.fori_loop(0, packs, pack_high, 0)
    for i in range(packs - 2, packs):
        packed_store(i, i % 2).wait()
    for i in range(count - 2, count):
        for c in norm_stores(i, i % 2):
            c.wait()
    for c in [gall_store, gin_own, info_store] + stores + stores_late:
        c.wait()
    for i in range(steps):
        for c in a_store(i):
            c.wait()
    for k in range(1, peers):
        z_copy(k).wait()


def front(x, g, weights, lengths, norms, rm, ids, peers, experts, capacity):
    rows, wide = x.shape
    width = weights[0].shape[1]
    half = capacity // 2
    anywhere = pl.BlockSpec(memory_space=pl.ANY)
    vmem = pl.BlockSpec(memory_space=pltpu.VMEM)

    def like(*shape, kind=BF16):
        return jax.ShapeDtypeStruct(shape, kind)

    return pl.pallas_call(
        partial(
            front_kernel,
            peers=peers,
            experts=experts,
            half=half,
            heads_count=width // HEAD_DIM,
        ),
        in_specs=[anywhere] * 6 + [pl.BlockSpec(memory_space=pltpu.SMEM)] + [vmem] * 3,
        out_specs=[anywhere] * 12 + [vmem],
        out_shape=[
            like(rows, wide),
            like(rows, 3 * width),
            like(rows, width),
            like(rows, width),
            like(wide, width),
            like(rows, wide),
            like(rows, wide, kind=F32),
            like(rows, wide),
            like(rows, LANES, kind=F32),
            like(experts * capacity, wide),
            like(peers, half, wide),
            like(rows, LANES, kind=F32),
            like(width // PAIR, 2, rows, kind=F32),
        ],
        scratch_shapes=[pltpu.VMEM((rows, wide), BF16)]
        + [pltpu.VMEM((wide, width), BF16)] * 5
        + [
            pltpu.VMEM((rows, wide), BF16),
            pltpu.VMEM((rows, 3 * width), BF16),
            pltpu.VMEM((width // PAIR, PAIR, rows), BF16),
            pltpu.VMEM((rows, width), BF16),
            pltpu.VMEM((rows, width), BF16),

            pltpu.VMEM((rows, wide), BF16),
            pltpu.VMEM((peers * half, wide), BF16),
            pltpu.VMEM((rows, wide), BF16),
            pltpu.VMEM((2, 256, wide), F32),
            pltpu.VMEM((2, 256, LANES), F32),
            pltpu.VMEM((2, 512, wide), BF16),
            pltpu.VMEM((experts * capacity, wide), BF16),
            pltpu.VMEM((1, rows), jnp.int32),
            pltpu.VMEM((1, rows), jnp.int32),
            pltpu.VMEM((rows, LANES), F32),
            pltpu.SemaphoreType.DMA((4,)),
            pltpu.SemaphoreType.DMA((rows // 512,)),
            pltpu.SemaphoreType.DMA((rows // 512, 2)),
            pltpu.SemaphoreType.DMA((5,)),
            pltpu.SemaphoreType.DMA((2,)),
            pltpu.SemaphoreType.DMA((2,)),
            pltpu.SemaphoreType.DMA((peers,)),
            pltpu.SemaphoreType.DMA((peers,)),
            pltpu.SemaphoreType.DMA((rows // 512,)),
            pltpu.SemaphoreType.DMA((rows // 512,)),
            pltpu.SemaphoreType.DMA((peers,)),
            pltpu.SemaphoreType.DMA((peers,)),
            pltpu.SemaphoreType.DMA((9,)),
        ],
        cost_estimate=cost(20 * rows * wide * wide, 30 * rows * wide),
        compiler_params=pltpu.CompilerParams(
            vmem_limit_bytes=BIG_VMEM, collective_id=2, has_side_effects=True
        ),
        name="layer_front",
    )(x, g, *weights, lengths, norms, rm, ids)


def nets_kernel(
    x_hbm,
    g_hbm,
    out_hbm,
    gin_hbm,
    sel_ref,
    rm_ref,
    wd1_hbm,
    wd2_hbm,
    we1_hbm,
    we2_hbm,
    y_hbm,
    dx_hbm,
    dot_hbm,
    gd1_hbm,
    gd2_hbm,
    ge1_hbm,
    ge2_hbm,
    in_hbm,
    res_hbm,
    pull_hbm,
    edot_hbm,
    pulls_hbm,
    edots_hbm,
    gin2_hbm,
    wd1,
    wd2,
    we1,
    we2,
    a1,
    a2,
    xb,
    gb,
    yb,
    dxb,
    dotb,
    rowb,
    ya,
    dxa,
    dyb,
    dyt,
    xt,
    w_sem,
    load_sem,
    store_sem,
    grad_sem,
    home_sem,
    local_sem,
    send_sem,
    recv_sem,
    back_send,
    back_recv,
    dot_send,
    dot_recv,
    relay_sem,
    swap_send,
    swap_recv,
    keep,
    give,
    got,
    hv,
    pv,
    *,
    peers,
    capacity,
    rb,
    ft,
    relayed,
):
    experts = peers
    me = lax.axis_index("ep")
    hidden = wd1.shape[1]
    per = rb // capacity
    quarter = peers // 4
    dense_steps = x_hbm.shape[0] // rb
    expert_steps = peers // per

    weight_copies = [
        pltpu.make_async_copy(src, dst, w_sem.at[j])
        for j, (src, dst) in enumerate(
            ((wd1_hbm, wd1), (wd2_hbm, wd2), (we1_hbm, we1), (we2_hbm, we2))
        )
    ]
    weight_copies[0].start()
    weight_copies[1].start()

    def load(t):
        rows = pl.ds(pl.multiple_of(t * rb, rb), rb)
        return [
            pltpu.make_async_copy(x_hbm.at[rows, :], xb, load_sem.at[0, 0]),
            pltpu.make_async_copy(g_hbm.at[rows, :], gb, load_sem.at[1, 0]),
        ]

    for c in load(0):
        c.start()

    barrier = pltpu.get_barrier_semaphore()
    for k in range(1, peers):
        pl.semaphore_signal(
            barrier,
            inc=1,
            device_id={"ep": jnp.bitwise_xor(me, k)},
            device_id_type=pl.DeviceIdType.MESH,
        )
    tp_me = lax.axis_index("tp")
    across = {"tp": 1 - tp_me}
    half = capacity // 2
    if relayed:
        pl.semaphore_signal(
            barrier, inc=1, device_id=across, device_id_type=pl.DeviceIdType.MESH
        )
    pl.semaphore_wait(barrier, peers if relayed else peers - 1)
    relay = pltpu.make_async_remote_copy(
        src_ref=gin_hbm,
        dst_ref=gin2_hbm,
        send_sem=relay_sem.at[0],
        recv_sem=relay_sem.at[1],
        device_id=across,
        device_id_type=pl.DeviceIdType.MESH,
    )
    if relayed:
        relay.start()

    def remote(src, dst, send, recv, k):
        peer = jnp.bitwise_xor(me, k)
        return pltpu.make_async_remote_copy(
            src_ref=src,
            dst_ref=dst,
            send_sem=send.at[k],
            recv_sem=recv.at[k],
            device_id={"ep": peer},
            device_id_type=pl.DeviceIdType.MESH,
        )

    def row_copy(k):
        return remote(
            out_hbm.at[jnp.bitwise_xor(me, k)], in_hbm.at[me], send_sem, recv_sem, k
        )

    def back_copy(k):
        return remote(
            pull_hbm.at[jnp.bitwise_xor(me, k)], pulls_hbm.at[me], back_send, back_recv, k
        )

    def dot_copy(k):
        return remote(
            edot_hbm.at[jnp.bitwise_xor(me, k)], edots_hbm.at[me], dot_send, dot_recv, k
        )

    far = list(range(2 * quarter, peers))
    near = list(range(1, 2 * quarter))
    for k in far[:quarter] + near[quarter - 1 :] + far[quarter:] + near[: quarter - 1]:
        row_copy(k).start()
    own_rows = pltpu.make_async_copy(out_hbm.at[me], in_hbm.at[me], home_sem.at[0])
    own_rows.start()
    weight_copies[2].start()
    weight_copies[3].start()

    def outputs(routed, w1_ref, w2_ref):
        x = xb[...]
        g = gb[...].astype(F32)
        chances = router_and_mix(dot(x, rm_ref[...]), experts)
        if routed:
            gate = jnp.sum(chances * sel_ref[...], axis=-1, keepdims=True)
            dy = g * lane_of(chances, experts + 1) * gate
        else:
            dy = g * lane_of(chances, experts)
        dy = dy.astype(BF16)
        dyb[...] = dy
        dyt[...] = dy.T
        xt[...] = x.T

        def products(f, _):
            cols = pl.ds(pl.multiple_of(f * ft, ft), ft)
            w1 = w1_ref[:, cols]
            w2 = w2_ref[:, cols]
            act, slope = gelu_and_slope(dot(xb[...], w1))
            h = act.astype(BF16)
            pre_grad = (slope * dot(dyb[...], w2)).astype(BF16)
            hv[:, cols] = h
            pv[:, cols] = pre_grad
            ya[...] += dot_nt(h, w2)
            dxa[...] += dot_nt(pre_grad, w1)
            return 0

        ya[...] = jnp.zeros_like(ya)
        dxa[...] = jnp.zeros_like(dxa)
        lax.fori_loop(0, hidden // ft, products, 0)

    def row_dots():
        return jnp.sum(ya[...] * gb[...].astype(F32), axis=1, keepdims=True)

    def gradients(first, last=None):
        wide_step = ft

        def at(f):
            return pl.ds(pl.multiple_of(f * wide_step, wide_step), wide_step)

        def put(f, _):
            a2[:, at(f)] = dot(dyt[...], hv[:, at(f)])
            a1[:, at(f)] = dot(xt[...], pv[:, at(f)])
            return 0

        def add(f, _):
            a2[:, at(f)] += dot(dyt[...], hv[:, at(f)])
            a1[:, at(f)] += dot(xt[...], pv[:, at(f)])
            return 0

        def round_off(f, _):
            wd2[:, at(f)] = (a2[:, at(f)] + dot(dyt[...], hv[:, at(f)])).astype(BF16)
            wd1[:, at(f)] = (a1[:, at(f)] + dot(xt[...], pv[:, at(f)])).astype(BF16)
            return 0

        @pl.when(first)
        def _():
            lax.fori_loop(0, hidden // wide_step, put, 0)

        if last is None:
            middle = jnp.logical_not(first)
        else:
            middle = jnp.logical_not(first | last)

            @pl.when(last)
            def _():
                lax.fori_loop(0, hidden // wide_step, round_off, 0)

        @pl.when(middle)
        def _():
            lax.fori_loop(0, hidden // wide_step, add, 0)

    weight_copies[0].wait()
    weight_copies[1].wait()

    def dense_stores(t, slot):
        rows = pl.ds(pl.multiple_of(t * rb, rb), rb)
        return [
            pltpu.make_async_copy(yb, y_hbm.at[rows, :], store_sem.at[slot, 0, 0]),
            pltpu.make_async_copy(dxb, dx_hbm.at[rows, :], store_sem.at[slot, 1, 0]),
            pltpu.make_async_copy(dotb.at[slot], dot_hbm.at[rows, :], store_sem.at[slot, 2, 0]),
        ]

    def dense_step(t, _):
        slot = lax.rem(t, 2)
        for c in load(t):
            c.wait()
        outputs(False, wd1, wd2)

        @pl.when(t >= 1)
        def _():
            for c in dense_stores(t - 1, 1 - slot):
                c.wait()

        yb[...] = ya[...].astype(BF16)
        dxb[...] = dxa[...].astype(BF16)
        dotb[slot] = jnp.broadcast_to(row_dots(), (rb, LANES))

        @pl.when(t + 1 < dense_steps)
        def _():
            for c in load(t + 1):
                c.start()

        for c in dense_stores(t, slot):
            c.start()
        gradients(t == 0, t == dense_steps - 1)
        return 0

    lax.fori_loop(0, dense_steps, dense_step, 0)
    for c in dense_stores(dense_steps - 1, (dense_steps - 1) % 2):
        c.wait()

    dense_grads = [
        pltpu.make_async_copy(wd1, gd1_hbm, grad_sem.at[0]),
        pltpu.make_async_copy(wd2, gd2_hbm, grad_sem.at[1]),
    ]
    for c in dense_grads:
        c.start()
    weight_copies[2].wait()
    weight_copies[3].wait()
    own_rows.wait()
    if relayed:
        relay.wait()

    def first_of(p):
        if expert_steps != 4:
            return (expert_steps - 1 - p) * per
        return jnp.where(p == 0, 2, jnp.where(p == 1, 1, jnp.where(p == 2, 3, 0))) * per

    def swap_copy(p, j):
        slot = lax.rem(p, 2)
        return pltpu.make_async_remote_copy(
            src_ref=give.at[slot, j],
            dst_ref=got.at[slot, j],
            send_sem=swap_send.at[slot, j],
            recv_sem=swap_recv.at[slot, j],
            device_id=across,
            device_id_type=pl.DeviceIdType.MESH,
        )

    size = half if relayed else capacity

    def back_stores(p, j, source_ref):
        to = (pull_hbm, res_hbm)[j]
        return [
            pltpu.make_async_copy(
                source_ref.at[pl.ds(c * size, size), :],
                to.at[jnp.bitwise_xor(me, first_of(p) + c)],
                store_sem.at[0, j, c],
            )
            for c in range(per)
        ]

    def dot_stores(p):
        return [
            pltpu.make_async_copy(
                rowb.at[c], edot_hbm.at[jnp.bitwise_xor(me, first_of(p) + c)], store_sem.at[1, 2, c]
            )
            for c in range(per)
        ]

    def to_peers(p, copy):
        for c in range(per):
            k = first_of(p) + c

            @pl.when(k > 0)
            def _(k=k):
                copy(k).start()

    def sum_shares(p, j):
        swap_copy(p, j).wait()
        stage = (dxb, yb)[j]
        stage[: per * half, :] = (keep[j] + got[lax.rem(p, 2), j].astype(F32)).astype(BF16)
        for c in back_stores(p, j, stage):
            c.start()

    def stored(p, j, source_ref):
        for c in back_stores(p, j, source_ref):
            c.wait()

    def fetch(p):
        for c in range(per):
            k = first_of(p) + c

            @pl.when(k > 0)
            def _(k=k):
                row_copy(k).wait()

        for c in fetches(p):
            c.start()

    def fetches(p):
        loads = []
        for c in range(per):
            source = jnp.bitwise_xor(me, first_of(p) + c)
            rows = pl.ds(c * capacity, capacity)
            loads.append(
                pltpu.make_async_copy(in_hbm.at[source], xb.at[rows, :], load_sem.at[0, c])
            )
            if relayed:
                for j, src, which in ((1, gin_hbm, tp_me), (2, gin2_hbm, 1 - tp_me)):
                    at = pl.ds(pl.multiple_of(c * capacity + which * half, half), half)
                    loads.append(
                        pltpu.make_async_copy(
                            src.at[source], gb.at[at, :], load_sem.at[j, c]
                        )
                    )
            else:
                loads.append(
                    pltpu.make_async_copy(
                        gin_hbm.at[source], gb.at[rows, :], load_sem.at[1, c]
                    )
                )
        return loads

    fetch(0)

    def expert_step(p, _):
        slot = lax.rem(p, 2)
        for c in fetches(p):
            c.wait()
        outputs(True, we1, we2)
        across_dots = jnp.broadcast_to(row_dots(), (rb, LANES)).T
        for c in range(per):
            rowb[c] = across_dots[:8, c * capacity : (c + 1) * capacity]
        for c in dot_stores(p):
            c.start()
        if relayed:

            @pl.when(p > 0)
            def _():
                for j in range(2):
                    sum_shares(p - 1, j)

            for j, total in ((0, dxa), (1, ya)):
                for c in range(per):
                    rows = slice(c * half, (c + 1) * half)
                    at = pl.ds(pl.multiple_of(c * capacity + tp_me * half, half), half)
                    other = pl.ds(pl.multiple_of(c * capacity + (1 - tp_me) * half, half), half)
                    keep[j, rows, :] = total[at, :]
                    give[slot, j, rows, :] = total[other, :].astype(BF16)
                swap_copy(p, j).start()
        else:
            dxb[...] = dxa[...].astype(BF16)
            yb[...] = ya[...].astype(BF16)
            for j, source_ref in ((0, dxb), (1, yb)):
                for c in back_stores(p, j, source_ref):
                    c.start()

        @pl.when(p + 1 < expert_steps)
        def _():
            fetch(p + 1)

        gradients(p == 0)
        for c in dot_stores(p):
            c.wait()
        to_peers(p, dot_copy)
        if relayed:

            @pl.when(p > 0)
            def _():
                for j in range(2):
                    stored(p - 1, j, (dxb, yb)[j])
                to_peers(p - 1, back_copy)
        else:
            for j, source_ref in ((0, dxb), (1, yb)):
                stored(p, j, source_ref)
            to_peers(p, back_copy)
        return 0

    lax.fori_loop(0, expert_steps, expert_step, 0)
    expert_grads = [
        pltpu.make_async_copy(a1, ge1_hbm, local_sem.at[0]),
        pltpu.make_async_copy(a2, ge2_hbm, local_sem.at[1]),
        pltpu.make_async_copy(edot_hbm.at[me], edots_hbm.at[me], home_sem.at[2]),
    ]
    for c in expert_grads:
        c.start()
    if relayed:
        final = expert_steps - 1
        sum_shares(final, 0)
        stored(final, 0, dxb)
        to_peers(final, back_copy)
        sum_shares(final, 1)
        stored(final, 1, yb)
    own_back = pltpu.make_async_copy(pull_hbm.at[me], pulls_hbm.at[me], home_sem.at[1])
    own_back.start()
    for c in dense_grads + expert_grads + [own_back]:
        c.wait()
    for k in range(1, peers):
        back_copy(k).wait()
        dot_copy(k).wait()


def nets(x, g, out_rows, in_grads, sel, rm, dense_weights, expert_weights, rb=512, ft=512):
    rows, wide = x.shape
    hidden = dense_weights[0].shape[1]
    peers, capacity, _ = out_rows.shape
    per = rb // capacity
    anywhere = pl.BlockSpec(memory_space=pl.ANY)
    vmem = pl.BlockSpec(memory_space=pltpu.VMEM)
    sheet = jax.ShapeDtypeStruct((rows, wide), BF16)
    relayed = in_grads.shape[1] < capacity
    blocks = jax.ShapeDtypeStruct((peers, capacity, wide), BF16)
    backs = jax.ShapeDtypeStruct(in_grads.shape, BF16)
    part = (rb * in_grads.shape[1] // capacity, wide) if relayed else (16, wide)
    strips = jax.ShapeDtypeStruct((peers, 8, capacity), F32)
    return pl.pallas_call(
        partial(nets_kernel, peers=peers, capacity=capacity, rb=rb, ft=ft, relayed=relayed),
        in_specs=[anywhere] * 4 + [vmem] * 2 + [anywhere] * 4,
        out_specs=[anywhere] * 14,
        out_shape=[
            sheet,
            sheet,
            jax.ShapeDtypeStruct((rows, LANES), F32),
            jax.ShapeDtypeStruct((wide, hidden), BF16),
            jax.ShapeDtypeStruct((wide, hidden), BF16),
            jax.ShapeDtypeStruct((wide, hidden), F32),
            jax.ShapeDtypeStruct((wide, hidden), F32),
            blocks,
            backs,
            backs,
            strips,
            backs,
            strips,
            backs,
        ],
        scratch_shapes=[pltpu.VMEM((wide, hidden), BF16)] * 4
        + [pltpu.VMEM((wide, hidden), F32)] * 2
        + [pltpu.VMEM((rb, wide), BF16)] * 4
        + [
            pltpu.VMEM((2, rb, LANES), F32),
            pltpu.VMEM((per, 8, capacity), F32),
            pltpu.VMEM((rb, wide), F32),
            pltpu.VMEM((rb, wide), F32),
            pltpu.VMEM((rb, wide), BF16),
            pltpu.VMEM((wide, rb), BF16),
            pltpu.VMEM((wide, rb), BF16),
            pltpu.SemaphoreType.DMA((4,)),
            pltpu.SemaphoreType.DMA((3, per)),
            pltpu.SemaphoreType.DMA((2, 3, per)),
            pltpu.SemaphoreType.DMA((2,)),
            pltpu.SemaphoreType.DMA((3,)),
            pltpu.SemaphoreType.DMA((2,)),
        ]
        + [pltpu.SemaphoreType.DMA((peers,))] * 6
        + [
            pltpu.SemaphoreType.DMA((2,)),
            pltpu.SemaphoreType.DMA((2, 2)),
            pltpu.SemaphoreType.DMA((2, 2)),
            pltpu.VMEM((2, *part), F32),
            pltpu.VMEM((2, 2, *part), BF16),
            pltpu.VMEM((2, 2, *part), BF16),
            pltpu.VMEM((rb, hidden), BF16),
            pltpu.VMEM((rb, hidden), BF16),
        ],
        cost_estimate=cost(24 * rows * wide * hidden, 16 * rows * wide + 24 * wide * hidden),
        compiler_params=pltpu.CompilerParams(
            vmem_limit_bytes=67043328, collective_id=0, has_side_effects=True
        ),
        name="feed_forward_nets",
    )(x, g, out_rows, in_grads, sel, rm, *dense_weights, *expert_weights)


def expert_hot(place, capacity, experts):
    lane = lax.broadcasted_iota(jnp.int32, (place.shape[0], LANES), 1)
    low = lane * capacity
    return ((place >= low) & (place < low + capacity) & (lane < experts)).astype(F32)


def ffn_pull_kernel(*refs, parts, experts, capacity, shard, sent, outs):
    (
        info_ref,
        dx_ref,
        chance_ref,
        first_ref,
        f_ref,
        g_ref,
        resid_ref,
        gain_ref,
        rm_ref,
        slot_ref,
        dots_ref,
    ) = refs[:11]
    heads_out = refs[11 : 11 + outs]
    refs = refs[11 + outs :]
    weights = refs[:parts]
    r_ref = refs[parts]
    heads = list(refs[1 + parts : 1 + 2 * parts])
    sums_ref, rmg_ref, outer_ref, outer_acc = (
        *refs[1 + 2 * parts : 4 + 2 * parts],
        refs[4 + 2 * parts],
    )
    size = info_ref.shape[0]
    step = pl.program_id(0)
    if sent is not None:
        give, send_sem, recv_sem = refs[5 + 2 * parts :]
        got = heads[sent]
        across = {"tp": 1 - lax.axis_index("tp")}
        mesh = pl.DeviceIdType.MESH

        def share(b):
            at = pl.ds(pl.multiple_of(b * size, size), size)
            return pltpu.make_async_remote_copy(
                src_ref=give.at[at, :],
                dst_ref=got.at[at, :],
                send_sem=send_sem.at[b],
                recv_sem=recv_sem.at[b],
                device_id=across,
                device_id_type=mesh,
            )

        @pl.when(step == 0)
        def _():
            barrier = pltpu.get_barrier_semaphore()
            pl.semaphore_signal(barrier, inc=1, device_id=across, device_id_type=mesh)
            pl.semaphore_wait(barrier, 1)

    place = info_ref[:, 0:1].astype(jnp.int32)
    here = info_ref[:, 1:2].astype(jnp.int32)
    row = step * size + lax.broadcasted_iota(jnp.int32, (size, 1), 0)
    row = row - lax.axis_index("tp") * shard
    own = ((row >= 0) & (row < shard)).astype(F32)
    chances = chance_ref[...]
    hot = expert_hot(place, capacity, experts)
    gate = jnp.sum(hot * chances, axis=-1, keepdims=True)
    mix_0, mix_1 = lane_of(chances, experts), lane_of(chances, experts + 1)
    table = jnp.dot(
        hot, dots_ref[...], precision=lax.Precision.HIGHEST, preferred_element_type=F32
    )
    slot = lax.broadcasted_iota(jnp.int32, table.shape, 1)
    number = jnp.sum(hot * lax.broadcasted_iota(jnp.int32, hot.shape, 1).astype(F32), axis=-1)
    inside = place - number.astype(jnp.int32)[:, None] * capacity
    second = jnp.sum(jnp.where(slot == inside, table, 0.0), axis=-1, keepdims=True)
    first = lane_of(first_ref[...], 0)
    grad_0, grad_1 = first, gate * second
    inner = mix_0 * grad_0 + mix_1 * grad_1
    lane = lax.broadcasted_iota(jnp.int32, chances.shape, 1)
    low = (mix_1 * second * gate) * (hot - chances)
    low = jnp.where(lane == experts, mix_0 * (grad_0 - inner), low)
    low = jnp.where(lane == experts + 1, mix_1 * (grad_1 - inner), low)
    low = jnp.where(lane > experts + 1, 0.0, low).astype(BF16)
    grad = dx_ref[...].astype(F32) + unpacked(here, slot_ref) + dot_nt(low, rm_ref[...])
    normal, rstd = normalized(resid_ref[...])
    r = norm_pull(grad, normal, rstd, gain_ref[2:3, :]) + own * g_ref[...].astype(F32)
    r = r.astype(BF16)
    r_ref[...] = r
    if sent is not None:
        at = pl.ds(pl.multiple_of(step * size, size), size)
        give[at, :] = dot(r, weights[sent][...]).astype(BF16)
        share(step).start()
    for j, (h, w) in enumerate(zip(heads, weights)):
        if j != sent:
            h[...] = dot(r, w[...]).astype(BF16)

    @pl.when(pl.program_id(0) == 0)
    def _():
        sums_ref[...] = jnp.zeros_like(sums_ref)
        rmg_ref[...] = jnp.zeros_like(rmg_ref)
        outer_acc[...] = jnp.zeros_like(outer_acc)

    sums_ref[0:1, :] += jnp.sum(grad * normal, axis=0, keepdims=True)
    sums_ref[1:2, :] += jnp.sum(grad, axis=0, keepdims=True)
    rmg_ref[...] += dot(low.T, f_ref[...])
    left = r.T
    col = 0
    for h in heads_out:
        outer_acc[:, col : col + h.shape[1]] += dot(left, h[...])
        col += h.shape[1]

    @pl.when(step == pl.num_programs(0) - 1)
    def _():
        outer_ref[...] = outer_acc[...].astype(BF16)

    if sent is not None:

        @pl.when(step == pl.num_programs(0) - 1)
        def _():
            for b in range(give.shape[0] // size):
                share(b).wait()


def ffn_pull(
    info,
    dx,
    chances,
    first,
    f,
    g,
    resid,
    gain,
    rm,
    slot_rows,
    dots,
    heads,
    weights,
    experts,
    shard,
    sent=None,
    rb=512,
):
    rows, wide = dx.shape
    capacity = dots.shape[1]
    dots = jnp.pad(dots, ((0, LANES - experts), (0, 0)))
    block = pl.BlockSpec((rb, wide), lambda i: (i, 0))
    narrow = pl.BlockSpec((rb, LANES), lambda i: (i, 0))
    head_specs = [
        pl.BlockSpec(memory_space=pl.ANY) if j == sent else pl.BlockSpec((rb, size), lambda i: (i, 0))
        for j, (_, _, size) in enumerate(weights)
    ]
    outer_width = sum(h.shape[1] for h in heads)
    scratch, extra = [pltpu.VMEM((wide, outer_width), F32)], {}
    if sent is not None:
        scratch += [
            pltpu.VMEM((rows, weights[sent][2]), BF16),
            pltpu.SemaphoreType.DMA((rows // rb,)),
            pltpu.SemaphoreType.DMA((rows // rb,)),
        ]
        extra = dict(collective_id=3, has_side_effects=True)
    return pl.pallas_call(
        partial(
            ffn_pull_kernel,
            parts=len(weights),
            experts=experts,
            capacity=capacity,
            shard=shard,
            sent=sent,
            outs=len(heads),
        ),
        grid=(rows // rb,),
        in_specs=[narrow, block, narrow, narrow, block, block, block]
        + [resident(gain.shape), resident((wide, LANES))]
        + [resident(slot_rows.shape), resident(dots.shape)]
        + [pl.BlockSpec((rb, h.shape[1]), lambda i: (i, 0)) for h in heads]
        + [
            pl.BlockSpec((wide, size), lambda i, j=j: (0, j), pipeline_mode=pl.Buffered(1))
            for _, j, size in weights
        ],
        out_specs=[block]
        + head_specs
        + [resident((8, wide)), resident((LANES, wide)), resident((wide, outer_width))],
        out_shape=[jax.ShapeDtypeStruct((rows, wide), BF16)]
        + [jax.ShapeDtypeStruct((rows, size), BF16) for _, _, size in weights]
        + [jax.ShapeDtypeStruct((8, wide), F32), jax.ShapeDtypeStruct((LANES, wide), F32)]
        + [jax.ShapeDtypeStruct((wide, outer_width), BF16)],
        scratch_shapes=scratch,
        cost_estimate=cost(6 * rows * wide * wide, 16 * rows * wide),
        compiler_params=pltpu.CompilerParams(vmem_limit_bytes=56 * 1024 * 1024, **extra),
        name="ffn_norm_pull",
    )(
        info,
        dx,
        chances,
        first,
        f,
        g,
        resid,
        gain,
        rm,
        slot_rows,
        dots,
        *heads,
        *[w for w, _, _ in weights],
    )


def outer_kernel(left_ref, *refs, parts):
    rights = refs[:parts]
    o_ref, acc_ref = refs[parts:]

    @pl.when(pl.program_id(0) == 0)
    def _():
        acc_ref[...] = jnp.zeros_like(acc_ref)

    left = left_ref[...].T
    at = 0
    for r in rights:
        width = r.shape[1]
        acc_ref[:, at : at + width] += dot(left, r[...])
        at += width

    @pl.when(pl.program_id(0) == pl.num_programs(0) - 1)
    def _():
        o_ref[...] = acc_ref[...].astype(BF16)


def outer(left, rights, rb=512):
    rows, wide = left.shape
    total = sum(r.shape[1] for r in rights)
    return pl.pallas_call(
        partial(outer_kernel, parts=len(rights)),
        grid=(rows // rb,),
        in_specs=[pl.BlockSpec((rb, wide), lambda i: (i, 0))]
        + [pl.BlockSpec((rb, r.shape[1]), lambda i: (i, 0)) for r in rights],
        out_specs=resident((wide, total)),
        out_shape=jax.ShapeDtypeStruct((wide, total), BF16),
        scratch_shapes=[pltpu.VMEM((wide, total), F32)],
        cost_estimate=cost(2 * rows * wide * total, 2 * rows * (wide + total)),
        name="outer_product",
    )(left, *rights)


def attn_pull_kernel(at_ref, x_ref, r_ref, gain_ref, *refs, groups):
    grads = refs[: 3 * groups]
    weights = refs[3 * groups : 3 * groups + 3]
    t_ref, sums_ref = refs[3 * groups + 3 :]
    del at_ref
    total = None
    for k in range(3):
        at = 0
        for j in range(groups):
            d = grads[k * groups + j]
            width = d.shape[1]
            part = dot_nt(d[...], weights[k][:, at : at + width])
            total = part if total is None else total + part
            at += width
    normal, rstd = normalized(x_ref[...].astype(F32))
    t = norm_pull(total, normal, rstd, gain_ref[...]) + r_ref[...].astype(F32)
    t_ref[...] = t.astype(t_ref.dtype)

    @pl.when(pl.program_id(0) == 0)
    def _():
        sums_ref[...] = jnp.zeros_like(sums_ref)

    sums_ref[0:1, :] += jnp.sum(total * normal, axis=0, keepdims=True)
    sums_ref[1:2, :] += jnp.sum(total, axis=0, keepdims=True)


def attn_pull(first_row, count, x, r, gain, grads, weights, out_type, rb=256):
    wide = x.shape[1]
    groups = len(grads) // 3

    def rows(width):
        return pl.BlockSpec((rb, width), lambda i, at: (at[0] + i, 0))

    return pl.pallas_call(
        partial(attn_pull_kernel, groups=groups),
        grid_spec=pltpu.PrefetchScalarGridSpec(
            num_scalar_prefetch=1,
            grid=(count // rb,),
            in_specs=[rows(wide), rows(wide), resident((1, wide))]
            + [rows(d.shape[1]) for d in grads]
            + [resident(w.shape) for w in weights],
            out_specs=[pl.BlockSpec((rb, wide), lambda i, at: (i, 0)), resident((8, wide))],
        ),
        out_shape=[
            jax.ShapeDtypeStruct((count, wide), out_type),
            jax.ShapeDtypeStruct((8, wide), F32),
        ],
        cost_estimate=cost(6 * count * wide * weights[0].shape[1], 10 * count * wide),
        name="attention_norm_pull",
    )((first_row // rb).astype(jnp.int32).reshape(1), x, r, gain, *grads, *weights)


def combine_kernel(
    at_ref, info_ref, y_ref, chance_ref, slot_ref, other_ref, own_ref, *, experts, capacity
):
    del at_ref
    place = info_ref[:, 0:1].astype(jnp.int32)
    here = info_ref[:, 1:2].astype(jnp.int32)
    chances = chance_ref[...]
    gate = jnp.sum(expert_hot(place, capacity, experts) * chances, axis=-1, keepdims=True)
    moe = unpacked(here, slot_ref) * (lane_of(chances, experts + 1) * gate)
    total = (lane_of(chances, experts) * y_ref[...].astype(F32) + moe).astype(BF16)
    first = pl.program_id(0) < pl.num_programs(0) // 2

    @pl.when(first)
    def _():
        other_ref[...] = total

    @pl.when(jnp.logical_not(first))
    def _():
        own_ref[...] = total


def combine(first_row, info, y, coef, slot_rows, experts, capacity, rb=512):
    rows, wide = y.shape
    half = rows // rb // 2

    def block(width):
        return pl.BlockSpec((rb, width), lambda i, at: (lax.rem(at[0] + half + i, 2 * half), 0))

    part = jax.ShapeDtypeStruct((rows // 2, wide), BF16)
    return pl.pallas_call(
        partial(combine_kernel, experts=experts, capacity=capacity),
        grid_spec=pltpu.PrefetchScalarGridSpec(
            num_scalar_prefetch=1,
            grid=(2 * half,),
            in_specs=[block(LANES), block(wide), block(LANES), resident(slot_rows.shape)],
            out_specs=[
                pl.BlockSpec((rb, wide), lambda i, _: (jnp.minimum(i, half - 1), 0)),
                pl.BlockSpec((rb, wide), lambda i, _: (jnp.maximum(i - half, 0), 0)),
            ],
        ),
        out_shape=[part, part],
        cost_estimate=cost(4 * rows * wide * wide, 8 * rows * wide),
        name="combine_nets",
    )((first_row // rb).astype(jnp.int32).reshape(1), info, y, coef, slot_rows)


class Halving:
    def __init__(self, total, gives, gots, send, recv, me, size, order):
        self.total, self.gives, self.gots = total, gives, gots
        self.send, self.recv, self.me, self.size = send, recv, me, size
        self.order = order
        self.rows = total.shape[0] // size

    def block(self, index):
        return pl.ds(pl.multiple_of(index * self.rows, self.rows), self.rows)

    def copy(self, s):
        return pltpu.make_async_remote_copy(
            src_ref=self.gives[s],
            dst_ref=self.gots[s],
            send_sem=self.send.at[s],
            recv_sem=self.recv.at[s],
            device_id={"ep": jnp.bitwise_xor(self.me, 1 << self.order[s])},
            device_id_type=pl.DeviceIdType.MESH,
        )

    def bit(self, s):
        return lax.rem(lax.div(self.me, 1 << self.order[s]), 2)

    def each(self, s, body):
        place = sum(1 for b in self.order[s:] if b < self.order[s])
        low = 1 << place

        def step(i, _):
            body(self.block(i), lax.div(i, low) * (2 * low) + lax.rem(i, low), low)
            return 0

        lax.fori_loop(0, self.size >> (s + 1), step, 0)

    def start(self, s):
        def give(rows, at, step):
            other = self.total[self.block(at + (1 - self.bit(s)) * step), :]
            self.gives[s][rows, :] = other.astype(BF16)

        self.each(s, give)
        self.copy(s).start()

    def finish(self, s):
        self.copy(s).wait()

        def keep(rows, at, step):
            kept = self.total[self.block(at + self.bit(s) * step), :]
            self.total[rows, :] = kept + self.gots[s][rows, :].astype(F32)

        self.each(s, keep)

    def step(self, s):
        self.finish(s)
        if s + 1 < len(self.order):
            self.start(s + 1)


class Rounds:
    def __init__(self, total, gives, gots, send, recv, me, tp_me):
        self.total, self.gives, self.gots = total, gives, gots
        self.send, self.recv, self.me, self.tp_me = send, recv, me, tp_me

    def copy(self, s):
        peer = {"tp": 1 - self.tp_me} if s == 0 else {"ep": jnp.bitwise_xor(self.me, 1 << (s - 1))}
        return pltpu.make_async_remote_copy(
            src_ref=self.gives[s],
            dst_ref=self.gots[s],
            send_sem=self.send.at[s],
            recv_sem=self.recv.at[s],
            device_id=peer,
            device_id_type=pl.DeviceIdType.MESH,
        )

    def start(self, s):
        self.gives[s][...] = self.total[...]
        self.copy(s).start()

    def finish(self, s):
        self.copy(s).wait()
        self.total[...] += self.gots[s][...]

    def step(self, s):
        self.finish(s)
        if s + 1 < len(self.gives):
            self.start(s + 1)


def tail_kernel(*refs, groups, size, rb, small_rows):
    refs = list(refs)

    def take(count):
        taken = refs[:count]
        del refs[:count]
        return taken

    x_hbm, r_hbm, a_hbm, out_hbm = take(4)
    grads_hbm = take(3 * groups)
    small_ref, gain_ref = take(2)
    weights = take(3)
    own_hbm, got_hbm, square_ref, outsum_ref, total_ref = take(5)
    xv, rv, av = take(3)
    grads = take(3 * groups)
    gov, acc_a, acc_b, goacc, give_rows, own_buf = take(6)
    steps = size.bit_length() - 1
    hops = steps + 1
    gives, gots = take(steps), take(steps)
    gives_b, gots_b = take(steps), take(steps)
    go_gives, go_gots = take(steps), take(steps)
    small_gives, small_gots = take(hops), take(hops)
    late_gives, late_gots = take(hops), take(hops)
    (
        load_sem,
        own_sem,
        row_send,
        row_recv,
        half_send,
        half_recv,
        half_send_b,
        half_recv_b,
        go_send,
        go_recv,
        small_send,
        small_recv,
        late_send,
        late_recv,
        out_sem,
        out_give,
        out_got,
    ) = refs
    me = lax.axis_index("ep")
    tp_me = lax.axis_index("tp")
    rows = x_hbm.shape[0]
    shard = rows // 2
    count = shard // rb

    out_load = pltpu.make_async_copy(out_hbm, gov, load_sem.at[0, 0])
    a_load = pltpu.make_async_copy(a_hbm, av, load_sem.at[1, 0])

    def loads(which, line):
        at = pl.ds(pl.multiple_of(which * shard, shard), shard)
        return [
            pltpu.make_async_copy(
                src.at[at, :], dst.at[at, :], load_sem.at[line, j + 1]
            )
            for j, (src, dst) in enumerate(zip([x_hbm, r_hbm, *grads_hbm], [xv, rv, *grads]))
        ]

    theirs_loads, own_loads = loads(1 - tp_me, 0), loads(tp_me, 1)
    for c in theirs_loads:
        c.start()
    out_load.start()
    for c in own_loads:
        c.start()
    a_load.start()

    barrier = pltpu.get_barrier_semaphore()
    mesh = pl.DeviceIdType.MESH
    pl.semaphore_signal(barrier, inc=1, device_id={"tp": 1 - tp_me}, device_id_type=mesh)
    for s in range(steps):
        pl.semaphore_signal(
            barrier, inc=1, device_id={"ep": jnp.bitwise_xor(me, 1 << s)}, device_id_type=mesh
        )
    pl.semaphore_wait(barrier, hops)

    order = list(range(steps))
    other_order = [0, 2, 1] + order[3:] if steps > 2 else order
    qkv = [
        Halving(acc_a, gives, gots, half_send, half_recv, me, size, order),
        Halving(acc_b, gives_b, gots_b, half_send_b, half_recv_b, me, size, other_order),
    ]
    go = Halving(goacc, go_gives, go_gots, go_send, go_recv, me, size, order)
    early = Rounds(
        total_ref.at[:small_rows, :], small_gives, small_gots, small_send, small_recv, me, tp_me
    )
    late = Rounds(
        total_ref.at[small_rows:, :], late_gives, late_gots, late_send, late_recv, me, tp_me
    )

    for c in theirs_loads:
        c.wait()

    total_ref[:small_rows, :] = small_ref[...]
    total_ref[small_rows:, :] = jnp.zeros((8, total_ref.shape[1]), F32)
    early.start(0)

    def pulled(at):
        total = None
        for k in range(3):
            col = 0
            for j in range(groups):
                d = grads[k * groups + j][at, :]
                width = d.shape[1]
                part = dot_nt(d, weights[k][:, col : col + width])
                total = part if total is None else total + part
                col += width
        normal, rstd = normalized(xv[at, :].astype(F32))
        total_ref[small_rows : small_rows + 1, :] += jnp.sum(total * normal, axis=0, keepdims=True)
        total_ref[small_rows + 1 : small_rows + 2, :] += jnp.sum(total, axis=0, keepdims=True)
        return norm_pull(total, normal, rstd, gain_ref[0:1, :]) + rv[at, :].astype(F32)

    def row_copy(b):
        at = pl.ds(pl.multiple_of(b * rb, rb), rb)
        return pltpu.make_async_remote_copy(
            src_ref=give_rows.at[at, :],
            dst_ref=got_hbm.at[at, :],
            send_sem=row_send.at[b],
            recv_sem=row_recv.at[b],
            device_id={"tp": 1 - tp_me},
            device_id_type=mesh,
        )

    def theirs(b, _):
        at = pl.ds(pl.multiple_of((1 - tp_me) * shard + b * rb, rb), rb)
        give_rows[pl.ds(pl.multiple_of(b * rb, rb), rb), :] = pulled(at).astype(BF16)
        row_copy(b).start()
        return 0

    lax.fori_loop(0, count // 2, theirs, 0)
    out_load.wait()
    goacc[...] = gov[...].astype(F32)
    go.start(0)
    early.step(0)
    for c in own_loads + [a_load]:
        c.wait()
    cut = len(grads) // 2
    for acc in (acc_a, acc_b):
        acc[...] = jnp.zeros_like(acc)

    for acc, some, chain in ((acc_a, grads[:cut], qkv[0]), (acc_b, grads[cut:], qkv[1])):

        def outer_step(b, _, acc=acc, some=some):
            at = pl.ds(pl.multiple_of(b * 512, 512), 512)
            left = av[at, :].T
            col = 0
            for g in some:
                width = g.shape[1]
                acc[:, col : col + width] += dot(left, g[at, :])
                col += width
            return 0

        lax.fori_loop(0, rows // 512, outer_step, 0)
        chain.start(0)
        if chain is qkv[0]:
            go.step(0)
            early.step(1)
    qkv[0].step(0)
    early.step(2)
    lax.fori_loop(count // 2, count, theirs, 0)

    def own_copy(b):
        at = pl.ds(pl.multiple_of(b * rb, rb), rb)
        return pltpu.make_async_copy(own_buf.at[at, :], own_hbm.at[at, :], own_sem.at[b])

    def own_step(b, _):
        at = pl.ds(pl.multiple_of(tp_me * shard + b * rb, rb), rb)
        own_buf[pl.ds(pl.multiple_of(b * rb, rb), rb), :] = pulled(at)
        own_copy(b).start()
        return 0

    qkv[1].step(0)
    early.step(3)
    lax.fori_loop(0, count // 2, own_step, 0)
    go.step(1)
    qkv[0].step(1)
    for s in range(4, hops):
        early.step(s)
    lax.fori_loop(count // 2, count, own_step, 0)

    for s in range(hops):
        late.start(s)
        if s + 2 < steps:
            go.step(s + 2)
        if s == 1:
            qkv[1].step(1)
            qkv[0].step(2)
        if s == 2:
            qkv[1].step(2)
        late.finish(s)
        if s == max(0, steps - 3):
            own_width = outsum_ref.shape[1]
            out_give[...] = goacc[: goacc.shape[0] // size, own_width:].astype(BF16)
            out_copy = pltpu.make_async_remote_copy(
                src_ref=out_give,
                dst_ref=out_got,
                send_sem=out_sem.at[0],
                recv_sem=out_sem.at[1],
                device_id={"tp": 1 - tp_me},
                device_id_type=mesh,
            )
            out_copy.start()
    for chain in qkv:
        for s in range(3, steps):
            chain.step(s)
    col = 0
    for acc in (acc_a, acc_b):
        square_ref[:, col : col + acc.shape[1]] = acc[: acc.shape[0] // size, :]
        col += acc.shape[1]
    out_copy.wait()
    outsum_ref[...] = goacc[: goacc.shape[0] // size, :own_width] + out_got[...].astype(F32)
    for b in range(count):
        own_copy(b).wait()
        row_copy(b).wait()


def tail(x, r, a, out_part, grads, small, gain, weights, size, rb=256):
    rows, wide = x.shape
    shard = rows // 2
    groups = len(grads) // 3
    total = sum(g.shape[1] for g in grads)
    out_width = out_part.shape[1]
    small_rows = small.shape[0]
    steps = size.bit_length() - 1
    kept = wide // size
    anywhere = pl.BlockSpec(memory_space=pl.ANY)
    vmem = pl.BlockSpec(memory_space=pltpu.VMEM)

    def halves(width):
        return [pltpu.VMEM((wide >> (s + 1), width), BF16) for s in range(steps)]

    return pl.pallas_call(
        partial(tail_kernel, groups=groups, size=size, rb=rb, small_rows=small_rows),
        in_specs=[anywhere] * (4 + 3 * groups) + [vmem] * 5,
        out_specs=[anywhere, anywhere, vmem, vmem, vmem],
        out_shape=[
            jax.ShapeDtypeStruct((shard, wide), F32),
            jax.ShapeDtypeStruct((shard, wide), BF16),
            jax.ShapeDtypeStruct((kept, total), F32),
            jax.ShapeDtypeStruct((kept, out_width // 2), F32),
            jax.ShapeDtypeStruct((small_rows + 8, wide), F32),
        ],
        scratch_shapes=[pltpu.VMEM((rows, wide), BF16)] * 3
        + [pltpu.VMEM(g.shape, BF16) for g in grads]
        + [
            pltpu.VMEM((wide, out_width), BF16),
            pltpu.VMEM((wide, total // 2), F32),
            pltpu.VMEM((wide, total // 2), F32),
            pltpu.VMEM((wide, out_width), F32),
            pltpu.VMEM((shard, wide), BF16),
            pltpu.VMEM((shard, wide), F32),
        ]
        + halves(total // 2) * 4
        + halves(out_width) * 2
        + [pltpu.VMEM((small_rows, wide), F32)] * (2 * (steps + 1))
        + [pltpu.VMEM((8, wide), F32)] * (2 * (steps + 1))
        + [
            pltpu.SemaphoreType.DMA((2, 3 + 3 * groups)),
            pltpu.SemaphoreType.DMA((shard // rb,)),
            pltpu.SemaphoreType.DMA((shard // rb,)),
            pltpu.SemaphoreType.DMA((shard // rb,)),
        ]
        + [pltpu.SemaphoreType.DMA((steps,))] * 6
        + [pltpu.SemaphoreType.DMA((steps + 1,))] * 4
        + [
            pltpu.SemaphoreType.DMA((2,)),
            pltpu.VMEM((kept, out_width // 2), BF16),
            pltpu.VMEM((kept, out_width // 2), BF16),
        ],
        cost_estimate=cost(12 * rows * wide * total // 3, 16 * rows * wide),
        compiler_params=pltpu.CompilerParams(
            vmem_limit_bytes=BIG_VMEM, collective_id=1, has_side_effects=True
        ),
        name="backward_tail",
    )(x, r, a, out_part, *grads, small, gain, *weights)


def results_kernel(
    at_ref,
    len_ref,
    own_ref,
    got_ref,
    resid_ref,
    mine_ref,
    theirs_ref,
    square_ref,
    small_ref,
    h_ref,
    r_ref,
    token_ref,
    block_ref,
    q_ref,
    k_ref,
    v_ref,
    gh_ref,
    gr_ref,
    router_ref,
    mix_ref,
    gain1_ref,
    bias1_ref,
    gain2_ref,
    bias2_ref,
    *,
    length,
):
    token_ref[...] = own_ref[...] + got_ref[...].astype(F32)
    size = own_ref.shape[0]
    position = (at_ref[0] + pl.program_id(0)) * size + lax.broadcasted_iota(jnp.int32, own_ref.shape, 0)
    live = None
    for s in range(len_ref.shape[0]):
        inside = (position >= s * length) & (position < s * length + len_ref[s])
        live = inside if live is None else live | inside
    nets_sum = mine_ref[...].astype(F32) + theirs_ref[...].astype(F32)
    block_ref[...] = jnp.where(live, resid_ref[...] + nets_sum, 0.0).astype(BF16)

    @pl.when(pl.program_id(0) == 0)
    def _():
        width = q_ref.shape[1]
        for j, ref in enumerate((q_ref, k_ref, v_ref)):
            ref[...] = square_ref[:, j * width : (j + 1) * width]
        gh_ref[...] = h_ref[...].astype(F32)
        gr_ref[...] = r_ref[...].astype(F32)
        experts = router_ref.shape[0]
        router_ref[...] = small_ref[8 : 8 + experts, :]
        mix_ref[...] = small_ref[8 + experts : 10 + experts, :]
        end = small_ref.shape[0] - 8
        for ref, at in ((gain1_ref, end), (bias1_ref, end + 1), (gain2_ref, 0), (bias2_ref, 1)):
            ref[...] = small_ref[at : at + 1, :]


def results(first_row, lengths, own, got, resid, weighted, theirs, square, small, gh, gr, experts, rb=256):
    rows, wide = own.shape
    kept, width = square.shape[0], square.shape[1] // 3
    block = pl.BlockSpec((rb, wide), lambda i, *_: (i, 0))
    shifted = pl.BlockSpec((rb, wide), lambda i, at, _: (at[0] + i, 0))
    shapes = [(kept, width)] * 3 + [gh.shape, gr.shape, (experts, wide), (2, wide)] + [(1, wide)] * 4
    return pl.pallas_call(
        partial(results_kernel, length=resid.shape[0] // lengths.shape[0]),
        grid_spec=pltpu.PrefetchScalarGridSpec(
            num_scalar_prefetch=2,
            grid=(rows // rb,),
            in_specs=[block, block, shifted, block, block]
            + [resident(v.shape) for v in (square, small, gh, gr)],
            out_specs=[block, block] + [resident(s) for s in shapes],
        ),
        out_shape=[jax.ShapeDtypeStruct((rows, wide), F32), jax.ShapeDtypeStruct((rows, wide), BF16)]
        + [jax.ShapeDtypeStruct(s, F32) for s in shapes],
        cost_estimate=cost(rows * wide, 22 * rows * wide),
        name="results",
    )(
        (first_row // rb).astype(jnp.int32).reshape(1),
        lengths,
        own,
        got,
        resid,
        weighted,
        theirs,
        square,
        small,
        gh,
        gr,
    )


def on_device(
    sizes,
    tokens,
    out_grad,
    lengths,
    expert_ids,
    w_query,
    w_key,
    w_value,
    w_output,
    w_hidden,
    w_return,
    router,
    mix_weight,
    gain_attn,
    bias_attn,
    gain_ffn,
    bias_ffn,
    expert_in,
    expert_out,
):
    tp, ep = sizes
    shard_rows = out_grad.shape[0]
    all_rows = tokens.shape[0]
    model_width = tokens.shape[1]
    experts = router.shape[1]
    capacity = all_rows // experts
    seq_count = lengths.shape[0]
    seq_len = all_rows // seq_count
    local_width = w_query.shape[1]
    local_heads = local_width // HEAD_DIM
    pairs = local_heads // 2
    splits = 2 if pairs % 2 == 0 else 1
    each = pairs // splits
    tp_index = lax.axis_index("tp")
    ep_index = lax.axis_index("ep")
    first_row = tp_index * shard_rows
    swap = [(0, 1), (1, 0)]

    def shard_of(values, axis=0):
        return lax.dynamic_slice_in_dim(values, first_row, shard_rows, axis)

    def swapped(values):
        return lax.ppermute(values, "tp", swap)

    def exchange(values):
        return lax.all_to_all(values, "ep", split_axis=0, concat_axis=0, tiled=True)

    def after(values, *others):
        return lax.optimization_barrier((values, others))[0]

    def summed_over(values, axis, size):
        step = 1
        while step < size:
            values = values + lax.ppermute(values, axis, [(i, i ^ step) for i in range(size)])
            step *= 2
        return values

    def over_sequences(values):
        return lax.psum_scatter(values, "ep", scatter_dimension=0, tiled=True)

    positions = jnp.arange(all_rows)
    seq_index = positions // seq_len
    row_limit = jnp.sum(
        jnp.where(seq_index[:, None] == jnp.arange(seq_count)[None, :], lengths[None, :], 0), axis=1
    )
    live_all = positions % seq_len < row_limit
    slot_count = experts * capacity
    blocks = (experts, capacity, model_width)

    rm = jnp.pad(
        jnp.concatenate([router, mix_weight], axis=1), ((0, 0), (0, LANES - experts - 2))
    )
    norms = jnp.concatenate([gain_attn, bias_attn, gain_ffn, bias_ffn]).astype(F32)
    norms = norms.reshape(4, model_width)
    projections = (w_query, w_key, w_value)
    if tp == 2:
        (
            attn_in,
            projected,
            heads,
            others,
            w_other,
            grad_all,
            resid,
            ffn_in,
            chances,
            packed,
            grad_rows,
            info,
            lse,
        ) = front(
            tokens,
            out_grad,
            (*projections, w_output),
            lengths,
            norms,
            rm,
            expert_ids[None, :],
            ep,
            experts,
            capacity,
        )
        all_heads = [heads, others]
        wide_weights = [(w, s, each * PAIR) for w in (w_output, w_other) for s in range(splits)]
    else:
        one_hot = (expert_ids[:, None] == jnp.arange(experts)[None, :]) & live_all[:, None]
        routed = one_hot.astype(F32)
        slots = jnp.sum((jnp.cumsum(routed, axis=0) - routed) * routed, axis=1).astype(jnp.int32)
        sound = live_all & (slots < capacity)
        place = jnp.where(sound, expert_ids * capacity + slots, -1)
        place_row = place[None, :]
        info = jnp.broadcast_to(place[:, None], (all_rows, LANES)).astype(F32)
        live_grad = jnp.where(shard_of(live_all)[:, None], out_grad, jnp.zeros_like(out_grad))
        w_all = lax.all_gather(w_output, "tp", axis=1, tiled=True)
        grad_all = lax.all_gather(live_grad, "tp", axis=0, tiled=True)
        grad_rows = exchange(pack(place_row, grad_all, slot_count).reshape(blocks))
        attn_in, projected = norm_project(tokens, norms[0:1], norms[1:2], projections)
        heads, lse = attention_forward(projected, seq_count, local_heads, 0, pairs)
        all_heads = [lax.all_gather(heads, "tp", axis=1, tiled=True)]
        wide_weights = [(w_all, 0, model_width)]
        resid, ffn_in, chances = output_norm(
            tokens, norms[2:3], norms[3:4], rm, all_heads, [(w_all, 0)], experts
        )
        packed = pack(place_row, ffn_in, slot_count)

    sel = (jnp.arange(LANES) == ep_index).astype(F32)[None, :]
    (
        dense,
        dense_pull,
        first_dot,
        grad_hidden,
        grad_return,
        grad_expert_in,
        grad_expert_out,
        _,
        sums_back,
        _,
        _,
        pulls,
        dots,
        _,
    ) = nets(
        ffn_in,
        grad_all,
        packed.reshape(blocks),
        grad_rows,
        sel,
        rm,
        (w_hidden, w_return),
        (expert_in[0], expert_out[0]),
    )
    returned = exchange(sums_back).reshape(-1, model_width)
    pulls = pulls.reshape(-1, model_width)
    dots = dots[:, 0, :]
    part, *rest = ffn_pull(
        info,
        dense_pull,
        chances,
        first_dot,
        ffn_in,
        grad_all,
        resid,
        norms,
        rm,
        pulls,
        dots,
        all_heads,
        wide_weights,
        experts,
        shard_rows,
        sent=splits if tp == 2 else None,
    )
    *head_parts, ffn_sums, rm_sums, out_part = rest
    if tp == 2:
        head_grads = [
            [m, o if s == 0 else swapped(o)]
            for s, (m, o) in enumerate(zip(head_parts[:splits], head_parts[splits:]))
        ]
    else:
        local = lax.psum_scatter(head_parts[0], "tp", scatter_dimension=1, tiled=True)
        head_grads = [
            [local[:, s * each * PAIR : (s + 1) * each * PAIR]] for s in range(splits)
        ]
    grad_hidden = over_sequences(grad_hidden)
    grad_return = over_sequences(grad_return)

    expert_grads = [grad_expert_in, grad_expert_out]
    pull_heads = partial(
        attention_backward, out=heads, lse=lse, seqs=seq_count, heads=local_heads
    )
    if tp == 2 and each > 1:
        first_qkv = pull_heads(projected, out_grads=head_grads[0], first=0, count=1)
        dense, first_qkv = lax.optimization_barrier((dense, first_qkv))
        weighted = combine(first_row, info, dense, chances, returned, experts, capacity)
        projected, weighted, head_grads[1] = lax.optimization_barrier(
            (projected, weighted, head_grads[1])
        )
        first_qkv = pull_heads(
            projected, out_grads=head_grads[0], first=1, count=each - 1, place=1, into=first_qkv
        )
        *second_qkv, expert_grads[0], expert_grads[1] = pull_heads(
            projected, out_grads=head_grads[1], first=each, count=each, carry=expert_grads
        )
        qkv = [first_qkv, second_qkv]
    else:
        weighted = combine(
            first_row if tp == 2 else jnp.zeros((), jnp.int32),
            info,
            dense,
            chances,
            returned,
            experts,
            capacity,
        )
        qkv = [
            pull_heads(projected, out_grads=head_grads[s], first=s * each, count=each)
            for s in range(splits)
        ]
    flat = [qkv[s][k] for k in range(3) for s in range(splits)]
    rows_kept = -(-(experts + 2) // 8) * 8
    small = jnp.concatenate([ffn_sums, rm_sums[:rows_kept]], axis=0)
    if tp == 2:
        theirs = swapped(weighted[0])
        own_part, got, square, grad_output, small = tail(
            tokens,
            part,
            attn_in,
            out_part,
            flat,
            small,
            norms,
            projections,
            ep,
        )
        (
            token_grad,
            block_out,
            grad_query,
            grad_key,
            grad_value,
            grad_hidden,
            grad_return,
            grad_router,
            grad_mix,
            *vectors,
        ) = results(
            first_row,
            lengths,
            own_part,
            got,
            resid,
            weighted[1],
            theirs,
            square,
            small,
            grad_hidden,
            grad_return,
            experts,
        )
        vectors = [v[0] for v in vectors]
    else:
        whole, attn_sums = attn_pull(
            jnp.zeros((), jnp.int32), all_rows, tokens, part, norms[0:1], flat, projections, BF16
        )
        token_grad = lax.psum_scatter(whole, "tp", scatter_dimension=0, tiled=True).astype(F32)
        weighted = jnp.concatenate(weighted[::-1], axis=0)
        summed = lax.psum_scatter(weighted, "tp", scatter_dimension=0, tiled=True).astype(F32)
        block_out = jnp.where(shard_of(live_all)[:, None], shard_of(resid) + summed, 0.0).astype(BF16)
        square = over_sequences(outer(attn_in, flat))
        grad_output = lax.psum_scatter(
            over_sequences(out_part).astype(BF16), "tp", scatter_dimension=1, tiled=True
        ).astype(F32)
        small = summed_over(summed_over(small, "tp", tp), "ep", ep)
        attn_sums = summed_over(summed_over(attn_sums, "tp", tp), "ep", ep)
        grad_query, grad_key, grad_value = jnp.split(square.astype(F32), 3, axis=1)
        grad_hidden, grad_return = grad_hidden.astype(F32), grad_return.astype(F32)
        grad_router, grad_mix = small[8 : 8 + experts], small[8 + experts : 10 + experts]
        vectors = [attn_sums[0], attn_sums[1], small[0], small[1]]
    return (
        block_out,
        token_grad,
        grad_query,
        grad_key,
        grad_value,
        grad_output,
        grad_hidden,
        grad_return,
        grad_router.T,
        grad_mix.T,
        *vectors,
        expert_grads[0][None],
        expert_grads[1][None],
    )


def solution(mesh):
    in_specs = (
        P("ep", None),
        P(("ep", "tp"), None),
        P("ep"),
        P("ep"),
        P(None, "tp"),
        P(None, "tp"),
        P(None, "tp"),
        P(None, "tp"),
        P(None, "tp"),
        P(None, "tp"),
        P(),
        P(),
        P(),
        P(),
        P(),
        P(),
        P("ep", None, "tp"),
        P("ep", None, "tp"),
    )
    out_specs = (
        P(("ep", "tp"), None),
        P(("ep", "tp"), None),
        P("ep", "tp"),
        P("ep", "tp"),
        P("ep", "tp"),
        P("ep", "tp"),
        P("ep", "tp"),
        P("ep", "tp"),
        P(),
        P(),
        P(),
        P(),
        P(),
        P(),
        P("ep", None, "tp"),
        P("ep", None, "tp"),
    )
    return jax.shard_map(
        partial(on_device, (mesh.shape["tp"], mesh.shape["ep"])),
        mesh=mesh,
        in_specs=in_specs,
        out_specs=out_specs,
        check_vma=False,
    )
```

```python
import math
from functools import partial

import jax
import jax.numpy as jnp
from jax import lax
from jax.experimental import pallas as pl
from jax.experimental.pallas import tpu as pltpu
from jax.sharding import PartitionSpec as P

HEAD_DIM = 64
PAIR = 2 * HEAD_DIM


EPS = 1e-05
NEG = -1e30
F32 = jnp.float32
BF16 = jnp.bfloat16
NT = (((1,), (1,)), ((), ()))


LANES = 128
GELU_C = math.sqrt(2.0 / math.pi)
GELU_A = 0.044715
BIG_VMEM = 62 * 1024 * 1024


def dot(left, right):
    return jnp.dot(left, right, preferred_element_type=F32)


def dot_nt(left, right):
    return lax.dot_general(left, right, NT, preferred_element_type=F32)


def normalized(values):
    middle = jnp.mean(values, axis=-1, keepdims=True)
    centred = values - middle
    rstd = lax.rsqrt(jnp.mean(centred * centred, axis=-1, keepdims=True) + EPS)
    return centred * rstd, rstd


def norm_pull(grad, normal, rstd, gain):
    q = grad * gain
    along = jnp.mean(q * normal, axis=-1, keepdims=True)
    return rstd * (q - jnp.mean(q, axis=-1, keepdims=True) - normal * along)


def gelu_and_slope(v):
    square = v * v
    t = jnp.tanh(v * (GELU_C + (GELU_C * GELU_A) * square))
    half = 0.5 + 0.5 * t
    slope = half + v * (0.5 - 0.5 * (t * t)) * (GELU_C + (3.0 * GELU_C * GELU_A) * square)
    return v * half, slope


def router_and_mix(logits, experts):
    lane = lax.broadcasted_iota(jnp.int32, logits.shape, 1)
    out = jnp.zeros_like(logits)
    for low, high in ((0, experts), (experts, experts + 2)):
        inside = (lane >= low) & (lane < high)
        top = jnp.max(jnp.where(inside, logits, NEG), axis=-1, keepdims=True)
        e = jnp.where(inside, jnp.exp(jnp.where(inside, logits - top, 0.0)), 0.0)
        out = out + e / jnp.sum(e, axis=-1, keepdims=True)
    return out


def lane_of(values, index):
    lane = lax.broadcasted_iota(jnp.int32, values.shape, 1)
    return jnp.sum(jnp.where(lane == index, values, 0.0), axis=-1, keepdims=True)


def resident(shape):
    return pl.BlockSpec(shape, lambda i, *_: (0,) * len(shape), pipeline_mode=pl.Buffered(1))


def cost(flops, bytes_accessed):
    return pl.CostEstimate(flops=flops // 64, bytes_accessed=bytes_accessed // 64, transcendentals=0)


def attend_block(qi, q, keys, values_t, bq, bk, scale):
    lane = lax.broadcasted_iota(jnp.int32, (bq, PAIR), 1)
    q = q * jnp.asarray(scale, BF16)
    zero = jnp.zeros_like(q)
    halves = [jnp.where(lane < HEAD_DIM, q, zero), jnp.where(lane < HEAD_DIM, zero, q)]

    def step(j, carry, masked):
        off = pl.multiple_of(j * bk, bk)
        k = keys(pl.ds(off, bk))
        vt = values_t(pl.ds(off, bk))
        scores = [lax.dot_general(k, half, NT, preferred_element_type=F32) for half in halves]
        if masked:
            key_pos = off + lax.broadcasted_iota(jnp.int32, (bk, bq), 0)
            query_pos = qi * bq + lax.broadcasted_iota(jnp.int32, (bk, bq), 1)
            allowed = key_pos <= query_pos
            scores = [jnp.where(allowed, s, NEG) for s in scores]
        new = []
        for h in range(2):
            m, l, acc = carry[h]
            m_new = jnp.maximum(m, jnp.max(scores[h], axis=0, keepdims=True))
            alpha = jnp.exp(m - m_new)
            p = jnp.exp(scores[h] - m_new)
            l = l * alpha + jnp.sum(p, axis=0, keepdims=True)
            part = dot(vt[h * HEAD_DIM : (h + 1) * HEAD_DIM], p.astype(BF16))
            new.append((m_new, l, acc * alpha + part))
        return tuple(new)

    init = tuple(
        (jnp.full((1, bq), NEG, F32), jnp.zeros((1, bq), F32), jnp.zeros((HEAD_DIM, bq), F32))
        for _ in range(2)
    )
    full = qi * (bq // bk)
    carry = lax.fori_loop(0, full, lambda j, c: step(j, c, False), init)
    for d in range(bq // bk):
        carry = step(full + d, carry, True)
    out = jnp.concatenate([acc / l for _, l, acc in carry], axis=0).T.astype(BF16)
    return out, [m + jnp.log(l) for m, l, _ in carry]


def attention_forward_kernel(q_ref, k_ref, v_ref, o_ref, lse_ref, vt_ref, *, bq, bk, scale):
    qi = pl.program_id(2)

    @pl.when(qi == 0)
    def _():
        vt_ref[...] = v_ref[...].T

    out, lse = attend_block(
        qi, q_ref[...], lambda s: k_ref[s, :], lambda s: vt_ref[:, s], bq, bk, scale
    )
    o_ref[...] = out
    for h in range(2):
        lse_ref[0, h : h + 1, :] = lse[h]


def attention_forward(proj, seqs, heads, first, count, bq=512, bk=512):
    rows = proj.shape[0]
    length = rows // seqs
    pairs = heads // 2
    nq = length // bq
    flops = 2 * rows * length * count * PAIR
    return pl.pallas_call(
        partial(attention_forward_kernel, bq=bq, bk=bk, scale=HEAD_DIM**-0.5),
        grid=(seqs, count, nq),
        in_specs=[
            pl.BlockSpec((bq, PAIR), lambda s, p, i: (s * nq + i, first + p)),
            pl.BlockSpec((length, PAIR), lambda s, p, i: (s, pairs + first + p)),
            pl.BlockSpec((length, PAIR), lambda s, p, i: (s, 2 * pairs + first + p)),
        ],
        out_specs=[
            pl.BlockSpec((bq, PAIR), lambda s, p, i: (s * nq + i, p)),
            pl.BlockSpec((1, 2, bq), lambda s, p, i: (p, 0, s * nq + i)),
        ],
        out_shape=[
            jax.ShapeDtypeStruct((rows, count * PAIR), BF16),
            jax.ShapeDtypeStruct((count, 2, rows), F32),
        ],
        scratch_shapes=[pltpu.VMEM((PAIR, length), BF16)],
        cost_estimate=cost(flops * 4, 8 * rows * count * PAIR),
        name="attention_forward",
    )(proj, proj, proj)


def attention_backward_kernel(
    q_ref,
    k_ref,
    v_ref,
    o_ref,
    lse_ref,
    *refs,
    terms,
    carried,
    bq,
    bk,
    scale,
    length,
):
    lane = lax.broadcasted_iota(jnp.int32, (length, PAIR), 1)
    first = lane < HEAD_DIM
    q = q_ref[...] * jnp.asarray(scale, BF16)
    do_refs = refs[:terms]
    refs = refs[terms:]
    if carried:
        from_hbm, dq_ref, dk_ref, dv_ref, to_hbm, *refs, held, carry_sem = refs
        way_in = pltpu.make_async_copy(from_hbm, held, carry_sem.at[0])
        way_out = pltpu.make_async_copy(held, to_hbm, carry_sem.at[1])
        at = pl.program_id(0) * pl.num_programs(1) + pl.program_id(1)
        final = pl.num_programs(0) * pl.num_programs(1) - 1

        @pl.when(at == 0)
        def _():
            way_in.start()

        @pl.when(at == final)
        def _():
            way_in.wait()
            way_out.start()

    else:
        dq_ref, dk_ref, dv_ref, *refs = refs
    dqt_ref, qs_ref, dos_ref, kt_ref, dl_ref = refs
    do = do_refs[0][...]
    if terms == 2:
        do = (do.astype(F32) + do_refs[1][...].astype(F32)).astype(BF16)
    zero = jnp.zeros_like(q)
    qs_ref[0] = jnp.where(first, q, zero)
    qs_ref[1] = jnp.where(first, zero, q)
    dos_ref[0] = jnp.where(first, do, zero)
    dos_ref[1] = jnp.where(first, zero, do)
    kt_ref[...] = (k_ref[...] * jnp.asarray(scale, BF16)).T
    prod = (do.astype(F32) * o_ref[...].astype(F32)).T
    dl_ref[0:1, :] = jnp.sum(prod[:HEAD_DIM], axis=0, keepdims=True)
    dl_ref[1:2, :] = jnp.sum(prod[HEAD_DIM:], axis=0, keepdims=True)
    dqt_ref[...] = jnp.zeros_like(dqt_ref)
    nq = length // bq
    nk = length // bk

    def key_block(j, _):
        koff = pl.multiple_of(j * bk, bk)
        k = k_ref[pl.ds(koff, bk), :]
        v = v_ref[pl.ds(koff, bk), :]
        kt = kt_ref[:, pl.ds(koff, bk)]

        def tile(qoff, wide, tall, masked):
            qoff = pl.multiple_of(qoff, wide)
            cols = pl.ds(qoff, wide)
            if masked:
                key_pos = koff + lax.broadcasted_iota(jnp.int32, (tall, wide), 0)
                query_pos = qoff + lax.broadcasted_iota(jnp.int32, (tall, wide), 1)
                allowed = key_pos <= query_pos
            qh = [qs_ref[h, cols, :] for h in range(2)]
            dh = [dos_ref[h, cols, :] for h in range(2)]
            scores = [lax.dot_general(k[:tall], x, NT, preferred_element_type=F32) for x in qh]
            pulls = [lax.dot_general(v[:tall], x, NT, preferred_element_type=F32) for x in dh]
            dk, dv, dqs = 0.0, 0.0, []
            for h in range(2):
                p = jnp.exp(scores[h] - lse_ref[0, h : h + 1, cols])
                if masked:
                    p = jnp.where(allowed, p, 0.0)
                ds = (p * (pulls[h] - dl_ref[h : h + 1, cols])).astype(BF16)
                dv = dv + dot(p.astype(BF16), dh[h])
                dk = dk + dot(ds, qh[h])
                dqs.append(dot(kt[h * HEAD_DIM : (h + 1) * HEAD_DIM, :tall], ds))
            dqt_ref[:, cols] += jnp.concatenate(dqs, axis=0)
            return dk, dv

        def step(i, carry):
            dk, dv = tile(i * bq, bq, bk, False)
            return carry[0] + dk, carry[1] + dv

        half = bk // 2
        dk, dv = tile(koff + half, half, bk, True)
        dk_0, dv_0 = tile(koff, half, half, True)
        rest = jnp.zeros((bk - half, PAIR), F32)
        carry = (
            dk + jnp.concatenate([dk_0, rest], axis=0),
            dv + jnp.concatenate([dv_0, rest], axis=0),
        )
        i0 = j * (bk // bq)
        dk, dv = lax.fori_loop(i0 + bk // bq, nq, step, carry)
        dk_ref[pl.ds(koff, bk), :] = dk.astype(BF16)
        dv_ref[pl.ds(koff, bk), :] = dv.astype(BF16)
        return 0

    lax.fori_loop(0, nk, key_block, 0)
    dq_ref[...] = dqt_ref[...].T.astype(BF16)
    if carried:

        @pl.when(at == final)
        def _():
            way_out.wait()


def attention_backward(proj, out, out_grads, lse, seqs, heads, first, count, carry=(), bq=512, bk=512):
    rows = out.shape[0]
    length = rows // seqs
    pairs = heads // 2
    width = count * PAIR

    def block(off):
        return pl.BlockSpec((length, PAIR), lambda s, p: (s, off + p))

    grad = jax.ShapeDtypeStruct((rows, width), BF16)
    terms = len(out_grads)
    return pl.pallas_call(
        partial(
            attention_backward_kernel,
            terms=terms,
            carried=bool(carry),
            bq=bq,
            bk=bk,
            scale=HEAD_DIM**-0.5,
            length=length,
        ),
        grid=(seqs, count),
        in_specs=[
            block(first),
            block(pairs + first),
            block(2 * pairs + first),
            block(first),
            pl.BlockSpec((1, 2, length), lambda s, p: (first + p, 0, s)),
        ]
        + [block(0)] * terms
        + [pl.BlockSpec(memory_space=pl.ANY) for _ in carry],
        out_specs=[block(0)] * 3 + [pl.BlockSpec(memory_space=pl.ANY) for _ in carry],
        out_shape=[grad] * 3 + [jax.ShapeDtypeStruct(c.shape, c.dtype) for c in carry],
        scratch_shapes=[
            pltpu.VMEM((PAIR, length), F32),
            pltpu.VMEM((2, length, PAIR), BF16),
            pltpu.VMEM((2, length, PAIR), BF16),
            pltpu.VMEM((PAIR, length), BF16),
            pltpu.VMEM((2, length), F32),
        ]
        + [s for c in carry for s in (pltpu.VMEM(c.shape, c.dtype), pltpu.SemaphoreType.DMA((2,)))],
        cost_estimate=cost(20 * rows * length * width, 16 * rows * width),
        compiler_params=pltpu.CompilerParams(vmem_limit_bytes=52 * 1024 * 1024),
        name="attention_backward",
    )(proj, proj, proj, out, lse, *out_grads, *carry)


def norm_project_kernel(x_ref, gain_ref, bias_ref, wq_ref, wk_ref, wv_ref, a_ref, p_ref):
    normal, _ = normalized(x_ref[...].astype(F32))
    a = (normal * gain_ref[...] + bias_ref[...]).astype(BF16)
    a_ref[...] = a
    width = wq_ref.shape[1]
    for j, w in enumerate((wq_ref, wk_ref, wv_ref)):
        p_ref[:, j * width : (j + 1) * width] = dot(a, w[...]).astype(BF16)


def norm_project(x, gain, bias, weights, rb=512):
    rows, wide = x.shape
    width = weights[0].shape[1]
    return pl.pallas_call(
        norm_project_kernel,
        grid=(rows // rb,),
        in_specs=[pl.BlockSpec((rb, wide), lambda i: (i, 0)), resident((1, wide)), resident((1, wide))]
        + [resident((wide, width))] * 3,
        out_specs=[
            pl.BlockSpec((rb, wide), lambda i: (i, 0)),
            pl.BlockSpec((rb, 3 * width), lambda i: (i, 0)),
        ],
        out_shape=[
            jax.ShapeDtypeStruct((rows, wide), BF16),
            jax.ShapeDtypeStruct((rows, 3 * width), BF16),
        ],
        cost_estimate=cost(6 * rows * wide * width, 8 * rows * wide),
        name="norm_project",
    )(x, gain, bias, *weights)


def output_norm_kernel(*refs, parts, experts):
    x_ref, gain_ref, bias_ref, rm_ref = refs[:4]
    heads = refs[4 : 4 + parts]
    weights = refs[4 + parts : 4 + 2 * parts]
    resid_ref, f_ref, chance_ref = refs[4 + 2 * parts :]
    total = dot_nt(heads[0][...], weights[0][...])
    for h, w in zip(heads[1:], weights[1:]):
        total = total + dot_nt(h[...], w[...])
    resid = x_ref[...].astype(F32) + total
    resid_ref[...] = resid
    normal, _ = normalized(resid)
    f = (normal * gain_ref[...] + bias_ref[...]).astype(BF16)
    f_ref[...] = f
    chance_ref[...] = router_and_mix(dot(f, rm_ref[...]), experts)


def output_norm(x, gain, bias, rm, heads, weights, experts, rb=256):
    rows, wide = x.shape
    block = pl.BlockSpec((rb, wide), lambda i: (i, 0))
    weight_specs = [
        pl.BlockSpec(
            (wide, h.shape[1]), lambda i, j=j: (0, j), pipeline_mode=pl.Buffered(1)
        )
        for h, (_, j) in zip(heads, weights)
    ]
    return pl.pallas_call(
        partial(output_norm_kernel, parts=len(heads), experts=experts),
        grid=(rows // rb,),
        in_specs=[block, resident((1, wide)), resident((1, wide)), resident((wide, LANES))]
        + [pl.BlockSpec((rb, h.shape[1]), lambda i: (i, 0)) for h in heads]
        + weight_specs,
        out_specs=[block, block, pl.BlockSpec((rb, LANES), lambda i: (i, 0))],
        out_shape=[
            jax.ShapeDtypeStruct((rows, wide), F32),
            jax.ShapeDtypeStruct((rows, wide), BF16),
            jax.ShapeDtypeStruct((rows, LANES), F32),
        ],
        cost_estimate=cost(2 * rows * wide * wide, 12 * rows * wide),
        name="output_norm",
    )(x, gain, bias, rm, *heads, *[w for w, _ in weights])


def pack_kernel(place_ref, x_ref, o_ref):
    count, rows = o_ref.shape[0], x_ref.shape[0]
    slot = pl.program_id(0) * count + lax.broadcasted_iota(jnp.int32, (count, rows), 0)
    hot = jnp.where(slot == place_ref[...], 1.0, 0.0).astype(BF16)
    o_ref[...] = dot(hot, x_ref[...]).astype(BF16)


def pack(place, x, count, sb=512):
    rows, wide = x.shape
    return pl.pallas_call(
        pack_kernel,
        grid=(count // sb,),
        in_specs=[resident((1, rows)), resident((rows, wide))],
        out_specs=pl.BlockSpec((sb, wide), lambda i: (i, 0)),
        out_shape=jax.ShapeDtypeStruct((count, wide), BF16),
        cost_estimate=cost(2 * rows * wide * count, 4 * rows * wide),
        name="pack_rows",
    )(place, x)


def unpacked(place, all_ref):
    slot = lax.broadcasted_iota(jnp.int32, (place.shape[0], all_ref.shape[0]), 1)
    return dot(jnp.where(slot == place, 1.0, 0.0).astype(BF16), all_ref[...])


def front_kernel(*refs, peers, experts, half, heads_count):
    refs = list(refs)

    def take(count):
        taken = refs[:count]
        del refs[:count]
        return taken

    x_hbm, g_hbm, wq_hbm, wk_hbm, wv_hbm, wo_hbm = take(6)
    len_ref, norms_ref, rm_ref, ids_ref = take(4)
    a_hbm, p_hbm, heads_hbm, others_hbm, wo2_hbm = take(5)
    gall_hbm, resid_hbm, f_hbm, chance_hbm, packed_hbm, gin_hbm, info_hbm, lse_ref = take(8)
    xv, wq, wk, wv, wo, wo2, av, pv, vt, hv, ov, gv, pk, fv, rb, cb, hbuf, pa = take(18)
    place_ref, place_g_ref, info = take(3)
    (
        load_sem,
        x_sem,
        a_sem,
        home_sem,
        grad_sem,
        w_sem,
        w_send,
        w_recv,
        head_send,
        head_recv,
        z_send,
        z_recv,
        out_sem,
    ) = refs
    me = lax.axis_index("ep")
    tp_me = lax.axis_index("tp")
    mesh = pl.DeviceIdType.MESH
    across = {"tp": 1 - tp_me}
    rows, wide = xv.shape
    shard = rows // 2
    width = wq.shape[1]
    block = 512
    steps = rows // block

    def rows_at(i, size):
        return pl.ds(pl.multiple_of(i * size, size), size)

    def x_load(i):
        return pltpu.make_async_copy(
            x_hbm.at[rows_at(i, block), :], xv.at[rows_at(i, block), :], x_sem.at[i]
        )

    weight_loads = [
        pltpu.make_async_copy(src, dst, load_sem.at[j])
        for j, (src, dst) in enumerate(((wq_hbm, wq), (wk_hbm, wk), (wv_hbm, wv), (wo_hbm, wo)))
    ]
    for c in weight_loads[:3]:
        c.start()
    for i in range(steps):
        x_load(i).start()
    weight_loads[3].start()
    own_rows = pl.ds(pl.multiple_of(tp_me * shard, shard), shard)
    own_grad = pltpu.make_async_copy(g_hbm, gv.at[own_rows, :], home_sem.at[0])
    own_grad.start()

    barrier = pltpu.get_barrier_semaphore()
    pl.semaphore_signal(barrier, inc=1, device_id=across, device_id_type=mesh)
    for k in range(1, peers):
        pl.semaphore_signal(
            barrier, inc=1, device_id={"ep": jnp.bitwise_xor(me, k)}, device_id_type=mesh
        )
    pl.semaphore_wait(barrier, peers)

    def remote(src, dst, send, recv, to):
        return pltpu.make_async_remote_copy(
            src_ref=src,
            dst_ref=dst,
            send_sem=send,
            recv_sem=recv,
            device_id=to,
            device_id_type=mesh,
        )

    def w_rows(index):
        return wo2.at[rows_at(index, wide // peers), :]

    w_copy = remote(
        wo_hbm.at[rows_at(me, wide // peers), :], w_rows(me), w_sem.at[0], w_sem.at[1], across
    )
    w_copy.start()
    grad_copy = remote(g_hbm, gv.at[own_rows, :], grad_sem.at[0], grad_sem.at[1], across)
    grad_copy.start()

    def w_pass(k):
        return remote(
            w_rows(me), w_rows(me), w_send.at[k], w_recv.at[k], {"ep": jnp.bitwise_xor(me, k)}
        )

    for c in weight_loads[:3]:
        c.wait()

    def a_store(i):
        return [
            pltpu.make_async_copy(
                av.at[rows_at(i, block), :], a_hbm.at[rows_at(i, block), :], a_sem.at[i, 0]
            ),
            pltpu.make_async_copy(
                pv.at[rows_at(i, block), :], p_hbm.at[rows_at(i, block), :], a_sem.at[i, 1]
            ),
        ]

    def project(i):
        at = rows_at(i, block)
        x_load(i).wait()
        normal, _ = normalized(xv[at, :].astype(F32))
        a = (normal * norms_ref[0:1, :] + norms_ref[1:2, :]).astype(BF16)
        av[at, :] = a
        for j, w in enumerate((wq, wk, wv)):
            pv[at, j * width : (j + 1) * width] = dot(a, w[...]).astype(BF16)
        for c in a_store(i):
            c.start()

    pairs = heads_count // 2

    def head_copy(i):
        at = rows_at(i, block)
        return remote(hv.at[at, :], ov.at[at, :], head_send.at[i], head_recv.at[i], across)

    def is_live(position):
        count = len_ref.shape[0]
        length = rows // count
        inside = None
        for s in range(count):
            here = (position >= s * length) & (position < s * length + len_ref[s])
            inside = here if inside is None else inside | here
        return inside

    span = 256
    run = jnp.zeros((experts, 1), F32)
    triangle = jnp.where(
        lax.broadcasted_iota(jnp.int32, (span, span), 0)
        < lax.broadcasted_iota(jnp.int32, (span, span), 1),
        1.0,
        0.0,
    ).astype(BF16)
    capacity = 2 * half
    for b in range(rows // span):
        at = slice(b * span, (b + 1) * span)
        ids = ids_ref[:, at]
        live = is_live(b * span + lax.broadcasted_iota(jnp.int32, (1, span), 1))
        hot = (lax.broadcasted_iota(jnp.int32, (experts, span), 0) == ids) & live
        hot = jnp.where(hot, 1.0, 0.0)
        before = dot(hot.astype(BF16), triangle) + run
        run = run + jnp.sum(hot, axis=1, keepdims=True)
        slot = jnp.sum(before * hot, axis=0, keepdims=True).astype(jnp.int32)
        sound = live & (slot < capacity)
        place = jnp.where(sound, ids * capacity + slot, -1)
        inside = slot - tp_me * half
        mine = sound & (inside >= 0) & (inside < half)
        place_g = jnp.where(mine, ids * half + inside, -1)
        place_ref[:, at] = place
        place_g_ref[:, at] = place_g
        line = lax.broadcasted_iota(jnp.int32, (LANES, span), 0)
        both = jnp.where(line == 0, place.astype(F32), place_g.astype(F32))
        info[at, :] = both.T
    info_store = pltpu.make_async_copy(info, info_hbm, home_sem.at[4])
    info_store.start()

    gall_store = pltpu.make_async_copy(gv, gall_hbm, home_sem.at[1])
    gin_own = pltpu.make_async_copy(pk.at[rows_at(me, half), :], gin_hbm.at[me], home_sem.at[2])

    def mask(i, _):
        at = rows_at(i, block)
        live = is_live(i * block + lax.broadcasted_iota(jnp.int32, (block, wide), 0))
        gv[at, :] = jnp.where(live, gv[at, :], jnp.zeros((block, wide), BF16))
        return 0

    def pack_g(i, _):
        slot = i * block + lax.broadcasted_iota(jnp.int32, (block, rows), 0)
        hot = jnp.where(slot == place_g_ref[...], 1.0, 0.0).astype(BF16)
        pk[rows_at(i, block), :] = dot(hot, gv[...]).astype(BF16)
        return 0

    def z_copy(k):
        peer = jnp.bitwise_xor(me, k)
        return remote(
            pk.at[rows_at(peer, half), :], gin_hbm.at[me], z_send.at[k], z_recv.at[k], {"ep": peer}
        )

    def send_gradient():
        own_grad.wait()
        grad_copy.wait()
        lax.fori_loop(0, steps, mask, 0)
        gall_store.start()
        lax.fori_loop(0, peers * half // block, pack_g, 0)
        for k in list(range(peers // 2, peers)) + list(range(1, peers // 2)):
            z_copy(k).start()
        gin_own.start()

    def attend(i, _):
        project(i)
        at = rows_at(i, block)
        for pair in range(pairs):
            cols = [slice(j * width + pair * PAIR, j * width + (pair + 1) * PAIR) for j in range(3)]
            vt[pair, :, at] = pv[at, cols[2]].T
            out, lse = attend_block(
                i,
                pv[at, cols[0]],
                lambda s, cols=cols: pv[s, cols[1]],
                lambda s, pair=pair: vt[pair, :, s],
                block,
                block,
                HEAD_DIM**-0.5,
            )
            hv[at, pair * PAIR : (pair + 1) * PAIR] = out
            for h in range(2):
                lse_ref[pair, h : h + 1, at] = lse[h]
        head_copy(i).start()

        @pl.when(i == 0)
        def _():
            w_copy.wait()
            for k in range(1, peers):
                w_pass(k).start()

        pl.when(i == steps - 2)(send_gradient)
        return 0

    lax.fori_loop(0, steps, attend, 0)
    weight_loads[3].wait()
    for k in range(1, peers):
        w_pass(k).wait()
    stores = [
        pltpu.make_async_copy(hv, heads_hbm, out_sem.at[0]),
        pltpu.make_async_copy(wo2, wo2_hbm, out_sem.at[1]),
    ]
    for c in stores:
        c.start()
    small = rb.shape[1]

    def norm_stores(i, slot):
        at = rows_at(i, small)
        return [
            pltpu.make_async_copy(rb.at[slot], resid_hbm.at[at, :], out_sem.at[3 + slot]),
            pltpu.make_async_copy(cb.at[slot], chance_hbm.at[at, :], out_sem.at[5 + slot]),
        ]

    def norm_step(i, _):
        at = rows_at(i, small)
        slot = lax.rem(i, 2)

        @pl.when(slot == 0)
        def _():
            head_copy(i // 2).wait()

        @pl.when(i >= 2)
        def _():
            for c in norm_stores(i - 2, slot):
                c.wait()

        total = dot_nt(hv[at, :], wo[...]) + dot_nt(ov[at, :], wo2[...])
        resid = xv[at, :].astype(F32) + total
        rb[slot] = resid
        normal, _ = normalized(resid)
        f = (normal * norms_ref[2:3, :] + norms_ref[3:4, :]).astype(BF16)
        fv[at, :] = f
        cb[slot] = router_and_mix(dot(f, rm_ref[...]), experts)
        for c in norm_stores(i, slot):
            c.start()
        return 0

    def packed_part(i, first, size):
        at = i * block + lax.broadcasted_iota(jnp.int32, (block, size), 0)
        hot = jnp.where(at == place_ref[:, first : first + size], 1.0, 0.0).astype(BF16)
        return dot(hot, fv[first : first + size, :])

    count = rows // small
    packs = packed_hbm.shape[0] // block
    lax.fori_loop(0, count // 2, norm_step, 0)

    def pack_low(i, _):
        pa[rows_at(i, block), :] = packed_part(i, 0, rows // 2).astype(BF16)
        return 0

    lax.fori_loop(0, packs, pack_low, 0)
    lax.fori_loop(count // 2, count, norm_step, 0)
    stores_late = [
        pltpu.make_async_copy(ov, others_hbm, out_sem.at[2]),
        pltpu.make_async_copy(fv, f_hbm, home_sem.at[3]),
    ]
    for c in stores_late:
        c.start()

    def packed_store(i, slot):
        return pltpu.make_async_copy(
            hbuf.at[slot], packed_hbm.at[rows_at(i, block), :], out_sem.at[7 + slot]
        )

    def pack_high(i, _):
        slot = lax.rem(i, 2)

        @pl.when(i >= 2)
        def _():
            packed_store(i - 2, slot).wait()

        both = packed_part(i, rows // 2, rows // 2) + pa[rows_at(i, block), :].astype(F32)
        hbuf[slot] = both.astype(BF16)
        packed_store(i, slot).start()
        return 0

    lax.fori_loop(0, packs, pack_high, 0)
    for i in range(packs - 2, packs):
        packed_store(i, i % 2).wait()
    for i in range(count - 2, count):
        for c in norm_stores(i, i % 2):
            c.wait()
    for c in [gall_store, gin_own, info_store] + stores + stores_late:
        c.wait()
    for i in range(steps):
        for c in a_store(i):
            c.wait()
    for k in range(1, peers):
        z_copy(k).wait()


def front(x, g, weights, lengths, norms, rm, ids, peers, experts, capacity):
    rows, wide = x.shape
    width = weights[0].shape[1]
    half = capacity // 2
    anywhere = pl.BlockSpec(memory_space=pl.ANY)
    vmem = pl.BlockSpec(memory_space=pltpu.VMEM)

    def like(*shape, kind=BF16):
        return jax.ShapeDtypeStruct(shape, kind)

    return pl.pallas_call(
        partial(
            front_kernel,
            peers=peers,
            experts=experts,
            half=half,
            heads_count=width // HEAD_DIM,
        ),
        in_specs=[anywhere] * 6 + [pl.BlockSpec(memory_space=pltpu.SMEM)] + [vmem] * 3,
        out_specs=[anywhere] * 12 + [vmem],
        out_shape=[
            like(rows, wide),
            like(rows, 3 * width),
            like(rows, width),
            like(rows, width),
            like(wide, width),
            like(rows, wide),
            like(rows, wide, kind=F32),
            like(rows, wide),
            like(rows, LANES, kind=F32),
            like(experts * capacity, wide),
            like(peers, half, wide),
            like(rows, LANES, kind=F32),
            like(width // PAIR, 2, rows, kind=F32),
        ],
        scratch_shapes=[pltpu.VMEM((rows, wide), BF16)]
        + [pltpu.VMEM((wide, width), BF16)] * 5
        + [
            pltpu.VMEM((rows, wide), BF16),
            pltpu.VMEM((rows, 3 * width), BF16),
            pltpu.VMEM((width // PAIR, PAIR, rows), BF16),
            pltpu.VMEM((rows, width), BF16),
            pltpu.VMEM((rows, width), BF16),

            pltpu.VMEM((rows, wide), BF16),
            pltpu.VMEM((peers * half, wide), BF16),
            pltpu.VMEM((rows, wide), BF16),
            pltpu.VMEM((2, 256, wide), F32),
            pltpu.VMEM((2, 256, LANES), F32),
            pltpu.VMEM((2, 512, wide), BF16),
            pltpu.VMEM((experts * capacity, wide), BF16),
            pltpu.VMEM((1, rows), jnp.int32),
            pltpu.VMEM((1, rows), jnp.int32),
            pltpu.VMEM((rows, LANES), F32),
            pltpu.SemaphoreType.DMA((4,)),
            pltpu.SemaphoreType.DMA((rows // 512,)),
            pltpu.SemaphoreType.DMA((rows // 512, 2)),
            pltpu.SemaphoreType.DMA((5,)),
            pltpu.SemaphoreType.DMA((2,)),
            pltpu.SemaphoreType.DMA((2,)),
            pltpu.SemaphoreType.DMA((peers,)),
            pltpu.SemaphoreType.DMA((peers,)),
            pltpu.SemaphoreType.DMA((rows // 512,)),
            pltpu.SemaphoreType.DMA((rows // 512,)),
            pltpu.SemaphoreType.DMA((peers,)),
            pltpu.SemaphoreType.DMA((peers,)),
            pltpu.SemaphoreType.DMA((9,)),
        ],
        cost_estimate=cost(20 * rows * wide * wide, 30 * rows * wide),
        compiler_params=pltpu.CompilerParams(
            vmem_limit_bytes=BIG_VMEM, collective_id=2, has_side_effects=True
        ),
        name="layer_front",
    )(x, g, *weights, lengths, norms, rm, ids)


def nets_kernel(
    x_hbm,
    g_hbm,
    out_hbm,
    gin_hbm,
    sel_ref,
    rm_ref,
    wd1_hbm,
    wd2_hbm,
    we1_hbm,
    we2_hbm,
    y_hbm,
    dx_hbm,
    dot_hbm,
    gd1_hbm,
    gd2_hbm,
    ge1_hbm,
    ge2_hbm,
    in_hbm,
    res_hbm,
    pull_hbm,
    edot_hbm,
    pulls_hbm,
    edots_hbm,
    gin2_hbm,
    wd1,
    wd2,
    we1,
    we2,
    a1,
    a2,
    xb,
    gb,
    yb,
    dxb,
    dotb,
    rowb,
    ya,
    dxa,
    dyb,
    dyt,
    xt,
    w_sem,
    load_sem,
    store_sem,
    grad_sem,
    home_sem,
    local_sem,
    send_sem,
    recv_sem,
    back_send,
    back_recv,
    dot_send,
    dot_recv,
    relay_sem,
    swap_send,
    swap_recv,
    keep,
    give,
    got,
    hv,
    pv,
    *,
    peers,
    capacity,
    rb,
    ft,
    relayed,
):
    experts = peers
    me = lax.axis_index("ep")
    hidden = wd1.shape[1]
    per = rb // capacity
    quarter = peers // 4
    dense_steps = x_hbm.shape[0] // rb
    expert_steps = peers // per

    weight_copies = [
        pltpu.make_async_copy(src, dst, w_sem.at[j])
        for j, (src, dst) in enumerate(
            ((wd1_hbm, wd1), (wd2_hbm, wd2), (we1_hbm, we1), (we2_hbm, we2))
        )
    ]
    weight_copies[0].start()
    weight_copies[1].start()

    def load(t):
        rows = pl.ds(pl.multiple_of(t * rb, rb), rb)
        return [
            pltpu.make_async_copy(x_hbm.at[rows, :], xb, load_sem.at[0, 0]),
            pltpu.make_async_copy(g_hbm.at[rows, :], gb, load_sem.at[1, 0]),
        ]

    for c in load(0):
        c.start()

    barrier = pltpu.get_barrier_semaphore()
    for k in range(1, peers):
        pl.semaphore_signal(
            barrier,
            inc=1,
            device_id={"ep": jnp.bitwise_xor(me, k)},
            device_id_type=pl.DeviceIdType.MESH,
        )
    tp_me = lax.axis_index("tp")
    across = {"tp": 1 - tp_me}
    half = capacity // 2
    if relayed:
        pl.semaphore_signal(
            barrier, inc=1, device_id=across, device_id_type=pl.DeviceIdType.MESH
        )
    pl.semaphore_wait(barrier, peers if relayed else peers - 1)
    relay = pltpu.make_async_remote_copy(
        src_ref=gin_hbm,
        dst_ref=gin2_hbm,
        send_sem=relay_sem.at[0],
        recv_sem=relay_sem.at[1],
        device_id=across,
        device_id_type=pl.DeviceIdType.MESH,
    )
    if relayed:
        relay.start()

    def remote(src, dst, send, recv, k):
        peer = jnp.bitwise_xor(me, k)
        return pltpu.make_async_remote_copy(
            src_ref=src,
            dst_ref=dst,
            send_sem=send.at[k],
            recv_sem=recv.at[k],
            device_id={"ep": peer},
            device_id_type=pl.DeviceIdType.MESH,
        )

    def row_copy(k):
        return remote(
            out_hbm.at[jnp.bitwise_xor(me, k)], in_hbm.at[me], send_sem, recv_sem, k
        )

    def back_copy(k):
        return remote(
            pull_hbm.at[jnp.bitwise_xor(me, k)], pulls_hbm.at[me], back_send, back_recv, k
        )

    def dot_copy(k):
        return remote(
            edot_hbm.at[jnp.bitwise_xor(me, k)], edots_hbm.at[me], dot_send, dot_recv, k
        )

    far = list(range(2 * quarter, peers))
    near = list(range(1, 2 * quarter))
    for k in far[:quarter] + near[quarter - 1 :] + far[quarter:] + near[: quarter - 1]:
        row_copy(k).start()
    own_rows = pltpu.make_async_copy(out_hbm.at[me], in_hbm.at[me], home_sem.at[0])
    own_rows.start()
    weight_copies[2].start()
    weight_copies[3].start()

    def outputs(routed, w1_ref, w2_ref):
        x = xb[...]
        g = gb[...].astype(F32)
        chances = router_and_mix(dot(x, rm_ref[...]), experts)
        if routed:
            gate = jnp.sum(chances * sel_ref[...], axis=-1, keepdims=True)
            dy = g * lane_of(chances, experts + 1) * gate
        else:
            dy = g * lane_of(chances, experts)
        dy = dy.astype(BF16)
        dyb[...] = dy
        dyt[...] = dy.T
        xt[...] = x.T

        def products(f, _):
            cols = pl.ds(pl.multiple_of(f * ft, ft), ft)
            w1 = w1_ref[:, cols]
            w2 = w2_ref[:, cols]
            act, slope = gelu_and_slope(dot(xb[...], w1))
            h = act.astype(BF16)
            pre_grad = (slope * dot(dyb[...], w2)).astype(BF16)
            hv[:, cols] = h
            pv[:, cols] = pre_grad
            ya[...] += dot_nt(h, w2)
            dxa[...] += dot_nt(pre_grad, w1)
            return 0

        ya[...] = jnp.zeros_like(ya)
        dxa[...] = jnp.zeros_like(dxa)
        lax.fori_loop(0, hidden // ft, products, 0)

    def row_dots():
        return jnp.sum(ya[...] * gb[...].astype(F32), axis=1, keepdims=True)

    def gradients(first, last=None):
        wide_step = ft

        def at(f):
            return pl.ds(pl.multiple_of(f * wide_step, wide_step), wide_step)

        def put(f, _):
            a2[:, at(f)] = dot(dyt[...], hv[:, at(f)])
            a1[:, at(f)] = dot(xt[...], pv[:, at(f)])
            return 0

        def add(f, _):
            a2[:, at(f)] += dot(dyt[...], hv[:, at(f)])
            a1[:, at(f)] += dot(xt[...], pv[:, at(f)])
            return 0

        def round_off(f, _):
            wd2[:, at(f)] = (a2[:, at(f)] + dot(dyt[...], hv[:, at(f)])).astype(BF16)
            wd1[:, at(f)] = (a1[:, at(f)] + dot(xt[...], pv[:, at(f)])).astype(BF16)
            return 0

        @pl.when(first)
        def _():
            lax.fori_loop(0, hidden // wide_step, put, 0)

        if last is None:
            middle = jnp.logical_not(first)
        else:
            middle = jnp.logical_not(first | last)

            @pl.when(last)
            def _():
                lax.fori_loop(0, hidden // wide_step, round_off, 0)

        @pl.when(middle)
        def _():
            lax.fori_loop(0, hidden // wide_step, add, 0)

    weight_copies[0].wait()
    weight_copies[1].wait()

    def dense_stores(t, slot):
        rows = pl.ds(pl.multiple_of(t * rb, rb), rb)
        return [
            pltpu.make_async_copy(yb, y_hbm.at[rows, :], store_sem.at[slot, 0, 0]),
            pltpu.make_async_copy(dxb, dx_hbm.at[rows, :], store_sem.at[slot, 1, 0]),
            pltpu.make_async_copy(dotb.at[slot], dot_hbm.at[rows, :], store_sem.at[slot, 2, 0]),
        ]

    def dense_step(t, _):
        slot = lax.rem(t, 2)
        for c in load(t):
            c.wait()
        outputs(False, wd1, wd2)

        @pl.when(t >= 1)
        def _():
            for c in dense_stores(t - 1, 1 - slot):
                c.wait()

        yb[...] = ya[...].astype(BF16)
        dxb[...] = dxa[...].astype(BF16)
        dotb[slot] = jnp.broadcast_to(row_dots(), (rb, LANES))

        @pl.when(t + 1 < dense_steps)
        def _():
            for c in load(t + 1):
                c.start()

        for c in dense_stores(t, slot):
            c.start()
        gradients(t == 0, t == dense_steps - 1)
        return 0

    lax.fori_loop(0, dense_steps, dense_step, 0)
    for c in dense_stores(dense_steps - 1, (dense_steps - 1) % 2):
        c.wait()

    dense_grads = [
        pltpu.make_async_copy(wd1, gd1_hbm, grad_sem.at[0]),
        pltpu.make_async_copy(wd2, gd2_hbm, grad_sem.at[1]),
    ]
    for c in dense_grads:
        c.start()
    weight_copies[2].wait()
    weight_copies[3].wait()
    own_rows.wait()
    if relayed:
        relay.wait()

    def first_of(p):
        if expert_steps != 4:
            return (expert_steps - 1 - p) * per
        return jnp.where(p == 0, 2, jnp.where(p == 1, 1, jnp.where(p == 2, 3, 0))) * per

    def swap_copy(p, j):
        slot = lax.rem(p, 2)
        return pltpu.make_async_remote_copy(
            src_ref=give.at[slot, j],
            dst_ref=got.at[slot, j],
            send_sem=swap_send.at[slot, j],
            recv_sem=swap_recv.at[slot, j],
            device_id=across,
            device_id_type=pl.DeviceIdType.MESH,
        )

    size = half if relayed else capacity

    def back_stores(p, j, source_ref):
        to = (pull_hbm, res_hbm)[j]
        return [
            pltpu.make_async_copy(
                source_ref.at[pl.ds(c * size, size), :],
                to.at[jnp.bitwise_xor(me, first_of(p) + c)],
                store_sem.at[0, j, c],
            )
            for c in range(per)
        ]

    def dot_stores(p):
        return [
            pltpu.make_async_copy(
                rowb.at[c], edot_hbm.at[jnp.bitwise_xor(me, first_of(p) + c)], store_sem.at[1, 2, c]
            )
            for c in range(per)
        ]

    def to_peers(p, copy):
        for c in range(per):
            k = first_of(p) + c

            @pl.when(k > 0)
            def _(k=k):
                copy(k).start()

    def sum_shares(p, j):
        swap_copy(p, j).wait()
        stage = (dxb, yb)[j]
        stage[: per * half, :] = (keep[j] + got[lax.rem(p, 2), j].astype(F32)).astype(BF16)
        for c in back_stores(p, j, stage):
            c.start()

    def stored(p, j, source_ref):
        for c in back_stores(p, j, source_ref):
            c.wait()

    def fetch(p):
        for c in range(per):
            k = first_of(p) + c

            @pl.when(k > 0)
            def _(k=k):
                row_copy(k).wait()

        for c in fetches(p):
            c.start()

    def fetches(p):
        loads = []
        for c in range(per):
            source = jnp.bitwise_xor(me, first_of(p) + c)
            rows = pl.ds(c * capacity, capacity)
            loads.append(
                pltpu.make_async_copy(in_hbm.at[source], xb.at[rows, :], load_sem.at[0, c])
            )
            if relayed:
                for j, src, which in ((1, gin_hbm, tp_me), (2, gin2_hbm, 1 - tp_me)):
                    at = pl.ds(pl.multiple_of(c * capacity + which * half, half), half)
                    loads.append(
                        pltpu.make_async_copy(
                            src.at[source], gb.at[at, :], load_sem.at[j, c]
                        )
                    )
            else:
                loads.append(
                    pltpu.make_async_copy(
                        gin_hbm.at[source], gb.at[rows, :], load_sem.at[1, c]
                    )
                )
        return loads

    fetch(0)

    def expert_step(p, _):
        slot = lax.rem(p, 2)
        for c in fetches(p):
            c.wait()
        outputs(True, we1, we2)
        across_dots = jnp.broadcast_to(row_dots(), (rb, LANES)).T
        for c in range(per):
            rowb[c] = across_dots[:8, c * capacity : (c + 1) * capacity]
        for c in dot_stores(p):
            c.start()
        if relayed:

            @pl.when(p > 0)
            def _():
                for j in range(2):
                    sum_shares(p - 1, j)

            for j, total in ((0, dxa), (1, ya)):
                for c in range(per):
                    rows = slice(c * half, (c + 1) * half)
                    at = pl.ds(pl.multiple_of(c * capacity + tp_me * half, half), half)
                    other = pl.ds(pl.multiple_of(c * capacity + (1 - tp_me) * half, half), half)
                    keep[j, rows, :] = total[at, :]
                    give[slot, j, rows, :] = total[other, :].astype(BF16)
                swap_copy(p, j).start()
        else:
            dxb[...] = dxa[...].astype(BF16)
            yb[...] = ya[...].astype(BF16)
            for j, source_ref in ((0, dxb), (1, yb)):
                for c in back_stores(p, j, source_ref):
                    c.start()

        @pl.when(p + 1 < expert_steps)
        def _():
            fetch(p + 1)

        gradients(p == 0)
        for c in dot_stores(p):
            c.wait()
        to_peers(p, dot_copy)
        if relayed:

            @pl.when(p > 0)
            def _():
                for j in range(2):
                    stored(p - 1, j, (dxb, yb)[j])
                to_peers(p - 1, back_copy)
        else:
            for j, source_ref in ((0, dxb), (1, yb)):
                stored(p, j, source_ref)
            to_peers(p, back_copy)
        return 0

    lax.fori_loop(0, expert_steps, expert_step, 0)
    expert_grads = [
        pltpu.make_async_copy(a1, ge1_hbm, local_sem.at[0]),
        pltpu.make_async_copy(a2, ge2_hbm, local_sem.at[1]),
        pltpu.make_async_copy(edot_hbm.at[me], edots_hbm.at[me], home_sem.at[2]),
    ]
    for c in expert_grads:
        c.start()
    if relayed:
        final = expert_steps - 1
        sum_shares(final, 0)
        stored(final, 0, dxb)
        to_peers(final, back_copy)
        sum_shares(final, 1)
        stored(final, 1, yb)
    own_back = pltpu.make_async_copy(pull_hbm.at[me], pulls_hbm.at[me], home_sem.at[1])
    own_back.start()
    for c in dense_grads + expert_grads + [own_back]:
        c.wait()
    for k in range(1, peers):
        back_copy(k).wait()
        dot_copy(k).wait()


def nets(x, g, out_rows, in_grads, sel, rm, dense_weights, expert_weights, rb=512, ft=512):
    rows, wide = x.shape
    hidden = dense_weights[0].shape[1]
    peers, capacity, _ = out_rows.shape
    per = rb // capacity
    anywhere = pl.BlockSpec(memory_space=pl.ANY)
    vmem = pl.BlockSpec(memory_space=pltpu.VMEM)
    sheet = jax.ShapeDtypeStruct((rows, wide), BF16)
    relayed = in_grads.shape[1] < capacity
    blocks = jax.ShapeDtypeStruct((peers, capacity, wide), BF16)
    backs = jax.ShapeDtypeStruct(in_grads.shape, BF16)
    part = (rb * in_grads.shape[1] // capacity, wide) if relayed else (16, wide)
    strips = jax.ShapeDtypeStruct((peers, 8, capacity), F32)
    return pl.pallas_call(
        partial(nets_kernel, peers=peers, capacity=capacity, rb=rb, ft=ft, relayed=relayed),
        in_specs=[anywhere] * 4 + [vmem] * 2 + [anywhere] * 4,
        out_specs=[anywhere] * 14,
        out_shape=[
            sheet,
            sheet,
            jax.ShapeDtypeStruct((rows, LANES), F32),
            jax.ShapeDtypeStruct((wide, hidden), BF16),
            jax.ShapeDtypeStruct((wide, hidden), BF16),
            jax.ShapeDtypeStruct((wide, hidden), F32),
            jax.ShapeDtypeStruct((wide, hidden), F32),
            blocks,
            backs,
            backs,
            strips,
            backs,
            strips,
            backs,
        ],
        scratch_shapes=[pltpu.VMEM((wide, hidden), BF16)] * 4
        + [pltpu.VMEM((wide, hidden), F32)] * 2
        + [pltpu.VMEM((rb, wide), BF16)] * 4
        + [
            pltpu.VMEM((2, rb, LANES), F32),
            pltpu.VMEM((per, 8, capacity), F32),
            pltpu.VMEM((rb, wide), F32),
            pltpu.VMEM((rb, wide), F32),
            pltpu.VMEM((rb, wide), BF16),
            pltpu.VMEM((wide, rb), BF16),
            pltpu.VMEM((wide, rb), BF16),
            pltpu.SemaphoreType.DMA((4,)),
            pltpu.SemaphoreType.DMA((3, per)),
            pltpu.SemaphoreType.DMA((2, 3, per)),
            pltpu.SemaphoreType.DMA((2,)),
            pltpu.SemaphoreType.DMA((3,)),
            pltpu.SemaphoreType.DMA((2,)),
        ]
        + [pltpu.SemaphoreType.DMA((peers,))] * 6
        + [
            pltpu.SemaphoreType.DMA((2,)),
            pltpu.SemaphoreType.DMA((2, 2)),
            pltpu.SemaphoreType.DMA((2, 2)),
            pltpu.VMEM((2, *part), F32),
            pltpu.VMEM((2, 2, *part), BF16),
            pltpu.VMEM((2, 2, *part), BF16),
            pltpu.VMEM((rb, hidden), BF16),
            pltpu.VMEM((rb, hidden), BF16),
        ],
        cost_estimate=cost(24 * rows * wide * hidden, 16 * rows * wide + 24 * wide * hidden),
        compiler_params=pltpu.CompilerParams(
            vmem_limit_bytes=67043328, collective_id=0, has_side_effects=True
        ),
        name="feed_forward_nets",
    )(x, g, out_rows, in_grads, sel, rm, *dense_weights, *expert_weights)


def expert_hot(place, capacity, experts):
    lane = lax.broadcasted_iota(jnp.int32, (place.shape[0], LANES), 1)
    low = lane * capacity
    return ((place >= low) & (place < low + capacity) & (lane < experts)).astype(F32)


def ffn_pull_kernel(*refs, parts, experts, capacity, shard, sent, outs):
    (
        info_ref,
        dx_ref,
        chance_ref,
        first_ref,
        f_ref,
        g_ref,
        resid_ref,
        gain_ref,
        rm_ref,
        slot_ref,
        dots_ref,
    ) = refs[:11]
    heads_out = refs[11 : 11 + outs]
    refs = refs[11 + outs :]
    weights = refs[:parts]
    r_ref = refs[parts]
    heads = list(refs[1 + parts : 1 + 2 * parts])
    sums_ref, rmg_ref, outer_ref, outer_acc = (
        *refs[1 + 2 * parts : 4 + 2 * parts],
        refs[4 + 2 * parts],
    )
    size = info_ref.shape[0]
    step = pl.program_id(0)
    if sent is not None:
        give, send_sem, recv_sem = refs[5 + 2 * parts :]
        got = heads[sent]
        across = {"tp": 1 - lax.axis_index("tp")}
        mesh = pl.DeviceIdType.MESH

        def share(b):
            at = pl.ds(pl.multiple_of(b * size, size), size)
            return pltpu.make_async_remote_copy(
                src_ref=give.at[at, :],
                dst_ref=got.at[at, :],
                send_sem=send_sem.at[b],
                recv_sem=recv_sem.at[b],
                device_id=across,
                device_id_type=mesh,
            )

        @pl.when(step == 0)
        def _():
            barrier = pltpu.get_barrier_semaphore()
            pl.semaphore_signal(barrier, inc=1, device_id=across, device_id_type=mesh)
            pl.semaphore_wait(barrier, 1)

    place = info_ref[:, 0:1].astype(jnp.int32)
    here = info_ref[:, 1:2].astype(jnp.int32)
    row = step * size + lax.broadcasted_iota(jnp.int32, (size, 1), 0)
    row = row - lax.axis_index("tp") * shard
    own = ((row >= 0) & (row < shard)).astype(F32)
    chances = chance_ref[...]
    hot = expert_hot(place, capacity, experts)
    gate = jnp.sum(hot * chances, axis=-1, keepdims=True)
    mix_0, mix_1 = lane_of(chances, experts), lane_of(chances, experts + 1)
    table = jnp.dot(
        hot, dots_ref[...], precision=lax.Precision.HIGHEST, preferred_element_type=F32
    )
    slot = lax.broadcasted_iota(jnp.int32, table.shape, 1)
    number = jnp.sum(hot * lax.broadcasted_iota(jnp.int32, hot.shape, 1).astype(F32), axis=-1)
    inside = place - number.astype(jnp.int32)[:, None] * capacity
    second = jnp.sum(jnp.where(slot == inside, table, 0.0), axis=-1, keepdims=True)
    first = lane_of(first_ref[...], 0)
    grad_0, grad_1 = first, gate * second
    inner = mix_0 * grad_0 + mix_1 * grad_1
    lane = lax.broadcasted_iota(jnp.int32, chances.shape, 1)
    low = (mix_1 * second * gate) * (hot - chances)
    low = jnp.where(lane == experts, mix_0 * (grad_0 - inner), low)
    low = jnp.where(lane == experts + 1, mix_1 * (grad_1 - inner), low)
    low = jnp.where(lane > experts + 1, 0.0, low).astype(BF16)
    grad = dx_ref[...].astype(F32) + unpacked(here, slot_ref) + dot_nt(low, rm_ref[...])
    normal, rstd = normalized(resid_ref[...])
    r = norm_pull(grad, normal, rstd, gain_ref[2:3, :]) + own * g_ref[...].astype(F32)
    r = r.astype(BF16)
    r_ref[...] = r
    if sent is not None:
        at = pl.ds(pl.multiple_of(step * size, size), size)
        give[at, :] = dot(r, weights[sent][...]).astype(BF16)
        share(step).start()
    for j, (h, w) in enumerate(zip(heads, weights)):
        if j != sent:
            h[...] = dot(r, w[...]).astype(BF16)

    @pl.when(pl.program_id(0) == 0)
    def _():
        sums_ref[...] = jnp.zeros_like(sums_ref)
        rmg_ref[...] = jnp.zeros_like(rmg_ref)
        outer_acc[...] = jnp.zeros_like(outer_acc)

    sums_ref[0:1, :] += jnp.sum(grad * normal, axis=0, keepdims=True)
    sums_ref[1:2, :] += jnp.sum(grad, axis=0, keepdims=True)
    rmg_ref[...] += dot(low.T, f_ref[...])
    left = r.T
    col = 0
    for h in heads_out:
        outer_acc[:, col : col + h.shape[1]] += dot(left, h[...])
        col += h.shape[1]

    @pl.when(step == pl.num_programs(0) - 1)
    def _():
        outer_ref[...] = outer_acc[...].astype(BF16)

    if sent is not None:

        @pl.when(step == pl.num_programs(0) - 1)
        def _():
            for b in range(give.shape[0] // size):
                share(b).wait()


def ffn_pull(
    info,
    dx,
    chances,
    first,
    f,
    g,
    resid,
    gain,
    rm,
    slot_rows,
    dots,
    heads,
    weights,
    experts,
    shard,
    sent=None,
    rb=512,
):
    rows, wide = dx.shape
    capacity = dots.shape[1]
    dots = jnp.pad(dots, ((0, LANES - experts), (0, 0)))
    block = pl.BlockSpec((rb, wide), lambda i: (i, 0))
    narrow = pl.BlockSpec((rb, LANES), lambda i: (i, 0))
    head_specs = [
        pl.BlockSpec(memory_space=pl.ANY) if j == sent else pl.BlockSpec((rb, size), lambda i: (i, 0))
        for j, (_, _, size) in enumerate(weights)
    ]
    outer_width = sum(h.shape[1] for h in heads)
    scratch, extra = [pltpu.VMEM((wide, outer_width), F32)], {}
    if sent is not None:
        scratch += [
            pltpu.VMEM((rows, weights[sent][2]), BF16),
            pltpu.SemaphoreType.DMA((rows // rb,)),
            pltpu.SemaphoreType.DMA((rows // rb,)),
        ]
        extra = dict(collective_id=3, has_side_effects=True)
    return pl.pallas_call(
        partial(
            ffn_pull_kernel,
            parts=len(weights),
            experts=experts,
            capacity=capacity,
            shard=shard,
            sent=sent,
            outs=len(heads),
        ),
        grid=(rows // rb,),
        in_specs=[narrow, block, narrow, narrow, block, block, block]
        + [resident(gain.shape), resident((wide, LANES))]
        + [resident(slot_rows.shape), resident(dots.shape)]
        + [pl.BlockSpec((rb, h.shape[1]), lambda i: (i, 0)) for h in heads]
        + [
            pl.BlockSpec((wide, size), lambda i, j=j: (0, j), pipeline_mode=pl.Buffered(1))
            for _, j, size in weights
        ],
        out_specs=[block]
        + head_specs
        + [resident((8, wide)), resident((LANES, wide)), resident((wide, outer_width))],
        out_shape=[jax.ShapeDtypeStruct((rows, wide), BF16)]
        + [jax.ShapeDtypeStruct((rows, size), BF16) for _, _, size in weights]
        + [jax.ShapeDtypeStruct((8, wide), F32), jax.ShapeDtypeStruct((LANES, wide), F32)]
        + [jax.ShapeDtypeStruct((wide, outer_width), BF16)],
        scratch_shapes=scratch,
        cost_estimate=cost(6 * rows * wide * wide, 16 * rows * wide),
        compiler_params=pltpu.CompilerParams(vmem_limit_bytes=56 * 1024 * 1024, **extra),
        name="ffn_norm_pull",
    )(
        info,
        dx,
        chances,
        first,
        f,
        g,
        resid,
        gain,
        rm,
        slot_rows,
        dots,
        *heads,
        *[w for w, _, _ in weights],
    )


def outer_kernel(left_ref, *refs, parts):
    rights = refs[:parts]
    o_ref, acc_ref = refs[parts:]

    @pl.when(pl.program_id(0) == 0)
    def _():
        acc_ref[...] = jnp.zeros_like(acc_ref)

    left = left_ref[...].T
    at = 0
    for r in rights:
        width = r.shape[1]
        acc_ref[:, at : at + width] += dot(left, r[...])
        at += width

    @pl.when(pl.program_id(0) == pl.num_programs(0) - 1)
    def _():
        o_ref[...] = acc_ref[...].astype(BF16)


def outer(left, rights, rb=512):
    rows, wide = left.shape
    total = sum(r.shape[1] for r in rights)
    return pl.pallas_call(
        partial(outer_kernel, parts=len(rights)),
        grid=(rows // rb,),
        in_specs=[pl.BlockSpec((rb, wide), lambda i: (i, 0))]
        + [pl.BlockSpec((rb, r.shape[1]), lambda i: (i, 0)) for r in rights],
        out_specs=resident((wide, total)),
        out_shape=jax.ShapeDtypeStruct((wide, total), BF16),
        scratch_shapes=[pltpu.VMEM((wide, total), F32)],
        cost_estimate=cost(2 * rows * wide * total, 2 * rows * (wide + total)),
        name="outer_product",
    )(left, *rights)


def attn_pull_kernel(at_ref, x_ref, r_ref, gain_ref, *refs, groups):
    grads = refs[: 3 * groups]
    weights = refs[3 * groups : 3 * groups + 3]
    t_ref, sums_ref = refs[3 * groups + 3 :]
    del at_ref
    total = None
    for k in range(3):
        at = 0
        for j in range(groups):
            d = grads[k * groups + j]
            width = d.shape[1]
            part = dot_nt(d[...], weights[k][:, at : at + width])
            total = part if total is None else total + part
            at += width
    normal, rstd = normalized(x_ref[...].astype(F32))
    t = norm_pull(total, normal, rstd, gain_ref[...]) + r_ref[...].astype(F32)
    t_ref[...] = t.astype(t_ref.dtype)

    @pl.when(pl.program_id(0) == 0)
    def _():
        sums_ref[...] = jnp.zeros_like(sums_ref)

    sums_ref[0:1, :] += jnp.sum(total * normal, axis=0, keepdims=True)
    sums_ref[1:2, :] += jnp.sum(total, axis=0, keepdims=True)


def attn_pull(first_row, count, x, r, gain, grads, weights, out_type, rb=256):
    wide = x.shape[1]
    groups = len(grads) // 3

    def rows(width):
        return pl.BlockSpec((rb, width), lambda i, at: (at[0] + i, 0))

    return pl.pallas_call(
        partial(attn_pull_kernel, groups=groups),
        grid_spec=pltpu.PrefetchScalarGridSpec(
            num_scalar_prefetch=1,
            grid=(count // rb,),
            in_specs=[rows(wide), rows(wide), resident((1, wide))]
            + [rows(d.shape[1]) for d in grads]
            + [resident(w.shape) for w in weights],
            out_specs=[pl.BlockSpec((rb, wide), lambda i, at: (i, 0)), resident((8, wide))],
        ),
        out_shape=[
            jax.ShapeDtypeStruct((count, wide), out_type),
            jax.ShapeDtypeStruct((8, wide), F32),
        ],
        cost_estimate=cost(6 * count * wide * weights[0].shape[1], 10 * count * wide),
        name="attention_norm_pull",
    )((first_row // rb).astype(jnp.int32).reshape(1), x, r, gain, *grads, *weights)


def combine_kernel(
    at_ref, info_ref, y_ref, chance_ref, slot_ref, other_ref, own_ref, *, experts, capacity
):
    del at_ref
    place = info_ref[:, 0:1].astype(jnp.int32)
    here = info_ref[:, 1:2].astype(jnp.int32)
    chances = chance_ref[...]
    gate = jnp.sum(expert_hot(place, capacity, experts) * chances, axis=-1, keepdims=True)
    moe = unpacked(here, slot_ref) * (lane_of(chances, experts + 1) * gate)
    total = (lane_of(chances, experts) * y_ref[...].astype(F32) + moe).astype(BF16)
    first = pl.program_id(0) < pl.num_programs(0) // 2

    @pl.when(first)
    def _():
        other_ref[...] = total

    @pl.when(jnp.logical_not(first))
    def _():
        own_ref[...] = total


def combine(first_row, info, y, coef, slot_rows, experts, capacity, rb=512):
    rows, wide = y.shape
    half = rows // rb // 2

    def block(width):
        return pl.BlockSpec((rb, width), lambda i, at: (lax.rem(at[0] + half + i, 2 * half), 0))

    part = jax.ShapeDtypeStruct((rows // 2, wide), BF16)
    return pl.pallas_call(
        partial(combine_kernel, experts=experts, capacity=capacity),
        grid_spec=pltpu.PrefetchScalarGridSpec(
            num_scalar_prefetch=1,
            grid=(2 * half,),
            in_specs=[block(LANES), block(wide), block(LANES), resident(slot_rows.shape)],
            out_specs=[
                pl.BlockSpec((rb, wide), lambda i, _: (jnp.minimum(i, half - 1), 0)),
                pl.BlockSpec((rb, wide), lambda i, _: (jnp.maximum(i - half, 0), 0)),
            ],
        ),
        out_shape=[part, part],
        cost_estimate=cost(4 * rows * wide * wide, 8 * rows * wide),
        name="combine_nets",
    )((first_row // rb).astype(jnp.int32).reshape(1), info, y, coef, slot_rows)


class Halving:
    def __init__(self, total, gives, gots, send, recv, me, size, order):
        self.total, self.gives, self.gots = total, gives, gots
        self.send, self.recv, self.me, self.size = send, recv, me, size
        self.order = order
        self.rows = total.shape[0] // size

    def block(self, index):
        return pl.ds(pl.multiple_of(index * self.rows, self.rows), self.rows)

    def copy(self, s):
        return pltpu.make_async_remote_copy(
            src_ref=self.gives[s],
            dst_ref=self.gots[s],
            send_sem=self.send.at[s],
            recv_sem=self.recv.at[s],
            device_id={"ep": jnp.bitwise_xor(self.me, 1 << self.order[s])},
            device_id_type=pl.DeviceIdType.MESH,
        )

    def bit(self, s):
        return lax.rem(lax.div(self.me, 1 << self.order[s]), 2)

    def each(self, s, body):
        place = sum(1 for b in self.order[s:] if b < self.order[s])
        low = 1 << place

        def step(i, _):
            body(self.block(i), lax.div(i, low) * (2 * low) + lax.rem(i, low), low)
            return 0

        lax.fori_loop(0, self.size >> (s + 1), step, 0)

    def start(self, s):
        def give(rows, at, step):
            other = self.total[self.block(at + (1 - self.bit(s)) * step), :]
            self.gives[s][rows, :] = other.astype(BF16)

        self.each(s, give)
        self.copy(s).start()

    def finish(self, s):
        self.copy(s).wait()

        def keep(rows, at, step):
            kept = self.total[self.block(at + self.bit(s) * step), :]
            self.total[rows, :] = kept + self.gots[s][rows, :].astype(F32)

        self.each(s, keep)

    def step(self, s):
        self.finish(s)
        if s + 1 < len(self.order):
            self.start(s + 1)


class Rounds:
    def __init__(self, total, gives, gots, send, recv, me, tp_me):
        self.total, self.gives, self.gots = total, gives, gots
        self.send, self.recv, self.me, self.tp_me = send, recv, me, tp_me

    def copy(self, s):
        peer = {"tp": 1 - self.tp_me} if s == 0 else {"ep": jnp.bitwise_xor(self.me, 1 << (s - 1))}
        return pltpu.make_async_remote_copy(
            src_ref=self.gives[s],
            dst_ref=self.gots[s],
            send_sem=self.send.at[s],
            recv_sem=self.recv.at[s],
            device_id=peer,
            device_id_type=pl.DeviceIdType.MESH,
        )

    def start(self, s):
        self.gives[s][...] = self.total[...]
        self.copy(s).start()

    def finish(self, s):
        self.copy(s).wait()
        self.total[...] += self.gots[s][...]

    def step(self, s):
        self.finish(s)
        if s + 1 < len(self.gives):
            self.start(s + 1)


def tail_kernel(*refs, groups, size, rb, small_rows):
    refs = list(refs)

    def take(count):
        taken = refs[:count]
        del refs[:count]
        return taken

    x_hbm, r_hbm, a_hbm, out_hbm = take(4)
    grads_hbm = take(3 * groups)
    small_ref, gain_ref = take(2)
    weights = take(3)
    own_hbm, got_hbm, square_ref, outsum_ref, total_ref = take(5)
    xv, rv, av = take(3)
    grads = take(3 * groups)
    gov, acc_a, acc_b, goacc, give_rows, own_buf = take(6)
    steps = size.bit_length() - 1
    hops = steps + 1
    gives, gots = take(steps), take(steps)
    gives_b, gots_b = take(steps), take(steps)
    go_gives, go_gots = take(steps), take(steps)
    small_gives, small_gots = take(hops), take(hops)
    late_gives, late_gots = take(hops), take(hops)
    (
        load_sem,
        own_sem,
        row_send,
        row_recv,
        half_send,
        half_recv,
        half_send_b,
        half_recv_b,
        go_send,
        go_recv,
        small_send,
        small_recv,
        late_send,
        late_recv,
        out_sem,
        out_give,
        out_got,
    ) = refs
    me = lax.axis_index("ep")
    tp_me = lax.axis_index("tp")
    rows = x_hbm.shape[0]
    shard = rows // 2
    count = shard // rb

    out_load = pltpu.make_async_copy(out_hbm, gov, load_sem.at[0, 0])
    a_load = pltpu.make_async_copy(a_hbm, av, load_sem.at[1, 0])

    def loads(which, line):
        at = pl.ds(pl.multiple_of(which * shard, shard), shard)
        return [
            pltpu.make_async_copy(
                src.at[at, :], dst.at[at, :], load_sem.at[line, j + 1]
            )
            for j, (src, dst) in enumerate(zip([x_hbm, r_hbm, *grads_hbm], [xv, rv, *grads]))
        ]

    theirs_loads, own_loads = loads(1 - tp_me, 0), loads(tp_me, 1)
    for c in theirs_loads:
        c.start()
    out_load.start()
    for c in own_loads:
        c.start()
    a_load.start()

    barrier = pltpu.get_barrier_semaphore()
    mesh = pl.DeviceIdType.MESH
    pl.semaphore_signal(barrier, inc=1, device_id={"tp": 1 - tp_me}, device_id_type=mesh)
    for s in range(steps):
        pl.semaphore_signal(
            barrier, inc=1, device_id={"ep": jnp.bitwise_xor(me, 1 << s)}, device_id_type=mesh
        )
    pl.semaphore_wait(barrier, hops)

    order = list(range(steps))
    other_order = [0, 2, 1] + order[3:] if steps > 2 else order
    qkv = [
        Halving(acc_a, gives, gots, half_send, half_recv, me, size, order),
        Halving(acc_b, gives_b, gots_b, half_send_b, half_recv_b, me, size, other_order),
    ]
    go = Halving(goacc, go_gives, go_gots, go_send, go_recv, me, size, order)
    early = Rounds(
        total_ref.at[:small_rows, :], small_gives, small_gots, small_send, small_recv, me, tp_me
    )
    late = Rounds(
        total_ref.at[small_rows:, :], late_gives, late_gots, late_send, late_recv, me, tp_me
    )

    for c in theirs_loads:
        c.wait()

    total_ref[:small_rows, :] = small_ref[...]
    total_ref[small_rows:, :] = jnp.zeros((8, total_ref.shape[1]), F32)
    early.start(0)

    def pulled(at):
        total = None
        for k in range(3):
            col = 0
            for j in range(groups):
                d = grads[k * groups + j][at, :]
                width = d.shape[1]
                part = dot_nt(d, weights[k][:, col : col + width])
                total = part if total is None else total + part
                col += width
        normal, rstd = normalized(xv[at, :].astype(F32))
        total_ref[small_rows : small_rows + 1, :] += jnp.sum(total * normal, axis=0, keepdims=True)
        total_ref[small_rows + 1 : small_rows + 2, :] += jnp.sum(total, axis=0, keepdims=True)
        return norm_pull(total, normal, rstd, gain_ref[0:1, :]) + rv[at, :].astype(F32)

    def row_copy(b):
        at = pl.ds(pl.multiple_of(b * rb, rb), rb)
        return pltpu.make_async_remote_copy(
            src_ref=give_rows.at[at, :],
            dst_ref=got_hbm.at[at, :],
            send_sem=row_send.at[b],
            recv_sem=row_recv.at[b],
            device_id={"tp": 1 - tp_me},
            device_id_type=mesh,
        )

    def theirs(b, _):
        at = pl.ds(pl.multiple_of((1 - tp_me) * shard + b * rb, rb), rb)
        give_rows[pl.ds(pl.multiple_of(b * rb, rb), rb), :] = pulled(at).astype(BF16)
        row_copy(b).start()
        return 0

    lax.fori_loop(0, count // 2, theirs, 0)
    out_load.wait()
    goacc[...] = gov[...].astype(F32)
    go.start(0)
    early.step(0)
    for c in own_loads + [a_load]:
        c.wait()
    cut = len(grads) // 2
    for acc in (acc_a, acc_b):
        acc[...] = jnp.zeros_like(acc)

    for acc, some, chain in ((acc_a, grads[:cut], qkv[0]), (acc_b, grads[cut:], qkv[1])):

        def outer_step(b, _, acc=acc, some=some):
            at = pl.ds(pl.multiple_of(b * 512, 512), 512)
            left = av[at, :].T
            col = 0
            for g in some:
                width = g.shape[1]
                acc[:, col : col + width] += dot(left, g[at, :])
                col += width
            return 0

        lax.fori_loop(0, rows // 512, outer_step, 0)
        chain.start(0)
        if chain is qkv[0]:
            go.step(0)
            early.step(1)
    qkv[0].step(0)
    early.step(2)
    lax.fori_loop(count // 2, count, theirs, 0)

    def own_copy(b):
        at = pl.ds(pl.multiple_of(b * rb, rb), rb)
        return pltpu.make_async_copy(own_buf.at[at, :], own_hbm.at[at, :], own_sem.at[b])

    def own_step(b, _):
        at = pl.ds(pl.multiple_of(tp_me * shard + b * rb, rb), rb)
        own_buf[pl.ds(pl.multiple_of(b * rb, rb), rb), :] = pulled(at)
        own_copy(b).start()
        return 0

    qkv[1].step(0)
    early.step(3)
    lax.fori_loop(0, count // 2, own_step, 0)
    go.step(1)
    qkv[0].step(1)
    for s in range(4, hops):
        early.step(s)
    lax.fori_loop(count // 2, count, own_step, 0)

    for s in range(hops):
        late.start(s)
        if s + 2 < steps:
            go.step(s + 2)
        if s == 1:
            qkv[1].step(1)
            qkv[0].step(2)
        if s == 2:
            qkv[1].step(2)
        late.finish(s)
        if s == max(0, steps - 3):
            own_width = outsum_ref.shape[1]
            out_give[...] = goacc[: goacc.shape[0] // size, own_width:].astype(BF16)
            out_copy = pltpu.make_async_remote_copy(
                src_ref=out_give,
                dst_ref=out_got,
                send_sem=out_sem.at[0],
                recv_sem=out_sem.at[1],
                device_id={"tp": 1 - tp_me},
                device_id_type=mesh,
            )
            out_copy.start()
    for chain in qkv:
        for s in range(3, steps):
            chain.step(s)
    col = 0
    for acc in (acc_a, acc_b):
        square_ref[:, col : col + acc.shape[1]] = acc[: acc.shape[0] // size, :]
        col += acc.shape[1]
    out_copy.wait()
    outsum_ref[...] = goacc[: goacc.shape[0] // size, :own_width] + out_got[...].astype(F32)
    for b in range(count):
        own_copy(b).wait()
        row_copy(b).wait()


def tail(x, r, a, out_part, grads, small, gain, weights, size, rb=256):
    rows, wide = x.shape
    shard = rows // 2
    groups = len(grads) // 3
    total = sum(g.shape[1] for g in grads)
    out_width = out_part.shape[1]
    small_rows = small.shape[0]
    steps = size.bit_length() - 1
    kept = wide // size
    anywhere = pl.BlockSpec(memory_space=pl.ANY)
    vmem = pl.BlockSpec(memory_space=pltpu.VMEM)

    def halves(width):
        return [pltpu.VMEM((wide >> (s + 1), width), BF16) for s in range(steps)]

    return pl.pallas_call(
        partial(tail_kernel, groups=groups, size=size, rb=rb, small_rows=small_rows),
        in_specs=[anywhere] * (4 + 3 * groups) + [vmem] * 5,
        out_specs=[anywhere, anywhere, vmem, vmem, vmem],
        out_shape=[
            jax.ShapeDtypeStruct((shard, wide), F32),
            jax.ShapeDtypeStruct((shard, wide), BF16),
            jax.ShapeDtypeStruct((kept, total), F32),
            jax.ShapeDtypeStruct((kept, out_width // 2), F32),
            jax.ShapeDtypeStruct((small_rows + 8, wide), F32),
        ],
        scratch_shapes=[pltpu.VMEM((rows, wide), BF16)] * 3
        + [pltpu.VMEM(g.shape, BF16) for g in grads]
        + [
            pltpu.VMEM((wide, out_width), BF16),
            pltpu.VMEM((wide, total // 2), F32),
            pltpu.VMEM((wide, total // 2), F32),
            pltpu.VMEM((wide, out_width), F32),
            pltpu.VMEM((shard, wide), BF16),
            pltpu.VMEM((shard, wide), F32),
        ]
        + halves(total // 2) * 4
        + halves(out_width) * 2
        + [pltpu.VMEM((small_rows, wide), F32)] * (2 * (steps + 1))
        + [pltpu.VMEM((8, wide), F32)] * (2 * (steps + 1))
        + [
            pltpu.SemaphoreType.DMA((2, 3 + 3 * groups)),
            pltpu.SemaphoreType.DMA((shard // rb,)),
            pltpu.SemaphoreType.DMA((shard // rb,)),
            pltpu.SemaphoreType.DMA((shard // rb,)),
        ]
        + [pltpu.SemaphoreType.DMA((steps,))] * 6
        + [pltpu.SemaphoreType.DMA((steps + 1,))] * 4
        + [
            pltpu.SemaphoreType.DMA((2,)),
            pltpu.VMEM((kept, out_width // 2), BF16),
            pltpu.VMEM((kept, out_width // 2), BF16),
        ],
        cost_estimate=cost(12 * rows * wide * total // 3, 16 * rows * wide),
        compiler_params=pltpu.CompilerParams(
            vmem_limit_bytes=BIG_VMEM, collective_id=1, has_side_effects=True
        ),
        name="backward_tail",
    )(x, r, a, out_part, *grads, small, gain, *weights)


def results_kernel(
    at_ref,
    len_ref,
    own_ref,
    got_ref,
    resid_ref,
    mine_ref,
    theirs_ref,
    square_ref,
    small_ref,
    h_ref,
    r_ref,
    token_ref,
    block_ref,
    q_ref,
    k_ref,
    v_ref,
    gh_ref,
    gr_ref,
    router_ref,
    mix_ref,
    gain1_ref,
    bias1_ref,
    gain2_ref,
    bias2_ref,
    *,
    length,
):
    token_ref[...] = own_ref[...] + got_ref[...].astype(F32)
    size = own_ref.shape[0]
    position = (at_ref[0] + pl.program_id(0)) * size + lax.broadcasted_iota(jnp.int32, own_ref.shape, 0)
    live = None
    for s in range(len_ref.shape[0]):
        inside = (position >= s * length) & (position < s * length + len_ref[s])
        live = inside if live is None else live | inside
    nets_sum = mine_ref[...].astype(F32) + theirs_ref[...].astype(F32)
    block_ref[...] = jnp.where(live, resid_ref[...] + nets_sum, 0.0).astype(BF16)

    @pl.when(pl.program_id(0) == 0)
    def _():
        width = q_ref.shape[1]
        for j, ref in enumerate((q_ref, k_ref, v_ref)):
            ref[...] = square_ref[:, j * width : (j + 1) * width]
        gh_ref[...] = h_ref[...].astype(F32)
        gr_ref[...] = r_ref[...].astype(F32)
        experts = router_ref.shape[0]
        router_ref[...] = small_ref[8 : 8 + experts, :]
        mix_ref[...] = small_ref[8 + experts : 10 + experts, :]
        end = small_ref.shape[0] - 8
        for ref, at in ((gain1_ref, end), (bias1_ref, end + 1), (gain2_ref, 0), (bias2_ref, 1)):
            ref[...] = small_ref[at : at + 1, :]


def results(first_row, lengths, own, got, resid, weighted, theirs, square, small, gh, gr, experts, rb=256):
    rows, wide = own.shape
    kept, width = square.shape[0], square.shape[1] // 3
    block = pl.BlockSpec((rb, wide), lambda i, *_: (i, 0))
    shifted = pl.BlockSpec((rb, wide), lambda i, at, _: (at[0] + i, 0))
    shapes = [(kept, width)] * 3 + [gh.shape, gr.shape, (experts, wide), (2, wide)] + [(1, wide)] * 4
    return pl.pallas_call(
        partial(results_kernel, length=resid.shape[0] // lengths.shape[0]),
        grid_spec=pltpu.PrefetchScalarGridSpec(
            num_scalar_prefetch=2,
            grid=(rows // rb,),
            in_specs=[block, block, shifted, block, block]
            + [resident(v.shape) for v in (square, small, gh, gr)],
            out_specs=[block, block] + [resident(s) for s in shapes],
        ),
        out_shape=[jax.ShapeDtypeStruct((rows, wide), F32), jax.ShapeDtypeStruct((rows, wide), BF16)]
        + [jax.ShapeDtypeStruct(s, F32) for s in shapes],
        cost_estimate=cost(rows * wide, 22 * rows * wide),
        name="results",
    )(
        (first_row // rb).astype(jnp.int32).reshape(1),
        lengths,
        own,
        got,
        resid,
        weighted,
        theirs,
        square,
        small,
        gh,
        gr,
    )


def on_device(
    sizes,
    tokens,
    out_grad,
    lengths,
    expert_ids,
    w_query,
    w_key,
    w_value,
    w_output,
    w_hidden,
    w_return,
    router,
    mix_weight,
    gain_attn,
    bias_attn,
    gain_ffn,
    bias_ffn,
    expert_in,
    expert_out,
):
    tp, ep = sizes
    shard_rows = out_grad.shape[0]
    all_rows = tokens.shape[0]
    model_width = tokens.shape[1]
    experts = router.shape[1]
    capacity = all_rows // experts
    seq_count = lengths.shape[0]
    seq_len = all_rows // seq_count
    local_width = w_query.shape[1]
    local_heads = local_width // HEAD_DIM
    pairs = local_heads // 2
    splits = 2 if pairs % 2 == 0 else 1
    each = pairs // splits
    tp_index = lax.axis_index("tp")
    ep_index = lax.axis_index("ep")
    first_row = tp_index * shard_rows
    swap = [(0, 1), (1, 0)]

    def shard_of(values, axis=0):
        return lax.dynamic_slice_in_dim(values, first_row, shard_rows, axis)

    def swapped(values):
        return lax.ppermute(values, "tp", swap)

    def exchange(values):
        return lax.all_to_all(values, "ep", split_axis=0, concat_axis=0, tiled=True)

    def after(values, *others):
        return lax.optimization_barrier((values, others))[0]

    def summed_over(values, axis, size):
        step = 1
        while step < size:
            values = values + lax.ppermute(values, axis, [(i, i ^ step) for i in range(size)])
            step *= 2
        return values

    def over_sequences(values):
        return lax.psum_scatter(values, "ep", scatter_dimension=0, tiled=True)

    positions = jnp.arange(all_rows)
    seq_index = positions // seq_len
    row_limit = jnp.sum(
        jnp.where(seq_index[:, None] == jnp.arange(seq_count)[None, :], lengths[None, :], 0), axis=1
    )
    live_all = positions % seq_len < row_limit
    slot_count = experts * capacity
    blocks = (experts, capacity, model_width)

    rm = jnp.pad(
        jnp.concatenate([router, mix_weight], axis=1), ((0, 0), (0, LANES - experts - 2))
    )
    norms = jnp.concatenate([gain_attn, bias_attn, gain_ffn, bias_ffn]).astype(F32)
    norms = norms.reshape(4, model_width)
    projections = (w_query, w_key, w_value)
    if tp == 2:
        (
            attn_in,
            projected,
            heads,
            others,
            w_other,
            grad_all,
            resid,
            ffn_in,
            chances,
            packed,
            grad_rows,
            info,
            lse,
        ) = front(
            tokens,
            out_grad,
            (*projections, w_output),
            lengths,
            norms,
            rm,
            expert_ids[None, :],
            ep,
            experts,
            capacity,
        )
        all_heads = [heads, others]
        wide_weights = [(w, s, each * PAIR) for w in (w_output, w_other) for s in range(splits)]
    else:
        one_hot = (expert_ids[:, None] == jnp.arange(experts)[None, :]) & live_all[:, None]
        routed = one_hot.astype(F32)
        slots = jnp.sum((jnp.cumsum(routed, axis=0) - routed) * routed, axis=1).astype(jnp.int32)
        sound = live_all & (slots < capacity)
        place = jnp.where(sound, expert_ids * capacity + slots, -1)
        place_row = place[None, :]
        info = jnp.broadcast_to(place[:, None], (all_rows, LANES)).astype(F32)
        live_grad = jnp.where(shard_of(live_all)[:, None], out_grad, jnp.zeros_like(out_grad))
        w_all = lax.all_gather(w_output, "tp", axis=1, tiled=True)
        grad_all = lax.all_gather(live_grad, "tp", axis=0, tiled=True)
        grad_rows = exchange(pack(place_row, grad_all, slot_count).reshape(blocks))
        attn_in, projected = norm_project(tokens, norms[0:1], norms[1:2], projections)
        heads, lse = attention_forward(projected, seq_count, local_heads, 0, pairs)
        all_heads = [lax.all_gather(heads, "tp", axis=1, tiled=True)]
        wide_weights = [(w_all, 0, model_width)]
        resid, ffn_in, chances = output_norm(
            tokens, norms[2:3], norms[3:4], rm, all_heads, [(w_all, 0)], experts
        )
        packed = pack(place_row, ffn_in, slot_count)

    sel = (jnp.arange(LANES) == ep_index).astype(F32)[None, :]
    (
        dense,
        dense_pull,
        first_dot,
        grad_hidden,
        grad_return,
        grad_expert_in,
        grad_expert_out,
        _,
        sums_back,
        _,
        _,
        pulls,
        dots,
        _,
    ) = nets(
        ffn_in,
        grad_all,
        packed.reshape(blocks),
        grad_rows,
        sel,
        rm,
        (w_hidden, w_return),
        (expert_in[0], expert_out[0]),
    )
    returned = exchange(sums_back).reshape(-1, model_width)
    pulls = pulls.reshape(-1, model_width)
    dots = dots[:, 0, :]
    part, *rest = ffn_pull(
        info,
        dense_pull,
        chances,
        first_dot,
        ffn_in,
        grad_all,
        resid,
        norms,
        rm,
        pulls,
        dots,
        all_heads,
        wide_weights,
        experts,
        shard_rows,
        sent=splits if tp == 2 else None,
    )
    *head_parts, ffn_sums, rm_sums, out_part = rest
    if tp == 2:
        head_grads = [
            [m, o if s == 0 else swapped(o)]
            for s, (m, o) in enumerate(zip(head_parts[:splits], head_parts[splits:]))
        ]
    else:
        local = lax.psum_scatter(head_parts[0], "tp", scatter_dimension=1, tiled=True)
        head_grads = [
            [local[:, s * each * PAIR : (s + 1) * each * PAIR]] for s in range(splits)
        ]
    grad_hidden = over_sequences(grad_hidden)
    grad_return = over_sequences(grad_return)

    qkv = []
    expert_grads = [grad_expert_in, grad_expert_out]
    for s in range(splits):
        if s == splits - 1:
            if qkv:
                dense, qkv[-1], head_grads[s] = lax.optimization_barrier(
                    (dense, qkv[-1], head_grads[s])
                )
            weighted = combine(
                first_row if tp == 2 else jnp.zeros((), jnp.int32), info, dense, chances, returned, experts, capacity
            )
            projected, weighted = lax.optimization_barrier((projected, weighted))
        *grads3, expert_grads[s] = attention_backward(
            projected,
            heads,
            head_grads[s],
            lse,
            seq_count,
            local_heads,
            s * each,
            each,
            (expert_grads[s],),
        )
        qkv.append(grads3)
    flat = [qkv[s][k] for k in range(3) for s in range(splits)]
    rows_kept = -(-(experts + 2) // 8) * 8
    small = jnp.concatenate([ffn_sums, rm_sums[:rows_kept]], axis=0)
    if tp == 2:
        theirs = swapped(weighted[0])
        own_part, got, square, grad_output, small = tail(
            tokens,
            part,
            attn_in,
            out_part,
            flat,
            small,
            norms,
            projections,
            ep,
        )
        (
            token_grad,
            block_out,
            grad_query,
            grad_key,
            grad_value,
            grad_hidden,
            grad_return,
            grad_router,
            grad_mix,
            *vectors,
        ) = results(
            first_row,
            lengths,
            own_part,
            got,
            resid,
            weighted[1],
            theirs,
            square,
            small,
            grad_hidden,
            grad_return,
            experts,
        )
        vectors = [v[0] for v in vectors]
    else:
        whole, attn_sums = attn_pull(
            jnp.zeros((), jnp.int32), all_rows, tokens, part, norms[0:1], flat, projections, BF16
        )
        token_grad = lax.psum_scatter(whole, "tp", scatter_dimension=0, tiled=True).astype(F32)
        weighted = jnp.concatenate(weighted[::-1], axis=0)
        summed = lax.psum_scatter(weighted, "tp", scatter_dimension=0, tiled=True).astype(F32)
        block_out = jnp.where(shard_of(live_all)[:, None], shard_of(resid) + summed, 0.0).astype(BF16)
        square = over_sequences(outer(attn_in, flat))
        grad_output = lax.psum_scatter(
            over_sequences(out_part).astype(BF16), "tp", scatter_dimension=1, tiled=True
        ).astype(F32)
        small = summed_over(summed_over(small, "tp", tp), "ep", ep)
        attn_sums = summed_over(summed_over(attn_sums, "tp", tp), "ep", ep)
        grad_query, grad_key, grad_value = jnp.split(square.astype(F32), 3, axis=1)
        grad_hidden, grad_return = grad_hidden.astype(F32), grad_return.astype(F32)
        grad_router, grad_mix = small[8 : 8 + experts], small[8 + experts : 10 + experts]
        vectors = [attn_sums[0], attn_sums[1], small[0], small[1]]
    return (
        block_out,
        token_grad,
        grad_query,
        grad_key,
        grad_value,
        grad_output,
        grad_hidden,
        grad_return,
        grad_router.T,
        grad_mix.T,
        *vectors,
        expert_grads[0][None],
        expert_grads[1][None],
    )


def solution(mesh):
    in_specs = (
        P("ep", None),
        P(("ep", "tp"), None),
        P("ep"),
        P("ep"),
        P(None, "tp"),
        P(None, "tp"),
        P(None, "tp"),
        P(None, "tp"),
        P(None, "tp"),
        P(None, "tp"),
        P(),
        P(),
        P(),
        P(),
        P(),
        P(),
        P("ep", None, "tp"),
        P("ep", None, "tp"),
    )
    out_specs = (
        P(("ep", "tp"), None),
        P(("ep", "tp"), None),
        P("ep", "tp"),
        P("ep", "tp"),
        P("ep", "tp"),
        P("ep", "tp"),
        P("ep", "tp"),
        P("ep", "tp"),
        P(),
        P(),
        P(),
        P(),
        P(),
        P(),
        P("ep", None, "tp"),
        P("ep", None, "tp"),
    )
    return jax.shard_map(
        partial(on_device, (mesh.shape["tp"], mesh.shape["ep"])),
        mesh=mesh,
        in_specs=in_specs,
        out_specs=out_specs,
        check_vma=False,
    )
```
